32 devices in a mesh: dp: 8 (over z, x), sub: 4 (over y, core).
Axes of the slice: x: 2, y: 2, z: 4, core: 2. Of those that a mesh axis runs over, the one named last changes fastest.
Arguments:
- big_maps: bfloat16 [256, 2, 7, 7, 2048], P(('dp', 'sub')), may hold values from -6 to 6
- small_maps: bfloat16 [256, 6, 3, 3, 2048], P(('dp', 'sub')), may hold values from -6 to 6
- live_counts: int32 [32], P(('dp', 'sub')), may hold values from 1 to 8, as said below
- queue: bfloat16 [2, 30720, 128], P(None, ('dp', 'sub')), may hold values from -0.5 to 0.5
- bottleneck_outer: float32 [2, 2048, 512], P(None, 'dp'), may hold values from -6 to 6
- bottleneck_inner: float32 [9, 512, 512], P(None, 'dp'), may hold values from -6 to 6
- proj_hidden: float32 [2048, 2048], P('dp'), may hold values from -6 to 6
- proj_out: float32 [2048, 128], P('dp'), may hold values from -6 to 6
- prototypes: float32 [3000, 128], replicated, may hold values from -6 to 6
- norm_params: float32 [2, 5120], replicated, may hold values from 0.1 to 1.9
- mom_outer: float32 [2, 2048, 512], P(None, 'dp'), may hold values from -6 to 6
- mom_inner: float32 [9, 512, 512], P(None, 'dp'), may hold values from -6 to 6
- mom_hidden: float32 [2048, 2048], P('dp'), may hold values from -6 to 6
- mom_out: float32 [2048, 128], P('dp'), may hold values from -6 to 6
- mom_protos: float32 [3000, 128], replicated, may hold values from -6 to 6
- mom_norms: float32 [2, 5120], replicated, may hold values from -6 to 6
- avg_outer: float32 [2, 2048, 512], P(None, 'dp'), may hold values from -6 to 6
- avg_inner: float32 [9, 512, 512], P(None, 'dp'), may hold values from -6 to 6
- avg_hidden: float32 [2048, 2048], P('dp'), may hold values from -6 to 6
- avg_out: float32 [2048, 128], P('dp'), may hold values from -6 to 6
- avg_protos: float32 [3000, 128], replicated, may hold values from -6 to 6
- avg_norms: float32 [2, 5120], replicated, may hold values from 0.1 to 1.9
Outputs:
- loss_sum: float32 [], replicated
- live_total: float32 [], replicated
- new_outer: float32 [2, 2048, 512], P(None, 'dp')
- new_inner: float32 [9, 512, 512], P(None, 'dp')
- new_hidden: float32 [2048, 2048], P('dp')
- new_out: float32 [2048, 128], P('dp')
- new_protos: float32 [3000, 128], replicated
- new_norms: float32 [2, 5120], replicated
- next_mom_outer: float32 [2, 2048, 512], P(None, 'dp')
- next_mom_inner: float32 [9, 512, 512], P(None, 'dp')
- next_mom_hidden: float32 [2048, 2048], P('dp')
- next_mom_out: float32 [2048, 128], P('dp')
- next_mom_protos: float32 [3000, 128], replicated
- next_mom_norms: float32 [2, 5120], replicated
- next_avg_outer: float32 [2, 2048, 512], P(None, 'dp')
- next_avg_inner: float32 [9, 512, 512], P(None, 'dp')
- next_avg_hidden: float32 [2048, 2048], P('dp')
- next_avg_out: float32 [2048, 128], P('dp')
- next_avg_protos: float32 [3000, 128], replicated
- next_avg_norms: float32 [2, 5120], replicated
- copy_outer: bfloat16 [2, 2048, 512], P(None, 'dp')
- copy_inner: bfloat16 [9, 512, 512], P(None, 'dp')
- copy_hidden: bfloat16 [2048, 2048], P('dp')
- copy_out: bfloat16 [2048, 128], P('dp')
The draws below stay inside these ranges and needn't reach their ends.
Inputs may be any that keep to these rules, and one draw needn't show every extreme that they name: live_counts[d] is the number of live images on device d, which are its first slots; the last device has exactly 8.
All inputs are finite; a program needn't handle non-finite values.
Results may differ from the reference program's by a relative error of at most 0.02.
Values may be sent and summed in bfloat16 or wider, within the bound.
A program may use at most 448 MiB of HBM per device.

```python
import jax
import jax.numpy as jnp
from jax import lax

C = 2048
MID = 512
PH = 2048
OUTD = 128
PROTOS = 3000
NBIG = 2
NSMALL = 6
BIG = 7
SMALL = 3
TAPS = 9
ITERS = 3
IMG_DEV = 8
QUEUE_DEV = 960
GROUP = 32
IMAGES = 256
QUEUE = 30720
NORMS = 5120
N_DP = 8
N_SUB = 4


def draw_live_counts(key, part):
    devices = N_DP * N_SUB
    span = 64
    index = jnp.arange(devices, dtype=jnp.int32)
    data_pos = index // N_SUB * span // (N_DP - 1)
    sub_pos = index % N_SUB * span // (N_SUB - 1)
    jitter = jax.random.randint(jax.random.fold_in(key, 17), (devices,), 0, span)
    counts = 1 + ((IMG_DEV - 1) * (data_pos + sub_pos) + jitter) // (2 * span)
    counts = jnp.minimum(counts, IMG_DEV)
    return counts.astype(jnp.int32)


def block_levels(rng, shape, cuts, smallest, high):
    gain, own = 1.0, jax.random.fold_in(rng, 6)
    for dim, blocks in cuts:
        steps = jnp.exp(jax.random.uniform(jax.random.fold_in(own, dim), (blocks,), jnp.float32, smallest / len(cuts), high / len(cuts)))
        gain = gain * jnp.repeat(steps, shape[dim] // blocks).reshape([-1 if axis == dim else 1 for axis in range(len(shape))])
    return gain


def noise(key, shape, scale, reach, split=(), held_as=jnp.bfloat16):
    drawn = scale * jax.random.normal(key, shape, jnp.float32)
    if split:
        drawn = drawn * block_levels(key, shape, split, -0.22, 0.18)
    return jnp.clip(drawn, -reach, reach).astype(held_as)


def setup_inputs(seed: int = 0) -> dict:
    arg_keys = jax.random.split(jax.random.key(seed), 23)
    return {
        "big_maps": noise(arg_keys[0], (IMAGES, NBIG, BIG, BIG, C), 1.0, 6.0, ((0, 32),)),
        "small_maps": noise(arg_keys[1], (IMAGES, NSMALL, SMALL, SMALL, C), 1.0, 6.0, ((0, 32),)),
        "live_counts": draw_live_counts(jax.random.fold_in(arg_keys[22], 71), 0),
        "queue": noise(arg_keys[3], (NBIG, QUEUE, OUTD), OUTD ** -0.5, 0.5, ((1, 32),)),
        "bottleneck_outer": noise(arg_keys[4], (2, C, MID), 1.0, 6.0, ((1, 8),), jnp.float32),
        "bottleneck_inner": noise(arg_keys[5], (TAPS, MID, MID), 1.0, 6.0, ((1, 8),), jnp.float32),
        "proj_hidden": noise(arg_keys[6], (C, PH), 1.0, 6.0, ((0, 8),), jnp.float32),
        "proj_out": noise(arg_keys[7], (PH, OUTD), 1.0, 6.0, ((0, 8),), jnp.float32),
        "prototypes": noise(arg_keys[8], (PROTOS, OUTD), 1.0, 6.0, (), jnp.float32),
        "norm_params": jnp.clip(1.0 + 0.18 * jax.random.normal(arg_keys[9], (2, NORMS), jnp.float32), 0.1, 1.9),
        "mom_outer": noise(arg_keys[10], (2, C, MID), 0.5, 6.0, ((1, 8),), jnp.float32),
        "mom_inner": noise(arg_keys[11], (TAPS, MID, MID), 0.5, 6.0, ((1, 8),), jnp.float32),
        "mom_hidden": noise(arg_keys[12], (C, PH), 0.5, 6.0, ((0, 8),), jnp.float32),
        "mom_out": noise(arg_keys[13], (PH, OUTD), 0.5, 6.0, ((0, 8),), jnp.float32),
        "mom_protos": noise(arg_keys[14], (PROTOS, OUTD), 0.5, 6.0, (), jnp.float32),
        "mom_norms": noise(arg_keys[15], (2, NORMS), 0.5, 6.0, (), jnp.float32),
        "avg_outer": noise(arg_keys[16], (2, C, MID), 1.0, 6.0, ((1, 8),), jnp.float32),
        "avg_inner": noise(arg_keys[17], (TAPS, MID, MID), 1.0, 6.0, ((1, 8),), jnp.float32),
        "avg_hidden": noise(arg_keys[18], (C, PH), 1.0, 6.0, ((0, 8),), jnp.float32),
        "avg_out": noise(arg_keys[19], (PH, OUTD), 1.0, 6.0, ((0, 8),), jnp.float32),
        "avg_protos": noise(arg_keys[20], (PROTOS, OUTD), 1.0, 6.0, (), jnp.float32),
        "avg_norms": jnp.clip(1.0 + 0.18 * jax.random.normal(arg_keys[21], (2, NORMS), jnp.float32), 0.1, 1.9),
    }


sink_temp = 0.05
softmax_temp = 0.1
norm_eps = 1e-05
unit_eps = 1e-12
trust_rate = 0.5
learn_rate = 1.0
momentum_rate = 0.5
average_rate = 0.5

@jax.custom_vjp
def low(v):
    return lax.optimization_barrier(v.astype(jnp.bfloat16)).astype(jnp.float32)

@jax.custom_vjp
def low_back(v):
    return v

def low_keep(v):
    return (low(v), None)

def low_pass(kept, grad):
    return (grad,)

def back_keep(v):
    return (v, None)

def back_low(kept, grad):
    return (low(grad),)
low.defvjp(low_keep, low_pass)
low_back.defvjp(back_keep, back_low)

def matmul(left, right):
    return jnp.dot(left, right, precision=lax.Precision.HIGHEST, preferred_element_type=jnp.float32)

def patches(active, crop_count, extent):
    spatial = active.reshape(crop_count, extent, extent, active.shape[-1])
    padded = jnp.pad(spatial, ((0, 0), (1, 1), (1, 1), (0, 0)))
    pieces = [padded[:, row_off:row_off + extent, col_off:col_off + extent, :] for row_off in range(3) for col_off in range(3)]
    return jnp.concatenate(pieces, axis=-1).reshape(crop_count * extent * extent, -1)

def unit_rows(values):
    return values * lax.rsqrt(lax.optimization_barrier(jnp.sum(values * values, 1, keepdims=True)) + unit_eps)

def normed(values, row_mask, count_all, gain_vec, bias_vec):
    row_mean = lax.optimization_barrier(jnp.sum(values * row_mask[:, None], 0)) / count_all
    spread = lax.optimization_barrier(jnp.sum(values * values * row_mask[:, None], 0)) / count_all - row_mean * row_mean
    normal = (values - row_mean) * lax.rsqrt(spread + norm_eps)
    return gain_vec * normal + bias_vec

def forward(params, big_group, small_group, image_mask):
    outer_w, inner_w, hidden_w, out_w, proto_w, norm_w = params
    first_w = low(outer_w[0])
    last_w = low(outer_w[1])
    middle_w = low(inner_w).reshape(TAPS * MID, MID)
    hidden_low = low(hidden_w)
    out_low = low(out_w)
    images = big_group.shape[0]
    per_image = NBIG * BIG * BIG + NSMALL * SMALL * SMALL
    big_rows = images * NBIG * BIG * BIG
    inputs = jnp.concatenate([big_group.reshape(-1, C), small_group.reshape(-1, C)], 0)
    row_mask = jnp.concatenate([jnp.repeat(image_mask, NBIG * BIG * BIG), jnp.repeat(image_mask, NSMALL * SMALL * SMALL)])
    live_all = jnp.sum(image_mask)
    bounds = [0, MID, 2 * MID, 2 * MID + C, 2 * MID + C + PH]
    gains = [norm_w[0, bounds[layer_idx]:bounds[layer_idx + 1]] for layer_idx in range(4)]
    biases = [norm_w[1, bounds[layer_idx]:bounds[layer_idx + 1]] for layer_idx in range(4)]
    hidden_one = low_back(matmul(inputs, first_w))
    act_one = low(jax.nn.silu(normed(hidden_one, row_mask, live_all * per_image, gains[0], biases[0])))
    columns = jnp.concatenate([patches(act_one[:big_rows], images * NBIG, BIG), patches(act_one[big_rows:], images * NSMALL, SMALL)], 0)
    hidden_two = low_back(matmul(columns, middle_w))
    act_two = low(jax.nn.silu(normed(hidden_two, row_mask, live_all * per_image, gains[1], biases[1])))
    hidden_three = low_back(matmul(act_two, last_w.T))
    output = jax.nn.silu(normed(hidden_three, row_mask, live_all * per_image, gains[2], biases[2]) + inputs)
    big_part = lax.optimization_barrier(jnp.mean(output[:big_rows].reshape(images, NBIG, BIG * BIG, C), 2))
    small_part = lax.optimization_barrier(jnp.mean(output[big_rows:].reshape(images, NSMALL, SMALL * SMALL, C), 2))
    pooled = low(jnp.concatenate([big_part, small_part], 1).reshape(-1, C))
    crop_mask = jnp.repeat(image_mask, NBIG + NSMALL)
    proj_pre = low_back(matmul(pooled, hidden_low))
    act_four = low(jax.nn.silu(normed(proj_pre, crop_mask, live_all * (NBIG + NSMALL), gains[3], biases[3])))
    embedding = low_back(matmul(act_four, out_low))
    unit_low = low(unit_rows(embedding))
    centers = low(unit_rows(proto_w))
    scores = low_back(matmul(unit_low, centers.T))
    return scores.reshape(images, NBIG + NSMALL, PROTOS)

def codes_of(big_scores, queue_scores, image_mask):
    shares = jnp.exp(big_scores / sink_temp) * image_mask[None, :, None]
    others = jnp.exp(queue_scores / sink_temp)
    for iteration in range(ITERS):
        totals = lax.optimization_barrier(jnp.sum(shares, 1)) + lax.optimization_barrier(jnp.sum(others, 1))
        shares = shares / totals[:, None, :]
        others = others / totals[:, None, :]
        shares = shares / (lax.optimization_barrier(jnp.sum(shares, 2, keepdims=True)) + (1.0 - image_mask)[None, :, None])
        others = others / lax.optimization_barrier(jnp.sum(others, 2, keepdims=True))
    return jnp.transpose(shares, (1, 0, 2))

def loss_of_codes(scores, code_rows):
    log_probs = jax.nn.log_softmax(scores / softmax_temp, axis=-1)
    every_crop = lax.optimization_barrier(jnp.sum(log_probs, 1))
    return -jnp.sum(code_rows * (every_crop[:, None, :] - log_probs[:, :NBIG])) / (NBIG * (NBIG + NSMALL - 1))

def ratio_of(weight, gradient, over_axes):
    return trust_rate * jnp.sqrt(lax.optimization_barrier(jnp.sum(weight * weight, over_axes, keepdims=True))) / (jnp.sqrt(lax.optimization_barrier(jnp.sum(gradient * gradient, over_axes, keepdims=True))) + 1e-12)

def advance(weight, gradient, moment, average, trust):
    step_now = trust * gradient
    moment_new = momentum_rate * moment + step_now
    weight_new = weight - learn_rate * (step_now + momentum_rate * moment_new)
    average_new = average_rate * average + (1.0 - average_rate) * weight_new
    return (weight_new, moment_new, average_new)

def reference(big_maps, small_maps, live_counts, queue, bottleneck_outer, bottleneck_inner, proj_hidden, proj_out, prototypes, norm_params, mom_outer, mom_inner, mom_hidden, mom_out, mom_protos, mom_norms, avg_outer, avg_inner, avg_hidden, avg_out, avg_protos, avg_norms):
    big_all = big_maps.astype(jnp.float32).reshape(N_DP, GROUP, NBIG, BIG, BIG, C)
    small_all = small_maps.astype(jnp.float32).reshape(N_DP, GROUP, NSMALL, SMALL, SMALL, C)
    slot_ids = jnp.arange(IMG_DEV, dtype=jnp.int32)
    mask_all = (slot_ids[None, :] < live_counts[:, None]).astype(jnp.float32).reshape(N_DP, GROUP)
    queues = jnp.transpose(queue.astype(jnp.float32).reshape(NBIG, N_DP, N_SUB * QUEUE_DEV, OUTD), (1, 0, 2, 3))
    params = (bottleneck_outer, bottleneck_inner, proj_hidden, proj_out, prototypes, norm_params)
    centers = low(unit_rows(prototypes))

    def one_group(state_now, group_inputs):
        grad_sums, numer_sum = state_now
        big_group, small_group, image_mask, queue_group = group_inputs

        def run_forward(values):
            return forward(values, big_group, small_group, image_mask)
        scores, pull_back = jax.vjp(run_forward, params)
        queue_scores = matmul(queue_group.reshape(-1, OUTD), centers.T).reshape(NBIG, -1, PROTOS)
        code_rows = codes_of(jnp.transpose(scores[:, :NBIG], (1, 0, 2)), queue_scores, image_mask)

        def loss_of(values):
            return loss_of_codes(values, code_rows)
        group_numer, loss_back = jax.vjp(loss_of, scores)
        grad_scores, = loss_back(jnp.ones((), jnp.float32))
        grad_params, = pull_back(grad_scores)
        return ((jax.tree.map(jnp.add, grad_sums, grad_params), numer_sum + group_numer), None)
    zero_grads = tuple((jnp.zeros(param.shape, jnp.float32) for param in params))
    (grad_sums, numer_sum), unused = lax.scan(one_group, (zero_grads, jnp.zeros((), jnp.float32)), (big_all, small_all, mask_all, queues))
    live_total = jnp.sum(live_counts).astype(jnp.float32)
    axes_list = [(1, 2), (0, 1, 2), (0, 1), (0, 1), (0, 1), (1,)]
    moments_old = (mom_outer, mom_inner, mom_hidden, mom_out, mom_protos, mom_norms)
    averages_old = (avg_outer, avg_inner, avg_hidden, avg_out, avg_protos, avg_norms)
    results = [advance(params[which_one], grad_sums[which_one], moments_old[which_one], averages_old[which_one], ratio_of(params[which_one], grad_sums[which_one], axes_list[which_one])) for which_one in range(6)]
    news = [entry[0] for entry in results]
    moms = [entry[1] for entry in results]
    avgs = [entry[2] for entry in results]
    return (numer_sum, live_total, news[0], news[1], news[2], news[3], news[4], news[5], moms[0], moms[1], moms[2], moms[3], moms[4], moms[5], avgs[0], avgs[1], avgs[2], avgs[3], avgs[4], avgs[5], news[0].astype(jnp.bfloat16), news[1].astype(jnp.bfloat16), news[2].astype(jnp.bfloat16), news[3].astype(jnp.bfloat16))
```

```python
import functools
import math

import jax
import jax.numpy as jnp
from jax import lax
from jax.experimental import pallas as pl
from jax.experimental.pallas import tpu as pltpu
from jax.sharding import PartitionSpec as P

NBIG = 2
NSMALL = 6
CROPS = NBIG + NSMALL
BIG = 7
SMALL = 3
TAPS = 9
ITERS = 3
LANES = 128

sink_temp = 0.05
softmax_temp = 0.1
norm_eps = 1e-05
unit_eps = 1e-12
trust_rate = 0.5
learn_rate = 1.0
momentum_rate = 0.5
average_rate = 0.5

MESH = pl.DeviceIdType.MESH
MIB = 1 << 20
LOG2E = math.log2(math.e)
SINK2 = LOG2E / sink_temp
SOFT2 = LOG2E / softmax_temp
PAIRS = NBIG * (CROPS - 1)


def silu_slope(values):
    sigma = jax.nn.sigmoid(values)
    return sigma * (1.0 + values * (1.0 - sigma))


def cross_rows(left, right):
    return lax.dot_general(
        left, right, (((0,), (0,)), ((), ())), preferred_element_type=jnp.float32
    )


def against(left, right):
    return lax.dot_general(
        left, right, (((1,), (1,)), ((), ())), preferred_element_type=jnp.float32
    )


def forward_dot(left, right):
    return jnp.dot(left, right, preferred_element_type=jnp.float32)


def unit_rows(values):
    return values * lax.rsqrt(jnp.sum(values * values, 1, keepdims=True) + unit_eps)


def greet(axis, count):
    me = lax.axis_index(axis)
    barrier = pltpu.get_barrier_semaphore()
    for hop in range(1, count):
        pl.semaphore_signal(
            barrier, inc=1, device_id={axis: lax.rem(me + hop, count)}, device_id_type=MESH
        )
    pl.semaphore_wait(barrier, count - 1)


def exchange_kernel(axis, count, scatter, x_ref, o_ref, send_sem, recv_sem, own_sem):
    me = lax.axis_index(axis)
    greet(axis, count)
    copies = []
    for hop in range(1, count):
        to = lax.rem(me + hop, count)
        copy = pltpu.make_async_remote_copy(
            src_ref=x_ref.at[to] if scatter else x_ref,
            dst_ref=o_ref.at[me],
            send_sem=send_sem.at[hop],
            recv_sem=recv_sem.at[hop],
            device_id={axis: to},
            device_id_type=MESH,
        )
        copy.start()
        copies.append(copy)
    own = pltpu.make_async_copy(x_ref.at[me] if scatter else x_ref, o_ref.at[me], own_sem)
    own.start()
    own.wait()
    for copy in copies:
        copy.wait()


class Exchanger:
    def __init__(self, sizes):
        self.sizes = sizes
        self.used = 0

    def next_id(self):
        self.used += 1
        return self.used

    def __call__(self, values, axis, scatter=False, name="exchange"):
        count = self.sizes[axis]
        block = values.shape[1:] if scatter else values.shape
        return pl.pallas_call(
            functools.partial(exchange_kernel, axis, count, scatter),
            out_shape=jax.ShapeDtypeStruct((count,) + block, values.dtype),
            in_specs=[pl.BlockSpec(memory_space=pltpu.VMEM)],
            out_specs=pl.BlockSpec(memory_space=pltpu.VMEM),
            scratch_shapes=[
                pltpu.SemaphoreType.DMA((count,)),
                pltpu.SemaphoreType.DMA((count,)),
                pltpu.SemaphoreType.DMA,
            ],
            compiler_params=pltpu.CompilerParams(
                collective_id=self.next_id(), has_side_effects=True, vmem_limit_bytes=32 * MIB
            ),
            name=name,
        )(values)


def row_tile(rows):
    return next(size for size in (192, 160, 128, 96, 64, 48, 32, 24, 16, 8) if rows % size == 0)


def column_sums_kernel(queue_ref, turned_ref, o_ref, total):
    views, rows, _ = queue_ref.shape
    width = turned_ref.shape[1]
    tile = row_tile(rows)
    part = 256
    for view in range(views):
        total[...] = jnp.zeros_like(total)

        def step(index, carry):
            lines = queue_ref[view, pl.ds(index * tile, tile), :]
            for start in range(0, width, part):
                cols = pl.ds(start, part)
                scores = jnp.dot(lines, turned_ref[:, cols], preferred_element_type=jnp.float32)
                shares = jnp.exp2(scores * SINK2)
                total[:, cols] += jnp.sum(shares.reshape(tile // 8, 8, part), 0)
            return carry

        lax.fori_loop(0, rows // tile, step, 0)
        o_ref[pl.ds(view, 1), :] = jnp.sum(total[...], 0, keepdims=True)


def column_sums(queue, turned):
    width = turned.shape[1]
    return pl.pallas_call(
        column_sums_kernel,
        out_shape=jax.ShapeDtypeStruct((queue.shape[0], width), jnp.float32),
        in_specs=[pl.BlockSpec(memory_space=pltpu.VMEM)] * 2,
        out_specs=pl.BlockSpec(memory_space=pltpu.VMEM),
        scratch_shapes=[pltpu.VMEM((8, width), jnp.float32)],
        compiler_params=pltpu.CompilerParams(vmem_limit_bytes=32 * MIB),
        cost_estimate=pl.CostEstimate(
            flops=2 * queue.size * width,
            bytes_accessed=2 * queue.size,
            transcendentals=queue.size // queue.shape[2] * width,
        ),
        name="column_sums",
    )(queue, turned)


def sinkhorn_kernel(
    axis,
    count,
    protos,
    queue_ref,
    turned_ref,
    unit_ref,
    live_ref,
    first_ref,
    grad_ref,
    loss_ref,
    kept,
    scores,
    mine,
    landed,
    shift,
    total,
    send_sem,
    recv_sem,
):
    me = lax.axis_index(axis)
    views, rows, _ = queue_ref.shape
    width = turned_ref.shape[1]
    images = live_ref.shape[0]
    tile = row_tile(rows)
    part = 512
    parts = range(0, width, part)
    mask = live_ref[...]
    greet(axis, count)

    def sum_group(turn):
        copies = []
        for hop in range(1, count):
            copy = pltpu.make_async_remote_copy(
                src_ref=mine.at[turn],
                dst_ref=landed.at[turn, hop],
                send_sem=send_sem.at[turn, hop],
                recv_sem=recv_sem.at[turn, hop],
                device_id={axis: lax.rem(me + hop, count)},
                device_id_type=MESH,
            )
            copy.start()
            copies.append(copy)
        for copy in copies:
            copy.wait()
        whole = mine[turn]
        for hop in range(1, count):
            whole = whole + landed[turn, hop]
        return whole

    for start in parts:
        cols = pl.ds(start, part)
        scores[:, cols] = jnp.dot(
            unit_ref[...], turned_ref[:, cols], preferred_element_type=jnp.float32
        )
        for view in range(views):
            lines = pl.ds(view * images, images)
            shares = jnp.exp2(scores[lines, cols] * SINK2) * mask
            mine[0, pl.ds(view, 1), cols] = first_ref[pl.ds(view, 1), cols] + jnp.sum(
                shares, 0, keepdims=True
            )
    real = lax.broadcasted_iota(jnp.int32, (1, width), 1) < protos
    first = sum_group(0)
    shift[...] = jnp.where(real, jnp.log2(first), 1e30)

    for turn in range(1, ITERS):
        for view in range(views):
            lines = pl.ds(view * images, images)
            row = pl.ds(view, 1)
            if turn == 1:
                own = jnp.exp2(scores[lines, :] * SINK2 - shift[row, :]) * mask
                weight = jnp.sum(own, 1, keepdims=True)
            else:
                own = jnp.exp2(scores[lines, :] * SINK2 - first_log[row, :]) * mask
                weight = jnp.sum(own * shift[row, :], 1, keepdims=True)
            total[...] = own / (weight + (1.0 - mask))

            def step(index, carry):
                span = pl.ds(index * tile, tile)
                if turn == 1:
                    lines = queue_ref[view, span, :]
                sums = jnp.zeros((tile, LANES), jnp.float32)
                for start in parts:
                    cols = pl.ds(start, part)
                    if turn == 1:
                        raw = jnp.dot(lines, turned_ref[:, cols], preferred_element_type=jnp.float32)
                        shares = jnp.exp2(raw * SINK2 - shift[row, cols])
                        kept[view, span, cols] = shares
                    else:
                        shares = kept[view, span, cols] * shift[row, cols]
                    for lane in range(0, part, LANES):
                        sums = sums + shares[:, lane : lane + LANES]
                scale = 1.0 / jnp.sum(sums, 1, keepdims=True)
                for start in parts:
                    cols = pl.ds(start, part)
                    scaled = kept[view, span, cols] * scale
                    total[:, cols] += jnp.sum(scaled.reshape(tile // 8, 8, part), 0)
                return carry

            lax.fori_loop(0, rows // tile, step, 0)
            mine[turn, row, :] = jnp.sum(total[...], 0, keepdims=True)
        if turn == 1:
            first_log = shift[...]
        whole = sum_group(turn)
        shift[...] = jnp.where(real, 1.0 / whole, 0.0)

    codes = []
    for view in range(views):
        lines = pl.ds(view * images, images)
        own = jnp.exp2(scores[lines, :] * SINK2 - first_log[view : view + 1, :]) * mask
        own = own * shift[pl.ds(view, 1), :]
        codes.append(own / (jnp.sum(own, 1, keepdims=True) + (1.0 - mask)))
    code_total = codes[0] + codes[1]
    loss = jnp.zeros((images, 1), jnp.float32)
    for crop in range(CROPS):
        lines = pl.ds(crop * images, images)
        raw = jnp.where(real, scores[lines, :] * SOFT2, -1e30)
        raw = raw - jnp.max(raw, 1, keepdims=True)
        powers = jnp.exp2(raw)
        norm = jnp.sum(powers, 1, keepdims=True)
        others = code_total - codes[crop] if crop < NBIG else code_total
        logs = jnp.where(real, (raw - jnp.log2(norm)) / LOG2E, 0.0)
        loss = loss - jnp.sum(others * logs, 1, keepdims=True)
        weight = (NBIG - 1.0 if crop < NBIG else float(NBIG)) * mask / norm
        grad = (weight * powers - others) / (PAIRS * softmax_temp)
        grad_ref[lines, :] = grad.astype(grad_ref.dtype)
    loss_ref[...] = jnp.broadcast_to(
        jnp.sum(loss, 0, keepdims=True) / PAIRS, loss_ref.shape
    )


def sinkhorn(sizes, collective_id, protos, queue, turned, unit, live, first):
    count = sizes["sub"]
    views, rows, depth = queue.shape
    width = turned.shape[1]
    crops = unit.shape[0]
    return pl.pallas_call(
        functools.partial(sinkhorn_kernel, "sub", count, protos),
        out_shape=(
            jax.ShapeDtypeStruct((crops, width), jnp.bfloat16),
            jax.ShapeDtypeStruct((8, LANES), jnp.float32),
        ),
        in_specs=[pl.BlockSpec(memory_space=pltpu.VMEM)] * 5,
        out_specs=(pl.BlockSpec(memory_space=pltpu.VMEM),) * 2,
        scratch_shapes=[
            pltpu.VMEM((views, rows, width), jnp.float32),
            pltpu.VMEM((crops, width), jnp.float32),
            pltpu.VMEM((ITERS, views, width), jnp.float32),
            pltpu.VMEM((ITERS, count, views, width), jnp.float32),
            pltpu.VMEM((views, width), jnp.float32),
            pltpu.VMEM((8, width), jnp.float32),
            pltpu.SemaphoreType.DMA((ITERS, count)),
            pltpu.SemaphoreType.DMA((ITERS, count)),
        ],
        compiler_params=pltpu.CompilerParams(
            collective_id=collective_id, has_side_effects=True, vmem_limit_bytes=48 * MIB
        ),
        name="sinkhorn",
    )(queue, turned, unit, live, first)


def split_rows(values, images):
    big = BIG * BIG * NBIG * images
    wide = values.shape[1]
    return (
        values[:big].reshape(BIG, BIG, NBIG * images, wide),
        values[big:].reshape(SMALL, SMALL, NSMALL * images, wide),
    )


def patches(values, images, flip):
    parts = []
    for spatial in split_rows(values, images):
        extent = spatial.shape[0]
        padded = jnp.pad(spatial, ((1, 1), (1, 1), (0, 0), (0, 0)))
        pieces = [
            padded[row : row + extent, col : col + extent]
            for row in range(3)
            for col in range(3)
        ]
        if flip:
            pieces = pieces[::-1]
        parts.append(jnp.concatenate(pieces, -1).reshape(-1, TAPS * values.shape[1]))
    return jnp.concatenate(parts, 0)


def spread_crops(values, images):
    wide = values.shape[1]
    big = jnp.broadcast_to(
        values[: NBIG * images] / (BIG * BIG), (BIG * BIG, NBIG * images, wide)
    ).reshape(-1, wide)
    small = jnp.broadcast_to(
        values[NBIG * images :] / (SMALL * SMALL), (SMALL * SMALL, NSMALL * images, wide)
    ).reshape(-1, wide)
    return jnp.concatenate([big, small], 0)


def pool_crops(values, images):
    big, small = split_rows(values, images)
    return jnp.concatenate([jnp.mean(big, (0, 1)), jnp.mean(small, (0, 1))], 0)


def advance(weight, gradient, moment, average, trust):
    step_now = trust * gradient
    moment_new = momentum_rate * moment + step_now
    weight_new = weight - learn_rate * (step_now + momentum_rate * moment_new)
    average_new = average_rate * average + (1.0 - average_rate) * weight_new
    return (weight_new, moment_new, average_new)


def per_device(
    sizes,
    big_maps,
    small_maps,
    live_counts,
    queue,
    bottleneck_outer,
    bottleneck_inner,
    proj_hidden,
    proj_out,
    prototypes,
    norm_params,
    mom_outer,
    mom_inner,
    mom_hidden,
    mom_out,
    mom_protos,
    mom_norms,
    avg_outer,
    avg_inner,
    avg_hidden,
    avg_out,
    avg_protos,
    avg_norms,
):
    n_sub = sizes["sub"]
    exchange = Exchanger(sizes)
    images = big_maps.shape[0]
    channels = big_maps.shape[-1]
    middle = bottleneck_inner.shape[-1]
    hidden_width = proj_hidden.shape[1]
    out_width = proj_out.shape[1]
    proto_count = prototypes.shape[0]
    proto_width = -(-proto_count // 512) * 512
    here = lax.axis_index("sub")
    share = hidden_width // n_sub

    outer_low = lax.all_gather(bottleneck_outer.astype(jnp.bfloat16), "dp", axis=1, tiled=True)
    inner_low = lax.all_gather(bottleneck_inner.astype(jnp.bfloat16), "dp", axis=1, tiled=True)
    hidden_cols = lax.dynamic_slice_in_dim(proj_hidden, here * share, share, 1)
    hidden_low = lax.all_gather(hidden_cols.astype(jnp.bfloat16), "dp", axis=0, tiled=True)
    out_low = lax.all_gather(proj_out.astype(jnp.bfloat16), "dp", axis=0, tiled=True)
    out_low = lax.dynamic_slice_in_dim(out_low, here * share, share, 0)
    first_w = outer_low[0]
    last_w = outer_low[1]
    middle_w = inner_low.reshape(TAPS * middle, middle)
    middle_t = jnp.transpose(inner_low, (0, 2, 1)).reshape(TAPS * middle, middle)

    bounds = [0, middle, 2 * middle, 2 * middle + channels, 2 * middle + channels + hidden_width]
    gains = [norm_params[0, bounds[k] : bounds[k + 1]] for k in range(4)]
    biases = [norm_params[1, bounds[k] : bounds[k + 1]] for k in range(4)]
    gains[3] = lax.dynamic_slice_in_dim(gains[3], here * share, share, 0)
    biases[3] = lax.dynamic_slice_in_dim(biases[3], here * share, share, 0)

    proto_inv = lax.rsqrt(jnp.sum(prototypes * prototypes, 1, keepdims=True) + unit_eps)
    centers_low = (prototypes * proto_inv).astype(jnp.bfloat16)
    centers_low = jnp.pad(centers_low, ((0, proto_width - proto_count), (0, 0)))
    turned = centers_low.T
    first_sums = column_sums(queue, turned)

    live_float = live_counts[0].astype(jnp.float32)
    image_mask = (jnp.arange(images) < live_counts[0]).astype(jnp.float32)[:, None]
    per_image = NBIG * BIG * BIG + NSMALL * SMALL * SMALL
    rows = per_image * images
    row_mask = jnp.broadcast_to(image_mask, (per_image, images, 1)).reshape(rows, 1)

    inputs = jnp.concatenate(
        [
            jnp.transpose(big_maps, (2, 3, 1, 0, 4)).reshape(-1, channels),
            jnp.transpose(small_maps, (2, 3, 1, 0, 4)).reshape(-1, channels),
        ],
        0,
    )

    hidden_one = forward_dot(inputs, first_w)
    masked = hidden_one * row_mask
    sums = exchange(
        jnp.stack(
            [
                jnp.sum(masked, 0),
                jnp.sum(masked * hidden_one, 0),
                jnp.broadcast_to(live_float, (middle,)),
            ]
        ),
        "sub",
        name="sums_one",
    )
    lives = sums[:, 2, 0]
    count_all = jnp.sum(lives) * per_image

    def stats(total, squares, count):
        mean = total / count
        return mean, lax.rsqrt(squares / count - mean * mean + norm_eps)

    def group_stats(values, name):
        masked = values * row_mask
        both = exchange(
            jnp.stack([jnp.sum(masked, 0), jnp.sum(masked * values, 0)]), "sub", name=name
        )
        both = jnp.sum(both, 0)
        return stats(both[0], both[1], count_all)

    sums = jnp.sum(sums, 0)
    mean_one, inv_one = stats(sums[0], sums[1], count_all)
    normal_one = (hidden_one - mean_one) * inv_one
    pre_one = gains[0] * normal_one + biases[0]
    act_one = jax.nn.silu(pre_one).astype(jnp.bfloat16)
    columns = patches(act_one, images, False)
    hidden_two = forward_dot(columns, middle_w)
    mean_two, inv_two = group_stats(hidden_two, "sums_two")
    normal_two = (hidden_two - mean_two) * inv_two
    pre_two = gains[1] * normal_two + biases[1]
    act_two = jax.nn.silu(pre_two).astype(jnp.bfloat16)
    hidden_three = against(act_two, last_w)
    mean_three, inv_three = group_stats(hidden_three, "sums_three")
    normal_three = (hidden_three - mean_three) * inv_three
    summed = gains[2] * normal_three + biases[2] + inputs.astype(jnp.float32)
    pooled_low = pool_crops(jax.nn.silu(summed), images).astype(jnp.bfloat16)

    crops = CROPS * images
    pooled_all = exchange(pooled_low, "sub", name="pooled").reshape(n_sub * crops, channels)
    group_mask = (jnp.arange(images)[None, :] < lives[:, None]).astype(jnp.float32)
    group_mask = jnp.broadcast_to(group_mask[:, None, :], (n_sub, CROPS, images))
    group_mask = group_mask.reshape(n_sub * crops, 1)
    count_crops = jnp.sum(lives) * CROPS
    proj_pre = forward_dot(pooled_all, hidden_low)
    masked = proj_pre * group_mask
    mean_four, inv_four = stats(jnp.sum(masked, 0), jnp.sum(masked * proj_pre, 0), count_crops)
    normal_four = (proj_pre - mean_four) * inv_four
    pre_four = gains[3] * normal_four + biases[3]
    act_four = jax.nn.silu(pre_four).astype(jnp.bfloat16)
    partial = forward_dot(act_four, out_low).reshape(n_sub, crops, out_width)
    embedding = jnp.sum(exchange(partial, "sub", scatter=True, name="embedding"), 0)
    unit_embed, embed_back = jax.vjp(unit_rows, embedding)
    unit_low = unit_embed.astype(jnp.bfloat16)

    grad_low, loss_tile = sinkhorn(
        sizes, exchange.next_id(), proto_count, queue, turned, unit_low, image_mask, first_sums
    )
    (grad_embed,) = embed_back(forward_dot(grad_low, centers_low))
    grad_centers = cross_rows(grad_low, unit_low)
    embed_low = grad_embed.astype(jnp.bfloat16)
    embed_all = exchange(embed_low, "sub", name="embed_grad").reshape(n_sub * crops, out_width)

    d_out = cross_rows(act_four, embed_all)
    grad_four = against(embed_all, out_low) * silu_slope(pre_four)
    bias_four = jnp.sum(grad_four, 0)
    gain_four = jnp.sum(grad_four * normal_four, 0)
    proj_low = (
        gains[3]
        * inv_four
        * (grad_four - group_mask * (bias_four + normal_four * gain_four) / count_crops)
    ).astype(jnp.bfloat16)
    d_hidden = cross_rows(pooled_all, proj_low)
    partial = against(proj_low, hidden_low).astype(jnp.bfloat16).reshape(n_sub, crops, channels)
    grad_pooled = exchange(partial, "sub", scatter=True, name="pooled_grad")
    grad_pooled = jnp.sum(grad_pooled.astype(jnp.float32), 0)

    hidden_sum = lax.psum_scatter(d_hidden.astype(jnp.bfloat16), "dp", scatter_dimension=0, tiled=True)
    out_group = exchange(d_out.astype(jnp.bfloat16), "sub", name="out_grad")
    out_sum = lax.psum_scatter(
        out_group.reshape(hidden_width, out_width), "dp", scatter_dimension=0, tiled=True
    )
    shard_hidden = exchange(hidden_sum, "sub", name="hidden_shard")
    shard_hidden = jnp.transpose(shard_hidden, (1, 0, 2)).reshape(-1, hidden_width)
    shard_hidden = shard_hidden.astype(jnp.float32)
    shard_out = out_sum.astype(jnp.float32)

    def norm_back(grad_out, normal, inv_std, gain_vec, name):
        bias_local = jnp.sum(grad_out, 0)
        gain_local = jnp.sum(grad_out * normal, 0)
        both = jnp.sum(exchange(jnp.stack([bias_local, gain_local]), "sub", name=name), 0)
        grad_in = (
            gain_vec * inv_std * (grad_out - row_mask * (both[0] + normal * both[1]) / count_all)
        )
        return grad_in.astype(jnp.bfloat16), gain_local, bias_local

    grad_summed = spread_crops(grad_pooled, images) * silu_slope(summed)
    three_low, gain_three, bias_three = norm_back(
        grad_summed, normal_three, inv_three, gains[2], "back_three"
    )
    d_last = cross_rows(three_low, act_two)
    grad_act_two = forward_dot(three_low, last_w) * silu_slope(pre_two)
    two_low, gain_two, bias_two = norm_back(
        grad_act_two, normal_two, inv_two, gains[1], "back_two"
    )
    d_middle = cross_rows(columns, two_low)
    grad_act_one = forward_dot(patches(two_low, images, True), middle_t) * silu_slope(pre_one)
    one_low, gain_one, bias_one = norm_back(
        grad_act_one, normal_one, inv_one, gains[0], "back_one"
    )
    d_first = cross_rows(inputs, one_low)

    wide_four = jnp.zeros((2, hidden_width), jnp.float32)
    wide_four = lax.dynamic_update_slice(
        wide_four, jnp.stack([gain_four, bias_four]), (0, here * share)
    )
    grad_norms = jnp.concatenate(
        [
            jnp.stack(
                [
                    jnp.concatenate([gain_one, gain_two, gain_three]),
                    jnp.concatenate([bias_one, bias_two, bias_three]),
                ]
            ),
            wide_four,
        ],
        1,
    )
    centers_sum, norm_sum, numer_all, live_all = lax.psum(
        (grad_centers, grad_norms, loss_tile[0, 0], live_float), ("dp", "sub")
    )
    centers_sum = centers_sum[:proto_count]
    proto_unit = prototypes * proto_inv
    proto_sum = proto_inv * (
        centers_sum - proto_unit * jnp.sum(proto_unit * centers_sum, 1, keepdims=True)
    )
    grad_outer = jnp.stack([d_first, d_last]).astype(jnp.bfloat16)
    grad_inner = d_middle.reshape(TAPS, middle, middle).astype(jnp.bfloat16)
    shard_outer = lax.psum(
        lax.psum_scatter(grad_outer, "dp", scatter_dimension=1, tiled=True), "sub"
    ).astype(jnp.float32)
    shard_inner = lax.psum(
        lax.psum_scatter(grad_inner, "dp", scatter_dimension=1, tiled=True), "sub"
    ).astype(jnp.float32)

    squares = jnp.concatenate(
        [
            jnp.sum(bottleneck_outer * bottleneck_outer, (1, 2)),
            jnp.sum(bottleneck_inner * bottleneck_inner)[None],
            jnp.sum(proj_hidden * proj_hidden)[None],
            jnp.sum(proj_out * proj_out)[None],
            jnp.sum(shard_outer * shard_outer, (1, 2)),
            jnp.sum(shard_inner * shard_inner)[None],
            jnp.sum(shard_hidden * shard_hidden)[None],
            jnp.sum(shard_out * shard_out)[None],
        ]
    )
    squares = jnp.broadcast_to(jnp.pad(squares, (0, 6))[:, None], (16, LANES))
    squares = jnp.sum(exchange(squares, "dp", name="norms"), 0)[:, 0]
    weight_all, grad_all = squares[:5], squares[5:10]
    trusts = trust_rate * jnp.sqrt(weight_all) / (jnp.sqrt(grad_all) + 1e-12)
    proto_trust = (
        trust_rate
        * jnp.sqrt(jnp.sum(prototypes * prototypes))
        / (jnp.sqrt(jnp.sum(proto_sum * proto_sum)) + 1e-12)
    )
    norm_trust = (
        trust_rate
        * jnp.sqrt(jnp.sum(norm_params * norm_params, 1, keepdims=True))
        / (jnp.sqrt(jnp.sum(norm_sum * norm_sum, 1, keepdims=True)) + 1e-12)
    )
    outer_new = advance(
        bottleneck_outer, shard_outer, mom_outer, avg_outer, trusts[:2][:, None, None]
    )
    inner_new = advance(bottleneck_inner, shard_inner, mom_inner, avg_inner, trusts[2])
    hidden_new = advance(proj_hidden, shard_hidden, mom_hidden, avg_hidden, trusts[3])
    out_new = advance(proj_out, shard_out, mom_out, avg_out, trusts[4])
    protos_new = advance(prototypes, proto_sum, mom_protos, avg_protos, proto_trust)
    norms_new = advance(norm_params, norm_sum, mom_norms, avg_norms, norm_trust)
    news = (outer_new, inner_new, hidden_new, out_new, protos_new, norms_new)
    return (
        (numer_all, live_all)
        + tuple(new[0] for new in news)
        + tuple(new[1] for new in news)
        + tuple(new[2] for new in news)
        + tuple(new[0].astype(jnp.bfloat16) for new in news[:4])
    )


def solution(mesh):
    data = P(("dp", "sub"), None, None, None, None)
    trees = (P(None, "dp", None), P(None, "dp", None), P("dp", None), P("dp", None), P(), P())
    in_specs = (data, data, P(("dp", "sub")), P(None, ("dp", "sub"), None)) + trees * 3
    out_specs = (P(), P()) + trees * 3 + trees[:4]
    sizes = {axis: mesh.shape[axis] for axis in ("dp", "sub")}
    return jax.shard_map(
        functools.partial(per_device, sizes),
        mesh=mesh,
        in_specs=in_specs,
        out_specs=out_specs,
        check_vma=False,
    )
```

```python
import functools
import math

import jax
import jax.numpy as jnp
from jax import lax
from jax.experimental import pallas as pl
from jax.experimental.pallas import tpu as pltpu
from jax.sharding import PartitionSpec as P

NBIG = 2
NSMALL = 6
CROPS = NBIG + NSMALL
BIG = 7
SMALL = 3
TAPS = 9
ITERS = 3
LANES = 128

sink_temp = 0.05
softmax_temp = 0.1
norm_eps = 1e-05
unit_eps = 1e-12
trust_rate = 0.5
learn_rate = 1.0
momentum_rate = 0.5
average_rate = 0.5

MESH = pl.DeviceIdType.MESH
MIB = 1 << 20
LOG2E = math.log2(math.e)
SINK2 = LOG2E / sink_temp
SOFT2 = LOG2E / softmax_temp
PAIRS = NBIG * (CROPS - 1)


def silu_slope(values):
    sigma = jax.nn.sigmoid(values)
    return sigma * (1.0 + values * (1.0 - sigma))


def cross_rows(left, right):
    return lax.dot_general(
        left, right, (((0,), (0,)), ((), ())), preferred_element_type=jnp.float32
    )


def against(left, right):
    return lax.dot_general(
        left, right, (((1,), (1,)), ((), ())), preferred_element_type=jnp.float32
    )


def forward_dot(left, right):
    return jnp.dot(left, right, preferred_element_type=jnp.float32)


def unit_rows(values):
    return values * lax.rsqrt(jnp.sum(values * values, 1, keepdims=True) + unit_eps)


def greet(axis, count):
    me = lax.axis_index(axis)
    barrier = pltpu.get_barrier_semaphore()
    for hop in range(1, count):
        pl.semaphore_signal(
            barrier, inc=1, device_id={axis: lax.rem(me + hop, count)}, device_id_type=MESH
        )
    pl.semaphore_wait(barrier, count - 1)


def exchange_kernel(axis, count, scatter, x_ref, o_ref, send_sem, recv_sem, own_sem):
    me = lax.axis_index(axis)
    greet(axis, count)
    copies = []
    for hop in range(1, count):
        to = lax.rem(me + hop, count)
        copy = pltpu.make_async_remote_copy(
            src_ref=x_ref.at[to] if scatter else x_ref,
            dst_ref=o_ref.at[me],
            send_sem=send_sem.at[hop],
            recv_sem=recv_sem.at[hop],
            device_id={axis: to},
            device_id_type=MESH,
        )
        copy.start()
        copies.append(copy)
    own = pltpu.make_async_copy(x_ref.at[me] if scatter else x_ref, o_ref.at[me], own_sem)
    own.start()
    own.wait()
    for copy in copies:
        copy.wait()


class Exchanger:
    def __init__(self, sizes):
        self.sizes = sizes
        self.used = 0

    def next_id(self):
        self.used += 1
        return self.used

    def __call__(self, values, axis, scatter=False, name="exchange"):
        count = self.sizes[axis]
        block = values.shape[1:] if scatter else values.shape
        return pl.pallas_call(
            functools.partial(exchange_kernel, axis, count, scatter),
            out_shape=jax.ShapeDtypeStruct((count,) + block, values.dtype),
            in_specs=[pl.BlockSpec(memory_space=pltpu.VMEM)],
            out_specs=pl.BlockSpec(memory_space=pltpu.VMEM),
            scratch_shapes=[
                pltpu.SemaphoreType.DMA((count,)),
                pltpu.SemaphoreType.DMA((count,)),
                pltpu.SemaphoreType.DMA,
            ],
            compiler_params=pltpu.CompilerParams(
                collective_id=self.next_id(), has_side_effects=True, vmem_limit_bytes=32 * MIB
            ),
            name=name,
        )(values)


class Links:
    def __init__(self, send_sem, recv_sem):
        self.send_sem = send_sem
        self.recv_sem = recv_sem
        self.used = 0

    def __call__(self, source, target, device):
        copy = pltpu.make_async_remote_copy(
            src_ref=source,
            dst_ref=target,
            send_sem=self.send_sem.at[self.used],
            recv_sem=self.recv_sem.at[self.used],
            device_id=device,
            device_id_type=MESH,
        )
        self.used += 1
        copy.start()
        return copy


def wait_all(copies):
    for copy in copies:
        copy.wait()


def lanes_of(index, width=LANES):
    return pl.ds(pl.multiple_of(index * width, LANES), width)


class Place:
    def __init__(self, n_dp):
        self.n_dp = n_dp
        self.span = n_dp // 2
        dp, self.sub = lax.axis_index("dp"), lax.axis_index("sub")
        self.dp = dp
        self.near, self.far = dp // 2, dp % 2
        row, core = self.sub // 2, self.sub % 2
        self.row, self.core = row, core
        self.row_sub = 2 * (1 - row) + core
        self.core_sub = 2 * row + (1 - core)
        self.far_peer = {"dp": self.near * 2 + (1 - self.far)}
        self.row_peer = {"sub": self.row_sub}
        self.core_peer = {"sub": self.core_sub}

    def near_index(self, hop):
        return (self.near + hop) % self.span

    def near_peer(self, hop):
        return {"dp": self.near_index(hop) * 2 + self.far}

    def dp_peers(self):
        return [{"dp": (self.dp + hop) % self.n_dp} for hop in range(1, self.n_dp)]

    def sub_peers(self):
        return [{"sub": (self.sub + hop) % 4} for hop in range(1, 4)]

    def greet(self, peers):
        barrier = pltpu.get_barrier_semaphore()
        for peer in peers:
            pl.semaphore_signal(barrier, inc=1, device_id=peer, device_id_type=MESH)
        pl.semaphore_wait(barrier, len(peers))


ALL = slice(None)


def gather_kernel(n_dp, *refs):
    w_first, w_mid, w_last, w_hid, w_out = refs[:5]
    o_first, o_mid, o_last, o_hid, o_out = refs[5:10]
    send_sem, recv_sem, own_sem = refs[10:]
    at = Place(n_dp)
    links = Links(send_sem, recv_sem)
    at.greet(
        [at.near_peer(hop) for hop in range(1, at.span)]
        + [at.far_peer, at.row_peer, at.core_peer]
    )
    mine, beside = lanes_of(at.sub), lanes_of(at.row_sub)

    def flat(source, target, split):
        return (
            lambda cols: source.at[:, cols],
            lambda near, far, cols: target.at[near, far, :, cols],
            split,
        )

    def taps(start):
        some = pl.ds(start, 3)
        return (
            lambda cols: w_mid.at[some, :, cols],
            lambda near, far, cols: o_mid.at[some, near, far, :, cols],
            True,
        )

    pieces = [
        flat(w_first, o_first, True),
        taps(0),
        taps(3),
        taps(6),
        flat(w_last, o_last, True),
        flat(w_hid, o_hid, False),
        flat(w_out, o_out, False),
    ]
    count = len(pieces)
    own, first, second, third, fourth = [], [], [], [], []
    for index, (source, target, split) in enumerate(pieces):
        cols = mine if split else ALL
        copy = pltpu.make_async_copy(source(cols), target(at.near, at.far, cols), own_sem.at[index])
        copy.start()
        own.append(copy)
    for source, target, split in pieces:
        cols = mine if split else ALL
        first.append(
            [
                links(source(cols), target(at.near, at.far, cols), at.near_peer(hop))
                for hop in range(1, at.span)
            ]
        )
    for tick in range(count + 2):
        if tick < count:
            source, target, split = pieces[tick]
            cols = mine if split else ALL
            own[tick].wait()
            wait_all(first[tick])
            slab = target(ALL, at.far, cols)
            second.append(links(slab, slab, at.far_peer))
        if 1 <= tick < count + 1:
            source, target, split = pieces[tick - 1]
            second[tick - 1].wait()
            if split:
                slab = target(ALL, ALL, mine)
                third.append(links(slab, slab, at.row_peer))
            else:
                third.append(None)
        if tick >= 2:
            source, target, split = pieces[tick - 2]
            if split:
                third[tick - 2].wait()
                for cols in (mine, beside):
                    slab = target(ALL, ALL, cols)
                    fourth.append(links(slab, slab, at.core_peer))
    wait_all(fourth)


def gather_weights(n_dp, collective_id, first, mid, last, hid, out):
    span = n_dp // 2
    rows, middle = first.shape
    some = jax.ShapeDtypeStruct
    low = jnp.bfloat16
    copies = 7 * (span + 4)
    return pl.pallas_call(
        functools.partial(gather_kernel, n_dp),
        out_shape=(
            some((span, 2, rows, middle), low),
            some((TAPS, span, 2, mid.shape[1], middle), low),
            some((span, 2, rows, middle), low),
            some((span, 2, rows, hid.shape[1]), low),
            some((span, 2, rows, out.shape[1]), low),
        ),
        in_specs=[pl.BlockSpec(memory_space=pltpu.VMEM)] * 5,
        out_specs=(pl.BlockSpec(memory_space=pl.ANY),) * 5,
        scratch_shapes=[
            pltpu.SemaphoreType.DMA((copies,)),
            pltpu.SemaphoreType.DMA((copies,)),
            pltpu.SemaphoreType.DMA((7,)),
        ],
        compiler_params=pltpu.CompilerParams(
            collective_id=collective_id, has_side_effects=True, vmem_limit_bytes=48 * MIB
        ),
        name="gather_weights",
    )(first, mid, last, hid, out)


def plus(left, right):
    return left.astype(jnp.float32) + right.astype(jnp.float32)


def reduce_kernel(n_dp, *refs):
    g_first, g_mid, g_last, g_hid, g_out, g_vec = refs[:6]
    o_first, o_mid, o_last, o_hid, o_out, o_vec = refs[6:12]
    bufs = refs[12:-9]
    hid_in, hid_sum, hid_land, out_in, out_sum, out_land, vec_land, send_sem, recv_sem = refs[-9:]
    at = Place(n_dp)
    links = Links(send_sem, recv_sem)
    span = at.span
    at.greet(at.dp_peers() + at.sub_peers())
    low = jnp.bfloat16
    wide = g_vec.shape[1] // 4
    vec_cols = lanes_of(at.sub, wide)
    vec_copies = [
        links(g_vec.at[:, vec_cols], vec_land.at[hop], peer)
        for hop, peer in enumerate(at.dp_peers())
    ]
    pieces = [(g_last, o_last, 0, 1), (g_mid, o_mid, 0, 3), (g_mid, o_mid, 3, 3), (g_mid, o_mid, 6, 3), (g_first, o_first, 0, 1)]
    count = len(pieces)
    mine, beside = lanes_of(at.sub), lanes_of(at.row_sub)

    pair = []
    for index, (source, target, start, taps) in enumerate(pieces):
        land = bufs[4 * index]
        sent = []
        for row in range(2):
            cols = lanes_of(2 * row + (1 - at.core))
            sent.append(
                links(source.at[pl.ds(start, taps), :, :, :, cols], land.at[row], at.core_peer)
            )
        pair.append(sent)

    wholes = [(g_hid, hid_in, hid_sum, hid_land), (g_out, out_in, out_sum, out_land)]
    far_copies = [
        links(source.at[:, 1 - at.far], landed, at.far_peer)
        for source, landed, total, land in wholes
    ]

    def whole_far(which):
        source, landed, total, land = wholes[which]
        far_copies[which].wait()
        for near in range(span):
            total[near] = plus(source[near, at.far], landed[near]).astype(low)
        return [
            links(total.at[at.near_index(hop)], land.at[hop - 1], at.near_peer(hop))
            for hop in range(1, span)
        ]

    def whole_near(which, copies):
        source, landed, total, land = wholes[which]
        wait_all(copies)
        value = total[at.near].astype(jnp.float32)
        for hop in range(1, span):
            value = value + land[hop - 1].astype(jnp.float32)
        return value.astype(low)

    def blocks(taps, body):
        def step(index, carry):
            rest = index // 2
            body(rest // span, rest % span, index % 2)
            return carry

        lax.fori_loop(0, taps * span * 2, step, 0)

    def lines(taps, body):
        def step(index, carry):
            body(index // span, index % span)
            return carry

        lax.fori_loop(0, taps * span, step, 0)

    def stage_pair(index):
        source, target, start, taps = pieces[index]
        land = bufs[4 * index]
        wait_all(pair[index])
        for row in range(2):
            cols = lanes_of(2 * row + at.core)

            def body(tap, near, far):
                land[row, tap, near, far] = plus(
                    source[start + tap, near, far, :, cols], land[row, tap, near, far]
                ).astype(low)

            blocks(taps, body)
        if index % 2 == 0:
            return links(land.at[1 - at.row], bufs[4 * index + 1], at.row_peer)
        return links(land.at[:, :, :, 1 - at.far], bufs[4 * index + 1], at.far_peer)

    def stage_second(index, copy):
        source, target, start, taps = pieces[index]
        held, land, total = bufs[4 * index], bufs[4 * index + 1], bufs[4 * index + 2]
        copy.wait()
        if index % 2 == 0:

            def body(tap, near, far):
                land[tap, near, far] = plus(
                    held[at.row, tap, near, far], land[tap, near, far]
                ).astype(low)

            blocks(taps, body)
            return links(land.at[:, :, 1 - at.far], total, at.far_peer)
        for row in range(2):

            def body(tap, near):
                land[row, tap, near] = plus(
                    held[row, tap, near, at.far], land[row, tap, near]
                ).astype(low)

            lines(taps, body)
        return links(land.at[1 - at.row], total, at.row_peer)

    def stage_third(index, copy):
        source, target, start, taps = pieces[index]
        held, total, land = bufs[4 * index + 1], bufs[4 * index + 2], bufs[4 * index + 3]
        copy.wait()

        def body(tap, near):
            part = held[tap, near, at.far] if index % 2 == 0 else held[at.row, tap, near]
            total[tap, near] = plus(part, total[tap, near]).astype(low)

        lines(taps, body)
        return [
            links(total.at[:, at.near_index(hop)], land.at[hop - 1], at.near_peer(hop))
            for hop in range(1, span)
        ]

    def stage_near(index, copies):
        source, target, start, taps = pieces[index]
        total, land = bufs[4 * index + 2], bufs[4 * index + 3]
        wait_all(copies)
        for tap in range(taps):
            value = total[tap, at.near].astype(jnp.float32)
            for hop in range(1, span):
                value = value + land[hop - 1, tap].astype(jnp.float32)
            target[start + tap, :, mine] = value.astype(low)
        slab = target.at[pl.ds(start, taps), :, mine]
        return links(slab, slab, at.row_peer)

    def stage_row(index, copy):
        source, target, start, taps = pieces[index]
        copy.wait()
        sent = []
        for cols in (mine, beside):
            slab = target.at[pl.ds(start, taps), :, cols]
            sent.append(links(slab, slab, at.core_peer))
        return sent

    hold = {}
    final = []
    for tick in range(count + 4):
        if tick < count:
            hold[0, tick] = stage_pair(tick)
        if tick == 0:
            near_hid = whole_far(0)
            near_out = whole_far(1)
        if 0 <= tick - 1 < count:
            hold[1, tick - 1] = stage_second(tick - 1, hold[0, tick - 1])
        if 0 <= tick - 2 < count:
            hold[2, tick - 2] = stage_third(tick - 2, hold[1, tick - 2])
        if tick == 2:
            o_hid[at.sub] = whole_near(0, near_hid)
            hid_row = links(o_hid.at[at.sub], o_hid.at[at.sub], at.row_peer)
            o_out[...] = whole_near(1, near_out)
            wait_all(vec_copies)
            value = g_vec[:, vec_cols]
            for hop in range(n_dp - 1):
                value = value + vec_land[hop]
            o_vec[:, vec_cols] = value
            vec_final = [
                links(o_vec.at[:, vec_cols], o_vec.at[:, vec_cols], peer)
                for peer in at.sub_peers()
            ]
        if 0 <= tick - 3 < count:
            hold[3, tick - 3] = stage_near(tick - 3, hold[2, tick - 3])
        if tick == 3:
            hid_row.wait()
            for which in (at.sub, at.row_sub):
                final.append(links(o_hid.at[which], o_hid.at[which], at.core_peer))
        if 0 <= tick - 4 < count:
            final += stage_row(tick - 4, hold[3, tick - 4])
    wait_all(final)
    wait_all(vec_final)


def reduce_gradients(n_dp, collective_id, first, mid, last, hid, out, vec):
    span = n_dp // 2
    low = jnp.bfloat16
    rows = first.shape[0] // n_dp
    mid_rows = mid.shape[1] // n_dp
    wide, narrow = first.shape[1], out.shape[1]
    some = jax.ShapeDtypeStruct
    bufs = []
    for index in range(5):
        taps, height = (3, mid_rows) if 1 <= index <= 3 else (1, rows)
        block = (height, LANES)
        bufs.append(pltpu.VMEM((2, taps, span, 2) + block, low))
        if index % 2 == 0:
            bufs.append(pltpu.VMEM((taps, span, 2) + block, low))
        else:
            bufs.append(pltpu.VMEM((2, taps, span) + block, low))
        bufs.append(pltpu.VMEM((taps, span) + block, low))
        bufs.append(pltpu.VMEM((span - 1, taps) + block, low))
    copies = 5 * (span + 8) + 2 * (span + 2) + n_dp + 8
    results = pl.pallas_call(
        functools.partial(reduce_kernel, n_dp),
        out_shape=(
            some((1, rows, wide), low),
            some((TAPS, mid_rows, wide), low),
            some((1, rows, wide), low),
            some((4, rows, hid.shape[1]), low),
            some((rows, narrow), low),
            some(vec.shape, vec.dtype),
        ),
        in_specs=[pl.BlockSpec(memory_space=pltpu.VMEM)] * 6,
        out_specs=(pl.BlockSpec(memory_space=pltpu.VMEM),) * 6,
        scratch_shapes=bufs
        + [
            pltpu.VMEM((span, rows, hid.shape[1]), low),
            pltpu.VMEM((span, rows, hid.shape[1]), low),
            pltpu.VMEM((span - 1, rows, hid.shape[1]), low),
            pltpu.VMEM((span, rows, narrow), low),
            pltpu.VMEM((span, rows, narrow), low),
            pltpu.VMEM((span - 1, rows, narrow), low),
            pltpu.VMEM((n_dp - 1, vec.shape[0], vec.shape[1] // 4), jnp.float32),
            pltpu.SemaphoreType.DMA((copies,)),
            pltpu.SemaphoreType.DMA((copies,)),
        ],
        compiler_params=pltpu.CompilerParams(
            collective_id=collective_id, has_side_effects=True, vmem_limit_bytes=56 * MIB
        ),
        name="reduce_gradients",
    )(
        first.reshape(1, span, 2, rows, wide),
        mid.reshape(TAPS, span, 2, mid_rows, wide),
        last.reshape(1, span, 2, rows, wide),
        hid.reshape(span, 2, rows, hid.shape[1]),
        out.reshape(span, 2, rows, narrow),
        vec,
    )
    return results


def row_tile(rows):
    return next(size for size in (192, 160, 128, 96, 64, 48, 32, 24, 16, 8) if rows % size == 0)


def column_sums_kernel(queue_ref, turned_ref, o_ref, total):
    views, rows, _ = queue_ref.shape
    width = turned_ref.shape[1]
    tile = row_tile(rows)
    part = 256
    for view in range(views):
        total[...] = jnp.zeros_like(total)

        def step(index, carry):
            lines = queue_ref[view, pl.ds(index * tile, tile), :]
            for start in range(0, width, part):
                cols = pl.ds(start, part)
                scores = jnp.dot(lines, turned_ref[:, cols], preferred_element_type=jnp.float32)
                shares = jnp.exp2(scores * SINK2)
                total[:, cols] += jnp.sum(shares.reshape(tile // 8, 8, part), 0)
            return carry

        lax.fori_loop(0, rows // tile, step, 0)
        o_ref[pl.ds(view, 1), :] = jnp.sum(total[...], 0, keepdims=True)


def column_sums(queue, turned):
    width = turned.shape[1]
    return pl.pallas_call(
        column_sums_kernel,
        out_shape=jax.ShapeDtypeStruct((queue.shape[0], width), jnp.float32),
        in_specs=[pl.BlockSpec(memory_space=pltpu.VMEM)] * 2,
        out_specs=pl.BlockSpec(memory_space=pltpu.VMEM),
        scratch_shapes=[pltpu.VMEM((8, width), jnp.float32)],
        compiler_params=pltpu.CompilerParams(vmem_limit_bytes=32 * MIB),
        cost_estimate=pl.CostEstimate(
            flops=2 * queue.size * width,
            bytes_accessed=2 * queue.size,
            transcendentals=queue.size // queue.shape[2] * width,
        ),
        name="column_sums",
    )(queue, turned)


def sinkhorn_kernel(
    axis,
    count,
    protos,
    queue_ref,
    turned_ref,
    unit_ref,
    live_ref,
    first_ref,
    grad_ref,
    loss_ref,
    kept,
    scores,
    mine,
    landed,
    shift,
    total,
    send_sem,
    recv_sem,
):
    me = lax.axis_index(axis)
    views, rows, _ = queue_ref.shape
    width = turned_ref.shape[1]
    images = live_ref.shape[0]
    tile = row_tile(rows)
    part = 512
    parts = range(0, width, part)
    mask = live_ref[...]
    greet(axis, count)

    def sum_group(turn):
        copies = []
        for hop in range(1, count):
            copy = pltpu.make_async_remote_copy(
                src_ref=mine.at[turn],
                dst_ref=landed.at[turn, hop],
                send_sem=send_sem.at[turn, hop],
                recv_sem=recv_sem.at[turn, hop],
                device_id={axis: lax.rem(me + hop, count)},
                device_id_type=MESH,
            )
            copy.start()
            copies.append(copy)
        for copy in copies:
            copy.wait()
        whole = mine[turn]
        for hop in range(1, count):
            whole = whole + landed[turn, hop]
        return whole

    for start in parts:
        cols = pl.ds(start, part)
        scores[:, cols] = jnp.dot(
            unit_ref[...], turned_ref[:, cols], preferred_element_type=jnp.float32
        )
        for view in range(views):
            lines = pl.ds(view * images, images)
            shares = jnp.exp2(scores[lines, cols] * SINK2) * mask
            mine[0, pl.ds(view, 1), cols] = first_ref[pl.ds(view, 1), cols] + jnp.sum(
                shares, 0, keepdims=True
            )
    real = lax.broadcasted_iota(jnp.int32, (1, width), 1) < protos
    first = sum_group(0)
    shift[...] = jnp.where(real, jnp.log2(first), 1e30)

    for turn in range(1, ITERS):
        for view in range(views):
            lines = pl.ds(view * images, images)
            row = pl.ds(view, 1)
            if turn == 1:
                own = jnp.exp2(scores[lines, :] * SINK2 - shift[row, :]) * mask
                weight = jnp.sum(own, 1, keepdims=True)
            else:
                own = jnp.exp2(scores[lines, :] * SINK2 - first_log[row, :]) * mask
                weight = jnp.sum(own * shift[row, :], 1, keepdims=True)
            total[...] = own / (weight + (1.0 - mask))

            def step(index, carry):
                span = pl.ds(index * tile, tile)
                if turn == 1:
                    lines = queue_ref[view, span, :]
                sums = jnp.zeros((tile, LANES), jnp.float32)
                for start in parts:
                    cols = pl.ds(start, part)
                    if turn == 1:
                        raw = jnp.dot(lines, turned_ref[:, cols], preferred_element_type=jnp.float32)
                        shares = jnp.exp2(raw * SINK2 - shift[row, cols])
                        kept[view, span, cols] = shares
                    else:
                        shares = kept[view, span, cols] * shift[row, cols]
                    for lane in range(0, part, LANES):
                        sums = sums + shares[:, lane : lane + LANES]
                scale = 1.0 / jnp.sum(sums, 1, keepdims=True)
                for start in parts:
                    cols = pl.ds(start, part)
                    scaled = kept[view, span, cols] * scale
                    total[:, cols] += jnp.sum(scaled.reshape(tile // 8, 8, part), 0)
                return carry

            lax.fori_loop(0, rows // tile, step, 0)
            mine[turn, row, :] = jnp.sum(total[...], 0, keepdims=True)
        if turn == 1:
            first_log = shift[...]
        whole = sum_group(turn)
        shift[...] = jnp.where(real, 1.0 / whole, 0.0)

    codes = []
    for view in range(views):
        lines = pl.ds(view * images, images)
        own = jnp.exp2(scores[lines, :] * SINK2 - first_log[view : view + 1, :]) * mask
        own = own * shift[pl.ds(view, 1), :]
        codes.append(own / (jnp.sum(own, 1, keepdims=True) + (1.0 - mask)))
    code_total = codes[0] + codes[1]
    loss = jnp.zeros((images, 1), jnp.float32)
    for crop in range(CROPS):
        lines = pl.ds(crop * images, images)
        raw = jnp.where(real, scores[lines, :] * SOFT2, -1e30)
        raw = raw - jnp.max(raw, 1, keepdims=True)
        powers = jnp.exp2(raw)
        norm = jnp.sum(powers, 1, keepdims=True)
        others = code_total - codes[crop] if crop < NBIG else code_total
        logs = jnp.where(real, (raw - jnp.log2(norm)) / LOG2E, 0.0)
        loss = loss - jnp.sum(others * logs, 1, keepdims=True)
        weight = (NBIG - 1.0 if crop < NBIG else float(NBIG)) * mask / norm
        grad = (weight * powers - others) / (PAIRS * softmax_temp)
        grad_ref[lines, :] = grad.astype(grad_ref.dtype)
    loss_ref[...] = jnp.broadcast_to(
        jnp.sum(loss, 0, keepdims=True) / PAIRS, loss_ref.shape
    )


def sinkhorn(sizes, collective_id, protos, queue, turned, unit, live, first):
    count = sizes["sub"]
    views, rows, depth = queue.shape
    width = turned.shape[1]
    crops = unit.shape[0]
    return pl.pallas_call(
        functools.partial(sinkhorn_kernel, "sub", count, protos),
        out_shape=(
            jax.ShapeDtypeStruct((crops, width), jnp.bfloat16),
            jax.ShapeDtypeStruct((8, LANES), jnp.float32),
        ),
        in_specs=[pl.BlockSpec(memory_space=pltpu.VMEM)] * 5,
        out_specs=(pl.BlockSpec(memory_space=pltpu.VMEM),) * 2,
        scratch_shapes=[
            pltpu.VMEM((views, rows, width), jnp.float32),
            pltpu.VMEM((crops, width), jnp.float32),
            pltpu.VMEM((ITERS, views, width), jnp.float32),
            pltpu.VMEM((ITERS, count, views, width), jnp.float32),
            pltpu.VMEM((views, width), jnp.float32),
            pltpu.VMEM((8, width), jnp.float32),
            pltpu.SemaphoreType.DMA((ITERS, count)),
            pltpu.SemaphoreType.DMA((ITERS, count)),
        ],
        compiler_params=pltpu.CompilerParams(
            collective_id=collective_id, has_side_effects=True, vmem_limit_bytes=48 * MIB
        ),
        name="sinkhorn",
    )(queue, turned, unit, live, first)


def split_rows(values, images):
    big = BIG * BIG * NBIG * images
    wide = values.shape[1]
    return (
        values[:big].reshape(BIG, BIG, NBIG * images, wide),
        values[big:].reshape(SMALL, SMALL, NSMALL * images, wide),
    )


def patches(values, images, flip):
    parts = []
    for spatial in split_rows(values, images):
        extent = spatial.shape[0]
        padded = jnp.pad(spatial, ((1, 1), (1, 1), (0, 0), (0, 0)))
        pieces = [
            padded[row : row + extent, col : col + extent]
            for row in range(3)
            for col in range(3)
        ]
        if flip:
            pieces = pieces[::-1]
        parts.append(jnp.concatenate(pieces, -1).reshape(-1, TAPS * values.shape[1]))
    return jnp.concatenate(parts, 0)


def spread_crops(values, images):
    wide = values.shape[1]
    big = jnp.broadcast_to(
        values[: NBIG * images] / (BIG * BIG), (BIG * BIG, NBIG * images, wide)
    ).reshape(-1, wide)
    small = jnp.broadcast_to(
        values[NBIG * images :] / (SMALL * SMALL), (SMALL * SMALL, NSMALL * images, wide)
    ).reshape(-1, wide)
    return jnp.concatenate([big, small], 0)


def pool_crops(values, images):
    big, small = split_rows(values, images)
    return jnp.concatenate([jnp.mean(big, (0, 1)), jnp.mean(small, (0, 1))], 0)


def advance(weight, gradient, moment, average, trust):
    step_now = trust * gradient
    moment_new = momentum_rate * moment + step_now
    weight_new = weight - learn_rate * (step_now + momentum_rate * moment_new)
    average_new = average_rate * average + (1.0 - average_rate) * weight_new
    return (weight_new, moment_new, average_new)


def per_device(
    sizes,
    big_maps,
    small_maps,
    live_counts,
    queue,
    bottleneck_outer,
    bottleneck_inner,
    proj_hidden,
    proj_out,
    prototypes,
    norm_params,
    mom_outer,
    mom_inner,
    mom_hidden,
    mom_out,
    mom_protos,
    mom_norms,
    avg_outer,
    avg_inner,
    avg_hidden,
    avg_out,
    avg_protos,
    avg_norms,
):
    n_dp, n_sub = sizes["dp"], sizes["sub"]
    exchange = Exchanger(sizes)
    images = big_maps.shape[0]
    channels = big_maps.shape[-1]
    middle = bottleneck_inner.shape[-1]
    hidden_width = proj_hidden.shape[1]
    out_width = proj_out.shape[1]
    proto_count = prototypes.shape[0]
    proto_width = -(-proto_count // 512) * 512
    here = lax.axis_index("sub")
    share = hidden_width // n_sub

    low = jnp.bfloat16
    hidden_cols = lax.dynamic_slice_in_dim(proj_hidden, here * share, share, 1)
    first_w, inner_low, last_w, hidden_low, out_low = gather_weights(
        n_dp,
        exchange.next_id(),
        bottleneck_outer[0].astype(low),
        bottleneck_inner.astype(low),
        bottleneck_outer[1].astype(low),
        hidden_cols.astype(low),
        proj_out.astype(low),
    )
    first_w = first_w.reshape(channels, middle)
    last_w = last_w.reshape(channels, middle)
    hidden_low = hidden_low.reshape(channels, share)
    out_low = lax.dynamic_slice_in_dim(out_low.reshape(hidden_width, out_width), here * share, share, 0)
    inner_low = inner_low.reshape(TAPS, middle, middle)
    middle_w = inner_low.reshape(TAPS * middle, middle)
    middle_t = jnp.transpose(inner_low, (0, 2, 1)).reshape(TAPS * middle, middle)

    bounds = [0, middle, 2 * middle, 2 * middle + channels, 2 * middle + channels + hidden_width]
    gains = [norm_params[0, bounds[k] : bounds[k + 1]] for k in range(4)]
    biases = [norm_params[1, bounds[k] : bounds[k + 1]] for k in range(4)]
    gains[3] = lax.dynamic_slice_in_dim(gains[3], here * share, share, 0)
    biases[3] = lax.dynamic_slice_in_dim(biases[3], here * share, share, 0)

    proto_inv = lax.rsqrt(jnp.sum(prototypes * prototypes, 1, keepdims=True) + unit_eps)
    centers_low = (prototypes * proto_inv).astype(jnp.bfloat16)
    centers_low = jnp.pad(centers_low, ((0, proto_width - proto_count), (0, 0)))
    turned = centers_low.T
    first_sums = column_sums(queue, turned)

    live_float = live_counts[0].astype(jnp.float32)
    image_mask = (jnp.arange(images) < live_counts[0]).astype(jnp.float32)[:, None]
    per_image = NBIG * BIG * BIG + NSMALL * SMALL * SMALL
    rows = per_image * images
    row_mask = jnp.broadcast_to(image_mask, (per_image, images, 1)).reshape(rows, 1)

    inputs = jnp.concatenate(
        [
            jnp.transpose(big_maps, (2, 3, 1, 0, 4)).reshape(-1, channels),
            jnp.transpose(small_maps, (2, 3, 1, 0, 4)).reshape(-1, channels),
        ],
        0,
    )

    hidden_one = forward_dot(inputs, first_w)
    masked = hidden_one * row_mask
    sums = exchange(
        jnp.stack(
            [
                jnp.sum(masked, 0),
                jnp.sum(masked * hidden_one, 0),
                jnp.broadcast_to(live_float, (middle,)),
            ]
        ),
        "sub",
        name="sums_one",
    )
    lives = sums[:, 2, 0]
    count_all = jnp.sum(lives) * per_image

    def stats(total, squares, count):
        mean = total / count
        return mean, lax.rsqrt(squares / count - mean * mean + norm_eps)

    def group_stats(values, name):
        masked = values * row_mask
        both = exchange(
            jnp.stack([jnp.sum(masked, 0), jnp.sum(masked * values, 0)]), "sub", name=name
        )
        both = jnp.sum(both, 0)
        return stats(both[0], both[1], count_all)

    sums = jnp.sum(sums, 0)
    mean_one, inv_one = stats(sums[0], sums[1], count_all)
    normal_one = (hidden_one - mean_one) * inv_one
    pre_one = gains[0] * normal_one + biases[0]
    act_one = jax.nn.silu(pre_one).astype(jnp.bfloat16)
    columns = patches(act_one, images, False)
    hidden_two = forward_dot(columns, middle_w)
    mean_two, inv_two = group_stats(hidden_two, "sums_two")
    normal_two = (hidden_two - mean_two) * inv_two
    pre_two = gains[1] * normal_two + biases[1]
    act_two = jax.nn.silu(pre_two).astype(jnp.bfloat16)
    hidden_three = against(act_two, last_w)
    mean_three, inv_three = group_stats(hidden_three, "sums_three")
    normal_three = (hidden_three - mean_three) * inv_three
    summed = gains[2] * normal_three + biases[2] + inputs.astype(jnp.float32)
    pooled_low = pool_crops(jax.nn.silu(summed), images).astype(jnp.bfloat16)

    crops = CROPS * images
    pooled_all = exchange(pooled_low, "sub", name="pooled").reshape(n_sub * crops, channels)
    group_mask = (jnp.arange(images)[None, :] < lives[:, None]).astype(jnp.float32)
    group_mask = jnp.broadcast_to(group_mask[:, None, :], (n_sub, CROPS, images))
    group_mask = group_mask.reshape(n_sub * crops, 1)
    count_crops = jnp.sum(lives) * CROPS
    proj_pre = forward_dot(pooled_all, hidden_low)
    masked = proj_pre * group_mask
    mean_four, inv_four = stats(jnp.sum(masked, 0), jnp.sum(masked * proj_pre, 0), count_crops)
    normal_four = (proj_pre - mean_four) * inv_four
    pre_four = gains[3] * normal_four + biases[3]
    act_four = jax.nn.silu(pre_four).astype(jnp.bfloat16)
    partial = forward_dot(act_four, out_low).reshape(n_sub, crops, out_width)
    embedding = jnp.sum(exchange(partial, "sub", scatter=True, name="embedding"), 0)
    unit_embed, embed_back = jax.vjp(unit_rows, embedding)
    unit_low = unit_embed.astype(jnp.bfloat16)

    grad_low, loss_tile = sinkhorn(
        sizes, exchange.next_id(), proto_count, queue, turned, unit_low, image_mask, first_sums
    )
    (grad_embed,) = embed_back(forward_dot(grad_low, centers_low))
    grad_centers = cross_rows(grad_low, unit_low)
    embed_low = grad_embed.astype(jnp.bfloat16)
    embed_all = exchange(embed_low, "sub", name="embed_grad").reshape(n_sub * crops, out_width)

    d_out = cross_rows(act_four, embed_all)
    grad_four = against(embed_all, out_low) * silu_slope(pre_four)
    bias_four = jnp.sum(grad_four, 0)
    gain_four = jnp.sum(grad_four * normal_four, 0)
    proj_low = (
        gains[3]
        * inv_four
        * (grad_four - group_mask * (bias_four + normal_four * gain_four) / count_crops)
    ).astype(jnp.bfloat16)
    d_hidden = cross_rows(pooled_all, proj_low)
    partial = against(proj_low, hidden_low).astype(jnp.bfloat16).reshape(n_sub, crops, channels)
    grad_pooled = exchange(partial, "sub", scatter=True, name="pooled_grad")
    grad_pooled = jnp.sum(grad_pooled.astype(jnp.float32), 0)

    out_group = exchange(d_out.astype(low), "sub", name="out_grad").reshape(hidden_width, out_width)
    four = exchange(
        jnp.stack([gain_four, bias_four, jnp.broadcast_to(loss_tile[0, 0], (share,))]),
        "sub",
        name="sums_four",
    )
    gain_four, bias_four = four[:, 0].reshape(-1), four[:, 1].reshape(-1)
    loss_group = jnp.sum(four[:, 2, 0])
    centers_sum = lax.psum(grad_centers, ("dp", "sub"))[:proto_count]

    def norm_back(grad_out, normal, inv_std, gain_vec, name):
        both = jnp.stack([jnp.sum(grad_out, 0), jnp.sum(grad_out * normal, 0)])
        both = jnp.sum(exchange(both, "sub", name=name), 0)
        grad_in = (
            gain_vec * inv_std * (grad_out - row_mask * (both[0] + normal * both[1]) / count_all)
        )
        return grad_in.astype(jnp.bfloat16), both[1], both[0]

    grad_summed = spread_crops(grad_pooled, images) * silu_slope(summed)
    three_low, gain_three, bias_three = norm_back(
        grad_summed, normal_three, inv_three, gains[2], "back_three"
    )
    d_last = cross_rows(three_low, act_two)
    grad_act_two = forward_dot(three_low, last_w) * silu_slope(pre_two)
    two_low, gain_two, bias_two = norm_back(
        grad_act_two, normal_two, inv_two, gains[1], "back_two"
    )
    d_middle = cross_rows(columns, two_low)
    grad_act_one = forward_dot(patches(two_low, images, True), middle_t) * silu_slope(pre_one)
    one_low, gain_one, bias_one = norm_back(
        grad_act_one, normal_one, inv_one, gains[0], "back_one"
    )
    d_first = cross_rows(inputs, one_low)

    vector = jnp.concatenate(
        [
            gain_one, gain_two, gain_three, gain_four, bias_one, bias_two, bias_three, bias_four,
            jnp.stack(
                [
                    loss_group,
                    jnp.sum(lives),
                    jnp.sum(bottleneck_outer[0] * bottleneck_outer[0]),
                    jnp.sum(bottleneck_outer[1] * bottleneck_outer[1]),
                    jnp.sum(bottleneck_inner * bottleneck_inner),
                    jnp.sum(proj_hidden * proj_hidden),
                    jnp.sum(proj_out * proj_out),
                ]
            ),
        ]
    )
    vec_width = -(-vector.shape[0] // 4096) * 512
    vector = jnp.pad(vector, (0, 8 * vec_width - vector.shape[0])).reshape(8, vec_width)
    shard_first, shard_inner, shard_last, shard_hidden, shard_out, vector = reduce_gradients(
        n_dp,
        exchange.next_id(),
        d_first.astype(low),
        d_middle.astype(low).reshape(TAPS, middle, middle),
        d_last.astype(low),
        d_hidden.astype(low),
        out_group,
        vector,
    )
    shard_outer = jnp.concatenate([shard_first, shard_last], 0).astype(jnp.float32)
    shard_inner = shard_inner.astype(jnp.float32)
    shard_hidden = jnp.transpose(shard_hidden, (1, 0, 2)).reshape(-1, hidden_width)
    shard_hidden = shard_hidden.astype(jnp.float32)
    shard_out = shard_out.astype(jnp.float32)
    vector = vector.reshape(-1)
    norms = norm_params.shape[1]
    norm_sum = vector[: 2 * norms].reshape(2, norms)
    numer_all, live_all = vector[2 * norms], vector[2 * norms + 1]
    weight_all = vector[2 * norms + 2 : 2 * norms + 7]
    proto_unit = prototypes * proto_inv
    proto_sum = proto_inv * (
        centers_sum - proto_unit * jnp.sum(proto_unit * centers_sum, 1, keepdims=True)
    )

    squares = jnp.concatenate(
        [
            jnp.sum(shard_outer * shard_outer, (1, 2)),
            jnp.sum(shard_inner * shard_inner)[None],
            jnp.sum(shard_hidden * shard_hidden)[None],
            jnp.sum(shard_out * shard_out)[None],
        ]
    )
    squares = jnp.broadcast_to(jnp.pad(squares, (0, 3))[:, None], (8, LANES))
    grad_all = jnp.sum(exchange(squares, "dp", name="norms"), 0)[:5, 0]
    trusts = trust_rate * jnp.sqrt(weight_all) / (jnp.sqrt(grad_all) + 1e-12)
    proto_trust = (
        trust_rate
        * jnp.sqrt(jnp.sum(prototypes * prototypes))
        / (jnp.sqrt(jnp.sum(proto_sum * proto_sum)) + 1e-12)
    )
    norm_trust = (
        trust_rate
        * jnp.sqrt(jnp.sum(norm_params * norm_params, 1, keepdims=True))
        / (jnp.sqrt(jnp.sum(norm_sum * norm_sum, 1, keepdims=True)) + 1e-12)
    )
    outer_new = advance(
        bottleneck_outer, shard_outer, mom_outer, avg_outer, trusts[:2][:, None, None]
    )
    inner_new = advance(bottleneck_inner, shard_inner, mom_inner, avg_inner, trusts[2])
    hidden_new = advance(proj_hidden, shard_hidden, mom_hidden, avg_hidden, trusts[3])
    out_new = advance(proj_out, shard_out, mom_out, avg_out, trusts[4])
    protos_new = advance(prototypes, proto_sum, mom_protos, avg_protos, proto_trust)
    norms_new = advance(norm_params, norm_sum, mom_norms, avg_norms, norm_trust)
    news = (outer_new, inner_new, hidden_new, out_new, protos_new, norms_new)
    return (
        (numer_all, live_all)
        + tuple(new[0] for new in news)
        + tuple(new[1] for new in news)
        + tuple(new[2] for new in news)
        + tuple(new[0].astype(jnp.bfloat16) for new in news[:4])
    )


def solution(mesh):
    data = P(("dp", "sub"), None, None, None, None)
    trees = (P(None, "dp", None), P(None, "dp", None), P("dp", None), P("dp", None), P(), P())
    in_specs = (data, data, P(("dp", "sub")), P(None, ("dp", "sub"), None)) + trees * 3
    out_specs = (P(), P()) + trees * 3 + trees[:4]
    sizes = {axis: mesh.shape[axis] for axis in ("dp", "sub")}
    return jax.shard_map(
        functools.partial(per_device, sizes),
        mesh=mesh,
        in_specs=in_specs,
        out_specs=out_specs,
        check_vma=False,
    )
```

```python
import functools
import math

import jax
import jax.numpy as jnp
from jax import lax
from jax.experimental import pallas as pl
from jax.experimental.pallas import tpu as pltpu
from jax.sharding import PartitionSpec as P

NBIG = 2
NSMALL = 6
CROPS = NBIG + NSMALL
BIG = 7
SMALL = 3
TAPS = 9
ITERS = 3
LANES = 128

sink_temp = 0.05
softmax_temp = 0.1
norm_eps = 1e-05
unit_eps = 1e-12
trust_rate = 0.5
learn_rate = 1.0
momentum_rate = 0.5
average_rate = 0.5

MESH = pl.DeviceIdType.MESH
MIB = 1 << 20
LOG2E = math.log2(math.e)
SINK2 = LOG2E / sink_temp
SOFT2 = LOG2E / softmax_temp
PAIRS = NBIG * (CROPS - 1)


def silu_slope(values):
    sigma = jax.nn.sigmoid(values)
    return sigma * (1.0 + values * (1.0 - sigma))


def cross_rows(left, right):
    return lax.dot_general(
        left, right, (((0,), (0,)), ((), ())), preferred_element_type=jnp.float32
    )


def against(left, right):
    return lax.dot_general(
        left, right, (((1,), (1,)), ((), ())), preferred_element_type=jnp.float32
    )


def forward_dot(left, right):
    return jnp.dot(left, right, preferred_element_type=jnp.float32)


def unit_rows(values):
    return values * lax.rsqrt(jnp.sum(values * values, 1, keepdims=True) + unit_eps)


def greet(axis, count):
    me = lax.axis_index(axis)
    barrier = pltpu.get_barrier_semaphore()
    for hop in range(1, count):
        pl.semaphore_signal(
            barrier, inc=1, device_id={axis: lax.rem(me + hop, count)}, device_id_type=MESH
        )
    pl.semaphore_wait(barrier, count - 1)


def exchange_kernel(axis, count, scatter, x_ref, o_ref, send_sem, recv_sem, own_sem):
    me = lax.axis_index(axis)
    greet(axis, count)
    copies = []
    for hop in range(1, count):
        to = lax.rem(me + hop, count)
        copy = pltpu.make_async_remote_copy(
            src_ref=x_ref.at[to] if scatter else x_ref,
            dst_ref=o_ref.at[me],
            send_sem=send_sem.at[hop],
            recv_sem=recv_sem.at[hop],
            device_id={axis: to},
            device_id_type=MESH,
        )
        copy.start()
        copies.append(copy)
    own = pltpu.make_async_copy(x_ref.at[me] if scatter else x_ref, o_ref.at[me], own_sem)
    own.start()
    own.wait()
    for copy in copies:
        copy.wait()


def relay_kernel(scatter, x_ref, o_ref, *rest):
    sub = lax.axis_index("sub")
    row, core = sub // 2, sub % 2
    row_sub, core_sub = 2 * (1 - row) + core, 2 * row + (1 - core)
    barrier = pltpu.get_barrier_semaphore()
    for peer in (row_sub, core_sub):
        pl.semaphore_signal(barrier, inc=1, device_id={"sub": peer}, device_id_type=MESH)
    pl.semaphore_wait(barrier, 2)
    links = Links(*rest[-2:])
    if scatter:
        landed, summed, arrived = rest[:3]
        pair = [
            links(x_ref.at[2 * line + (1 - core)], landed.at[line], {"sub": core_sub})
            for line in (1 - row, row)
        ]
        pair[0].wait()
        summed[...] = plus(x_ref[2 * (1 - row) + core], landed[1 - row]).astype(summed.dtype)
        over = links(summed, arrived, {"sub": row_sub})
        pair[1].wait()
        value = plus(x_ref[sub], landed[row])
        over.wait()
        o_ref[...] = value + arrived[...].astype(jnp.float32)
    else:
        over = links(x_ref, o_ref.at[sub], {"sub": row_sub})
        pair = links(x_ref, o_ref.at[sub], {"sub": core_sub})
        o_ref[sub] = x_ref[...]
        over.wait()
        last = links(o_ref.at[row_sub], o_ref.at[row_sub], {"sub": core_sub})
        pair.wait()
        last.wait()


def relay(collective_id, values, scatter, name):
    block = values.shape[1:] if scatter else values.shape
    held = [pltpu.VMEM((2,) + block, values.dtype)] + [pltpu.VMEM(block, values.dtype)] * 2
    return pl.pallas_call(
        functools.partial(relay_kernel, scatter),
        out_shape=jax.ShapeDtypeStruct(
            block if scatter else (4,) + block, jnp.float32 if scatter else values.dtype
        ),
        in_specs=[pl.BlockSpec(memory_space=pltpu.VMEM)],
        out_specs=pl.BlockSpec(memory_space=pltpu.VMEM),
        scratch_shapes=(held if scatter else [])
        + [pltpu.SemaphoreType.DMA((3,)), pltpu.SemaphoreType.DMA((3,))],
        compiler_params=pltpu.CompilerParams(
            collective_id=collective_id, has_side_effects=True, vmem_limit_bytes=32 * MIB
        ),
        name=name,
    )(values)


class Exchanger:
    def __init__(self, sizes):
        self.sizes = sizes
        self.used = 0

    def next_id(self):
        self.used += 1
        return self.used

    def __call__(self, values, axis, scatter=False, name="exchange"):
        count = self.sizes[axis]
        block = values.shape[1:] if scatter else values.shape
        return pl.pallas_call(
            functools.partial(exchange_kernel, axis, count, scatter),
            out_shape=jax.ShapeDtypeStruct((count,) + block, values.dtype),
            in_specs=[pl.BlockSpec(memory_space=pltpu.VMEM)],
            out_specs=pl.BlockSpec(memory_space=pltpu.VMEM),
            scratch_shapes=[
                pltpu.SemaphoreType.DMA((count,)),
                pltpu.SemaphoreType.DMA((count,)),
                pltpu.SemaphoreType.DMA,
            ],
            compiler_params=pltpu.CompilerParams(
                collective_id=self.next_id(), has_side_effects=True, vmem_limit_bytes=32 * MIB
            ),
            name=name,
        )(values)


class Links:
    def __init__(self, send_sem, recv_sem):
        self.send_sem = send_sem
        self.recv_sem = recv_sem
        self.used = 0

    def __call__(self, source, target, device):
        copy = pltpu.make_async_remote_copy(
            src_ref=source,
            dst_ref=target,
            send_sem=self.send_sem.at[self.used],
            recv_sem=self.recv_sem.at[self.used],
            device_id=device,
            device_id_type=MESH,
        )
        self.used += 1
        copy.start()
        return copy


def wait_all(copies):
    for copy in copies:
        copy.wait()


def lanes_of(index, width=LANES):
    return pl.ds(pl.multiple_of(index * width, LANES), width)


class Place:
    def __init__(self, n_dp):
        self.n_dp = n_dp
        self.span = n_dp // 2
        dp, self.sub = lax.axis_index("dp"), lax.axis_index("sub")
        self.dp = dp
        self.near, self.far = dp // 2, dp % 2
        row, core = self.sub // 2, self.sub % 2
        self.row, self.core = row, core
        self.row_sub = 2 * (1 - row) + core
        self.core_sub = 2 * row + (1 - core)
        self.far_peer = {"dp": self.near * 2 + (1 - self.far)}
        self.row_peer = {"sub": self.row_sub}
        self.core_peer = {"sub": self.core_sub}

    def near_index(self, hop):
        return (self.near + hop) % self.span

    def near_peer(self, hop):
        return {"dp": self.near_index(hop) * 2 + self.far}

    def dp_peers(self):
        return [{"dp": (self.dp + hop) % self.n_dp} for hop in range(1, self.n_dp)]

    def sub_peers(self):
        return [{"sub": (self.sub + hop) % 4} for hop in range(1, 4)]

    def greet(self, peers):
        barrier = pltpu.get_barrier_semaphore()
        for peer in peers:
            pl.semaphore_signal(barrier, inc=1, device_id=peer, device_id_type=MESH)
        pl.semaphore_wait(barrier, len(peers))


ALL = slice(None)


def gather_kernel(n_dp, *refs):
    w_first, w_mid, w_last, w_hid, w_out = refs[:5]
    o_first, o_mid, o_last, o_hid, o_out = refs[5:10]
    send_sem, recv_sem, own_sem = refs[10:]
    at = Place(n_dp)
    links = Links(send_sem, recv_sem)
    at.greet(
        [at.near_peer(hop) for hop in range(1, at.span)]
        + [at.far_peer, at.row_peer, at.core_peer]
    )
    mine, beside = lanes_of(at.sub), lanes_of(at.row_sub)

    def flat(source, target, split):
        return (
            lambda cols: source.at[:, cols],
            lambda near, far, cols: target.at[near, far, :, cols],
            split,
        )

    def taps(start):
        some = pl.ds(start, 3)
        return (
            lambda cols: w_mid.at[some, :, cols],
            lambda near, far, cols: o_mid.at[some, near, far, :, cols],
            True,
        )

    pieces = [
        flat(w_first, o_first, True),
        taps(0),
        taps(3),
        taps(6),
        flat(w_last, o_last, True),
        flat(w_hid, o_hid, False),
        flat(w_out, o_out, False),
    ]
    count = len(pieces)
    own, first, second, third, fourth = [], [], [], [], []
    for index, (source, target, split) in enumerate(pieces):
        cols = mine if split else ALL
        copy = pltpu.make_async_copy(source(cols), target(at.near, at.far, cols), own_sem.at[index])
        copy.start()
        own.append(copy)
    for source, target, split in pieces:
        cols = mine if split else ALL
        first.append(
            [
                links(source(cols), target(at.near, at.far, cols), at.near_peer(hop))
                for hop in range(1, at.span)
            ]
        )
    for tick in range(count + 2):
        if tick < count:
            source, target, split = pieces[tick]
            cols = mine if split else ALL
            own[tick].wait()
            wait_all(first[tick])
            slab = target(ALL, at.far, cols)
            second.append(links(slab, slab, at.far_peer))
        if 1 <= tick < count + 1:
            source, target, split = pieces[tick - 1]
            second[tick - 1].wait()
            if split:
                slab = target(ALL, ALL, mine)
                third.append(links(slab, slab, at.row_peer))
            else:
                third.append(None)
        if tick >= 2:
            source, target, split = pieces[tick - 2]
            if split:
                third[tick - 2].wait()
                for cols in (mine, beside):
                    slab = target(ALL, ALL, cols)
                    fourth.append(links(slab, slab, at.core_peer))
    wait_all(fourth)


def gather_weights(n_dp, collective_id, first, mid, last, hid, out):
    span = n_dp // 2
    rows, middle = first.shape
    some = jax.ShapeDtypeStruct
    low = jnp.bfloat16
    copies = 7 * (span + 4)
    return pl.pallas_call(
        functools.partial(gather_kernel, n_dp),
        out_shape=(
            some((span, 2, rows, middle), low),
            some((TAPS, span, 2, mid.shape[1], middle), low),
            some((span, 2, rows, middle), low),
            some((span, 2, rows, hid.shape[1]), low),
            some((span, 2, rows, out.shape[1]), low),
        ),
        in_specs=[pl.BlockSpec(memory_space=pltpu.VMEM)] * 5,
        out_specs=(pl.BlockSpec(memory_space=pl.ANY),) * 5,
        scratch_shapes=[
            pltpu.SemaphoreType.DMA((copies,)),
            pltpu.SemaphoreType.DMA((copies,)),
            pltpu.SemaphoreType.DMA((7,)),
        ],
        compiler_params=pltpu.CompilerParams(
            collective_id=collective_id, has_side_effects=True, vmem_limit_bytes=48 * MIB
        ),
        name="gather_weights",
    )(first, mid, last, hid, out)


def plus(left, right):
    return left.astype(jnp.float32) + right.astype(jnp.float32)


def reduce_kernel(n_dp, *refs):
    g_first, g_mid, g_last, g_hid, g_some, g_vec = refs[:6]
    o_first, o_mid, o_last, o_hid, o_out, o_vec, o_sq = refs[6:13]
    bufs = refs[13:-13]
    (
        hid_in, hid_sum, hid_land, g_out, out_in, out_sum, out_land, vec_land, sq_mine, sq_land,
        send_sem, recv_sem, own_sem,
    ) = refs[-13:]
    at = Place(n_dp)
    links = Links(send_sem, recv_sem)
    span = at.span
    at.greet(at.dp_peers() + at.sub_peers())
    low = jnp.bfloat16
    wide = g_vec.shape[1] // 4
    vec_cols = lanes_of(at.sub, wide)
    vec_copies = [
        links(g_vec.at[:, vec_cols], vec_land.at[hop], peer)
        for hop, peer in enumerate(at.dp_peers())
    ]
    pieces = [(g_last, o_last, 0, 1), (g_mid, o_mid, 0, 3), (g_mid, o_mid, 3, 3), (g_mid, o_mid, 6, 3), (g_first, o_first, 0, 1)]
    count = len(pieces)
    mine, beside = lanes_of(at.sub), lanes_of(at.row_sub)

    some = g_some.shape[0]
    block = g_out.at[pl.ds(at.sub * some, some)]
    own_out = pltpu.make_async_copy(g_some, block, own_sem)
    own_out.start()
    out_copies = [links(g_some, block, peer) for peer in at.sub_peers()]

    pair = []
    for index, (source, target, start, taps) in enumerate(pieces):
        land = bufs[4 * index]
        sent = []
        for row in range(2):
            cols = lanes_of(2 * row + (1 - at.core))
            sent.append(
                links(source.at[pl.ds(start, taps), :, :, :, cols], land.at[row], at.core_peer)
            )
        pair.append(sent)

    wholes = [(g_hid, hid_in, hid_sum, hid_land), (g_out, out_in, out_sum, out_land)]
    far_copies = [links(g_hid.at[:, 1 - at.far], hid_in, at.far_peer)]

    def whole_far(which):
        source, landed, total, land = wholes[which]
        far_copies[which].wait()
        for near in range(span):
            total[near] = plus(source[near, at.far], landed[near]).astype(low)
        return [
            links(total.at[at.near_index(hop)], land.at[hop - 1], at.near_peer(hop))
            for hop in range(1, span)
        ]

    def whole_near(which, copies):
        source, landed, total, land = wholes[which]
        wait_all(copies)
        value = total[at.near].astype(jnp.float32)
        for hop in range(1, span):
            value = value + land[hop - 1].astype(jnp.float32)
        return value.astype(low)

    def blocks(taps, body):
        def step(index, carry):
            rest = index // 2
            body(rest // span, rest % span, index % 2)
            return carry

        lax.fori_loop(0, taps * span * 2, step, 0)

    def lines(taps, body):
        def step(index, carry):
            body(index // span, index % span)
            return carry

        lax.fori_loop(0, taps * span, step, 0)

    def stage_pair(index):
        source, target, start, taps = pieces[index]
        land = bufs[4 * index]
        wait_all(pair[index])
        for row in range(2):
            cols = lanes_of(2 * row + at.core)

            def body(tap, near, far):
                land[row, tap, near, far] = plus(
                    source[start + tap, near, far, :, cols], land[row, tap, near, far]
                ).astype(low)

            blocks(taps, body)
        if index % 2 == 0:
            return links(land.at[1 - at.row], bufs[4 * index + 1], at.row_peer)
        return links(land.at[:, :, :, 1 - at.far], bufs[4 * index + 1], at.far_peer)

    def stage_second(index, copy):
        source, target, start, taps = pieces[index]
        held, land, total = bufs[4 * index], bufs[4 * index + 1], bufs[4 * index + 2]
        copy.wait()
        if index % 2 == 0:

            def body(tap, near, far):
                land[tap, near, far] = plus(
                    held[at.row, tap, near, far], land[tap, near, far]
                ).astype(low)

            blocks(taps, body)
            return links(land.at[:, :, 1 - at.far], total, at.far_peer)
        for row in range(2):

            def body(tap, near):
                land[row, tap, near] = plus(
                    held[row, tap, near, at.far], land[row, tap, near]
                ).astype(low)

            lines(taps, body)
        return links(land.at[1 - at.row], total, at.row_peer)

    def stage_third(index, copy):
        source, target, start, taps = pieces[index]
        held, total, land = bufs[4 * index + 1], bufs[4 * index + 2], bufs[4 * index + 3]
        copy.wait()

        def body(tap, near):
            part = held[tap, near, at.far] if index % 2 == 0 else held[at.row, tap, near]
            total[tap, near] = plus(part, total[tap, near]).astype(low)

        lines(taps, body)
        return [
            links(total.at[:, at.near_index(hop)], land.at[hop - 1], at.near_peer(hop))
            for hop in range(1, span)
        ]

    sq_mine[0] = jnp.zeros_like(sq_mine[0])

    def squares_of(matrix, value):
        value = value.astype(jnp.float32)
        line = jnp.sum(value * value, 0, keepdims=True)
        for lane in range(0, line.shape[1], LANES):
            sq_mine[0, pl.ds(matrix, 1), :] += line[:, lane : lane + LANES]

    def stage_near(index, copies):
        source, target, start, taps = pieces[index]
        total, land = bufs[4 * index + 2], bufs[4 * index + 3]
        wait_all(copies)
        for tap in range(taps):
            value = total[tap, at.near].astype(jnp.float32)
            for hop in range(1, span):
                value = value + land[hop - 1, tap].astype(jnp.float32)
            value = value.astype(low)
            squares_of({0: 2, count - 1: 0}.get(index, 1), value)
            target[start + tap, :, mine] = value
        slab = target.at[pl.ds(start, taps), :, mine]
        return links(slab, slab, at.row_peer)

    def stage_row(index, copy):
        source, target, start, taps = pieces[index]
        copy.wait()
        sent = []
        for cols in (mine, beside):
            slab = target.at[pl.ds(start, taps), :, cols]
            sent.append(links(slab, slab, at.core_peer))
        return sent

    hold = {}
    final = []
    for tick in range(count + 4):
        if tick < count:
            hold[0, tick] = stage_pair(tick)
        if tick == 0:
            near_hid = whole_far(0)
            own_out.wait()
            wait_all(out_copies)
            far_copies.append(links(g_out.at[:, 1 - at.far], out_in, at.far_peer))
        if tick == 1:
            near_out = whole_far(1)
        if 0 <= tick - 1 < count:
            hold[1, tick - 1] = stage_second(tick - 1, hold[0, tick - 1])
        if 0 <= tick - 2 < count:
            hold[2, tick - 2] = stage_third(tick - 2, hold[1, tick - 2])
        if tick == 2:
            hid_slabs = [
                o_hid.at[:, lanes_of(which, g_hid.shape[3])] for which in (at.sub, at.row_sub)
            ]
            value = whole_near(0, near_hid)
            squares_of(3, value)
            o_hid[:, lanes_of(at.sub, g_hid.shape[3])] = value
            hid_row = links(hid_slabs[0], hid_slabs[0], at.row_peer)
            value = whole_near(1, near_out)
            squares_of(4, value)
            o_out[...] = value
            wait_all(vec_copies)
            value = g_vec[:, vec_cols]
            for hop in range(n_dp - 1):
                value = value + vec_land[hop]
            o_vec[:, vec_cols] = value
            vec_final = [
                links(o_vec.at[:, vec_cols], o_vec.at[:, vec_cols], peer)
                for peer in at.sub_peers()
            ]
        if 0 <= tick - 3 < count:
            hold[3, tick - 3] = stage_near(tick - 3, hold[2, tick - 3])
        if tick == 3:
            hid_row.wait()
            for slab in hid_slabs:
                final.append(links(slab, slab, at.core_peer))
        if 0 <= tick - 4 < count:
            final += stage_row(tick - 4, hold[3, tick - 4])
        if tick == count + 2:
            sq_copies = [
                links(sq_mine.at[0], sq_land.at[hop], peer)
                for hop, peer in enumerate(at.dp_peers())
            ]
    wait_all(sq_copies)
    total = sq_mine[0]
    for hop in range(n_dp - 1):
        total = total + sq_land[hop]
    sq_mine[1] = total
    sq_copies = [
        links(sq_mine.at[1], sq_land.at[n_dp - 1 + hop], peer)
        for hop, peer in enumerate(at.sub_peers())
    ]
    wait_all(sq_copies)
    for hop in range(3):
        total = total + sq_land[n_dp - 1 + hop]
    o_sq[...] = total
    wait_all(final)
    wait_all(vec_final)


def reduce_gradients(n_dp, collective_id, first, mid, last, hid, out, vec):
    span = n_dp // 2
    low = jnp.bfloat16
    rows = first.shape[0] // n_dp
    mid_rows = mid.shape[1] // n_dp
    wide, narrow = first.shape[1], out.shape[1]
    some = jax.ShapeDtypeStruct
    bufs = []
    for index in range(5):
        taps, height = (3, mid_rows) if 1 <= index <= 3 else (1, rows)
        block = (height, LANES)
        bufs.append(pltpu.VMEM((2, taps, span, 2) + block, low))
        if index % 2 == 0:
            bufs.append(pltpu.VMEM((taps, span, 2) + block, low))
        else:
            bufs.append(pltpu.VMEM((2, taps, span) + block, low))
        bufs.append(pltpu.VMEM((taps, span) + block, low))
        bufs.append(pltpu.VMEM((span - 1, taps) + block, low))
    copies = 5 * (span + 8) + 2 * (span + 2) + 2 * n_dp + 16
    results = pl.pallas_call(
        functools.partial(reduce_kernel, n_dp),
        out_shape=(
            some((1, rows, wide), low),
            some((TAPS, mid_rows, wide), low),
            some((1, rows, wide), low),
            some((rows, 4 * hid.shape[1]), low),
            some((rows, narrow), low),
            some(vec.shape, vec.dtype),
            some((8, LANES), jnp.float32),
        ),
        in_specs=[pl.BlockSpec(memory_space=pltpu.VMEM)] * 6,
        out_specs=(pl.BlockSpec(memory_space=pltpu.VMEM),) * 7,
        scratch_shapes=bufs
        + [
            pltpu.VMEM((span, rows, hid.shape[1]), low),
            pltpu.VMEM((span, rows, hid.shape[1]), low),
            pltpu.VMEM((span - 1, rows, hid.shape[1]), low),
            pltpu.VMEM((span, 2, rows, narrow), low),
            pltpu.VMEM((span, rows, narrow), low),
            pltpu.VMEM((span, rows, narrow), low),
            pltpu.VMEM((span - 1, rows, narrow), low),
            pltpu.VMEM((n_dp - 1, vec.shape[0], vec.shape[1] // 4), jnp.float32),
            pltpu.VMEM((2, 8, LANES), jnp.float32),
            pltpu.VMEM((n_dp + 2, 8, LANES), jnp.float32),
            pltpu.SemaphoreType.DMA((copies,)),
            pltpu.SemaphoreType.DMA((copies,)),
            pltpu.SemaphoreType.DMA,
        ],
        compiler_params=pltpu.CompilerParams(
            collective_id=collective_id, has_side_effects=True, vmem_limit_bytes=56 * MIB
        ),
        name="reduce_gradients",
    )(
        first.reshape(1, span, 2, rows, wide),
        mid.reshape(TAPS, span, 2, mid_rows, wide),
        last.reshape(1, span, 2, rows, wide),
        hid.reshape(span, 2, rows, hid.shape[1]),
        out.reshape(span // 4, 2, rows, narrow),
        vec,
    )
    return results


def row_tile(rows):
    return next(size for size in (192, 160, 128, 96, 64, 48, 32, 24, 16, 8) if rows % size == 0)


def column_sums_kernel(queue_ref, proto_ref, centers_ref, turned_ref, o_ref, total):
    views, rows, _ = queue_ref.shape
    protos, depth = proto_ref.shape
    width = turned_ref.shape[1]
    tile = row_tile(rows)
    part = 256
    for start in range(0, width, part):
        here = max(0, min(part, protos - start))
        values = jnp.zeros((part, depth), jnp.float32)
        if here:
            values = proto_ref[pl.ds(start, here), :]
            values = values * lax.rsqrt(jnp.sum(values * values, 1, keepdims=True) + unit_eps)
        if here < part:
            values = jnp.concatenate([values, jnp.zeros((part - here, depth), jnp.float32)], 0)
        centers_ref[pl.ds(start, part), :] = values.astype(jnp.bfloat16)
        turned_ref[:, pl.ds(start, part)] = values.T.astype(jnp.bfloat16)
    for view in range(views):
        total[...] = jnp.zeros_like(total)

        def step(index, carry):
            lines = queue_ref[view, pl.ds(index * tile, tile), :]
            for start in range(0, width, part):
                cols = pl.ds(start, part)
                scores = jnp.dot(lines, turned_ref[:, cols], preferred_element_type=jnp.float32)
                shares = jnp.exp2(scores * SINK2)
                total[:, cols] += jnp.sum(shares.reshape(tile // 8, 8, part), 0)
            return carry

        lax.fori_loop(0, rows // tile, step, 0)
        o_ref[pl.ds(view, 1), :] = jnp.sum(total[...], 0, keepdims=True)


def column_sums(queue, prototypes, width):
    depth = prototypes.shape[1]
    return pl.pallas_call(
        column_sums_kernel,
        out_shape=(
            jax.ShapeDtypeStruct((width, depth), jnp.bfloat16),
            jax.ShapeDtypeStruct((depth, width), jnp.bfloat16),
            jax.ShapeDtypeStruct((queue.shape[0], width), jnp.float32),
        ),
        in_specs=[pl.BlockSpec(memory_space=pltpu.VMEM)] * 2,
        out_specs=(pl.BlockSpec(memory_space=pltpu.VMEM),) * 3,
        scratch_shapes=[pltpu.VMEM((8, width), jnp.float32)],
        compiler_params=pltpu.CompilerParams(vmem_limit_bytes=32 * MIB),
        cost_estimate=pl.CostEstimate(
            flops=2 * queue.size * width,
            bytes_accessed=2 * queue.size,
            transcendentals=queue.size // queue.shape[2] * width,
        ),
        name="column_sums",
    )(queue, prototypes)


def sinkhorn_kernel(
    axis,
    count,
    protos,
    queue_ref,
    centers_ref,
    turned_ref,
    partial_ref,
    live_ref,
    first_ref,
    embed_ref,
    proto_grad_ref,
    loss_ref,
    grad,
    parts_land,
    kept,
    scores,
    mine,
    landed,
    shift,
    total,
    send_sem,
    recv_sem,
):
    me = lax.axis_index(axis)
    views, rows, _ = queue_ref.shape
    width = turned_ref.shape[1]
    images = live_ref.shape[0]
    tile = row_tile(rows)
    part = 512
    parts = range(0, width, part)
    mask = live_ref[...]
    greet(axis, count)

    def to_group(turn, source, target):
        copies = []
        for hop in range(1, count):
            to = lax.rem(me + hop, count)
            copy = pltpu.make_async_remote_copy(
                src_ref=source(to),
                dst_ref=target(hop),
                send_sem=send_sem.at[turn, hop],
                recv_sem=recv_sem.at[turn, hop],
                device_id={axis: to},
                device_id_type=MESH,
            )
            copy.start()
            copies.append(copy)
        for copy in copies:
            copy.wait()

    to_group(ITERS, lambda to: partial_ref.at[to], lambda hop: parts_land.at[hop])
    embedding = partial_ref[me]
    for hop in range(1, count):
        embedding = embedding + parts_land[hop]
    inverse = lax.rsqrt(jnp.sum(embedding * embedding, 1, keepdims=True) + unit_eps)
    unit = embedding * inverse
    unit_low = unit.astype(jnp.bfloat16)

    def sum_group(turn):
        copies = []
        for hop in range(1, count):
            copy = pltpu.make_async_remote_copy(
                src_ref=mine.at[turn],
                dst_ref=landed.at[turn, hop],
                send_sem=send_sem.at[turn, hop],
                recv_sem=recv_sem.at[turn, hop],
                device_id={axis: lax.rem(me + hop, count)},
                device_id_type=MESH,
            )
            copy.start()
            copies.append(copy)
        for copy in copies:
            copy.wait()
        whole = mine[turn]
        for hop in range(1, count):
            whole = whole + landed[turn, hop]
        return whole

    for start in parts:
        cols = pl.ds(start, part)
        scores[:, cols] = jnp.dot(
            unit_low, turned_ref[:, cols], preferred_element_type=jnp.float32
        )
        for view in range(views):
            lines = pl.ds(view * images, images)
            shares = jnp.exp2(scores[lines, cols] * SINK2) * mask
            mine[0, pl.ds(view, 1), cols] = first_ref[pl.ds(view, 1), cols] + jnp.sum(
                shares, 0, keepdims=True
            )
    real = lax.broadcasted_iota(jnp.int32, (1, width), 1) < protos
    first = sum_group(0)
    shift[...] = jnp.where(real, jnp.log2(first), 1e30)

    for turn in range(1, ITERS):
        for view in range(views):
            lines = pl.ds(view * images, images)
            row = pl.ds(view, 1)
            if turn == 1:
                own = jnp.exp2(scores[lines, :] * SINK2 - shift[row, :]) * mask
                weight = jnp.sum(own, 1, keepdims=True)
            else:
                own = jnp.exp2(scores[lines, :] * SINK2 - first_log[row, :]) * mask
                weight = jnp.sum(own * shift[row, :], 1, keepdims=True)
            total[...] = own / (weight + (1.0 - mask))

            def step(index, carry):
                span = pl.ds(index * tile, tile)
                if turn == 1:
                    lines = queue_ref[view, span, :]
                sums = jnp.zeros((tile, LANES), jnp.float32)
                for start in parts:
                    cols = pl.ds(start, part)
                    if turn == 1:
                        raw = jnp.dot(lines, turned_ref[:, cols], preferred_element_type=jnp.float32)
                        shares = jnp.exp2(raw * SINK2 - shift[row, cols])
                        kept[view, span, cols] = shares
                    else:
                        shares = kept[view, span, cols] * shift[row, cols]
                    for lane in range(0, part, LANES):
                        sums = sums + shares[:, lane : lane + LANES]
                scale = 1.0 / jnp.sum(sums, 1, keepdims=True)
                for start in parts:
                    cols = pl.ds(start, part)
                    scaled = kept[view, span, cols] * scale
                    total[:, cols] += jnp.sum(scaled.reshape(tile // 8, 8, part), 0)
                return carry

            lax.fori_loop(0, rows // tile, step, 0)
            mine[turn, row, :] = jnp.sum(total[...], 0, keepdims=True)
        if turn == 1:
            first_log = shift[...]
        whole = sum_group(turn)
        shift[...] = jnp.where(real, 1.0 / whole, 0.0)

    codes = []
    for view in range(views):
        lines = pl.ds(view * images, images)
        own = jnp.exp2(scores[lines, :] * SINK2 - first_log[view : view + 1, :]) * mask
        own = own * shift[pl.ds(view, 1), :]
        codes.append(own / (jnp.sum(own, 1, keepdims=True) + (1.0 - mask)))
    code_total = codes[0] + codes[1]
    loss = jnp.zeros((images, 1), jnp.float32)
    for crop in range(CROPS):
        lines = pl.ds(crop * images, images)
        raw = jnp.where(real, scores[lines, :] * SOFT2, -1e30)
        raw = raw - jnp.max(raw, 1, keepdims=True)
        powers = jnp.exp2(raw)
        norm = jnp.sum(powers, 1, keepdims=True)
        others = code_total - codes[crop] if crop < NBIG else code_total
        logs = jnp.where(real, (raw - jnp.log2(norm)) / LOG2E, 0.0)
        loss = loss - jnp.sum(others * logs, 1, keepdims=True)
        weight = (NBIG - 1.0 if crop < NBIG else float(NBIG)) * mask / norm
        grad[lines, :] = (weight * powers - others) / (PAIRS * softmax_temp)
    loss_ref[...] = jnp.broadcast_to(
        jnp.sum(loss, 0, keepdims=True) / PAIRS, loss_ref.shape
    )
    grad_unit = jnp.zeros(unit.shape, jnp.float32)
    for start in parts:
        cols = pl.ds(start, part)
        some = grad[:, cols].astype(jnp.bfloat16)
        grad_unit = grad_unit + jnp.dot(
            some, centers_ref[cols, :], preferred_element_type=jnp.float32
        )
        proto_grad_ref[cols, :] = cross_rows(some, unit_low)
    grad_embed = inverse * (
        grad_unit - unit * jnp.sum(unit * grad_unit, 1, keepdims=True)
    )
    embed_ref[me] = grad_embed.astype(jnp.bfloat16)
    to_group(ITERS + 1, lambda to: embed_ref.at[me], lambda hop: embed_ref.at[me])


def sinkhorn(sizes, collective_id, protos, queue, centers, turned, partial, live, first):
    count = sizes["sub"]
    views, rows, depth = queue.shape
    width = turned.shape[1]
    crops = partial.shape[1]
    return pl.pallas_call(
        functools.partial(sinkhorn_kernel, "sub", count, protos),
        out_shape=(
            jax.ShapeDtypeStruct((count, crops, depth), jnp.bfloat16),
            jax.ShapeDtypeStruct((width, depth), jnp.float32),
            jax.ShapeDtypeStruct((8, LANES), jnp.float32),
        ),
        in_specs=[pl.BlockSpec(memory_space=pltpu.VMEM)] * 6,
        out_specs=(pl.BlockSpec(memory_space=pltpu.VMEM),) * 3,
        scratch_shapes=[
            pltpu.VMEM((crops, width), jnp.float32),
            pltpu.VMEM((count, crops, depth), jnp.float32),
            pltpu.VMEM((views, rows, width), jnp.float32),
            pltpu.VMEM((crops, width), jnp.float32),
            pltpu.VMEM((ITERS, views, width), jnp.float32),
            pltpu.VMEM((ITERS, count, views, width), jnp.float32),
            pltpu.VMEM((views, width), jnp.float32),
            pltpu.VMEM((8, width), jnp.float32),
            pltpu.SemaphoreType.DMA((ITERS + 2, count)),
            pltpu.SemaphoreType.DMA((ITERS + 2, count)),
        ],
        compiler_params=pltpu.CompilerParams(
            collective_id=collective_id, has_side_effects=True, vmem_limit_bytes=48 * MIB
        ),
        name="sinkhorn",
    )(queue, centers, turned, partial, live, first)


def split_rows(values, images):
    big = BIG * BIG * NBIG * images
    wide = values.shape[1]
    return (
        values[:big].reshape(BIG, BIG, NBIG * images, wide),
        values[big:].reshape(SMALL, SMALL, NSMALL * images, wide),
    )


def patches(values, images, flip):
    parts = []
    for spatial in split_rows(values, images):
        extent = spatial.shape[0]
        padded = jnp.pad(spatial, ((1, 1), (1, 1), (0, 0), (0, 0)))
        pieces = [
            padded[row : row + extent, col : col + extent]
            for row in range(3)
            for col in range(3)
        ]
        if flip:
            pieces = pieces[::-1]
        parts.append(jnp.concatenate(pieces, -1).reshape(-1, TAPS * values.shape[1]))
    return jnp.concatenate(parts, 0)


def spread_crops(values, images):
    wide = values.shape[1]
    big = jnp.broadcast_to(
        values[: NBIG * images] / (BIG * BIG), (BIG * BIG, NBIG * images, wide)
    ).reshape(-1, wide)
    small = jnp.broadcast_to(
        values[NBIG * images :] / (SMALL * SMALL), (SMALL * SMALL, NSMALL * images, wide)
    ).reshape(-1, wide)
    return jnp.concatenate([big, small], 0)


def pool_crops(values, images):
    big, small = split_rows(values, images)
    return jnp.concatenate([jnp.mean(big, (0, 1)), jnp.mean(small, (0, 1))], 0)


def advance(weight, gradient, moment, average, trust):
    step_now = trust * gradient
    moment_new = momentum_rate * moment + step_now
    weight_new = weight - learn_rate * (step_now + momentum_rate * moment_new)
    average_new = average_rate * average + (1.0 - average_rate) * weight_new
    return (weight_new, moment_new, average_new)


def per_device(
    sizes,
    big_maps,
    small_maps,
    live_counts,
    queue,
    bottleneck_outer,
    bottleneck_inner,
    proj_hidden,
    proj_out,
    prototypes,
    norm_params,
    mom_outer,
    mom_inner,
    mom_hidden,
    mom_out,
    mom_protos,
    mom_norms,
    avg_outer,
    avg_inner,
    avg_hidden,
    avg_out,
    avg_protos,
    avg_norms,
):
    n_dp, n_sub = sizes["dp"], sizes["sub"]
    exchange = Exchanger(sizes)
    images = big_maps.shape[0]
    channels = big_maps.shape[-1]
    middle = bottleneck_inner.shape[-1]
    hidden_width = proj_hidden.shape[1]
    out_width = proj_out.shape[1]
    proto_count = prototypes.shape[0]
    proto_width = -(-proto_count // 512) * 512
    here = lax.axis_index("sub")
    share = hidden_width // n_sub

    low = jnp.bfloat16
    hidden_cols = lax.dynamic_slice_in_dim(proj_hidden, here * share, share, 1)
    first_w, inner_low, last_w, hidden_low, out_low = gather_weights(
        n_dp,
        exchange.next_id(),
        bottleneck_outer[0].astype(low),
        bottleneck_inner.astype(low),
        bottleneck_outer[1].astype(low),
        hidden_cols.astype(low),
        proj_out.astype(low),
    )
    first_w = first_w.reshape(channels, middle)
    last_w = last_w.reshape(channels, middle)
    hidden_low = hidden_low.reshape(channels, share)
    out_low = lax.dynamic_slice_in_dim(out_low.reshape(hidden_width, out_width), here * share, share, 0)
    inner_low = inner_low.reshape(TAPS, middle, middle)
    middle_w = inner_low.reshape(TAPS * middle, middle)
    middle_t = jnp.transpose(inner_low, (0, 2, 1)).reshape(TAPS * middle, middle)

    bounds = [0, middle, 2 * middle, 2 * middle + channels, 2 * middle + channels + hidden_width]
    gains = [norm_params[0, bounds[k] : bounds[k + 1]] for k in range(4)]
    biases = [norm_params[1, bounds[k] : bounds[k + 1]] for k in range(4)]
    gains[3] = lax.dynamic_slice_in_dim(gains[3], here * share, share, 0)
    biases[3] = lax.dynamic_slice_in_dim(biases[3], here * share, share, 0)

    proto_inv = lax.rsqrt(jnp.sum(prototypes * prototypes, 1, keepdims=True) + unit_eps)
    centers_low, turned, first_sums = column_sums(queue, prototypes, proto_width)

    live_float = live_counts[0].astype(jnp.float32)
    image_mask = (jnp.arange(images) < live_counts[0]).astype(jnp.float32)[:, None]
    per_image = NBIG * BIG * BIG + NSMALL * SMALL * SMALL
    rows = per_image * images
    row_mask = jnp.broadcast_to(image_mask, (per_image, images, 1)).reshape(rows, 1)

    inputs = jnp.concatenate(
        [
            jnp.transpose(big_maps, (2, 3, 1, 0, 4)).reshape(-1, channels),
            jnp.transpose(small_maps, (2, 3, 1, 0, 4)).reshape(-1, channels),
        ],
        0,
    )

    hidden_one = forward_dot(inputs, first_w)
    masked = hidden_one * row_mask
    sums = exchange(
        jnp.stack(
            [
                jnp.sum(masked, 0),
                jnp.sum(masked * hidden_one, 0),
                jnp.broadcast_to(live_float, (middle,)),
            ]
        ),
        "sub",
        name="sums_one",
    )
    lives = sums[:, 2, 0]
    count_all = jnp.sum(lives) * per_image

    def stats(total, squares, count):
        mean = total / count
        return mean, lax.rsqrt(squares / count - mean * mean + norm_eps)

    def group_stats(values, name):
        masked = values * row_mask
        both = exchange(
            jnp.stack([jnp.sum(masked, 0), jnp.sum(masked * values, 0)]), "sub", name=name
        )
        both = jnp.sum(both, 0)
        return stats(both[0], both[1], count_all)

    sums = jnp.sum(sums, 0)
    mean_one, inv_one = stats(sums[0], sums[1], count_all)
    normal_one = (hidden_one - mean_one) * inv_one
    pre_one = gains[0] * normal_one + biases[0]
    act_one = jax.nn.silu(pre_one).astype(jnp.bfloat16)
    columns = patches(act_one, images, False)
    hidden_two = forward_dot(columns, middle_w)
    mean_two, inv_two = group_stats(hidden_two, "sums_two")
    normal_two = (hidden_two - mean_two) * inv_two
    pre_two = gains[1] * normal_two + biases[1]
    act_two = jax.nn.silu(pre_two).astype(jnp.bfloat16)
    hidden_three = against(act_two, last_w)
    mean_three, inv_three = group_stats(hidden_three, "sums_three")
    normal_three = (hidden_three - mean_three) * inv_three
    summed = gains[2] * normal_three + biases[2] + inputs.astype(jnp.float32)
    pooled_low = pool_crops(jax.nn.silu(summed), images).astype(jnp.bfloat16)

    crops = CROPS * images
    pooled_all = relay(exchange.next_id(), pooled_low, False, "pooled").reshape(n_sub * crops, channels)
    group_mask = (jnp.arange(images)[None, :] < lives[:, None]).astype(jnp.float32)
    group_mask = jnp.broadcast_to(group_mask[:, None, :], (n_sub, CROPS, images))
    group_mask = group_mask.reshape(n_sub * crops, 1)
    count_crops = jnp.sum(lives) * CROPS
    proj_pre = forward_dot(pooled_all, hidden_low)
    masked = proj_pre * group_mask
    mean_four, inv_four = stats(jnp.sum(masked, 0), jnp.sum(masked * proj_pre, 0), count_crops)
    normal_four = (proj_pre - mean_four) * inv_four
    pre_four = gains[3] * normal_four + biases[3]
    act_four = jax.nn.silu(pre_four).astype(jnp.bfloat16)
    partial = forward_dot(act_four, out_low).reshape(n_sub, crops, out_width)

    embed_all, grad_centers, loss_tile = sinkhorn(
        sizes,
        exchange.next_id(),
        proto_count,
        queue,
        centers_low,
        turned,
        partial,
        image_mask,
        first_sums,
    )
    embed_all = embed_all.reshape(n_sub * crops, out_width)

    d_out = cross_rows(act_four, embed_all)
    grad_four = against(embed_all, out_low) * silu_slope(pre_four)
    bias_four = jnp.sum(grad_four, 0)
    gain_four = jnp.sum(grad_four * normal_four, 0)
    proj_low = (
        gains[3]
        * inv_four
        * (grad_four - group_mask * (bias_four + normal_four * gain_four) / count_crops)
    ).astype(jnp.bfloat16)
    d_hidden = cross_rows(pooled_all, proj_low)
    partial = against(proj_low, hidden_low).astype(jnp.bfloat16).reshape(n_sub, crops, channels)
    grad_pooled = relay(exchange.next_id(), partial, True, "pooled_grad")

    four = exchange(
        jnp.stack([gain_four, bias_four, jnp.broadcast_to(loss_tile[0, 0], (share,))]),
        "sub",
        name="sums_four",
    )
    gain_four, bias_four = four[:, 0].reshape(-1), four[:, 1].reshape(-1)
    loss_group = jnp.sum(four[:, 2, 0])
    centers_sum = lax.psum(grad_centers, ("dp", "sub"))[:proto_count]

    def norm_back(grad_out, normal, inv_std, gain_vec, name):
        both = jnp.stack([jnp.sum(grad_out, 0), jnp.sum(grad_out * normal, 0)])
        both = jnp.sum(exchange(both, "sub", name=name), 0)
        grad_in = (
            gain_vec * inv_std * (grad_out - row_mask * (both[0] + normal * both[1]) / count_all)
        )
        return grad_in.astype(jnp.bfloat16), both[1], both[0]

    grad_summed = spread_crops(grad_pooled, images) * silu_slope(summed)
    three_low, gain_three, bias_three = norm_back(
        grad_summed, normal_three, inv_three, gains[2], "back_three"
    )
    d_last = cross_rows(three_low, act_two)
    grad_act_two = forward_dot(three_low, last_w) * silu_slope(pre_two)
    two_low, gain_two, bias_two = norm_back(
        grad_act_two, normal_two, inv_two, gains[1], "back_two"
    )
    d_middle = cross_rows(columns, two_low)
    grad_act_one = forward_dot(patches(two_low, images, True), middle_t) * silu_slope(pre_one)
    one_low, gain_one, bias_one = norm_back(
        grad_act_one, normal_one, inv_one, gains[0], "back_one"
    )
    d_first = cross_rows(inputs, one_low)

    scalars = jnp.stack(
        [
            loss_group,
            jnp.sum(lives),
            jnp.sum(bottleneck_outer[0] * bottleneck_outer[0]),
            jnp.sum(bottleneck_outer[1] * bottleneck_outer[1]),
            jnp.sum(bottleneck_inner * bottleneck_inner),
            jnp.sum(proj_hidden * proj_hidden),
            jnp.sum(proj_out * proj_out),
        ]
    )
    width = 4 * middle
    vector = jnp.concatenate(
        [
            jnp.concatenate([gain_one, gain_two, bias_one, bias_two]).reshape(1, width),
            gain_three.reshape(-1, width),
            gain_four.reshape(-1, width),
            bias_three.reshape(-1, width),
            bias_four.reshape(-1, width),
            jnp.pad(scalars, (0, width - 7))[None],
            jnp.zeros((2, width), jnp.float32),
        ],
        0,
    )
    shard_first, shard_inner, shard_last, shard_hidden, shard_out, vector, grad_all = reduce_gradients(
        n_dp,
        exchange.next_id(),
        d_first.astype(low),
        d_middle.astype(low).reshape(TAPS, middle, middle),
        d_last.astype(low),
        d_hidden.astype(low),
        d_out.astype(low),
        vector,
    )
    shard_outer = jnp.concatenate([shard_first, shard_last], 0).astype(jnp.float32)
    shard_inner = shard_inner.astype(jnp.float32)
    shard_hidden = shard_hidden.astype(jnp.float32)
    shard_out = shard_out.astype(jnp.float32)
    norm_sum = jnp.stack(
        [
            jnp.concatenate([vector[0, : 2 * middle], vector[1], vector[2]]),
            jnp.concatenate([vector[0, 2 * middle :], vector[3], vector[4]]),
        ]
    )
    numer_all, live_all, weight_all = vector[5, 0], vector[5, 1], vector[5, 2:7]
    proto_unit = prototypes * proto_inv
    proto_sum = proto_inv * (
        centers_sum - proto_unit * jnp.sum(proto_unit * centers_sum, 1, keepdims=True)
    )

    grad_all = jnp.sum(grad_all[:5], 1) / jnp.array([1.0, 1.0, 1.0, 1.0, 4.0], jnp.float32)
    grad_all = jnp.stack([grad_all[0], grad_all[2], grad_all[1], grad_all[3], grad_all[4]])
    trusts = trust_rate * jnp.sqrt(weight_all) / (jnp.sqrt(grad_all) + 1e-12)
    proto_trust = (
        trust_rate
        * jnp.sqrt(jnp.sum(prototypes * prototypes))
        / (jnp.sqrt(jnp.sum(proto_sum * proto_sum)) + 1e-12)
    )
    norm_trust = (
        trust_rate
        * jnp.sqrt(jnp.sum(norm_params * norm_params, 1, keepdims=True))
        / (jnp.sqrt(jnp.sum(norm_sum * norm_sum, 1, keepdims=True)) + 1e-12)
    )
    outer_new = advance(
        bottleneck_outer, shard_outer, mom_outer, avg_outer, trusts[:2][:, None, None]
    )
    inner_new = advance(bottleneck_inner, shard_inner, mom_inner, avg_inner, trusts[2])
    hidden_new = advance(proj_hidden, shard_hidden, mom_hidden, avg_hidden, trusts[3])
    out_new = advance(proj_out, shard_out, mom_out, avg_out, trusts[4])
    protos_new = advance(prototypes, proto_sum, mom_protos, avg_protos, proto_trust)
    norms_new = advance(norm_params, norm_sum, mom_norms, avg_norms, norm_trust)
    news = (outer_new, inner_new, hidden_new, out_new, protos_new, norms_new)
    return (
        (numer_all, live_all)
        + tuple(new[0] for new in news)
        + tuple(new[1] for new in news)
        + tuple(new[2] for new in news)
        + tuple(new[0].astype(jnp.bfloat16) for new in news[:4])
    )


def solution(mesh):
    data = P(("dp", "sub"), None, None, None, None)
    trees = (P(None, "dp", None), P(None, "dp", None), P("dp", None), P("dp", None), P(), P())
    in_specs = (data, data, P(("dp", "sub")), P(None, ("dp", "sub"), None)) + trees * 3
    out_specs = (P(), P()) + trees * 3 + trees[:4]
    sizes = {axis: mesh.shape[axis] for axis in ("dp", "sub")}
    return jax.shard_map(
        functools.partial(per_device, sizes),
        mesh=mesh,
        in_specs=in_specs,
        out_specs=out_specs,
        check_vma=False,
    )
```

```python
import functools
import math

import jax
import jax.numpy as jnp
from jax import lax
from jax.experimental import pallas as pl
from jax.experimental.pallas import tpu as pltpu
from jax.sharding import PartitionSpec as P

NBIG = 2
NSMALL = 6
CROPS = NBIG + NSMALL
BIG = 7
SMALL = 3
TAPS = 9
ITERS = 3
LANES = 128

sink_temp = 0.05
softmax_temp = 0.1
norm_eps = 1e-05
unit_eps = 1e-12
trust_rate = 0.5
learn_rate = 1.0
momentum_rate = 0.5
average_rate = 0.5

MESH = pl.DeviceIdType.MESH
MIB = 1 << 20
LOG2E = math.log2(math.e)
SINK2 = LOG2E / sink_temp
SOFT2 = LOG2E / softmax_temp
PAIRS = NBIG * (CROPS - 1)


def silu_slope(values):
    sigma = jax.nn.sigmoid(values)
    return sigma * (1.0 + values * (1.0 - sigma))


def cross_rows(left, right):
    return lax.dot_general(
        left, right, (((0,), (0,)), ((), ())), preferred_element_type=jnp.float32
    )


def against(left, right):
    return lax.dot_general(
        left, right, (((1,), (1,)), ((), ())), preferred_element_type=jnp.float32
    )


def forward_dot(left, right):
    return jnp.dot(left, right, preferred_element_type=jnp.float32)


def unit_rows(values):
    return values * lax.rsqrt(jnp.sum(values * values, 1, keepdims=True) + unit_eps)


def greet(axis, count):
    me = lax.axis_index(axis)
    barrier = pltpu.get_barrier_semaphore()
    for hop in range(1, count):
        pl.semaphore_signal(
            barrier, inc=1, device_id={axis: lax.rem(me + hop, count)}, device_id_type=MESH
        )
    pl.semaphore_wait(barrier, count - 1)


def exchange_kernel(axis, count, scatter, x_ref, o_ref, send_sem, recv_sem, own_sem):
    me = lax.axis_index(axis)
    greet(axis, count)
    copies = []
    for hop in range(1, count):
        to = lax.rem(me + hop, count)
        copy = pltpu.make_async_remote_copy(
            src_ref=x_ref.at[to] if scatter else x_ref,
            dst_ref=o_ref.at[me],
            send_sem=send_sem.at[hop],
            recv_sem=recv_sem.at[hop],
            device_id={axis: to},
            device_id_type=MESH,
        )
        copy.start()
        copies.append(copy)
    own = pltpu.make_async_copy(x_ref.at[me] if scatter else x_ref, o_ref.at[me], own_sem)
    own.start()
    own.wait()
    for copy in copies:
        copy.wait()


def relay_kernel(scatter, x_ref, o_ref, *rest):
    sub = lax.axis_index("sub")
    row, core = sub // 2, sub % 2
    row_sub, core_sub = 2 * (1 - row) + core, 2 * row + (1 - core)
    barrier = pltpu.get_barrier_semaphore()
    for peer in (row_sub, core_sub):
        pl.semaphore_signal(barrier, inc=1, device_id={"sub": peer}, device_id_type=MESH)
    pl.semaphore_wait(barrier, 2)
    links = Links(*rest[-2:])
    if scatter:
        landed, summed, arrived = rest[:3]
        pair = [
            links(x_ref.at[2 * line + (1 - core)], landed.at[line], {"sub": core_sub})
            for line in (1 - row, row)
        ]
        pair[0].wait()
        summed[...] = plus(x_ref[2 * (1 - row) + core], landed[1 - row]).astype(summed.dtype)
        over = links(summed, arrived, {"sub": row_sub})
        pair[1].wait()
        value = plus(x_ref[sub], landed[row])
        over.wait()
        o_ref[...] = value + arrived[...].astype(jnp.float32)
    else:
        over = links(x_ref, o_ref.at[sub], {"sub": row_sub})
        pair = links(x_ref, o_ref.at[sub], {"sub": core_sub})
        o_ref[sub] = x_ref[...]
        over.wait()
        last = links(o_ref.at[row_sub], o_ref.at[row_sub], {"sub": core_sub})
        pair.wait()
        last.wait()


def relay(collective_id, values, scatter, name):
    block = values.shape[1:] if scatter else values.shape
    held = [pltpu.VMEM((2,) + block, values.dtype)] + [pltpu.VMEM(block, values.dtype)] * 2
    return pl.pallas_call(
        functools.partial(relay_kernel, scatter),
        out_shape=jax.ShapeDtypeStruct(
            block if scatter else (4,) + block, jnp.float32 if scatter else values.dtype
        ),
        in_specs=[pl.BlockSpec(memory_space=pltpu.VMEM)],
        out_specs=pl.BlockSpec(memory_space=pltpu.VMEM),
        scratch_shapes=(held if scatter else [])
        + [pltpu.SemaphoreType.DMA((3,)), pltpu.SemaphoreType.DMA((3,))],
        compiler_params=pltpu.CompilerParams(
            collective_id=collective_id, has_side_effects=True, vmem_limit_bytes=32 * MIB
        ),
        name=name,
    )(values)


class Exchanger:
    def __init__(self, sizes):
        self.sizes = sizes
        self.used = 0

    def next_id(self):
        self.used += 1
        return self.used

    def __call__(self, values, axis, scatter=False, name="exchange"):
        count = self.sizes[axis]
        block = values.shape[1:] if scatter else values.shape
        return pl.pallas_call(
            functools.partial(exchange_kernel, axis, count, scatter),
            out_shape=jax.ShapeDtypeStruct((count,) + block, values.dtype),
            in_specs=[pl.BlockSpec(memory_space=pltpu.VMEM)],
            out_specs=pl.BlockSpec(memory_space=pltpu.VMEM),
            scratch_shapes=[
                pltpu.SemaphoreType.DMA((count,)),
                pltpu.SemaphoreType.DMA((count,)),
                pltpu.SemaphoreType.DMA,
            ],
            compiler_params=pltpu.CompilerParams(
                collective_id=self.next_id(), has_side_effects=True, vmem_limit_bytes=32 * MIB
            ),
            name=name,
        )(values)


class Links:
    def __init__(self, send_sem, recv_sem):
        self.send_sem = send_sem
        self.recv_sem = recv_sem
        self.used = 0

    def __call__(self, source, target, device):
        copy = pltpu.make_async_remote_copy(
            src_ref=source,
            dst_ref=target,
            send_sem=self.send_sem.at[self.used],
            recv_sem=self.recv_sem.at[self.used],
            device_id=device,
            device_id_type=MESH,
        )
        self.used += 1
        copy.start()
        return copy


def wait_all(copies):
    for copy in copies:
        copy.wait()


def lanes_of(index, width=LANES):
    return pl.ds(pl.multiple_of(index * width, LANES), width)


class Place:
    def __init__(self, n_dp):
        self.n_dp = n_dp
        self.span = n_dp // 2
        dp, self.sub = lax.axis_index("dp"), lax.axis_index("sub")
        self.dp = dp
        self.near, self.far = dp // 2, dp % 2
        row, core = self.sub // 2, self.sub % 2
        self.row, self.core = row, core
        self.row_sub = 2 * (1 - row) + core
        self.core_sub = 2 * row + (1 - core)
        self.far_peer = {"dp": self.near * 2 + (1 - self.far)}
        self.row_peer = {"sub": self.row_sub}
        self.core_peer = {"sub": self.core_sub}

    def near_index(self, hop):
        return (self.near + hop) % self.span

    def near_peer(self, hop):
        return {"dp": self.near_index(hop) * 2 + self.far}

    def dp_peers(self):
        return [{"dp": (self.dp + hop) % self.n_dp} for hop in range(1, self.n_dp)]

    def sub_peers(self):
        return [{"sub": (self.sub + hop) % 4} for hop in range(1, 4)]

    def greet(self, peers):
        barrier = pltpu.get_barrier_semaphore()
        for peer in peers:
            pl.semaphore_signal(barrier, inc=1, device_id=peer, device_id_type=MESH)
        pl.semaphore_wait(barrier, len(peers))


ALL = slice(None)


def sigmoid_of(values):
    return 0.5 * jnp.tanh(0.5 * values) + 0.5


def rows_at(start, size):
    return pl.ds(start if isinstance(start, int) else pl.multiple_of(start, 16), size)


def tap_blocks(images, flip):
    moves = [[] for _ in range(TAPS)]
    zeros = [[] for _ in range(TAPS)]
    base = 0
    for extent, lines in ((BIG, NBIG * images), (SMALL, NSMALL * images)):
        for tap in range(TAPS):
            down, right = tap // 3 - 1, tap % 3 - 1
            if flip:
                down, right = -down, -right
            for row in range(extent):
                start = base + row * extent * lines
                if not 0 <= row + down < extent:
                    zeros[tap].append((start, extent * lines))
                    continue
                left, stop = max(0, -right), min(extent, extent - right)
                moves[tap].append(
                    (
                        start + left * lines,
                        base + ((row + down) * extent + left + right) * lines,
                        (stop - left) * lines,
                    )
                )
                if left:
                    zeros[tap].append((start, left * lines))
                if stop < extent:
                    zeros[tap].append((start + stop * lines, (extent - stop) * lines))
        base += extent * extent * lines
    return moves, zeros


def fill_columns(columns, source, images, flip):
    wide = source.shape[1]
    moves, zeros = tap_blocks(images, flip)
    for tap in range(TAPS):
        cols = pl.ds(tap * wide, wide)
        for target, start, size in moves[tap]:
            columns[pl.ds(target, size), cols] = source[pl.ds(start, size), :]
        for target, size in zeros[tap]:
            columns[pl.ds(target, size), cols] = jnp.zeros((size, wide), columns.dtype)


def masked_sums(values, mask, total):
    rows, wide = values.shape
    blocks = values.reshape(rows // 8, 8, wide)
    masked = blocks * mask
    total[0] += jnp.sum(masked, 0)
    total[1] += jnp.sum(masked * blocks, 0)


class GroupSums:
    def __init__(self, at, links):
        self.at, self.links = at, links

    def start(self, mine, land):
        self.mine, self.land = mine, land
        self.copies = [
            self.links(mine, land.at[hop], peer) for hop, peer in enumerate(self.at.sub_peers())
        ]

    def finish(self):
        wait_all(self.copies)
        value = self.mine[...]
        for hop in range(3):
            value = value + self.land[hop]
        return value


def forward_kernel(n_dp, images, *refs):
    w_first, w_mid, w_last, w_hid, w_out, x_ref, norm_ref, live_ref = refs[:8]
    (
        o_mid, o_last, o_hid, o_out, o_columns, o_one, o_two, o_act, o_stat, o_pooled, o_live,
    ) = refs[8:19]
    (
        first_w, mid_w, last_w, columns, act_one, act_two, one, two, three, total, pool,
        sums_a, land_a, sums_b, land_b, sums_c, land_c, pooled, send_sem, recv_sem, own_sem,
    ) = refs[19:]
    at = Place(n_dp)
    links = Links(send_sem, recv_sem)
    at.greet(
        [at.near_peer(hop) for hop in range(1, at.span)] + [at.far_peer] + at.sub_peers()
    )
    low = jnp.bfloat16
    middle = first_w.shape[3]
    channels = x_ref.shape[1]
    rows = x_ref.shape[0]
    mask = live_ref[...][:, :1]
    half = middle // 2

    def flat(source, target, split):
        return (
            lambda cols: source.at[:, cols],
            lambda near, far, cols: target.at[near, far, :, cols],
            split,
        )

    def taps(start, split):
        some = pl.ds(start, 3)
        return (
            lambda cols: w_mid.at[some, :, cols],
            lambda near, far, cols: mid_w.at[some, near, far, :, cols],
            split,
        )

    pieces = [
        flat(w_first, first_w, 4),
        taps(0, 4),
        taps(3, 2),
        taps(6, 4),
        flat(w_last, last_w, 2),
        flat(w_hid, o_hid, 1),
        flat(w_out, o_out, 1),
    ]
    count = len(pieces)
    mine = {4: lanes_of(at.sub), 2: lanes_of(at.core, half), 1: ALL}
    own, first, second, third, fourth = [], [], [], [], []
    for index, (source, target, split) in enumerate(pieces):
        cols = mine[split]
        copy = pltpu.make_async_copy(source(cols), target(at.near, at.far, cols), own_sem.at[index])
        copy.start()
        own.append(copy)
    for source, target, split in pieces:
        cols = mine[split]
        first.append(
            [
                links(source(cols), target(at.near, at.far, cols), at.near_peer(hop))
                for hop in range(1, at.span)
            ]
        )

    def tick(now):
        if now < count:
            source, target, split = pieces[now]
            own[now].wait()
            wait_all(first[now])
            slab = target(ALL, at.far, mine[split])
            second.append(links(slab, slab, at.far_peer))
        if 0 <= now - 1 < count:
            source, target, split = pieces[now - 1]
            second[now - 1].wait()
            slab = target(ALL, ALL, mine[split])
            third.append(links(slab, slab, at.row_peer) if split == 4 else None)
            if split == 2:
                fourth.append([links(slab, slab, at.core_peer)])
            elif split == 1:
                fourth.append([])
            else:
                fourth.append(None)
        if 0 <= now - 2 < count and pieces[now - 2][2] == 4:
            source, target, split = pieces[now - 2]
            third[now - 2].wait()
            slabs = [target(ALL, ALL, cols) for cols in (mine[4], lanes_of(at.row_sub))]
            fourth[now - 2] = [links(slab, slab, at.core_peer) for slab in slabs]

    def arrived(index):
        wait_all(fourth[index])

    tile = rows // 4
    sums = GroupSums(at, links)

    def pack(target, wide):
        target[pl.ds(0, 1), :] = jnp.sum(total[0, :, :wide], 0, keepdims=True)
        target[pl.ds(1, 1), :] = jnp.sum(total[1, :, :wide], 0, keepdims=True)

    def settle(value, count_all, start, wide):
        mean = value[0:1] / count_all
        inverse = lax.rsqrt(value[1:2] / count_all - mean * mean + norm_eps)
        o_stat[pl.ds(0, 1), pl.ds(start, wide)] = mean
        o_stat[pl.ds(1, 1), pl.ds(start, wide)] = inverse
        scale = norm_ref[pl.ds(0, 1), pl.ds(start, wide)] * inverse
        return scale, norm_ref[pl.ds(1, 1), pl.ds(start, wide)] - scale * mean

    for now in range(4):
        tick(now)
    arrived(0)
    tick(4)

    total[...] = jnp.zeros_like(total)

    def step_one(index, carry):
        span = rows_at(index * tile, tile)
        value = jnp.dot(
            x_ref[span, :],
            first_w[...].reshape(channels, middle),
            preferred_element_type=jnp.float32,
        )
        one[span, :] = value
        masked_sums(value, mask, total.at[:, :, pl.ds(0, middle)])
        return carry

    lax.fori_loop(0, 4, step_one, 0)
    pack(sums_a, middle)
    live = jnp.sum(mask, 0, keepdims=True)
    sums_a[pl.ds(2, 1), :] = jnp.broadcast_to(live, (1, middle))
    sums.start(sums_a, land_a)
    tick(5)
    value = sums.finish()
    per_image = rows // images
    lives = value[2:3, :1]
    count_all = lives * per_image
    o_live[at.sub] = jnp.broadcast_to(live, o_live.shape[1:])
    for hop in range(3):
        o_live[(at.sub + 3 - hop) % 4] = jnp.broadcast_to(land_a[hop, 2:3, :1], o_live.shape[1:])
    scale, shift = settle(value, count_all, 0, middle)

    def step_act(source, target):
        def step(index, carry):
            span = rows_at(index * tile, tile)
            pre = source[span, :] * scale + shift
            target[span, :] = (pre * sigmoid_of(pre)).astype(low)
            return carry

        lax.fori_loop(0, 4, step, 0)

    step_act(one, act_one)
    save = [pltpu.make_async_copy(one, o_one, own_sem.at[count])]
    save[-1].start()
    tick(6)
    fill_columns(columns, act_one, images, False)
    save.append(pltpu.make_async_copy(columns, o_columns, own_sem.at[count + 1]))
    save[-1].start()

    total[...] = jnp.zeros_like(total)
    for part in range(3):
        arrived(1 + part)
        if part == 0:
            tick(7)

        def step_two(index, carry):
            span = rows_at(index * tile, tile)
            value = jnp.dot(
                columns[span, pl.ds(part * 3 * middle, 3 * middle)],
                mid_w[pl.ds(part * 3, 3)].reshape(3 * middle, middle),
                preferred_element_type=jnp.float32,
            )
            if part:
                value = value + two[span, :]
            two[span, :] = value
            if part == 2:
                masked_sums(value, mask, total.at[:, :, pl.ds(0, middle)])
            return carry

        lax.fori_loop(0, 4, step_two, 0)
    save.append(pltpu.make_async_copy(mid_w, o_mid, own_sem.at[count + 2]))
    save[-1].start()
    pack(sums_b, middle)
    sums.start(sums_b, land_b)
    tick(8)
    scale, shift = settle(sums.finish(), count_all, middle, middle)
    step_act(two, act_two)
    save.append(pltpu.make_async_copy(two, o_two, own_sem.at[count + 3]))
    save[-1].start()
    save.append(pltpu.make_async_copy(act_two, o_act, own_sem.at[count + 4]))
    save[-1].start()

    arrived(4)
    save.append(pltpu.make_async_copy(last_w, o_last, own_sem.at[count + 5]))
    save[-1].start()
    total[...] = jnp.zeros_like(total)

    def step_three(index, carry):
        span = rows_at(index * tile, tile)
        for quarter in range(4):
            wide = channels // 4
            cols = pl.ds(quarter * wide, wide)
            weights = last_w[pl.ds(quarter * (at.span // 4), at.span // 4)].reshape(wide, middle)
            value = against(act_two[span, :], weights)
            three[span, cols] = value
            masked_sums(value, mask, total.at[:, :, cols])
        return carry

    lax.fori_loop(0, 4, step_three, 0)
    pack(sums_c, channels)
    sums.start(sums_c, land_c)
    scale, shift = settle(sums.finish(), count_all, 2 * middle, channels)

    pool[...] = jnp.zeros_like(pool)
    base = 0
    for extent, crops in ((BIG, NBIG), (SMALL, NSMALL)):
        lines = crops * images
        into = pl.ds(0, lines) if extent == BIG else pl.ds(NBIG * images, lines)

        def step_out(index, carry):
            span = rows_at(base + index * extent * lines, extent * lines)
            for start in range(0, channels, 512):
                cols = pl.ds(start, 512)
                pre = three[span, cols] * scale[:, start : start + 512]
                pre = pre + shift[:, start : start + 512] + x_ref[span, cols].astype(jnp.float32)
                value = pre * sigmoid_of(pre)
                pool[into, cols] += jnp.sum(value.reshape(extent, lines, 512), 0)
            return carry

        lax.fori_loop(0, extent, step_out, 0)
        pooled[into, :] = (pool[into, :] * (1.0 / (extent * extent))).astype(low)
        base += extent * extent * lines

    over = links(pooled, o_pooled.at[at.sub], at.row_peer)
    pair = links(pooled, o_pooled.at[at.sub], at.core_peer)
    o_pooled[at.sub] = pooled[...]
    over.wait()
    last = links(o_pooled.at[at.row_sub], o_pooled.at[at.row_sub], at.core_peer)
    pair.wait()
    last.wait()
    for copy in save:
        copy.wait()


def forward_trunk(n_dp, collective_id, images, first, mid, last, hid, out, inputs, norms, live):
    span = n_dp // 2
    height, middle = first.shape
    rows, channels = inputs.shape
    some = jax.ShapeDtypeStruct
    low, full = jnp.bfloat16, jnp.float32
    copies = 7 * (span + 4) + 12
    vmem, anywhere = pl.BlockSpec(memory_space=pltpu.VMEM), pl.BlockSpec(memory_space=pl.ANY)
    return pl.pallas_call(
        functools.partial(forward_kernel, n_dp, images),
        out_shape=(
            some((TAPS, span, 2, mid.shape[1], middle), low),
            some((span, 2, height, middle), low),
            some((span, 2, height, hid.shape[1]), low),
            some((span, 2, height, out.shape[1]), low),
            some((rows, TAPS * middle), low),
            some((rows, middle), full),
            some((rows, middle), full),
            some((rows, middle), low),
            some((2, 2 * middle + channels), full),
            some((4, CROPS * images, channels), low),
            some((4, 8, LANES), full),
        ),
        in_specs=[vmem] * 8,
        out_specs=(anywhere,) * 8 + (vmem,) * 3,
        scratch_shapes=[
            pltpu.VMEM((span, 2, height, middle), low),
            pltpu.VMEM((TAPS, span, 2, mid.shape[1], middle), low),
            pltpu.VMEM((span, 2, height, middle), low),
            pltpu.VMEM((rows, TAPS * middle), low),
            pltpu.VMEM((rows, middle), low),
            pltpu.VMEM((rows, middle), low),
            pltpu.VMEM((rows, middle), full),
            pltpu.VMEM((rows, middle), full),
            pltpu.VMEM((rows, channels), full),
            pltpu.VMEM((2, 8, channels), full),
            pltpu.VMEM((CROPS * images, channels), full),
            pltpu.VMEM((3, middle), full),
            pltpu.VMEM((3, 3, middle), full),
            pltpu.VMEM((2, middle), full),
            pltpu.VMEM((3, 2, middle), full),
            pltpu.VMEM((2, channels), full),
            pltpu.VMEM((3, 2, channels), full),
            pltpu.VMEM((CROPS * images, channels), low),
            pltpu.SemaphoreType.DMA((copies,)),
            pltpu.SemaphoreType.DMA((copies,)),
            pltpu.SemaphoreType.DMA((7 + 6,)),
        ],
        compiler_params=pltpu.CompilerParams(
            collective_id=collective_id, has_side_effects=True, vmem_limit_bytes=60 * MIB
        ),
        name="forward_trunk",
    )(first, mid, last, hid, out, inputs, norms, live)


def plus(left, right):
    return left.astype(jnp.float32) + right.astype(jnp.float32)


def reduce_kernel(n_dp, *refs):
    g_first, g_mid, g_last, g_hid, g_some, g_vec = refs[:6]
    o_first, o_mid, o_last, o_hid, o_out, o_vec, o_sq = refs[6:13]
    bufs = refs[13:-13]
    (
        hid_in, hid_sum, hid_land, g_out, out_in, out_sum, out_land, vec_land, sq_mine, sq_land,
        send_sem, recv_sem, own_sem,
    ) = refs[-13:]
    at = Place(n_dp)
    links = Links(send_sem, recv_sem)
    span = at.span
    at.greet(at.dp_peers() + at.sub_peers())
    low = jnp.bfloat16
    wide = g_vec.shape[1] // 4
    vec_cols = lanes_of(at.sub, wide)
    vec_copies = [
        links(g_vec.at[:, vec_cols], vec_land.at[hop], peer)
        for hop, peer in enumerate(at.dp_peers())
    ]
    pieces = [(g_last, o_last, 0, 1), (g_mid, o_mid, 0, 3), (g_mid, o_mid, 3, 3), (g_mid, o_mid, 6, 3), (g_first, o_first, 0, 1)]
    count = len(pieces)
    mine, beside = lanes_of(at.sub), lanes_of(at.row_sub)

    some = g_some.shape[0]
    block = g_out.at[pl.ds(at.sub * some, some)]
    own_out = pltpu.make_async_copy(g_some, block, own_sem)
    own_out.start()
    out_copies = [links(g_some, block, peer) for peer in at.sub_peers()]

    pair = []
    for index, (source, target, start, taps) in enumerate(pieces):
        land = bufs[4 * index]
        sent = []
        for row in range(2):
            cols = lanes_of(2 * row + (1 - at.core))
            sent.append(
                links(source.at[pl.ds(start, taps), :, :, :, cols], land.at[row], at.core_peer)
            )
        pair.append(sent)

    wholes = [(g_hid, hid_in, hid_sum, hid_land), (g_out, out_in, out_sum, out_land)]
    far_copies = [links(g_hid.at[:, 1 - at.far], hid_in, at.far_peer)]

    def whole_far(which):
        source, landed, total, land = wholes[which]
        far_copies[which].wait()
        for near in range(span):
            total[near] = plus(source[near, at.far], landed[near]).astype(low)
        return [
            links(total.at[at.near_index(hop)], land.at[hop - 1], at.near_peer(hop))
            for hop in range(1, span)
        ]

    def whole_near(which, copies):
        source, landed, total, land = wholes[which]
        wait_all(copies)
        value = total[at.near].astype(jnp.float32)
        for hop in range(1, span):
            value = value + land[hop - 1].astype(jnp.float32)
        return value.astype(low)

    def blocks(taps, body):
        def step(index, carry):
            rest = index // 2
            body(rest // span, rest % span, index % 2)
            return carry

        lax.fori_loop(0, taps * span * 2, step, 0)

    def lines(taps, body):
        def step(index, carry):
            body(index // span, index % span)
            return carry

        lax.fori_loop(0, taps * span, step, 0)

    def stage_pair(index):
        source, target, start, taps = pieces[index]
        land = bufs[4 * index]
        wait_all(pair[index])
        for row in range(2):
            cols = lanes_of(2 * row + at.core)

            def body(tap, near, far):
                land[row, tap, near, far] = plus(
                    source[start + tap, near, far, :, cols], land[row, tap, near, far]
                ).astype(low)

            blocks(taps, body)
        if index % 2 == 0:
            return links(land.at[1 - at.row], bufs[4 * index + 1], at.row_peer)
        return links(land.at[:, :, :, 1 - at.far], bufs[4 * index + 1], at.far_peer)

    def stage_second(index, copy):
        source, target, start, taps = pieces[index]
        held, land, total = bufs[4 * index], bufs[4 * index + 1], bufs[4 * index + 2]
        copy.wait()
        if index % 2 == 0:

            def body(tap, near, far):
                land[tap, near, far] = plus(
                    held[at.row, tap, near, far], land[tap, near, far]
                ).astype(low)

            blocks(taps, body)
            return links(land.at[:, :, 1 - at.far], total, at.far_peer)
        for row in range(2):

            def body(tap, near):
                land[row, tap, near] = plus(
                    held[row, tap, near, at.far], land[row, tap, near]
                ).astype(low)

            lines(taps, body)
        return links(land.at[1 - at.row], total, at.row_peer)

    def stage_third(index, copy):
        source, target, start, taps = pieces[index]
        held, total, land = bufs[4 * index + 1], bufs[4 * index + 2], bufs[4 * index + 3]
        copy.wait()

        def body(tap, near):
            part = held[tap, near, at.far] if index % 2 == 0 else held[at.row, tap, near]
            total[tap, near] = plus(part, total[tap, near]).astype(low)

        lines(taps, body)
        return [
            links(total.at[:, at.near_index(hop)], land.at[hop - 1], at.near_peer(hop))
            for hop in range(1, span)
        ]

    sq_mine[0] = jnp.zeros_like(sq_mine[0])

    def squares_of(matrix, value):
        value = value.astype(jnp.float32)
        line = jnp.sum(value * value, 0, keepdims=True)
        for lane in range(0, line.shape[1], LANES):
            sq_mine[0, pl.ds(matrix, 1), :] += line[:, lane : lane + LANES]

    def stage_near(index, copies):
        source, target, start, taps = pieces[index]
        total, land = bufs[4 * index + 2], bufs[4 * index + 3]
        wait_all(copies)
        for tap in range(taps):
            value = total[tap, at.near].astype(jnp.float32)
            for hop in range(1, span):
                value = value + land[hop - 1, tap].astype(jnp.float32)
            value = value.astype(low)
            squares_of({0: 2, count - 1: 0}.get(index, 1), value)
            target[start + tap, :, mine] = value
        slab = target.at[pl.ds(start, taps), :, mine]
        return links(slab, slab, at.row_peer)

    def stage_row(index, copy):
        source, target, start, taps = pieces[index]
        copy.wait()
        sent = []
        for cols in (mine, beside):
            slab = target.at[pl.ds(start, taps), :, cols]
            sent.append(links(slab, slab, at.core_peer))
        return sent

    hold = {}
    final = []
    for tick in range(count + 4):
        if tick < count:
            hold[0, tick] = stage_pair(tick)
        if tick == 0:
            near_hid = whole_far(0)
            own_out.wait()
            wait_all(out_copies)
            far_copies.append(links(g_out.at[:, 1 - at.far], out_in, at.far_peer))
        if tick == 1:
            near_out = whole_far(1)
        if 0 <= tick - 1 < count:
            hold[1, tick - 1] = stage_second(tick - 1, hold[0, tick - 1])
        if 0 <= tick - 2 < count:
            hold[2, tick - 2] = stage_third(tick - 2, hold[1, tick - 2])
        if tick == 2:
            hid_slabs = [
                o_hid.at[:, lanes_of(which, g_hid.shape[3])] for which in (at.sub, at.row_sub)
            ]
            value = whole_near(0, near_hid)
            squares_of(3, value)
            o_hid[:, lanes_of(at.sub, g_hid.shape[3])] = value
            hid_row = links(hid_slabs[0], hid_slabs[0], at.row_peer)
            value = whole_near(1, near_out)
            squares_of(4, value)
            o_out[...] = value
            wait_all(vec_copies)
            value = g_vec[:, vec_cols]
            for hop in range(n_dp - 1):
                value = value + vec_land[hop]
            o_vec[:, vec_cols] = value
            vec_final = [
                links(o_vec.at[:, vec_cols], o_vec.at[:, vec_cols], peer)
                for peer in at.sub_peers()
            ]
        if 0 <= tick - 3 < count:
            hold[3, tick - 3] = stage_near(tick - 3, hold[2, tick - 3])
        if tick == 3:
            hid_row.wait()
            for slab in hid_slabs:
                final.append(links(slab, slab, at.core_peer))
        if 0 <= tick - 4 < count:
            final += stage_row(tick - 4, hold[3, tick - 4])
        if tick == count + 2:
            sq_copies = [
                links(sq_mine.at[0], sq_land.at[hop], peer)
                for hop, peer in enumerate(at.dp_peers())
            ]
    wait_all(sq_copies)
    total = sq_mine[0]
    for hop in range(n_dp - 1):
        total = total + sq_land[hop]
    sq_mine[1] = total
    sq_copies = [
        links(sq_mine.at[1], sq_land.at[n_dp - 1 + hop], peer)
        for hop, peer in enumerate(at.sub_peers())
    ]
    wait_all(sq_copies)
    for hop in range(3):
        total = total + sq_land[n_dp - 1 + hop]
    o_sq[...] = total
    wait_all(final)
    wait_all(vec_final)


def reduce_gradients(n_dp, collective_id, first, mid, last, hid, out, vec):
    span = n_dp // 2
    low = jnp.bfloat16
    rows = first.shape[0] // n_dp
    mid_rows = mid.shape[1] // n_dp
    wide, narrow = first.shape[1], out.shape[1]
    some = jax.ShapeDtypeStruct
    bufs = []
    for index in range(5):
        taps, height = (3, mid_rows) if 1 <= index <= 3 else (1, rows)
        block = (height, LANES)
        bufs.append(pltpu.VMEM((2, taps, span, 2) + block, low))
        if index % 2 == 0:
            bufs.append(pltpu.VMEM((taps, span, 2) + block, low))
        else:
            bufs.append(pltpu.VMEM((2, taps, span) + block, low))
        bufs.append(pltpu.VMEM((taps, span) + block, low))
        bufs.append(pltpu.VMEM((span - 1, taps) + block, low))
    copies = 5 * (span + 8) + 2 * (span + 2) + 2 * n_dp + 16
    results = pl.pallas_call(
        functools.partial(reduce_kernel, n_dp),
        out_shape=(
            some((1, rows, wide), low),
            some((TAPS, mid_rows, wide), low),
            some((1, rows, wide), low),
            some((rows, 4 * hid.shape[1]), low),
            some((rows, narrow), low),
            some(vec.shape, vec.dtype),
            some((8, LANES), jnp.float32),
        ),
        in_specs=[pl.BlockSpec(memory_space=pltpu.VMEM)] * 6,
        out_specs=(pl.BlockSpec(memory_space=pltpu.VMEM),) * 7,
        scratch_shapes=bufs
        + [
            pltpu.VMEM((span, rows, hid.shape[1]), low),
            pltpu.VMEM((span, rows, hid.shape[1]), low),
            pltpu.VMEM((span - 1, rows, hid.shape[1]), low),
            pltpu.VMEM((span, 2, rows, narrow), low),
            pltpu.VMEM((span, rows, narrow), low),
            pltpu.VMEM((span, rows, narrow), low),
            pltpu.VMEM((span - 1, rows, narrow), low),
            pltpu.VMEM((n_dp - 1, vec.shape[0], vec.shape[1] // 4), jnp.float32),
            pltpu.VMEM((2, 8, LANES), jnp.float32),
            pltpu.VMEM((n_dp + 2, 8, LANES), jnp.float32),
            pltpu.SemaphoreType.DMA((copies,)),
            pltpu.SemaphoreType.DMA((copies,)),
            pltpu.SemaphoreType.DMA,
        ],
        compiler_params=pltpu.CompilerParams(
            collective_id=collective_id, has_side_effects=True, vmem_limit_bytes=56 * MIB
        ),
        name="reduce_gradients",
    )(
        first.reshape(1, span, 2, rows, wide),
        mid.reshape(TAPS, span, 2, mid_rows, wide),
        last.reshape(1, span, 2, rows, wide),
        hid.reshape(span, 2, rows, hid.shape[1]),
        out.reshape(span // 4, 2, rows, narrow),
        vec,
    )
    return results


def row_tile(rows):
    return next(size for size in (192, 160, 128, 96, 64, 48, 32, 24, 16, 8) if rows % size == 0)


def column_sums_kernel(queue_ref, proto_ref, centers_ref, turned_ref, o_ref, total):
    views, rows, _ = queue_ref.shape
    protos, depth = proto_ref.shape
    width = turned_ref.shape[1]
    tile = row_tile(rows)
    part = 256
    for start in range(0, width, part):
        here = max(0, min(part, protos - start))
        values = jnp.zeros((part, depth), jnp.float32)
        if here:
            values = proto_ref[pl.ds(start, here), :]
            values = values * lax.rsqrt(jnp.sum(values * values, 1, keepdims=True) + unit_eps)
        if here < part:
            values = jnp.concatenate([values, jnp.zeros((part - here, depth), jnp.float32)], 0)
        centers_ref[pl.ds(start, part), :] = values.astype(jnp.bfloat16)
        turned_ref[:, pl.ds(start, part)] = values.T.astype(jnp.bfloat16)
    for view in range(views):
        total[...] = jnp.zeros_like(total)

        def step(index, carry):
            lines = queue_ref[view, pl.ds(index * tile, tile), :]
            for start in range(0, width, part):
                cols = pl.ds(start, part)
                scores = jnp.dot(lines, turned_ref[:, cols], preferred_element_type=jnp.float32)
                shares = jnp.exp2(scores * SINK2)
                total[:, cols] += jnp.sum(shares.reshape(tile // 8, 8, part), 0)
            return carry

        lax.fori_loop(0, rows // tile, step, 0)
        o_ref[pl.ds(view, 1), :] = jnp.sum(total[...], 0, keepdims=True)


def column_sums(queue, prototypes, width):
    depth = prototypes.shape[1]
    return pl.pallas_call(
        column_sums_kernel,
        out_shape=(
            jax.ShapeDtypeStruct((width, depth), jnp.bfloat16),
            jax.ShapeDtypeStruct((depth, width), jnp.bfloat16),
            jax.ShapeDtypeStruct((queue.shape[0], width), jnp.float32),
        ),
        in_specs=[pl.BlockSpec(memory_space=pltpu.VMEM)] * 2,
        out_specs=(pl.BlockSpec(memory_space=pltpu.VMEM),) * 3,
        scratch_shapes=[pltpu.VMEM((8, width), jnp.float32)],
        compiler_params=pltpu.CompilerParams(vmem_limit_bytes=32 * MIB),
        cost_estimate=pl.CostEstimate(
            flops=2 * queue.size * width,
            bytes_accessed=2 * queue.size,
            transcendentals=queue.size // queue.shape[2] * width,
        ),
        name="column_sums",
    )(queue, prototypes)


def sinkhorn_kernel(
    axis,
    count,
    protos,
    queue_ref,
    centers_ref,
    turned_ref,
    partial_ref,
    live_ref,
    first_ref,
    embed_ref,
    proto_grad_ref,
    loss_ref,
    grad,
    parts_land,
    kept,
    scores,
    mine,
    landed,
    shift,
    total,
    send_sem,
    recv_sem,
):
    me = lax.axis_index(axis)
    views, rows, _ = queue_ref.shape
    width = turned_ref.shape[1]
    images = live_ref.shape[0]
    tile = row_tile(rows)
    part = 512
    parts = range(0, width, part)
    mask = live_ref[...]
    greet(axis, count)

    def to_group(turn, source, target):
        copies = []
        for hop in range(1, count):
            to = lax.rem(me + hop, count)
            copy = pltpu.make_async_remote_copy(
                src_ref=source(to),
                dst_ref=target(hop),
                send_sem=send_sem.at[turn, hop],
                recv_sem=recv_sem.at[turn, hop],
                device_id={axis: to},
                device_id_type=MESH,
            )
            copy.start()
            copies.append(copy)
        for copy in copies:
            copy.wait()

    to_group(ITERS, lambda to: partial_ref.at[to], lambda hop: parts_land.at[hop])
    embedding = partial_ref[me]
    for hop in range(1, count):
        embedding = embedding + parts_land[hop]
    inverse = lax.rsqrt(jnp.sum(embedding * embedding, 1, keepdims=True) + unit_eps)
    unit = embedding * inverse
    unit_low = unit.astype(jnp.bfloat16)

    def sum_group(turn):
        copies = []
        for hop in range(1, count):
            copy = pltpu.make_async_remote_copy(
                src_ref=mine.at[turn],
                dst_ref=landed.at[turn, hop],
                send_sem=send_sem.at[turn, hop],
                recv_sem=recv_sem.at[turn, hop],
                device_id={axis: lax.rem(me + hop, count)},
                device_id_type=MESH,
            )
            copy.start()
            copies.append(copy)
        for copy in copies:
            copy.wait()
        whole = mine[turn]
        for hop in range(1, count):
            whole = whole + landed[turn, hop]
        return whole

    for start in parts:
        cols = pl.ds(start, part)
        scores[:, cols] = jnp.dot(
            unit_low, turned_ref[:, cols], preferred_element_type=jnp.float32
        )
        for view in range(views):
            lines = pl.ds(view * images, images)
            shares = jnp.exp2(scores[lines, cols] * SINK2) * mask
            mine[0, pl.ds(view, 1), cols] = first_ref[pl.ds(view, 1), cols] + jnp.sum(
                shares, 0, keepdims=True
            )
    real = lax.broadcasted_iota(jnp.int32, (1, width), 1) < protos
    first = sum_group(0)
    shift[...] = jnp.where(real, jnp.log2(first), 1e30)

    for turn in range(1, ITERS):
        for view in range(views):
            lines = pl.ds(view * images, images)
            row = pl.ds(view, 1)
            if turn == 1:
                own = jnp.exp2(scores[lines, :] * SINK2 - shift[row, :]) * mask
                weight = jnp.sum(own, 1, keepdims=True)
            else:
                own = jnp.exp2(scores[lines, :] * SINK2 - first_log[row, :]) * mask
                weight = jnp.sum(own * shift[row, :], 1, keepdims=True)
            total[...] = own / (weight + (1.0 - mask))

            def step(index, carry):
                span = pl.ds(index * tile, tile)
                if turn == 1:
                    lines = queue_ref[view, span, :]
                sums = jnp.zeros((tile, LANES), jnp.float32)
                for start in parts:
                    cols = pl.ds(start, part)
                    if turn == 1:
                        raw = jnp.dot(lines, turned_ref[:, cols], preferred_element_type=jnp.float32)
                        shares = jnp.exp2(raw * SINK2 - shift[row, cols])
                        kept[view, span, cols] = shares
                    else:
                        shares = kept[view, span, cols] * shift[row, cols]
                    for lane in range(0, part, LANES):
                        sums = sums + shares[:, lane : lane + LANES]
                scale = 1.0 / jnp.sum(sums, 1, keepdims=True)
                for start in parts:
                    cols = pl.ds(start, part)
                    scaled = kept[view, span, cols] * scale
                    total[:, cols] += jnp.sum(scaled.reshape(tile // 8, 8, part), 0)
                return carry

            lax.fori_loop(0, rows // tile, step, 0)
            mine[turn, row, :] = jnp.sum(total[...], 0, keepdims=True)
        if turn == 1:
            first_log = shift[...]
        whole = sum_group(turn)
        shift[...] = jnp.where(real, 1.0 / whole, 0.0)

    codes = []
    for view in range(views):
        lines = pl.ds(view * images, images)
        own = jnp.exp2(scores[lines, :] * SINK2 - first_log[view : view + 1, :]) * mask
        own = own * shift[pl.ds(view, 1), :]
        codes.append(own / (jnp.sum(own, 1, keepdims=True) + (1.0 - mask)))
    code_total = codes[0] + codes[1]
    loss = jnp.zeros((images, 1), jnp.float32)
    for crop in range(CROPS):
        lines = pl.ds(crop * images, images)
        raw = jnp.where(real, scores[lines, :] * SOFT2, -1e30)
        raw = raw - jnp.max(raw, 1, keepdims=True)
        powers = jnp.exp2(raw)
        norm = jnp.sum(powers, 1, keepdims=True)
        others = code_total - codes[crop] if crop < NBIG else code_total
        logs = jnp.where(real, (raw - jnp.log2(norm)) / LOG2E, 0.0)
        loss = loss - jnp.sum(others * logs, 1, keepdims=True)
        weight = (NBIG - 1.0 if crop < NBIG else float(NBIG)) * mask / norm
        grad[lines, :] = (weight * powers - others) / (PAIRS * softmax_temp)
    loss_ref[...] = jnp.broadcast_to(
        jnp.sum(loss, 0, keepdims=True) / PAIRS, loss_ref.shape
    )
    grad_unit = jnp.zeros(unit.shape, jnp.float32)
    for start in parts:
        cols = pl.ds(start, part)
        some = grad[:, cols].astype(jnp.bfloat16)
        grad_unit = grad_unit + jnp.dot(
            some, centers_ref[cols, :], preferred_element_type=jnp.float32
        )
        proto_grad_ref[cols, :] = cross_rows(some, unit_low)
    grad_embed = inverse * (
        grad_unit - unit * jnp.sum(unit * grad_unit, 1, keepdims=True)
    )
    embed_ref[me] = grad_embed.astype(jnp.bfloat16)
    to_group(ITERS + 1, lambda to: embed_ref.at[me], lambda hop: embed_ref.at[me])


def sinkhorn(sizes, collective_id, protos, queue, centers, turned, partial, live, first):
    count = sizes["sub"]
    views, rows, depth = queue.shape
    width = turned.shape[1]
    crops = partial.shape[1]
    return pl.pallas_call(
        functools.partial(sinkhorn_kernel, "sub", count, protos),
        out_shape=(
            jax.ShapeDtypeStruct((count, crops, depth), jnp.bfloat16),
            jax.ShapeDtypeStruct((width, depth), jnp.float32),
            jax.ShapeDtypeStruct((8, LANES), jnp.float32),
        ),
        in_specs=[pl.BlockSpec(memory_space=pltpu.VMEM)] * 6,
        out_specs=(pl.BlockSpec(memory_space=pltpu.VMEM),) * 3,
        scratch_shapes=[
            pltpu.VMEM((crops, width), jnp.float32),
            pltpu.VMEM((count, crops, depth), jnp.float32),
            pltpu.VMEM((views, rows, width), jnp.float32),
            pltpu.VMEM((crops, width), jnp.float32),
            pltpu.VMEM((ITERS, views, width), jnp.float32),
            pltpu.VMEM((ITERS, count, views, width), jnp.float32),
            pltpu.VMEM((views, width), jnp.float32),
            pltpu.VMEM((8, width), jnp.float32),
            pltpu.SemaphoreType.DMA((ITERS + 2, count)),
            pltpu.SemaphoreType.DMA((ITERS + 2, count)),
        ],
        compiler_params=pltpu.CompilerParams(
            collective_id=collective_id, has_side_effects=True, vmem_limit_bytes=48 * MIB
        ),
        name="sinkhorn",
    )(queue, centers, turned, partial, live, first)


def split_rows(values, images):
    big = BIG * BIG * NBIG * images
    wide = values.shape[1]
    return (
        values[:big].reshape(BIG, BIG, NBIG * images, wide),
        values[big:].reshape(SMALL, SMALL, NSMALL * images, wide),
    )


def patches(values, images, flip):
    parts = []
    for spatial in split_rows(values, images):
        extent = spatial.shape[0]
        padded = jnp.pad(spatial, ((1, 1), (1, 1), (0, 0), (0, 0)))
        pieces = [
            padded[row : row + extent, col : col + extent]
            for row in range(3)
            for col in range(3)
        ]
        if flip:
            pieces = pieces[::-1]
        parts.append(jnp.concatenate(pieces, -1).reshape(-1, TAPS * values.shape[1]))
    return jnp.concatenate(parts, 0)


def spread_crops(values, images):
    wide = values.shape[1]
    big = jnp.broadcast_to(
        values[: NBIG * images] / (BIG * BIG), (BIG * BIG, NBIG * images, wide)
    ).reshape(-1, wide)
    small = jnp.broadcast_to(
        values[NBIG * images :] / (SMALL * SMALL), (SMALL * SMALL, NSMALL * images, wide)
    ).reshape(-1, wide)
    return jnp.concatenate([big, small], 0)


def pool_crops(values, images):
    big, small = split_rows(values, images)
    return jnp.concatenate([jnp.mean(big, (0, 1)), jnp.mean(small, (0, 1))], 0)


def advance(weight, gradient, moment, average, trust):
    step_now = trust * gradient
    moment_new = momentum_rate * moment + step_now
    weight_new = weight - learn_rate * (step_now + momentum_rate * moment_new)
    average_new = average_rate * average + (1.0 - average_rate) * weight_new
    return (weight_new, moment_new, average_new)


def per_device(
    sizes,
    big_maps,
    small_maps,
    live_counts,
    queue,
    bottleneck_outer,
    bottleneck_inner,
    proj_hidden,
    proj_out,
    prototypes,
    norm_params,
    mom_outer,
    mom_inner,
    mom_hidden,
    mom_out,
    mom_protos,
    mom_norms,
    avg_outer,
    avg_inner,
    avg_hidden,
    avg_out,
    avg_protos,
    avg_norms,
):
    n_dp, n_sub = sizes["dp"], sizes["sub"]
    exchange = Exchanger(sizes)
    images = big_maps.shape[0]
    channels = big_maps.shape[-1]
    middle = bottleneck_inner.shape[-1]
    hidden_width = proj_hidden.shape[1]
    out_width = proj_out.shape[1]
    proto_count = prototypes.shape[0]
    proto_width = -(-proto_count // 512) * 512
    here = lax.axis_index("sub")
    share = hidden_width // n_sub

    low = jnp.bfloat16
    hidden_cols = lax.dynamic_slice_in_dim(proj_hidden, here * share, share, 1)
    bounds = [0, middle, 2 * middle, 2 * middle + channels, 2 * middle + channels + hidden_width]
    gains = [norm_params[0, bounds[k] : bounds[k + 1]] for k in range(4)]
    biases = [norm_params[1, bounds[k] : bounds[k + 1]] for k in range(4)]
    gains[3] = lax.dynamic_slice_in_dim(gains[3], here * share, share, 0)
    biases[3] = lax.dynamic_slice_in_dim(biases[3], here * share, share, 0)

    proto_inv = lax.rsqrt(jnp.sum(prototypes * prototypes, 1, keepdims=True) + unit_eps)
    centers_low, turned, first_sums = column_sums(queue, prototypes, proto_width)

    live_float = live_counts[0].astype(jnp.float32)
    image_mask = (jnp.arange(images) < live_counts[0]).astype(jnp.float32)[:, None]
    per_image = NBIG * BIG * BIG + NSMALL * SMALL * SMALL
    rows = per_image * images
    row_mask = jnp.broadcast_to(image_mask, (per_image, images, 1)).reshape(rows, 1)

    inputs = jnp.concatenate(
        [
            jnp.transpose(big_maps, (2, 3, 1, 0, 4)).reshape(-1, channels),
            jnp.transpose(small_maps, (2, 3, 1, 0, 4)).reshape(-1, channels),
        ],
        0,
    )

    (
        inner_low, last_w, hidden_low, out_low, columns, hidden_one, hidden_two, act_two,
        trunk_stat, pooled_all, lives,
    ) = forward_trunk(
        n_dp,
        exchange.next_id(),
        images,
        bottleneck_outer[0].astype(low),
        bottleneck_inner.astype(low),
        bottleneck_outer[1].astype(low),
        hidden_cols.astype(low),
        proj_out.astype(low),
        inputs,
        norm_params,
        jnp.broadcast_to(image_mask, (images, LANES)),
    )
    last_w = last_w.reshape(channels, middle)
    hidden_low = hidden_low.reshape(channels, share)
    out_low = lax.dynamic_slice_in_dim(out_low.reshape(hidden_width, out_width), here * share, share, 0)
    inner_low = inner_low.reshape(TAPS, middle, middle)
    middle_t = jnp.transpose(inner_low, (0, 2, 1)).reshape(TAPS * middle, middle)
    lives = lives[:, 0, 0]
    count_all = jnp.sum(lives) * per_image
    mean_one, mean_two, mean_three = [trunk_stat[0, bounds[k] : bounds[k + 1]] for k in range(3)]
    inv_one, inv_two, inv_three = [trunk_stat[1, bounds[k] : bounds[k + 1]] for k in range(3)]
    normal_one = (hidden_one - mean_one) * inv_one
    pre_one = gains[0] * normal_one + biases[0]
    normal_two = (hidden_two - mean_two) * inv_two
    pre_two = gains[1] * normal_two + biases[1]
    hidden_three = against(act_two, last_w)
    normal_three = (hidden_three - mean_three) * inv_three
    summed = gains[2] * normal_three + biases[2] + inputs.astype(jnp.float32)

    def stats(total, squares, count):
        mean = total / count
        return mean, lax.rsqrt(squares / count - mean * mean + norm_eps)

    crops = CROPS * images
    pooled_all = pooled_all.reshape(n_sub * crops, channels)
    group_mask = (jnp.arange(images)[None, :] < lives[:, None]).astype(jnp.float32)
    group_mask = jnp.broadcast_to(group_mask[:, None, :], (n_sub, CROPS, images))
    group_mask = group_mask.reshape(n_sub * crops, 1)
    count_crops = jnp.sum(lives) * CROPS
    proj_pre = forward_dot(pooled_all, hidden_low)
    masked = proj_pre * group_mask
    mean_four, inv_four = stats(jnp.sum(masked, 0), jnp.sum(masked * proj_pre, 0), count_crops)
    normal_four = (proj_pre - mean_four) * inv_four
    pre_four = gains[3] * normal_four + biases[3]
    act_four = jax.nn.silu(pre_four).astype(jnp.bfloat16)
    partial = forward_dot(act_four, out_low).reshape(n_sub, crops, out_width)

    embed_all, grad_centers, loss_tile = sinkhorn(
        sizes,
        exchange.next_id(),
        proto_count,
        queue,
        centers_low,
        turned,
        partial,
        image_mask,
        first_sums,
    )
    embed_all = embed_all.reshape(n_sub * crops, out_width)

    d_out = cross_rows(act_four, embed_all)
    grad_four = against(embed_all, out_low) * silu_slope(pre_four)
    bias_four = jnp.sum(grad_four, 0)
    gain_four = jnp.sum(grad_four * normal_four, 0)
    proj_low = (
        gains[3]
        * inv_four
        * (grad_four - group_mask * (bias_four + normal_four * gain_four) / count_crops)
    ).astype(jnp.bfloat16)
    d_hidden = cross_rows(pooled_all, proj_low)
    partial = against(proj_low, hidden_low).astype(jnp.bfloat16).reshape(n_sub, crops, channels)
    grad_pooled = relay(exchange.next_id(), partial, True, "pooled_grad")

    four = exchange(
        jnp.stack([gain_four, bias_four, jnp.broadcast_to(loss_tile[0, 0], (share,))]),
        "sub",
        name="sums_four",
    )
    gain_four, bias_four = four[:, 0].reshape(-1), four[:, 1].reshape(-1)
    loss_group = jnp.sum(four[:, 2, 0])
    centers_sum = lax.psum(grad_centers, ("dp", "sub"))[:proto_count]

    def norm_back(grad_out, normal, inv_std, gain_vec, name):
        both = jnp.stack([jnp.sum(grad_out, 0), jnp.sum(grad_out * normal, 0)])
        both = jnp.sum(exchange(both, "sub", name=name), 0)
        grad_in = (
            gain_vec * inv_std * (grad_out - row_mask * (both[0] + normal * both[1]) / count_all)
        )
        return grad_in.astype(jnp.bfloat16), both[1], both[0]

    grad_summed = spread_crops(grad_pooled, images) * silu_slope(summed)
    three_low, gain_three, bias_three = norm_back(
        grad_summed, normal_three, inv_three, gains[2], "back_three"
    )
    d_last = cross_rows(three_low, act_two)
    grad_act_two = forward_dot(three_low, last_w) * silu_slope(pre_two)
    two_low, gain_two, bias_two = norm_back(
        grad_act_two, normal_two, inv_two, gains[1], "back_two"
    )
    d_middle = cross_rows(columns, two_low)
    grad_act_one = forward_dot(patches(two_low, images, True), middle_t) * silu_slope(pre_one)
    one_low, gain_one, bias_one = norm_back(
        grad_act_one, normal_one, inv_one, gains[0], "back_one"
    )
    d_first = cross_rows(inputs, one_low)

    scalars = jnp.stack(
        [
            loss_group,
            jnp.sum(lives),
            jnp.sum(bottleneck_outer[0] * bottleneck_outer[0]),
            jnp.sum(bottleneck_outer[1] * bottleneck_outer[1]),
            jnp.sum(bottleneck_inner * bottleneck_inner),
            jnp.sum(proj_hidden * proj_hidden),
            jnp.sum(proj_out * proj_out),
        ]
    )
    width = 4 * middle
    vector = jnp.concatenate(
        [
            jnp.concatenate([gain_one, gain_two, bias_one, bias_two]).reshape(1, width),
            gain_three.reshape(-1, width),
            gain_four.reshape(-1, width),
            bias_three.reshape(-1, width),
            bias_four.reshape(-1, width),
            jnp.pad(scalars, (0, width - 7))[None],
            jnp.zeros((2, width), jnp.float32),
        ],
        0,
    )
    shard_first, shard_inner, shard_last, shard_hidden, shard_out, vector, grad_all = reduce_gradients(
        n_dp,
        exchange.next_id(),
        d_first.astype(low),
        d_middle.astype(low).reshape(TAPS, middle, middle),
        d_last.astype(low),
        d_hidden.astype(low),
        d_out.astype(low),
        vector,
    )
    shard_outer = jnp.concatenate([shard_first, shard_last], 0).astype(jnp.float32)
    shard_inner = shard_inner.astype(jnp.float32)
    shard_hidden = shard_hidden.astype(jnp.float32)
    shard_out = shard_out.astype(jnp.float32)
    norm_sum = jnp.stack(
        [
            jnp.concatenate([vector[0, : 2 * middle], vector[1], vector[2]]),
            jnp.concatenate([vector[0, 2 * middle :], vector[3], vector[4]]),
        ]
    )
    numer_all, live_all, weight_all = vector[5, 0], vector[5, 1], vector[5, 2:7]
    proto_unit = prototypes * proto_inv
    proto_sum = proto_inv * (
        centers_sum - proto_unit * jnp.sum(proto_unit * centers_sum, 1, keepdims=True)
    )

    grad_all = jnp.sum(grad_all[:5], 1) / jnp.array([1.0, 1.0, 1.0, 1.0, 4.0], jnp.float32)
    grad_all = jnp.stack([grad_all[0], grad_all[2], grad_all[1], grad_all[3], grad_all[4]])
    trusts = trust_rate * jnp.sqrt(weight_all) / (jnp.sqrt(grad_all) + 1e-12)
    proto_trust = (
        trust_rate
        * jnp.sqrt(jnp.sum(prototypes * prototypes))
        / (jnp.sqrt(jnp.sum(proto_sum * proto_sum)) + 1e-12)
    )
    norm_trust = (
        trust_rate
        * jnp.sqrt(jnp.sum(norm_params * norm_params, 1, keepdims=True))
        / (jnp.sqrt(jnp.sum(norm_sum * norm_sum, 1, keepdims=True)) + 1e-12)
    )
    outer_new = advance(
        bottleneck_outer, shard_outer, mom_outer, avg_outer, trusts[:2][:, None, None]
    )
    inner_new = advance(bottleneck_inner, shard_inner, mom_inner, avg_inner, trusts[2])
    hidden_new = advance(proj_hidden, shard_hidden, mom_hidden, avg_hidden, trusts[3])
    out_new = advance(proj_out, shard_out, mom_out, avg_out, trusts[4])
    protos_new = advance(prototypes, proto_sum, mom_protos, avg_protos, proto_trust)
    norms_new = advance(norm_params, norm_sum, mom_norms, avg_norms, norm_trust)
    news = (outer_new, inner_new, hidden_new, out_new, protos_new, norms_new)
    return (
        (numer_all, live_all)
        + tuple(new[0] for new in news)
        + tuple(new[1] for new in news)
        + tuple(new[2] for new in news)
        + tuple(new[0].astype(jnp.bfloat16) for new in news[:4])
    )


def solution(mesh):
    data = P(("dp", "sub"), None, None, None, None)
    trees = (P(None, "dp", None), P(None, "dp", None), P("dp", None), P("dp", None), P(), P())
    in_specs = (data, data, P(("dp", "sub")), P(None, ("dp", "sub"), None)) + trees * 3
    out_specs = (P(), P()) + trees * 3 + trees[:4]
    sizes = {axis: mesh.shape[axis] for axis in ("dp", "sub")}
    return jax.shard_map(
        functools.partial(per_device, sizes),
        mesh=mesh,
        in_specs=in_specs,
        out_specs=out_specs,
        check_vma=False,
    )
```

```python
import functools
import math

import jax
import jax.numpy as jnp
from jax import lax
from jax.experimental import pallas as pl
from jax.experimental.pallas import tpu as pltpu
from jax.sharding import PartitionSpec as P

NBIG = 2
NSMALL = 6
CROPS = NBIG + NSMALL
BIG = 7
SMALL = 3
TAPS = 9
ITERS = 3
LANES = 128

sink_temp = 0.05
softmax_temp = 0.1
norm_eps = 1e-05
unit_eps = 1e-12
trust_rate = 0.5
learn_rate = 1.0
momentum_rate = 0.5
average_rate = 0.5

MESH = pl.DeviceIdType.MESH
MIB = 1 << 20
LOG2E = math.log2(math.e)
SINK2 = LOG2E / sink_temp
SOFT2 = LOG2E / softmax_temp
PAIRS = NBIG * (CROPS - 1)


def silu_slope(values):
    sigma = jax.nn.sigmoid(values)
    return sigma * (1.0 + values * (1.0 - sigma))


def cross_rows(left, right):
    return lax.dot_general(
        left, right, (((0,), (0,)), ((), ())), preferred_element_type=jnp.float32
    )


def against(left, right):
    return lax.dot_general(
        left, right, (((1,), (1,)), ((), ())), preferred_element_type=jnp.float32
    )


def forward_dot(left, right):
    return jnp.dot(left, right, preferred_element_type=jnp.float32)


def unit_rows(values):
    return values * lax.rsqrt(jnp.sum(values * values, 1, keepdims=True) + unit_eps)


def greet(axis, count):
    me = lax.axis_index(axis)
    barrier = pltpu.get_barrier_semaphore()
    for hop in range(1, count):
        pl.semaphore_signal(
            barrier, inc=1, device_id={axis: lax.rem(me + hop, count)}, device_id_type=MESH
        )
    pl.semaphore_wait(barrier, count - 1)


def exchange_kernel(axis, count, scatter, x_ref, o_ref, send_sem, recv_sem, own_sem):
    me = lax.axis_index(axis)
    greet(axis, count)
    copies = []
    for hop in range(1, count):
        to = lax.rem(me + hop, count)
        copy = pltpu.make_async_remote_copy(
            src_ref=x_ref.at[to] if scatter else x_ref,
            dst_ref=o_ref.at[me],
            send_sem=send_sem.at[hop],
            recv_sem=recv_sem.at[hop],
            device_id={axis: to},
            device_id_type=MESH,
        )
        copy.start()
        copies.append(copy)
    own = pltpu.make_async_copy(x_ref.at[me] if scatter else x_ref, o_ref.at[me], own_sem)
    own.start()
    own.wait()
    for copy in copies:
        copy.wait()


class Exchanger:
    def __init__(self, sizes):
        self.sizes = sizes
        self.used = 0

    def next_id(self):
        self.used += 1
        return self.used

    def __call__(self, values, axis, scatter=False, name="exchange"):
        count = self.sizes[axis]
        block = values.shape[1:] if scatter else values.shape
        return pl.pallas_call(
            functools.partial(exchange_kernel, axis, count, scatter),
            out_shape=jax.ShapeDtypeStruct((count,) + block, values.dtype),
            in_specs=[pl.BlockSpec(memory_space=pltpu.VMEM)],
            out_specs=pl.BlockSpec(memory_space=pltpu.VMEM),
            scratch_shapes=[
                pltpu.SemaphoreType.DMA((count,)),
                pltpu.SemaphoreType.DMA((count,)),
                pltpu.SemaphoreType.DMA,
            ],
            compiler_params=pltpu.CompilerParams(
                collective_id=self.next_id(), has_side_effects=True, vmem_limit_bytes=32 * MIB
            ),
            name=name,
        )(values)


class Links:
    def __init__(self, send_sem, recv_sem):
        self.send_sem = send_sem
        self.recv_sem = recv_sem
        self.used = 0

    def __call__(self, source, target, device):
        copy = pltpu.make_async_remote_copy(
            src_ref=source,
            dst_ref=target,
            send_sem=self.send_sem.at[self.used],
            recv_sem=self.recv_sem.at[self.used],
            device_id=device,
            device_id_type=MESH,
        )
        self.used += 1
        copy.start()
        return copy


def wait_all(copies):
    for copy in copies:
        copy.wait()


def lanes_of(index, width=LANES):
    return pl.ds(pl.multiple_of(index * width, LANES), width)


class Place:
    def __init__(self, n_dp):
        self.n_dp = n_dp
        self.span = n_dp // 2
        dp, self.sub = lax.axis_index("dp"), lax.axis_index("sub")
        self.dp = dp
        self.near, self.far = dp // 2, dp % 2
        row, core = self.sub // 2, self.sub % 2
        self.row, self.core = row, core
        self.row_sub = 2 * (1 - row) + core
        self.core_sub = 2 * row + (1 - core)
        self.far_peer = {"dp": self.near * 2 + (1 - self.far)}
        self.row_peer = {"sub": self.row_sub}
        self.core_peer = {"sub": self.core_sub}

    def near_index(self, hop):
        return (self.near + hop) % self.span

    def near_peer(self, hop):
        return {"dp": self.near_index(hop) * 2 + self.far}

    def dp_peers(self):
        return [{"dp": (self.dp + hop) % self.n_dp} for hop in range(1, self.n_dp)]

    def sub_peers(self):
        return [{"sub": (self.sub + hop) % 4} for hop in range(1, 4)]

    def greet(self, peers):
        barrier = pltpu.get_barrier_semaphore()
        for peer in peers:
            pl.semaphore_signal(barrier, inc=1, device_id=peer, device_id_type=MESH)
        pl.semaphore_wait(barrier, len(peers))


ALL = slice(None)


def sigmoid_of(values):
    return 0.5 * jnp.tanh(0.5 * values) + 0.5


def rows_at(start, size):
    return pl.ds(start if isinstance(start, int) else pl.multiple_of(start, 16), size)


def tap_blocks(images, flip):
    moves = [[] for _ in range(TAPS)]
    zeros = [[] for _ in range(TAPS)]
    base = 0
    for extent, lines in ((BIG, NBIG * images), (SMALL, NSMALL * images)):
        for tap in range(TAPS):
            down, right = tap // 3 - 1, tap % 3 - 1
            if flip:
                down, right = -down, -right
            for row in range(extent):
                start = base + row * extent * lines
                if not 0 <= row + down < extent:
                    zeros[tap].append((start, extent * lines))
                    continue
                left, stop = max(0, -right), min(extent, extent - right)
                moves[tap].append(
                    (
                        start + left * lines,
                        base + ((row + down) * extent + left + right) * lines,
                        (stop - left) * lines,
                    )
                )
                if left:
                    zeros[tap].append((start, left * lines))
                if stop < extent:
                    zeros[tap].append((start + stop * lines, (extent - stop) * lines))
        base += extent * extent * lines
    return moves, zeros


def fill_columns(columns, source, images, flip):
    wide = source.shape[1]
    moves, zeros = tap_blocks(images, flip)
    for tap in range(TAPS):
        cols = pl.ds(tap * wide, wide)
        for target, start, size in moves[tap]:
            columns[pl.ds(target, size), cols] = source[pl.ds(start, size), :]
        for target, size in zeros[tap]:
            columns[pl.ds(target, size), cols] = jnp.zeros((size, wide), columns.dtype)


def masked_sums(values, mask, total):
    rows, wide = values.shape
    blocks = values.reshape(rows // 8, 8, wide)
    masked = blocks * mask
    total[0] += jnp.sum(masked, 0)
    total[1] += jnp.sum(masked * blocks, 0)


class GroupSums:
    def __init__(self, at, links):
        self.at, self.links = at, links

    def start(self, mine, land):
        self.mine, self.land = mine, land
        self.copies = [
            self.links(mine, land.at[hop], peer) for hop, peer in enumerate(self.at.sub_peers())
        ]

    def finish(self):
        wait_all(self.copies)
        value = self.mine[...]
        for hop in range(3):
            value = value + self.land[hop]
        return value


def forward_kernel(n_dp, images, *refs):
    w_first, w_mid, w_last, w_hid, w_out, x_ref, norm_ref, live_ref = refs[:8]
    (
        o_mid, o_last, o_hid, o_out, o_one, o_two, o_act, o_stat, o_pooled, o_live, o_slope,
    ) = refs[8:19]
    (
        first_w, mid_w, last_w, out_w, columns, act_one, act_two, one, two, three, total, pool,
        sums_a, land_a, sums_b, land_b, sums_c, land_c, pooled, send_sem, recv_sem, own_sem,
    ) = refs[19:]
    at = Place(n_dp)
    links = Links(send_sem, recv_sem)
    at.greet(
        [at.near_peer(hop) for hop in range(1, at.span)] + [at.far_peer] + at.sub_peers()
    )
    low = jnp.bfloat16
    middle = first_w.shape[3]
    channels = x_ref.shape[1]
    rows = x_ref.shape[0]
    mask = live_ref[...][:, :1]
    half = middle // 2

    def flat(source, target, part, parts, split):
        height = source.shape[0] // parts
        some = pl.ds(part * height, height)
        return (
            lambda cols: source.at[some, cols],
            lambda near, far, cols: target.at[near, far, some, cols],
            split,
        )

    def taps(start, size):
        some = pl.ds(start, size)
        return (
            lambda cols: w_mid.at[some, :, cols],
            lambda near, far, cols: mid_w.at[some, near, far, :, cols],
            4,
        )

    quarter = w_out.shape[0] // 4
    out_rows = pl.ds(at.sub * quarter, quarter)
    pieces = [flat(w_first, first_w, part, 2, 4) for part in range(2)]
    pieces += [taps(0, 1), taps(1, 2), taps(3, 1), taps(4, 2), taps(6, 1), taps(7, 2)]
    pieces += [flat(w_last, last_w, part, 4, 2) for part in range(4)]
    trunk_pieces = len(pieces)
    pieces += [flat(w_hid, o_hid, part, 4, 1) for part in range(4)]
    pieces.append(
        (
            lambda cols: w_out.at[out_rows],
            lambda near, far, cols: out_w.at[near, far],
            1,
        )
    )
    count = len(pieces)
    mine = {4: lanes_of(at.sub), 2: lanes_of(at.core, half), 1: ALL}
    own, first, second, third, fourth = [], [], [], [], []
    for index, (source, target, split) in enumerate(pieces):
        cols = mine[split]
        copy = pltpu.make_async_copy(source(cols), target(at.near, at.far, cols), own_sem.at[index])
        copy.start()
        own.append(copy)

    def begin(index):
        if index < count:
            source, target, split = pieces[index]
            cols = mine[split]
            first.append(
                [
                    links(source(cols), target(at.near, at.far, cols), at.near_peer(hop))
                    for hop in range(1, at.span)
                ]
            )

    for index in range(3):
        begin(index)
    lag = 2
    ticks = count + 2 * lag

    def tick(now):
        if now < count:
            source, target, split = pieces[now]
            own[now].wait()
            wait_all(first[now])
            begin(now + 3)
            slab = target(ALL, at.far, mine[split])
            second.append(links(slab, slab, at.far_peer))
        past = now - lag
        if 0 <= past < count:
            source, target, split = pieces[past]
            second[past].wait()
            slab = target(ALL, ALL, mine[split])
            third.append(links(slab, slab, at.row_peer) if split == 4 else None)
            fourth.append([links(slab, slab, at.core_peer)] if split == 2 else [])
        past = now - 2 * lag
        if 0 <= past < count and pieces[past][2] == 4:
            source, target, split = pieces[past]
            third[past].wait()
            slabs = [target(ALL, ALL, cols) for cols in (mine[4], lanes_of(at.row_sub))]
            fourth[past] = [links(slab, slab, at.core_peer) for slab in slabs]

    def arrived(index):
        wait_all(fourth[index])

    tile = rows // 4
    sums = GroupSums(at, links)

    def pack(target, wide):
        target[pl.ds(0, 1), :] = jnp.sum(total[0, :, :wide], 0, keepdims=True)
        target[pl.ds(1, 1), :] = jnp.sum(total[1, :, :wide], 0, keepdims=True)

    def settle(value, count_all, start, wide):
        mean = value[0:1] / count_all
        inverse = lax.rsqrt(value[1:2] / count_all - mean * mean + norm_eps)
        o_stat[pl.ds(0, 1), pl.ds(start, wide)] = mean
        o_stat[pl.ds(1, 1), pl.ds(start, wide)] = inverse
        scale = norm_ref[pl.ds(0, 1), pl.ds(start, wide)] * inverse
        return scale, norm_ref[pl.ds(1, 1), pl.ds(start, wide)] - scale * mean

    for now in range(6):
        tick(now)
    arrived(0)
    arrived(1)

    total[...] = jnp.zeros_like(total)

    def step_one(index, carry):
        span = rows_at(index * tile, tile)
        value = jnp.dot(
            x_ref[span, :],
            first_w[...].reshape(channels, middle),
            preferred_element_type=jnp.float32,
        )
        one[span, :] = value
        masked_sums(value, mask, total.at[:, :, pl.ds(0, middle)])
        return carry

    lax.fori_loop(0, 4, step_one, 0)
    pack(sums_a, middle)
    live = jnp.sum(mask, 0, keepdims=True)
    sums_a[pl.ds(2, 1), :] = jnp.broadcast_to(live, (1, middle))
    sums.start(sums_a, land_a)
    tick(6)
    value = sums.finish()
    per_image = rows // images
    lives = value[2:3, :1]
    count_all = lives * per_image
    o_live[at.sub] = jnp.broadcast_to(live, o_live.shape[1:])
    for hop in range(3):
        o_live[(at.sub + 3 - hop) % 4] = jnp.broadcast_to(land_a[hop, 2:3, :1], o_live.shape[1:])
    scale, shift = settle(value, count_all, 0, middle)

    def step_act(source, target):
        def step(index, carry):
            span = rows_at(index * tile, tile)
            pre = source[span, :] * scale + shift
            target[span, :] = (pre * sigmoid_of(pre)).astype(low)
            return carry

        lax.fori_loop(0, 4, step, 0)

    step_act(one, act_one)
    save = [pltpu.make_async_copy(one, o_one, own_sem.at[count])]
    save[-1].start()
    tick(7)
    fill_columns(columns, act_one, images, False)

    total[...] = jnp.zeros_like(total)
    for part in range(3):
        for now in range(2):
            tick(8 + 2 * part + now)
        for index in range(2):
            arrived(2 + 2 * part + index)

        def step_two(index, carry):
            span = rows_at(index * tile, tile)
            value = jnp.dot(
                columns[span, pl.ds(part * 3 * middle, 3 * middle)],
                mid_w[pl.ds(part * 3, 3)].reshape(3 * middle, middle),
                preferred_element_type=jnp.float32,
            )
            if part:
                value = value + two[span, :]
            two[span, :] = value
            if part == 2:
                masked_sums(value, mask, total.at[:, :, pl.ds(0, middle)])
            return carry

        lax.fori_loop(0, 4, step_two, 0)
    save.append(pltpu.make_async_copy(mid_w, o_mid, own_sem.at[count + 2]))
    save[-1].start()
    pack(sums_b, middle)
    sums.start(sums_b, land_b)
    scale, shift = settle(sums.finish(), count_all, middle, middle)
    step_act(two, act_two)
    save.append(pltpu.make_async_copy(two, o_two, own_sem.at[count + 3]))
    save[-1].start()
    save.append(pltpu.make_async_copy(act_two, o_act, own_sem.at[count + 4]))
    save[-1].start()

    for now in range(14, trunk_pieces + 2 * lag):
        tick(now)
    for index in range(trunk_pieces - 4, trunk_pieces):
        arrived(index)
    save.append(pltpu.make_async_copy(last_w, o_last, own_sem.at[count + 5]))
    save[-1].start()
    total[...] = jnp.zeros_like(total)

    def step_three(index, carry):
        span = rows_at(index * tile, tile)
        for quarter in range(4):
            wide = channels // 4
            cols = pl.ds(quarter * wide, wide)
            weights = last_w[pl.ds(quarter * (at.span // 4), at.span // 4)].reshape(wide, middle)
            value = against(act_two[span, :], weights)
            three[span, cols] = value
            masked_sums(value, mask, total.at[:, :, cols])
        return carry

    lax.fori_loop(0, 4, step_three, 0)
    pack(sums_c, channels)
    sums.start(sums_c, land_c)
    for now in range(trunk_pieces + 2 * lag, ticks):
        tick(now)
    some = at.span // 4
    out_own = out_w.at[pl.ds(at.sub * some, some)]
    into = o_out.at[:, :, out_rows]
    own.append(pltpu.make_async_copy(out_own, into, own_sem.at[count - 1]))
    own[-1].start()
    out_copies = [
        links(out_w.at[pl.ds(peer["sub"] * some, some)], into, peer) for peer in at.sub_peers()
    ]
    scale, shift = settle(sums.finish(), count_all, 2 * middle, channels)

    pool[...] = jnp.zeros_like(pool)
    o_slope[...] = jnp.zeros_like(o_slope)
    wide = pl.ds(2 * middle, channels)
    center = o_stat[pl.ds(0, 1), wide] * o_stat[pl.ds(1, 1), wide]
    base = 0
    for extent, crops in ((BIG, NBIG), (SMALL, NSMALL)):
        lines = crops * images
        into = pl.ds(0, lines) if extent == BIG else pl.ds(NBIG * images, lines)

        def step_out(index, carry):
            span = rows_at(base + index * extent * lines, extent * lines)
            for start in range(0, channels, 512):
                cols = pl.ds(start, 512)
                pre = three[span, cols] * scale[:, start : start + 512]
                pre = pre + shift[:, start : start + 512] + x_ref[span, cols].astype(jnp.float32)
                sigma = sigmoid_of(pre)
                value = pre * sigma
                slope = sigma + value * (1.0 - sigma)
                normal = three[span, cols] * o_stat[1:2, 2 * middle + start : 2 * middle + start + 512]
                normal = normal - center[:, start : start + 512]
                pool[into, cols] += jnp.sum(value.reshape(extent, lines, 512), 0)
                o_slope[0, into, cols] += jnp.sum(slope.reshape(extent, lines, 512), 0)
                slope = slope * normal
                o_slope[1, into, cols] += jnp.sum(slope.reshape(extent, lines, 512), 0)
            return carry

        lax.fori_loop(0, extent, step_out, 0)
        pooled[into, :] = (pool[into, :] * (1.0 / (extent * extent))).astype(low)
        base += extent * extent * lines

    over = links(pooled, o_pooled.at[at.sub], at.row_peer)
    pair = links(pooled, o_pooled.at[at.sub], at.core_peer)
    o_pooled[at.sub] = pooled[...]
    over.wait()
    last = links(o_pooled.at[at.row_sub], o_pooled.at[at.row_sub], at.core_peer)
    pair.wait()
    last.wait()
    own[-1].wait()
    wait_all(out_copies)
    for copy in save:
        copy.wait()


def forward_trunk(n_dp, collective_id, images, first, mid, last, hid, out, inputs, norms, live):
    span = n_dp // 2
    height, middle = first.shape
    rows, channels = inputs.shape
    some = jax.ShapeDtypeStruct
    low, full = jnp.bfloat16, jnp.float32
    copies = 17 * (span + 4) + 16
    vmem, anywhere = pl.BlockSpec(memory_space=pltpu.VMEM), pl.BlockSpec(memory_space=pl.ANY)
    return pl.pallas_call(
        functools.partial(forward_kernel, n_dp, images),
        out_shape=(
            some((TAPS, span, 2, mid.shape[1], middle), low),
            some((span, 2, height, middle), low),
            some((span, 2, height, hid.shape[1]), low),
            some((span // 4, 2, height, out.shape[1]), low),
            some((rows, middle), full),
            some((rows, middle), full),
            some((rows, middle), low),
            some((2, 2 * middle + channels), full),
            some((4, CROPS * images, channels), low),
            some((4, 8, LANES), full),
            some((2, CROPS * images, channels), full),
        ),
        in_specs=[vmem] * 8,
        out_specs=(anywhere,) * 7 + (vmem,) * 4,
        scratch_shapes=[
            pltpu.VMEM((span, 2, height, middle), low),
            pltpu.VMEM((TAPS, span, 2, mid.shape[1], middle), low),
            pltpu.VMEM((span, 2, height, middle), low),
            pltpu.VMEM((span, 2, height // 4, out.shape[1]), low),
            pltpu.VMEM((rows, TAPS * middle), low),
            pltpu.VMEM((rows, middle), low),
            pltpu.VMEM((rows, middle), low),
            pltpu.VMEM((rows, middle), full),
            pltpu.VMEM((rows, middle), full),
            pltpu.VMEM((rows, channels), full),
            pltpu.VMEM((2, 8, channels), full),
            pltpu.VMEM((CROPS * images, channels), full),
            pltpu.VMEM((3, middle), full),
            pltpu.VMEM((3, 3, middle), full),
            pltpu.VMEM((2, middle), full),
            pltpu.VMEM((3, 2, middle), full),
            pltpu.VMEM((2, channels), full),
            pltpu.VMEM((3, 2, channels), full),
            pltpu.VMEM((CROPS * images, channels), low),
            pltpu.SemaphoreType.DMA((copies,)),
            pltpu.SemaphoreType.DMA((copies,)),
            pltpu.SemaphoreType.DMA((17 + 6,)),
        ],
        compiler_params=pltpu.CompilerParams(
            collective_id=collective_id, has_side_effects=True, vmem_limit_bytes=60 * MIB
        ),
        name="forward_trunk",
    )(first, mid, last, hid, out, inputs, norms, live)


def plus(left, right):
    return left.astype(jnp.float32) + right.astype(jnp.float32)


def piece_list(n_dp, height, mid_height, refs):
    first, mid, last = refs
    half, quarter = height // 2, height // 4
    pieces = [last + (0, 1, part * half, half, 2) for part in range(2)]
    for start, taps in ((0, 1), (1, 1), (2, 1), (3, 1), (4, 1), (5, 1), (6, 1), (7, 2)):
        pieces.append(mid + (start, taps, 0, mid_height, 1))
    return pieces + [first + (0, 1, part * quarter, quarter, 0) for part in range(4)]


def backward_kernel(n_dp, images, *refs):
    p_pool, slope_ref, stat_ref, norm_ref, live_ref, lives_ref, extra_ref, g_hid, g_some = refs[:9]
    h_x, h_one, h_two, h_act, h_last, h_mid = refs[9:15]
    o_first, o_mid, o_last, o_hid, o_out, o_vec, o_sq = refs[15:22]
    (
        x_ref, one, two, act_two, last_w, mid_w, act_one, wide_low, work, thin_low, g_first, g_mid,
        g_last, total, pair_land, pair_sum, row_land, grad_pool, sums_a, land_a, sums_b, land_b,
        sums_c, land_c, hid_in, hid_sum, hid_land, g_out, out_in, out_sum, out_land, vec, vec_land,
        sq_mine, sq_land, send_sem, recv_sem, own_sem,
    ) = refs[22:60]
    bufs = refs[60:]
    at = Place(n_dp)
    links = Links(send_sem, recv_sem)
    span = at.span
    at.greet(at.dp_peers() + at.sub_peers())
    low = jnp.bfloat16
    rows, channels = x_ref.shape
    middle = one.shape[1]
    height = g_last.shape[3]
    mask = live_ref[...][:, :1]
    tile = rows // 4

    loads = {}
    for index, (name, source, target) in enumerate(
        (
            ("act", h_act, act_two), ("last", h_last, last_w), ("x", h_x, x_ref), ("two", h_two, two),
            ("one", h_one, one), ("mid", h_mid, mid_w),
        )
    ):
        loads[name] = pltpu.make_async_copy(source, target, own_sem.at[index])
        loads[name].start()

    pair = [
        links(p_pool.at[2 * line + (1 - at.core)], pair_land.at[line], at.core_peer)
        for line in (1 - at.row, at.row)
    ]
    far_copies = [links(g_hid.at[:, 1 - at.far], hid_in, at.far_peer)]
    some = g_some.shape[0]
    block = g_out.at[pl.ds(at.sub * some, some)]
    own_out = pltpu.make_async_copy(g_some, block, own_sem.at[6])
    own_out.start()
    out_copies = [links(g_some, block, peer) for peer in at.sub_peers()]
    pair[0].wait()
    pair_sum[...] = plus(p_pool[2 * (1 - at.row) + at.core], pair_land[1 - at.row]).astype(low)
    over = links(pair_sum, row_land, at.row_peer)
    pair[1].wait()

    wholes = [(g_hid, hid_in, hid_sum, hid_land), (g_out, out_in, out_sum, out_land)]

    def whole_far(which):
        source, landed, summed, land = wholes[which]
        far_copies[which].wait()
        for near in range(span):
            summed[near] = plus(source[near, at.far], landed[near]).astype(low)
        return [
            links(summed.at[at.near_index(hop)], land.at[hop - 1], at.near_peer(hop))
            for hop in range(1, span)
        ]

    def whole_near(which, copies):
        source, landed, summed, land = wholes[which]
        wait_all(copies)
        value = summed[at.near].astype(jnp.float32)
        for hop in range(1, span):
            value = value + land[hop - 1].astype(jnp.float32)
        return value.astype(low)

    sq_mine[0] = jnp.zeros_like(sq_mine[0])

    def squares_of(matrix, value):
        value = value.astype(jnp.float32)
        line = jnp.sum(value * value, 0, keepdims=True)
        for lane in range(0, line.shape[1], LANES):
            sq_mine[0, pl.ds(matrix, 1), :] += line[:, lane : lane + LANES]

    pieces = piece_list(
        n_dp, height, g_mid.shape[3], ((g_first, o_first), (g_mid, o_mid), (g_last, o_last))
    )
    mine, beside = lanes_of(at.sub), lanes_of(at.row_sub)
    state = [0] * len(pieces)
    flight = [None] * len(pieces)

    def loop(count, body):
        def step(index, carry):
            body(index)
            return carry

        lax.fori_loop(0, count, step, 0)

    def go(index):
        source, target, start, taps, line, size, matrix = pieces[index]
        held, second, third, nears = bufs[4 * index : 4 * index + 4]
        stage = state[index]
        state[index] += 1
        row_first = index % 2 == 0
        lines, some = pl.ds(line, size), pl.ds(start, taps)
        if stage == 0:
            flight[index] = [
                links(
                    source.at[some, :, :, lines, lanes_of(2 * row + (1 - at.core))],
                    held.at[row],
                    at.core_peer,
                )
                for row in range(2)
            ]
            return
        wait_all(flight[index])
        if stage == 1:
            for row in range(2):
                cols = lanes_of(2 * row + at.core)

                def body(at_block):
                    tap, near, far = at_block // (2 * span), at_block // 2 % span, at_block % 2
                    held[row, tap, near, far] = plus(
                        source[start + tap, near, far, lines, cols], held[row, tap, near, far]
                    ).astype(low)

                loop(taps * span * 2, body)
            if row_first:
                flight[index] = [links(held.at[1 - at.row], second, at.row_peer)]
            else:
                flight[index] = [links(held.at[:, :, :, 1 - at.far], second, at.far_peer)]
        elif stage == 2:
            if row_first:

                def body(at_block):
                    tap, near, far = at_block // (2 * span), at_block // 2 % span, at_block % 2
                    second[tap, near, far] = plus(
                        held[at.row, tap, near, far], second[tap, near, far]
                    ).astype(low)

                loop(taps * span * 2, body)
                flight[index] = [links(second.at[:, :, 1 - at.far], third, at.far_peer)]
            else:

                def body(at_block):
                    row, tap, near = at_block // (taps * span), at_block // span % taps, at_block % span
                    second[row, tap, near] = plus(
                        held[row, tap, near, at.far], second[row, tap, near]
                    ).astype(low)

                loop(taps * span * 2, body)
                flight[index] = [links(second.at[1 - at.row], third, at.row_peer)]
        elif stage == 3:

            def body(at_block):
                tap, near = at_block // span, at_block % span
                part = second[tap, near, at.far] if row_first else second[at.row, tap, near]
                third[tap, near] = plus(part, third[tap, near]).astype(low)

            loop(taps * span, body)
            flight[index] = [
                links(third.at[:, at.near_index(hop)], nears.at[hop - 1], at.near_peer(hop))
                for hop in range(1, span)
            ]
        elif stage == 4:
            for tap in range(taps):
                value = third[tap, at.near].astype(jnp.float32)
                for hop in range(1, span):
                    value = value + nears[hop - 1, tap].astype(jnp.float32)
                value = value.astype(low)
                squares_of(matrix, value)
                target[start + tap, lines, mine] = value
            slab = target.at[some, lines, mine]
            flight[index] = [links(slab, slab, at.row_peer)]
        elif stage == 5:
            slabs = [target.at[some, lines, cols] for cols in (mine, beside)]
            flight[index] = [links(slab, slab, at.core_peer) for slab in slabs]

    def go_pair(number):
        go(2 * number)
        go(2 * number + 1)

    count_all = jnp.sum(lives_ref[...][:, :1, :1], 0) * float(rows // images)
    sums = GroupSums(at, links)

    def terms(start, wide):
        cols = pl.ds(start, wide)
        mean, inverse = stat_ref[pl.ds(0, 1), cols], stat_ref[pl.ds(1, 1), cols]
        scale = norm_ref[pl.ds(0, 1), cols] * inverse
        return mean * inverse, inverse, scale, norm_ref[pl.ds(1, 1), cols] - scale * mean

    def slope_of(pre):
        sigma = sigmoid_of(pre)
        return sigma + pre * sigma * (1.0 - sigma)

    def pack(target, wide):
        target[pl.ds(0, 1), :] = jnp.sum(total[0, :, :wide], 0, keepdims=True)
        target[pl.ds(1, 1), :] = jnp.sum(total[1, :, :wide], 0, keepdims=True)

    center_one, inverse_one, scale_one, shift_one = terms(0, middle)
    center_two, inverse_two, scale_two, shift_two = terms(middle, middle)
    center_three, inverse_three, scale_three, shift_three = terms(2 * middle, channels)
    loads["one"].wait()

    def step_act(index):
        span_rows = rows_at(index * tile, tile)
        pre = one[span_rows, :] * scale_one + shift_one
        act_one[span_rows, :] = (pre * sigmoid_of(pre)).astype(low)

    loop(4, step_act)
    own_out.wait()
    wait_all(out_copies)
    far_copies.append(links(g_out.at[:, 1 - at.far], out_in, at.far_peer))
    value = plus(p_pool[at.sub], pair_land[at.row])
    over.wait()
    value = value + row_land[...].astype(jnp.float32)
    big = NBIG * images
    grad_pool[pl.ds(0, big), :] = value[:big] * (1.0 / (BIG * BIG))
    grad_pool[pl.ds(big, NSMALL * images), :] = value[big:] * (1.0 / (SMALL * SMALL))
    for which in range(2):
        sums_c[pl.ds(which, 1), :] = jnp.sum(grad_pool[...] * slope_ref[which], 0, keepdims=True)
    sums.start(sums_c, land_c)
    loads["act"].wait()
    loads["last"].wait()
    loads["x"].wait()
    both_three = sums.finish()
    vec[...] = extra_ref[...]
    vec[pl.ds(1, 1), :] = both_three[1:2]
    vec[pl.ds(3, 1), :] = both_three[0:1]
    both_three = both_three / count_all

    chunk = channels // 4
    for quarter in range(4):
        cols = pl.ds(quarter * chunk, chunk)
        here = slice(quarter * chunk, (quarter + 1) * chunk)
        weights = last_w[pl.ds(quarter * (span // 4), span // 4)].reshape(chunk, middle)

        def step_three(index):
            span_rows = rows_at(index * tile, tile)
            work[span_rows, :] = against(act_two[span_rows, :], weights)

        loop(4, step_three)
        base = 0
        for extent, crops in ((BIG, NBIG), (SMALL, NSMALL)):
            lines = crops * images
            into = pl.ds(0, lines) if extent == BIG else pl.ds(big, lines)

            def step_grad(index):
                span_rows = rows_at(base + index * extent * lines, extent * lines)
                hidden = work[span_rows, :]
                pre = hidden * scale_three[:, here] + shift_three[:, here]
                pre = pre + x_ref[span_rows, cols].astype(jnp.float32)
                grad = slope_of(pre).reshape(extent, lines, chunk) * grad_pool[into, cols]
                normal = hidden * inverse_three[:, here] - center_three[:, here]
                back = both_three[0:1, here] + normal * both_three[1:2, here]
                back = back.reshape(extent * crops, images, chunk) * mask
                grad = grad.reshape(extent * crops, images, chunk) - back
                grad = grad.reshape(extent * lines, chunk) * scale_three[:, here]
                wide_low[span_rows, cols] = grad.astype(low)

            loop(extent, step_grad)
            base += extent * extent * lines

    near_hid, near_out = whole_far(0), whole_far(1)

    def norm_sums(grad, normal):
        total[0, :, :middle] += jnp.sum(grad.reshape(tile // 8, 8, middle), 0)
        total[1, :, :middle] += jnp.sum((grad * normal).reshape(tile // 8, 8, middle), 0)

    loads["two"].wait()
    total[...] = jnp.zeros_like(total)

    def step_two(index):
        span_rows = rows_at(index * tile, tile)
        grad = jnp.dot(
            wide_low[span_rows, :],
            last_w[...].reshape(channels, middle),
            preferred_element_type=jnp.float32,
        )
        grad = grad * slope_of(two[span_rows, :] * scale_two + shift_two)
        work[span_rows, :] = grad
        norm_sums(grad, two[span_rows, :] * inverse_two - center_two)

    loop(4, step_two)
    pack(sums_a, middle)
    sums.start(sums_a, land_a)

    def weight_rows(target, left, right):
        part = 256
        shards = max(1, part // height)
        for index in range(channels // part):
            value = cross_rows(left[:, pl.ds(index * part, part)], right[...]).astype(low)
            if shards == 1:
                target[0, index // 2, index % 2] = value
            else:
                some = pl.ds(index * (shards // 2), shards // 2)
                target[0, some] = value.reshape(shards // 2, 2, height, middle)

    weight_rows(g_last, wide_low, act_two)
    go_pair(0)

    def settle_grad(source, center, inverse, scale, both):
        def step(index):
            span_rows = rows_at(index * tile, tile)
            normal = source[span_rows, :] * inverse - center
            back = both[0:1] + normal * both[1:2]
            back = (back.reshape(tile // 8, 8, middle) * mask).reshape(tile, middle)
            thin_low[span_rows, :] = ((work[span_rows, :] - back) * scale).astype(low)

        loop(4, step)

    both_two = sums.finish()
    settle_grad(two, center_two, inverse_two, scale_two, both_two / count_all)
    vec[pl.ds(0, 1), pl.ds(middle, middle)] = both_two[1:2]
    vec[pl.ds(0, 1), pl.ds(3 * middle, middle)] = both_two[0:1]
    go_pair(0)

    loads["mid"].wait()
    moves, zeros = tap_blocks(images, True)
    total[...] = jnp.zeros_like(total)
    for part in range(3):
        for slot in range(3):
            cols = pl.ds(slot * middle, middle)
            for target, start, size in moves[3 * part + slot]:
                wide_low[pl.ds(target, size), cols] = thin_low[pl.ds(start, size), :]
            for target, size in zeros[3 * part + slot]:
                wide_low[pl.ds(target, size), cols] = jnp.zeros((size, middle), low)

        def step_one(index):
            span_rows = rows_at(index * tile, tile)
            grad = against(
                wide_low[span_rows, pl.ds(0, middle)], mid_w[3 * part].reshape(middle, middle)
            )
            for slot in range(1, 3):
                grad = grad + against(
                    wide_low[span_rows, pl.ds(slot * middle, middle)],
                    mid_w[3 * part + slot].reshape(middle, middle),
                )
            if part:
                grad = grad + work[span_rows, :]
            if part == 2:
                grad = grad * slope_of(one[span_rows, :] * scale_one + shift_one)
                norm_sums(grad, one[span_rows, :] * inverse_one - center_one)
            work[span_rows, :] = grad

        loop(4, step_one)
        if part == 2:
            pack(sums_b, middle)
            sums.start(sums_b, land_b)
        for slot in range(3):
            value = cross_rows(act_one[...], wide_low[:, pl.ds(slot * middle, middle)]).astype(low)
            g_mid[3 * part + slot] = value.reshape(g_mid.shape[1:])
        if part == 0:
            go_pair(1)
            go_pair(0)
        elif part == 1:
            go_pair(2)
            go_pair(1)
            go_pair(0)
        else:
            go_pair(3)
            go_pair(4)
            go_pair(2)
            go_pair(1)
            go_pair(0)
            value = whole_near(0, near_hid)
            wide = g_hid.shape[3]
            squares_of(3, value)
            slabs = [o_hid.at[:, lanes_of(which, wide)] for which in (at.sub, at.row_sub)]
            o_hid[:, lanes_of(at.sub, wide)] = value
            hid_row = links(slabs[0], slabs[0], at.row_peer)
            value = whole_near(1, near_out)
            squares_of(4, value)
            o_out[...] = value

    both_one = sums.finish()
    settle_grad(one, center_one, inverse_one, scale_one, both_one / count_all)
    vec[pl.ds(0, 1), pl.ds(0, middle)] = both_one[1:2]
    vec[pl.ds(0, 1), pl.ds(2 * middle, middle)] = both_one[0:1]
    wide = vec.shape[1] // 4
    vec_cols = lanes_of(at.sub, wide)
    vec_copies = [
        links(vec.at[:, vec_cols], vec_land.at[hop], peer)
        for hop, peer in enumerate(at.dp_peers())
    ]
    go_pair(3)
    hid_row.wait()
    final = [links(slab, slab, at.core_peer) for slab in slabs]

    weight_rows(g_first, x_ref, thin_low)
    go_pair(5)
    go_pair(6)

    numbers = range(len(pieces) // 2)
    tick = 0
    sent = False
    while min(state) < 6:
        for number in numbers:
            if state[2 * number] < 6 and tick >= max(0, number - 4):
                go_pair(number)
        if tick == 1:
            wait_all(vec_copies)
            value = vec[:, vec_cols]
            for hop in range(n_dp - 1):
                value = value + vec_land[hop]
            o_vec[:, vec_cols] = value
            vec_final = [
                links(o_vec.at[:, vec_cols], o_vec.at[:, vec_cols], peer)
                for peer in at.sub_peers()
            ]
        if not sent and min(state) >= 5:
            sent = True
            sq_copies = [
                links(sq_mine.at[0], sq_land.at[hop], peer)
                for hop, peer in enumerate(at.dp_peers())
            ]
        tick += 1
    wait_all(sq_copies)
    value = sq_mine[0]
    for hop in range(n_dp - 1):
        value = value + sq_land[hop]
    sq_mine[1] = value
    sq_copies = [
        links(sq_mine.at[1], sq_land.at[n_dp - 1 + hop], peer)
        for hop, peer in enumerate(at.sub_peers())
    ]
    wait_all(sq_copies)
    for hop in range(3):
        value = value + sq_land[n_dp - 1 + hop]
    o_sq[...] = value
    for copies in flight:
        wait_all(copies)
    wait_all(final)
    wait_all(vec_final)


def backward_trunk(
    n_dp, collective_id, images, pooled, slopes, stat, norms, live, lives, extra, hid, out, inputs,
    one, two, act, last, mid,
):
    span = n_dp // 2
    low, full = jnp.bfloat16, jnp.float32
    rows, channels = inputs.shape
    middle = one.shape[1]
    height, mid_height = last.shape[2], mid.shape[3]
    narrow = out.shape[1]
    crops = CROPS * images
    some = jax.ShapeDtypeStruct
    bufs = []
    for index, piece in enumerate(piece_list(n_dp, height, mid_height, ((0, 0),) * 3)):
        taps, block = piece[3], (piece[5], LANES)
        bufs.append(pltpu.VMEM((2, taps, span, 2) + block, low))
        if index % 2 == 0:
            bufs.append(pltpu.VMEM((taps, span, 2) + block, low))
        else:
            bufs.append(pltpu.VMEM((2, taps, span) + block, low))
        bufs.append(pltpu.VMEM((taps, span) + block, low))
        bufs.append(pltpu.VMEM((span - 1, taps) + block, low))
    copies = 14 * (span + 6) + 2 * (span + 4) + 2 * n_dp + 40
    vmem, anywhere = pl.BlockSpec(memory_space=pltpu.VMEM), pl.BlockSpec(memory_space=pl.ANY)
    return pl.pallas_call(
        functools.partial(backward_kernel, n_dp, images),
        out_shape=(
            some((1, height, middle), low),
            some((TAPS, mid_height, middle), low),
            some((1, height, middle), low),
            some((height, 4 * hid.shape[1]), low),
            some((height, narrow), low),
            some(extra.shape, full),
            some((8, LANES), full),
        ),
        in_specs=[vmem] * 9 + [anywhere] * 6,
        out_specs=(vmem,) * 7,
        scratch_shapes=[
            pltpu.VMEM((rows, channels), low),
            pltpu.VMEM((rows, middle), full),
            pltpu.VMEM((rows, middle), full),
            pltpu.VMEM((rows, middle), low),
            pltpu.VMEM((span, 2, height, middle), low),
            pltpu.VMEM((TAPS, span, 2, mid_height, middle), low),
            pltpu.VMEM((rows, middle), low),
            pltpu.VMEM((rows, channels), low),
            pltpu.VMEM((rows, middle), full),
            pltpu.VMEM((rows, middle), low),
            pltpu.VMEM((1, span, 2, height, middle), low),
            pltpu.VMEM((TAPS, span, 2, mid_height, middle), low),
            pltpu.VMEM((1, span, 2, height, middle), low),
            pltpu.VMEM((2, 8, middle), full),
            pltpu.VMEM((2, crops, channels), low),
            pltpu.VMEM((crops, channels), low),
            pltpu.VMEM((crops, channels), low),
            pltpu.VMEM((crops, channels), full),
            pltpu.VMEM((2, middle), full),
            pltpu.VMEM((3, 2, middle), full),
            pltpu.VMEM((2, middle), full),
            pltpu.VMEM((3, 2, middle), full),
            pltpu.VMEM((2, channels), full),
            pltpu.VMEM((3, 2, channels), full),
            pltpu.VMEM((span, height, hid.shape[1]), low),
            pltpu.VMEM((span, height, hid.shape[1]), low),
            pltpu.VMEM((span - 1, height, hid.shape[1]), low),
            pltpu.VMEM((span, 2, height, narrow), low),
            pltpu.VMEM((span, height, narrow), low),
            pltpu.VMEM((span, height, narrow), low),
            pltpu.VMEM((span - 1, height, narrow), low),
            pltpu.VMEM(extra.shape, full),
            pltpu.VMEM((n_dp - 1, extra.shape[0], extra.shape[1] // 4), full),
            pltpu.VMEM((2, 8, LANES), full),
            pltpu.VMEM((n_dp + 2, 8, LANES), full),
            pltpu.SemaphoreType.DMA((copies,)),
            pltpu.SemaphoreType.DMA((copies,)),
            pltpu.SemaphoreType.DMA((7,)),
        ]
        + bufs,
        compiler_params=pltpu.CompilerParams(
            collective_id=collective_id, has_side_effects=True, vmem_limit_bytes=62 * MIB
        ),
        name="backward_trunk",
    )(
        pooled,
        slopes,
        stat,
        norms,
        live,
        lives,
        extra,
        hid.reshape(span, 2, height, hid.shape[1]),
        out.reshape(span // 4, 2, height, narrow),
        inputs,
        one,
        two,
        act,
        last,
        mid,
    )


def row_tile(rows):
    return next(size for size in (192, 160, 128, 96, 64, 48, 32, 24, 16, 8) if rows % size == 0)


def column_sums_kernel(queue_ref, proto_ref, centers_ref, turned_ref, o_ref, total):
    views, rows, _ = queue_ref.shape
    protos, depth = proto_ref.shape
    width = turned_ref.shape[1]
    tile = row_tile(rows)
    part = 256
    for start in range(0, width, part):
        here = max(0, min(part, protos - start))
        values = jnp.zeros((part, depth), jnp.float32)
        if here:
            values = proto_ref[pl.ds(start, here), :]
            values = values * lax.rsqrt(jnp.sum(values * values, 1, keepdims=True) + unit_eps)
        if here < part:
            values = jnp.concatenate([values, jnp.zeros((part - here, depth), jnp.float32)], 0)
        centers_ref[pl.ds(start, part), :] = values.astype(jnp.bfloat16)
        turned_ref[:, pl.ds(start, part)] = values.T.astype(jnp.bfloat16)
    for view in range(views):
        total[...] = jnp.zeros_like(total)

        def step(index, carry):
            lines = queue_ref[view, pl.ds(index * tile, tile), :]
            for start in range(0, width, part):
                cols = pl.ds(start, part)
                scores = jnp.dot(lines, turned_ref[:, cols], preferred_element_type=jnp.float32)
                shares = jnp.exp2(scores * SINK2)
                total[:, cols] += jnp.sum(shares.reshape(tile // 8, 8, part), 0)
            return carry

        lax.fori_loop(0, rows // tile, step, 0)
        o_ref[pl.ds(view, 1), :] = jnp.sum(total[...], 0, keepdims=True)


def column_sums(queue, prototypes, width):
    depth = prototypes.shape[1]
    return pl.pallas_call(
        column_sums_kernel,
        out_shape=(
            jax.ShapeDtypeStruct((width, depth), jnp.bfloat16),
            jax.ShapeDtypeStruct((depth, width), jnp.bfloat16),
            jax.ShapeDtypeStruct((queue.shape[0], width), jnp.float32),
        ),
        in_specs=[pl.BlockSpec(memory_space=pltpu.VMEM)] * 2,
        out_specs=(pl.BlockSpec(memory_space=pltpu.VMEM),) * 3,
        scratch_shapes=[pltpu.VMEM((8, width), jnp.float32)],
        compiler_params=pltpu.CompilerParams(vmem_limit_bytes=32 * MIB),
        cost_estimate=pl.CostEstimate(
            flops=2 * queue.size * width,
            bytes_accessed=2 * queue.size,
            transcendentals=queue.size // queue.shape[2] * width,
        ),
        name="column_sums",
    )(queue, prototypes)


def sinkhorn_kernel(
    axis,
    count,
    protos,
    queue_ref,
    centers_ref,
    turned_ref,
    partial_ref,
    live_ref,
    first_ref,
    embed_ref,
    proto_grad_ref,
    loss_ref,
    grad,
    parts_land,
    kept,
    scores,
    mine,
    landed,
    shift,
    total,
    send_sem,
    recv_sem,
):
    me = lax.axis_index(axis)
    views, rows, _ = queue_ref.shape
    width = turned_ref.shape[1]
    images = live_ref.shape[0]
    tile = row_tile(rows)
    part = 512
    parts = range(0, width, part)
    mask = live_ref[...]
    greet(axis, count)

    def to_group(turn, source, target):
        copies = []
        for hop in range(1, count):
            to = lax.rem(me + hop, count)
            copy = pltpu.make_async_remote_copy(
                src_ref=source(to),
                dst_ref=target(hop),
                send_sem=send_sem.at[turn, hop],
                recv_sem=recv_sem.at[turn, hop],
                device_id={axis: to},
                device_id_type=MESH,
            )
            copy.start()
            copies.append(copy)
        for copy in copies:
            copy.wait()

    to_group(ITERS, lambda to: partial_ref.at[to], lambda hop: parts_land.at[hop])
    embedding = partial_ref[me]
    for hop in range(1, count):
        embedding = embedding + parts_land[hop]
    inverse = lax.rsqrt(jnp.sum(embedding * embedding, 1, keepdims=True) + unit_eps)
    unit = embedding * inverse
    unit_low = unit.astype(jnp.bfloat16)

    def sum_group(turn):
        copies = []
        for hop in range(1, count):
            copy = pltpu.make_async_remote_copy(
                src_ref=mine.at[turn],
                dst_ref=landed.at[turn, hop],
                send_sem=send_sem.at[turn, hop],
                recv_sem=recv_sem.at[turn, hop],
                device_id={axis: lax.rem(me + hop, count)},
                device_id_type=MESH,
            )
            copy.start()
            copies.append(copy)
        for copy in copies:
            copy.wait()
        whole = mine[turn]
        for hop in range(1, count):
            whole = whole + landed[turn, hop]
        return whole

    for start in parts:
        cols = pl.ds(start, part)
        scores[:, cols] = jnp.dot(
            unit_low, turned_ref[:, cols], preferred_element_type=jnp.float32
        )
        for view in range(views):
            lines = pl.ds(view * images, images)
            shares = jnp.exp2(scores[lines, cols] * SINK2) * mask
            mine[0, pl.ds(view, 1), cols] = first_ref[pl.ds(view, 1), cols] + jnp.sum(
                shares, 0, keepdims=True
            )
    real = lax.broadcasted_iota(jnp.int32, (1, width), 1) < protos
    first = sum_group(0)
    shift[...] = jnp.where(real, jnp.log2(first), 1e30)

    for turn in range(1, ITERS):
        for view in range(views):
            lines = pl.ds(view * images, images)
            row = pl.ds(view, 1)
            if turn == 1:
                own = jnp.exp2(scores[lines, :] * SINK2 - shift[row, :]) * mask
                weight = jnp.sum(own, 1, keepdims=True)
            else:
                own = jnp.exp2(scores[lines, :] * SINK2 - first_log[row, :]) * mask
                weight = jnp.sum(own * shift[row, :], 1, keepdims=True)
            total[...] = own / (weight + (1.0 - mask))

            def step(index, carry):
                span = pl.ds(index * tile, tile)
                if turn == 1:
                    lines = queue_ref[view, span, :]
                sums = jnp.zeros((tile, LANES), jnp.float32)
                for start in parts:
                    cols = pl.ds(start, part)
                    if turn == 1:
                        raw = jnp.dot(lines, turned_ref[:, cols], preferred_element_type=jnp.float32)
                        shares = jnp.exp2(raw * SINK2 - shift[row, cols])
                        kept[view, span, cols] = shares
                    else:
                        shares = kept[view, span, cols] * shift[row, cols]
                    for lane in range(0, part, LANES):
                        sums = sums + shares[:, lane : lane + LANES]
                scale = 1.0 / jnp.sum(sums, 1, keepdims=True)
                for start in parts:
                    cols = pl.ds(start, part)
                    scaled = kept[view, span, cols] * scale
                    total[:, cols] += jnp.sum(scaled.reshape(tile // 8, 8, part), 0)
                return carry

            lax.fori_loop(0, rows // tile, step, 0)
            mine[turn, row, :] = jnp.sum(total[...], 0, keepdims=True)
        if turn == 1:
            first_log = shift[...]
        whole = sum_group(turn)
        shift[...] = jnp.where(real, 1.0 / whole, 0.0)

    codes = []
    for view in range(views):
        lines = pl.ds(view * images, images)
        own = jnp.exp2(scores[lines, :] * SINK2 - first_log[view : view + 1, :]) * mask
        own = own * shift[pl.ds(view, 1), :]
        codes.append(own / (jnp.sum(own, 1, keepdims=True) + (1.0 - mask)))
    code_total = codes[0] + codes[1]
    loss = jnp.zeros((images, 1), jnp.float32)
    for crop in range(CROPS):
        lines = pl.ds(crop * images, images)
        raw = jnp.where(real, scores[lines, :] * SOFT2, -1e30)
        raw = raw - jnp.max(raw, 1, keepdims=True)
        powers = jnp.exp2(raw)
        norm = jnp.sum(powers, 1, keepdims=True)
        others = code_total - codes[crop] if crop < NBIG else code_total
        logs = jnp.where(real, (raw - jnp.log2(norm)) / LOG2E, 0.0)
        loss = loss - jnp.sum(others * logs, 1, keepdims=True)
        weight = (NBIG - 1.0 if crop < NBIG else float(NBIG)) * mask / norm
        grad[lines, :] = (weight * powers - others) / (PAIRS * softmax_temp)
    loss_ref[...] = jnp.broadcast_to(
        jnp.sum(loss, 0, keepdims=True) / PAIRS, loss_ref.shape
    )
    grad_unit = jnp.zeros(unit.shape, jnp.float32)
    for start in parts:
        cols = pl.ds(start, part)
        some = grad[:, cols].astype(jnp.bfloat16)
        grad_unit = grad_unit + jnp.dot(
            some, centers_ref[cols, :], preferred_element_type=jnp.float32
        )
        proto_grad_ref[cols, :] = cross_rows(some, unit_low)
    grad_embed = inverse * (
        grad_unit - unit * jnp.sum(unit * grad_unit, 1, keepdims=True)
    )
    embed_ref[me] = grad_embed.astype(jnp.bfloat16)
    to_group(ITERS + 1, lambda to: embed_ref.at[me], lambda hop: embed_ref.at[me])


def sinkhorn(sizes, collective_id, protos, queue, centers, turned, partial, live, first):
    count = sizes["sub"]
    views, rows, depth = queue.shape
    width = turned.shape[1]
    crops = partial.shape[1]
    return pl.pallas_call(
        functools.partial(sinkhorn_kernel, "sub", count, protos),
        out_shape=(
            jax.ShapeDtypeStruct((count, crops, depth), jnp.bfloat16),
            jax.ShapeDtypeStruct((width, depth), jnp.float32),
            jax.ShapeDtypeStruct((8, LANES), jnp.float32),
        ),
        in_specs=[pl.BlockSpec(memory_space=pltpu.VMEM)] * 6,
        out_specs=(pl.BlockSpec(memory_space=pltpu.VMEM),) * 3,
        scratch_shapes=[
            pltpu.VMEM((crops, width), jnp.float32),
            pltpu.VMEM((count, crops, depth), jnp.float32),
            pltpu.VMEM((views, rows, width), jnp.float32),
            pltpu.VMEM((crops, width), jnp.float32),
            pltpu.VMEM((ITERS, views, width), jnp.float32),
            pltpu.VMEM((ITERS, count, views, width), jnp.float32),
            pltpu.VMEM((views, width), jnp.float32),
            pltpu.VMEM((8, width), jnp.float32),
            pltpu.SemaphoreType.DMA((ITERS + 2, count)),
            pltpu.SemaphoreType.DMA((ITERS + 2, count)),
        ],
        compiler_params=pltpu.CompilerParams(
            collective_id=collective_id, has_side_effects=True, vmem_limit_bytes=48 * MIB
        ),
        name="sinkhorn",
    )(queue, centers, turned, partial, live, first)


def advance(weight, gradient, moment, average, trust):
    step_now = trust * gradient
    moment_new = momentum_rate * moment + step_now
    weight_new = weight - learn_rate * (step_now + momentum_rate * moment_new)
    average_new = average_rate * average + (1.0 - average_rate) * weight_new
    return (weight_new, moment_new, average_new)


def per_device(
    sizes,
    big_maps,
    small_maps,
    live_counts,
    queue,
    bottleneck_outer,
    bottleneck_inner,
    proj_hidden,
    proj_out,
    prototypes,
    norm_params,
    mom_outer,
    mom_inner,
    mom_hidden,
    mom_out,
    mom_protos,
    mom_norms,
    avg_outer,
    avg_inner,
    avg_hidden,
    avg_out,
    avg_protos,
    avg_norms,
):
    n_dp, n_sub = sizes["dp"], sizes["sub"]
    exchange = Exchanger(sizes)
    images = big_maps.shape[0]
    channels = big_maps.shape[-1]
    middle = bottleneck_inner.shape[-1]
    hidden_width = proj_hidden.shape[1]
    out_width = proj_out.shape[1]
    proto_count = prototypes.shape[0]
    proto_width = -(-proto_count // 512) * 512
    here = lax.axis_index("sub")
    share = hidden_width // n_sub

    low = jnp.bfloat16
    hidden_cols = lax.dynamic_slice_in_dim(proj_hidden, here * share, share, 1)
    bounds = [0, middle, 2 * middle, 2 * middle + channels, 2 * middle + channels + hidden_width]
    gains = [norm_params[0, bounds[k] : bounds[k + 1]] for k in range(4)]
    biases = [norm_params[1, bounds[k] : bounds[k + 1]] for k in range(4)]
    gains[3] = lax.dynamic_slice_in_dim(gains[3], here * share, share, 0)
    biases[3] = lax.dynamic_slice_in_dim(biases[3], here * share, share, 0)

    proto_inv = lax.rsqrt(jnp.sum(prototypes * prototypes, 1, keepdims=True) + unit_eps)
    centers_low, turned, first_sums = column_sums(queue, prototypes, proto_width)

    live_float = live_counts[0].astype(jnp.float32)
    image_mask = (jnp.arange(images) < live_counts[0]).astype(jnp.float32)[:, None]
    per_image = NBIG * BIG * BIG + NSMALL * SMALL * SMALL
    rows = per_image * images
    row_mask = jnp.broadcast_to(image_mask, (per_image, images, 1)).reshape(rows, 1)

    inputs = jnp.concatenate(
        [
            jnp.transpose(big_maps, (2, 3, 1, 0, 4)).reshape(-1, channels),
            jnp.transpose(small_maps, (2, 3, 1, 0, 4)).reshape(-1, channels),
        ],
        0,
    )

    live_tile = jnp.broadcast_to(image_mask, (images, LANES))
    (
        inner_low, last_w, hidden_low, out_low, hidden_one, hidden_two, act_two, trunk_stat,
        pooled_all, lives_tile, slopes,
    ) = forward_trunk(
        n_dp,
        exchange.next_id(),
        images,
        bottleneck_outer[0].astype(low),
        bottleneck_inner.astype(low),
        bottleneck_outer[1].astype(low),
        hidden_cols.astype(low),
        proj_out.astype(low),
        inputs,
        norm_params,
        live_tile,
    )
    hidden_low = hidden_low.reshape(channels, share)
    out_low = out_low.reshape(share, out_width)
    lives = lives_tile[:, 0, 0]

    def stats(total, squares, count):
        mean = total / count
        return mean, lax.rsqrt(squares / count - mean * mean + norm_eps)

    crops = CROPS * images
    pooled_all = pooled_all.reshape(n_sub * crops, channels)
    group_mask = (jnp.arange(images)[None, :] < lives[:, None]).astype(jnp.float32)
    group_mask = jnp.broadcast_to(group_mask[:, None, :], (n_sub, CROPS, images))
    group_mask = group_mask.reshape(n_sub * crops, 1)
    count_crops = jnp.sum(lives) * CROPS
    proj_pre = forward_dot(pooled_all, hidden_low)
    masked = proj_pre * group_mask
    mean_four, inv_four = stats(jnp.sum(masked, 0), jnp.sum(masked * proj_pre, 0), count_crops)
    normal_four = (proj_pre - mean_four) * inv_four
    pre_four = gains[3] * normal_four + biases[3]
    act_four = jax.nn.silu(pre_four).astype(jnp.bfloat16)
    partial = forward_dot(act_four, out_low).reshape(n_sub, crops, out_width)

    embed_all, grad_centers, loss_tile = sinkhorn(
        sizes,
        exchange.next_id(),
        proto_count,
        queue,
        centers_low,
        turned,
        partial,
        image_mask,
        first_sums,
    )
    embed_all = embed_all.reshape(n_sub * crops, out_width)

    d_out = cross_rows(act_four, embed_all)
    grad_four = against(embed_all, out_low) * silu_slope(pre_four)
    bias_four = jnp.sum(grad_four, 0)
    gain_four = jnp.sum(grad_four * normal_four, 0)
    proj_low = (
        gains[3]
        * inv_four
        * (grad_four - group_mask * (bias_four + normal_four * gain_four) / count_crops)
    ).astype(jnp.bfloat16)
    d_hidden = cross_rows(pooled_all, proj_low)
    partial = against(proj_low, hidden_low).astype(jnp.bfloat16).reshape(n_sub, crops, channels)

    four = exchange(
        jnp.stack([gain_four, bias_four, jnp.broadcast_to(loss_tile[0, 0], (share,))]),
        "sub",
        name="sums_four",
    )
    gain_four, bias_four = four[:, 0].reshape(-1), four[:, 1].reshape(-1)
    loss_group = jnp.sum(four[:, 2, 0])
    centers_sum = lax.psum(grad_centers, ("dp", "sub"))[:proto_count]

    scalars = jnp.stack(
        [
            loss_group,
            jnp.sum(lives),
            jnp.sum(bottleneck_outer[0] * bottleneck_outer[0]),
            jnp.sum(bottleneck_outer[1] * bottleneck_outer[1]),
            jnp.sum(bottleneck_inner * bottleneck_inner),
            jnp.sum(proj_hidden * proj_hidden),
            jnp.sum(proj_out * proj_out),
        ]
    )
    width = 4 * middle
    zero = jnp.zeros((1, width), jnp.float32)
    extra = jnp.concatenate(
        [
            zero,
            zero,
            gain_four.reshape(-1, width),
            zero,
            bias_four.reshape(-1, width),
            jnp.pad(scalars, (0, width - 7))[None],
            zero,
            zero,
        ],
        0,
    )
    shard_first, shard_inner, shard_last, shard_hidden, shard_out, vector, grad_all = backward_trunk(
        n_dp,
        exchange.next_id(),
        images,
        partial,
        slopes,
        trunk_stat,
        norm_params,
        live_tile,
        lives_tile,
        extra,
        d_hidden.astype(low),
        d_out.astype(low),
        inputs,
        hidden_one,
        hidden_two,
        act_two,
        last_w,
        inner_low,
    )
    shard_outer = jnp.concatenate([shard_first, shard_last], 0).astype(jnp.float32)
    shard_inner = shard_inner.astype(jnp.float32)
    shard_hidden = shard_hidden.astype(jnp.float32)
    shard_out = shard_out.astype(jnp.float32)
    norm_sum = jnp.stack(
        [
            jnp.concatenate([vector[0, : 2 * middle], vector[1], vector[2]]),
            jnp.concatenate([vector[0, 2 * middle :], vector[3], vector[4]]),
        ]
    )
    numer_all, live_all, weight_all = vector[5, 0], vector[5, 1], vector[5, 2:7]
    proto_unit = prototypes * proto_inv
    proto_sum = proto_inv * (
        centers_sum - proto_unit * jnp.sum(proto_unit * centers_sum, 1, keepdims=True)
    )

    grad_all = jnp.sum(grad_all[:5], 1) / jnp.array([1.0, 1.0, 1.0, 1.0, 4.0], jnp.float32)
    grad_all = jnp.stack([grad_all[0], grad_all[2], grad_all[1], grad_all[3], grad_all[4]])
    trusts = trust_rate * jnp.sqrt(weight_all) / (jnp.sqrt(grad_all) + 1e-12)
    proto_trust = (
        trust_rate
        * jnp.sqrt(jnp.sum(prototypes * prototypes))
        / (jnp.sqrt(jnp.sum(proto_sum * proto_sum)) + 1e-12)
    )
    norm_trust = (
        trust_rate
        * jnp.sqrt(jnp.sum(norm_params * norm_params, 1, keepdims=True))
        / (jnp.sqrt(jnp.sum(norm_sum * norm_sum, 1, keepdims=True)) + 1e-12)
    )
    outer_new = advance(
        bottleneck_outer, shard_outer, mom_outer, avg_outer, trusts[:2][:, None, None]
    )
    inner_new = advance(bottleneck_inner, shard_inner, mom_inner, avg_inner, trusts[2])
    hidden_new = advance(proj_hidden, shard_hidden, mom_hidden, avg_hidden, trusts[3])
    out_new = advance(proj_out, shard_out, mom_out, avg_out, trusts[4])
    protos_new = advance(prototypes, proto_sum, mom_protos, avg_protos, proto_trust)
    norms_new = advance(norm_params, norm_sum, mom_norms, avg_norms, norm_trust)
    news = (outer_new, inner_new, hidden_new, out_new, protos_new, norms_new)
    return (
        (numer_all, live_all)
        + tuple(new[0] for new in news)
        + tuple(new[1] for new in news)
        + tuple(new[2] for new in news)
        + tuple(new[0].astype(jnp.bfloat16) for new in news[:4])
    )


def solution(mesh):
    data = P(("dp", "sub"), None, None, None, None)
    trees = (P(None, "dp", None), P(None, "dp", None), P("dp", None), P("dp", None), P(), P())
    in_specs = (data, data, P(("dp", "sub")), P(None, ("dp", "sub"), None)) + trees * 3
    out_specs = (P(), P()) + trees * 3 + trees[:4]
    sizes = {axis: mesh.shape[axis] for axis in ("dp", "sub")}
    return jax.shard_map(
        functools.partial(per_device, sizes),
        mesh=mesh,
        in_specs=in_specs,
        out_specs=out_specs,
        check_vma=False,
    )
```

```python
import functools
import math

import jax
import jax.numpy as jnp
from jax import lax
from jax.experimental import pallas as pl
from jax.experimental.pallas import tpu as pltpu
from jax.sharding import PartitionSpec as P

NBIG = 2
NSMALL = 6
CROPS = NBIG + NSMALL
BIG = 7
SMALL = 3
TAPS = 9
ITERS = 3
LANES = 128

sink_temp = 0.05
softmax_temp = 0.1
norm_eps = 1e-05
unit_eps = 1e-12
trust_rate = 0.5
learn_rate = 1.0
momentum_rate = 0.5
average_rate = 0.5

MESH = pl.DeviceIdType.MESH
MIB = 1 << 20
LOG2E = math.log2(math.e)
SINK2 = LOG2E / sink_temp
SOFT2 = LOG2E / softmax_temp
PAIRS = NBIG * (CROPS - 1)


def cross_rows(left, right):
    return lax.dot_general(
        left, right, (((0,), (0,)), ((), ())), preferred_element_type=jnp.float32
    )


def against(left, right):
    return lax.dot_general(
        left, right, (((1,), (1,)), ((), ())), preferred_element_type=jnp.float32
    )


def greet(axis, count):
    me = lax.axis_index(axis)
    barrier = pltpu.get_barrier_semaphore()
    for hop in range(1, count):
        pl.semaphore_signal(
            barrier, inc=1, device_id={axis: lax.rem(me + hop, count)}, device_id_type=MESH
        )
    pl.semaphore_wait(barrier, count - 1)


class Exchanger:
    def __init__(self, sizes):
        self.sizes = sizes
        self.used = 0

    def next_id(self):
        self.used += 1
        return self.used


class Links:
    def __init__(self, send_sem, recv_sem):
        self.send_sem = send_sem
        self.recv_sem = recv_sem
        self.used = 0

    def __call__(self, source, target, device):
        copy = pltpu.make_async_remote_copy(
            src_ref=source,
            dst_ref=target,
            send_sem=self.send_sem.at[self.used],
            recv_sem=self.recv_sem.at[self.used],
            device_id=device,
            device_id_type=MESH,
        )
        self.used += 1
        copy.start()
        return copy


def wait_all(copies):
    for copy in copies:
        copy.wait()


def lanes_of(index, width=LANES):
    return pl.ds(pl.multiple_of(index * width, LANES), width)


class Place:
    def __init__(self, n_dp):
        self.n_dp = n_dp
        self.span = n_dp // 2
        dp, self.sub = lax.axis_index("dp"), lax.axis_index("sub")
        self.dp = dp
        self.near, self.far = dp // 2, dp % 2
        row, core = self.sub // 2, self.sub % 2
        self.row, self.core = row, core
        self.row_sub = 2 * (1 - row) + core
        self.core_sub = 2 * row + (1 - core)
        self.far_peer = {"dp": self.near * 2 + (1 - self.far)}
        self.row_peer = {"sub": self.row_sub}
        self.core_peer = {"sub": self.core_sub}

    def near_index(self, hop):
        return (self.near + hop) % self.span

    def near_peer(self, hop):
        return {"dp": self.near_index(hop) * 2 + self.far}

    def dp_peers(self):
        return [{"dp": (self.dp + hop) % self.n_dp} for hop in range(1, self.n_dp)]

    def sub_peers(self):
        return [{"sub": (self.sub + hop) % 4} for hop in range(1, 4)]

    def greet(self, peers):
        barrier = pltpu.get_barrier_semaphore()
        for peer in peers:
            pl.semaphore_signal(barrier, inc=1, device_id=peer, device_id_type=MESH)
        pl.semaphore_wait(barrier, len(peers))


ALL = slice(None)


def sigmoid_of(values):
    return 0.5 * jnp.tanh(0.5 * values) + 0.5


def rows_at(start, size):
    return pl.ds(start if isinstance(start, int) else pl.multiple_of(start, 16), size)


def tap_blocks(images, flip):
    moves = [[] for _ in range(TAPS)]
    zeros = [[] for _ in range(TAPS)]
    base = 0
    for extent, lines in ((BIG, NBIG * images), (SMALL, NSMALL * images)):
        for tap in range(TAPS):
            down, right = tap // 3 - 1, tap % 3 - 1
            if flip:
                down, right = -down, -right
            for row in range(extent):
                start = base + row * extent * lines
                if not 0 <= row + down < extent:
                    zeros[tap].append((start, extent * lines))
                    continue
                left, stop = max(0, -right), min(extent, extent - right)
                moves[tap].append(
                    (
                        start + left * lines,
                        base + ((row + down) * extent + left + right) * lines,
                        (stop - left) * lines,
                    )
                )
                if left:
                    zeros[tap].append((start, left * lines))
                if stop < extent:
                    zeros[tap].append((start + stop * lines, (extent - stop) * lines))
        base += extent * extent * lines
    return moves, zeros


def fill_columns(columns, source, images, flip):
    wide = source.shape[1]
    moves, zeros = tap_blocks(images, flip)
    for tap in range(TAPS):
        cols = pl.ds(tap * wide, wide)
        for target, start, size in moves[tap]:
            columns[pl.ds(target, size), cols] = source[pl.ds(start, size), :]
        for target, size in zeros[tap]:
            columns[pl.ds(target, size), cols] = jnp.zeros((size, wide), columns.dtype)


def masked_sums(values, mask, total):
    rows, wide = values.shape
    blocks = values.reshape(rows // 8, 8, wide)
    masked = blocks * mask
    total[0] += jnp.sum(masked, 0)
    total[1] += jnp.sum(masked * blocks, 0)


def row_tile(rows):
    return next(size for size in (192, 160, 128, 96, 64, 48, 32, 24, 16, 8) if rows % size == 0)


def centers_of(proto_ref, centers_ref, turned_ref):
    protos, depth = proto_ref.shape
    part = 256
    for start in range(0, turned_ref.shape[1], part):
        here = max(0, min(part, protos - start))
        values = jnp.zeros((part, depth), jnp.float32)
        if here:
            values = proto_ref[pl.ds(start, here), :]
            values = values * lax.rsqrt(jnp.sum(values * values, 1, keepdims=True) + unit_eps)
        if 0 < here < part:
            values = jnp.concatenate([values, jnp.zeros((part - here, depth), jnp.float32)], 0)
        centers_ref[pl.ds(start, part), :] = values.astype(jnp.bfloat16)
        turned_ref[:, pl.ds(start, part)] = values.T.astype(jnp.bfloat16)


def queue_sums(queue_ref, turned_ref, o_ref, total, view):
    rows, width = queue_ref.shape[1], turned_ref.shape[1]
    tile, part = row_tile(rows), 256
    total[...] = jnp.zeros_like(total)

    def step(index, carry):
        lines = queue_ref[view, pl.ds(index * tile, tile), :]
        for start in range(0, width, part):
            cols = pl.ds(start, part)
            scores = jnp.dot(lines, turned_ref[:, cols], preferred_element_type=jnp.float32)
            shares = jnp.exp2(scores * SINK2)
            total[:, cols] += jnp.sum(shares.reshape(tile // 8, 8, part), 0)
        return carry

    lax.fori_loop(0, rows // tile, step, 0)
    o_ref[pl.ds(view, 1), :] = jnp.sum(total[...], 0, keepdims=True)


class GroupSums:
    def __init__(self, at, links):
        self.at, self.links = at, links

    def start(self, mine, land):
        self.mine, self.land = mine, land
        self.copies = [
            self.links(mine, land.at[hop], peer) for hop, peer in enumerate(self.at.sub_peers())
        ]

    def finish(self):
        wait_all(self.copies)
        value = self.mine[...]
        for hop in range(3):
            value = value + self.land[hop]
        return value


def copy_rows(big, small, target, sem):
    split = big.shape[0]
    copies = [
        pltpu.make_async_copy(big, target.at[pl.ds(0, split)], sem.at[0]),
        pltpu.make_async_copy(small, target.at[pl.ds(split, small.shape[0])], sem.at[1]),
    ]
    for copy in copies:
        copy.start()
    return copies


def weigh(target, line, values):
    sums = jnp.sum(values * values, 0, keepdims=True)
    for lane in range(0, sums.shape[1], LANES):
        target[pl.ds(line, 1), :] += sums[:, lane : lane + LANES]


def forward_kernel(n_dp, images, *refs):
    i_outer, i_mid, i_hid, i_out, h_big, h_small, norm_ref, live_ref, queue_ref, proto_ref = refs[:10]
    (
        o_mid, o_last, o_hid, o_out, o_one, o_two, o_act, o_curve, o_normal, o_stat, o_pooled, o_live,
        o_slope, o_weigh, o_centers, o_turned, o_queue,
    ) = refs[10:27]
    (
        x_ref, w_first, w_mid, w_last, w_hid, w_out, first_w, mid_w, last_w, out_w, columns, act_one,
        act_two, one, two, three, total, pool, sums_a, land_a, sums_b, land_b, sums_c, land_c, pooled,
        queue_total, send_sem, recv_sem, own_sem, x_sem,
    ) = refs[27:]
    at = Place(n_dp)
    links = Links(send_sem, recv_sem)
    x_copies = copy_rows(h_big, h_small, x_ref, x_sem)
    share = w_hid.shape[1]
    w_first[...] = i_outer[0].astype(w_first.dtype)
    w_last[...] = i_outer[1].astype(w_last.dtype)
    w_hid[...] = i_hid[:, lanes_of(at.sub, share)].astype(w_hid.dtype)
    w_out[...] = i_out[...].astype(w_out.dtype)

    def cast_tap(index, carry):
        w_mid[index] = i_mid[index].astype(w_mid.dtype)
        return carry

    lax.fori_loop(0, TAPS, cast_tap, 0)
    at.greet(
        [at.near_peer(hop) for hop in range(1, at.span)] + [at.far_peer] + at.sub_peers()
    )
    low = jnp.bfloat16
    middle = first_w.shape[3]
    channels = x_ref.shape[1]
    rows = x_ref.shape[0]
    mask = live_ref[...][:, :1]
    half = middle // 2

    def flat(source, target, part, parts, split):
        height = source.shape[0] // parts
        some = pl.ds(part * height, height)
        return (
            lambda cols: source.at[some, cols],
            lambda near, far, cols: target.at[near, far, some, cols],
            split,
        )

    def taps(start, size):
        some = pl.ds(start, size)
        return (
            lambda cols: w_mid.at[some, :, cols],
            lambda near, far, cols: mid_w.at[some, near, far, :, cols],
            4,
        )

    quarter = w_out.shape[0] // 4
    out_rows = pl.ds(at.sub * quarter, quarter)
    pieces = [flat(w_first, first_w, part, 2, 4) for part in range(2)]
    pieces += [taps(0, 1), taps(1, 2), taps(3, 1), taps(4, 2), taps(6, 1), taps(7, 2)]
    pieces += [flat(w_last, last_w, part, 4, 2) for part in range(4)]
    trunk_pieces = len(pieces)
    pieces += [flat(w_hid, o_hid, part, 4, 1) for part in range(4)]
    pieces.append(
        (
            lambda cols: w_out.at[out_rows],
            lambda near, far, cols: out_w.at[near, far],
            1,
        )
    )
    count = len(pieces)
    mine = {4: lanes_of(at.sub), 2: lanes_of(at.core, half), 1: ALL}
    own, first, second, third, fourth = [], [], [], [], []
    for index, (source, target, split) in enumerate(pieces):
        cols = mine[split]
        copy = pltpu.make_async_copy(source(cols), target(at.near, at.far, cols), own_sem.at[index])
        copy.start()
        own.append(copy)

    def begin(index):
        if index < count:
            source, target, split = pieces[index]
            cols = mine[split]
            first.append(
                [
                    links(source(cols), target(at.near, at.far, cols), at.near_peer(hop))
                    for hop in range(1, at.span)
                ]
            )

    for index in range(3):
        begin(index)
    lag = 2
    ticks = count + 2 * lag

    def tick(now):
        if now < count:
            source, target, split = pieces[now]
            own[now].wait()
            wait_all(first[now])
            begin(now + 3)
            slab = target(ALL, at.far, mine[split])
            second.append(links(slab, slab, at.far_peer))
        past = now - lag
        if 0 <= past < count:
            source, target, split = pieces[past]
            second[past].wait()
            slab = target(ALL, ALL, mine[split])
            third.append(links(slab, slab, at.row_peer) if split == 4 else None)
            fourth.append([links(slab, slab, at.core_peer)] if split == 2 else [])
        past = now - 2 * lag
        if 0 <= past < count and pieces[past][2] == 4:
            source, target, split = pieces[past]
            third[past].wait()
            slabs = [target(ALL, ALL, cols) for cols in (mine[4], lanes_of(at.row_sub))]
            fourth[past] = [links(slab, slab, at.core_peer) for slab in slabs]

    def arrived(index):
        wait_all(fourth[index])

    tile = rows // 4
    sums = GroupSums(at, links)

    def pack(target, wide):
        target[pl.ds(0, 1), :] = jnp.sum(total[0, :, :wide], 0, keepdims=True)
        target[pl.ds(1, 1), :] = jnp.sum(total[1, :, :wide], 0, keepdims=True)

    def settle(value, count_all, start, wide):
        mean = value[0:1] / count_all
        inverse = lax.rsqrt(value[1:2] / count_all - mean * mean + norm_eps)
        o_stat[pl.ds(0, 1), pl.ds(start, wide)] = mean
        o_stat[pl.ds(1, 1), pl.ds(start, wide)] = inverse
        scale = norm_ref[pl.ds(0, 1), pl.ds(start, wide)] * inverse
        return scale, norm_ref[pl.ds(1, 1), pl.ds(start, wide)] - scale * mean

    centers_of(proto_ref, o_centers, o_turned)
    tick(0)
    queue_sums(queue_ref, o_turned, o_queue, queue_total, 0)
    tick(1)
    queue_sums(queue_ref, o_turned, o_queue, queue_total, 1)
    tick(2)
    o_weigh[...] = jnp.zeros_like(o_weigh)
    weigh(o_weigh, 0, i_outer[0])
    weigh(o_weigh, 1, i_outer[1])
    weigh(o_weigh, 4, i_out[...])

    def weigh_tap(index, carry):
        weigh(o_weigh, 2, i_mid[index])
        return carry

    lax.fori_loop(0, TAPS, weigh_tap, 0)
    tick(3)

    def weigh_part(index, carry):
        weigh(o_weigh, 3, i_hid[:, lanes_of(index, 512)])
        return carry

    lax.fori_loop(0, i_hid.shape[1] // 512, weigh_part, 0)
    for now in range(4, 6):
        tick(now)
    arrived(0)
    arrived(1)
    for copy in x_copies:
        copy.wait()

    total[...] = jnp.zeros_like(total)

    def step_one(index, carry):
        span = rows_at(index * tile, tile)
        value = jnp.dot(
            x_ref[span, :],
            first_w[...].reshape(channels, middle),
            preferred_element_type=jnp.float32,
        )
        one[span, :] = value
        masked_sums(value, mask, total.at[:, :, pl.ds(0, middle)])
        return carry

    lax.fori_loop(0, 4, step_one, 0)
    pack(sums_a, middle)
    live = jnp.sum(mask, 0, keepdims=True)
    sums_a[pl.ds(2, 1), :] = jnp.broadcast_to(live, (1, middle))
    sums.start(sums_a, land_a)
    tick(6)
    value = sums.finish()
    per_image = rows // images
    lives = value[2:3, :1]
    count_all = lives * per_image
    o_live[at.sub] = jnp.broadcast_to(live, o_live.shape[1:])
    for hop in range(3):
        o_live[(at.sub + 3 - hop) % 4] = jnp.broadcast_to(land_a[hop, 2:3, :1], o_live.shape[1:])
    scale, shift = settle(value, count_all, 0, middle)

    def step_act(source, target):
        def step(index, carry):
            span = rows_at(index * tile, tile)
            pre = source[span, :] * scale + shift
            target[span, :] = (pre * sigmoid_of(pre)).astype(low)
            return carry

        lax.fori_loop(0, 4, step, 0)

    step_act(one, act_one)
    save = [pltpu.make_async_copy(one, o_one, own_sem.at[count])]
    save[-1].start()
    tick(7)
    fill_columns(columns, act_one, images, False)

    total[...] = jnp.zeros_like(total)
    for part in range(3):
        for now in range(2):
            tick(8 + 2 * part + now)
        for index in range(2):
            arrived(2 + 2 * part + index)

        def step_two(index, carry):
            span = rows_at(index * tile, tile)
            value = jnp.dot(
                columns[span, pl.ds(part * 3 * middle, 3 * middle)],
                mid_w[pl.ds(part * 3, 3)].reshape(3 * middle, middle),
                preferred_element_type=jnp.float32,
            )
            if part:
                value = value + two[span, :]
            two[span, :] = value
            if part == 2:
                masked_sums(value, mask, total.at[:, :, pl.ds(0, middle)])
            return carry

        lax.fori_loop(0, 4, step_two, 0)
    save.append(pltpu.make_async_copy(mid_w, o_mid, own_sem.at[count + 2]))
    save[-1].start()
    pack(sums_b, middle)
    sums.start(sums_b, land_b)
    scale, shift = settle(sums.finish(), count_all, middle, middle)
    step_act(two, act_two)
    save.append(pltpu.make_async_copy(two, o_two, own_sem.at[count + 3]))
    save[-1].start()
    save.append(pltpu.make_async_copy(act_two, o_act, own_sem.at[count + 4]))
    save[-1].start()

    for now in range(14, trunk_pieces + 2 * lag):
        tick(now)
    for index in range(trunk_pieces - 4, trunk_pieces):
        arrived(index)
    save.append(pltpu.make_async_copy(last_w, o_last, own_sem.at[count + 5]))
    save[-1].start()
    total[...] = jnp.zeros_like(total)

    def step_three(index, carry):
        span = rows_at(index * tile, tile)
        for quarter in range(4):
            wide = channels // 4
            cols = pl.ds(quarter * wide, wide)
            weights = last_w[pl.ds(quarter * (at.span // 4), at.span // 4)].reshape(wide, middle)
            value = against(act_two[span, :], weights)
            three[span, cols] = value
            masked_sums(value, mask, total.at[:, :, cols])
        return carry

    lax.fori_loop(0, 4, step_three, 0)
    pack(sums_c, channels)
    sums.start(sums_c, land_c)
    for now in range(trunk_pieces + 2 * lag, ticks):
        tick(now)
    some = at.span // 4
    out_own = out_w.at[pl.ds(at.sub * some, some)]
    into = o_out.at[:, :, out_rows]
    own.append(pltpu.make_async_copy(out_own, into, own_sem.at[count - 1]))
    own[-1].start()
    out_copies = [
        links(out_w.at[pl.ds(peer["sub"] * some, some)], into, peer) for peer in at.sub_peers()
    ]
    scale, shift = settle(sums.finish(), count_all, 2 * middle, channels)

    pool[...] = jnp.zeros_like(pool)
    o_slope[...] = jnp.zeros_like(o_slope)
    wide = pl.ds(2 * middle, channels)
    center = o_stat[pl.ds(0, 1), wide] * o_stat[pl.ds(1, 1), wide]
    base = 0
    for extent, crops in ((BIG, NBIG), (SMALL, NSMALL)):
        lines = crops * images
        into = pl.ds(0, lines) if extent == BIG else pl.ds(NBIG * images, lines)

        def step_out(index, carry):
            span = rows_at(base + index * extent * lines, extent * lines)
            for start in range(0, channels, 512):
                cols = pl.ds(start, 512)
                pre = three[span, cols] * scale[:, start : start + 512]
                pre = pre + shift[:, start : start + 512] + x_ref[span, cols].astype(jnp.float32)
                sigma = sigmoid_of(pre)
                value = pre * sigma
                slope = sigma + value * (1.0 - sigma)
                normal = three[span, cols] * o_stat[1:2, 2 * middle + start : 2 * middle + start + 512]
                normal = normal - center[:, start : start + 512]
                columns[span, cols] = slope.astype(low)
                columns[span, pl.ds(channels + start, 512)] = normal.astype(low)
                pool[into, cols] += jnp.sum(value.reshape(extent, lines, 512), 0)
                o_slope[0, into, cols] += jnp.sum(slope.reshape(extent, lines, 512), 0)
                slope = slope * normal
                o_slope[1, into, cols] += jnp.sum(slope.reshape(extent, lines, 512), 0)
            return carry

        lax.fori_loop(0, extent, step_out, 0)
        pooled[into, :] = (pool[into, :] * (1.0 / (extent * extent))).astype(low)
        base += extent * extent * lines

    for index, target in enumerate((o_curve, o_normal)):
        some = columns.at[:, pl.ds(index * channels, channels)]
        save.append(pltpu.make_async_copy(some, target, x_sem.at[index]))
        save[-1].start()

    over = links(pooled, o_pooled.at[at.sub], at.row_peer)
    pair = links(pooled, o_pooled.at[at.sub], at.core_peer)
    o_pooled[at.sub] = pooled[...]
    over.wait()
    last = links(o_pooled.at[at.row_sub], o_pooled.at[at.row_sub], at.core_peer)
    pair.wait()
    last.wait()
    own[-1].wait()
    wait_all(out_copies)
    for copy in save:
        copy.wait()


def forward_trunk(
    n_dp, collective_id, images, outer, mid, hid, out, big, small, norms, live, queue, prototypes, width
):
    span = n_dp // 2
    height, middle = outer.shape[1:]
    rows, channels = big.shape[0] + small.shape[0], big.shape[1]
    share, narrow = hid.shape[1] // 4, out.shape[1]
    some = jax.ShapeDtypeStruct
    low, full = jnp.bfloat16, jnp.float32
    copies = 17 * (span + 4) + 16
    vmem, anywhere = pl.BlockSpec(memory_space=pltpu.VMEM), pl.BlockSpec(memory_space=pl.ANY)
    return pl.pallas_call(
        functools.partial(forward_kernel, n_dp, images),
        out_shape=(
            some((TAPS, span, 2, mid.shape[1], middle), low),
            some((span, 2, height, middle), low),
            some((span, 2, height, share), low),
            some((span // 4, 2, height, narrow), low),
            some((rows, middle), full),
            some((rows, middle), full),
            some((rows, middle), low),
            some((rows, channels), low),
            some((rows, channels), low),
            some((2, 2 * middle + channels), full),
            some((4, CROPS * images, channels), low),
            some((4, 8, LANES), full),
            some((2, CROPS * images, channels), full),
            some((8, LANES), full),
            some((width, prototypes.shape[1]), low),
            some((prototypes.shape[1], width), low),
            some((queue.shape[0], width), full),
        ),
        in_specs=[vmem] * 4 + [anywhere] * 2 + [vmem] * 4,
        out_specs=(anywhere,) * 9 + (vmem,) * 8,
        scratch_shapes=[
            pltpu.VMEM((rows, channels), low),
            pltpu.VMEM((height, middle), low),
            pltpu.VMEM(mid.shape, low),
            pltpu.VMEM((height, middle), low),
            pltpu.VMEM((height, share), low),
            pltpu.VMEM((height, narrow), low),
            pltpu.VMEM((span, 2, height, middle), low),
            pltpu.VMEM((TAPS, span, 2, mid.shape[1], middle), low),
            pltpu.VMEM((span, 2, height, middle), low),
            pltpu.VMEM((span, 2, height // 4, narrow), low),
            pltpu.VMEM((rows, TAPS * middle), low),
            pltpu.VMEM((rows, middle), low),
            pltpu.VMEM((rows, middle), low),
            pltpu.VMEM((rows, middle), full),
            pltpu.VMEM((rows, middle), full),
            pltpu.VMEM((rows, channels), full),
            pltpu.VMEM((2, 8, channels), full),
            pltpu.VMEM((CROPS * images, channels), full),
            pltpu.VMEM((3, middle), full),
            pltpu.VMEM((3, 3, middle), full),
            pltpu.VMEM((2, middle), full),
            pltpu.VMEM((3, 2, middle), full),
            pltpu.VMEM((2, channels), full),
            pltpu.VMEM((3, 2, channels), full),
            pltpu.VMEM((CROPS * images, channels), low),
            pltpu.VMEM((8, width), full),
            pltpu.SemaphoreType.DMA((copies,)),
            pltpu.SemaphoreType.DMA((copies,)),
            pltpu.SemaphoreType.DMA((17 + 6,)),
            pltpu.SemaphoreType.DMA((2,)),
        ],
        compiler_params=pltpu.CompilerParams(
            collective_id=collective_id, has_side_effects=True, vmem_limit_bytes=62 * MIB
        ),
        name="forward_trunk",
    )(outer, mid, hid, out, big, small, norms, live, queue, prototypes)


def plus(left, right):
    return left.astype(jnp.float32) + right.astype(jnp.float32)


def piece_list(n_dp, height, mid_height, refs):
    first, mid, last = refs
    half, quarter = height // 2, height // 4
    pieces = [last + (0, 1, part * half, half, 2) for part in range(2)]
    for start, taps in ((0, 1), (1, 1), (2, 1), (3, 1), (4, 1), (5, 1), (6, 1), (7, 2)):
        pieces.append(mid + (start, taps, 0, mid_height, 1))
    return pieces + [first + (0, 1, part * quarter, quarter, 0) for part in range(4)]


def backward_kernel(n_dp, images, *refs):
    p_pool, slope_ref, stat_ref, norm_ref, live_ref, lives_ref, extra_ref, g_hid, g_some = refs[:9]
    h_big, h_small, h_curve, h_normal, h_one, h_two, h_act, h_last, h_mid = refs[9:18]
    o_first, o_mid, o_last, o_hid, o_out, o_vec, o_sq = refs[18:25]
    (
        x_ref, one, two, act_two, last_w, mid_w, act_one, wide_low, work, thin_low, g_first, g_mid,
        g_last, total, pair_land, pair_sum, row_land, grad_pool, sums_a, land_a, sums_b, land_b,
        sums_c, land_c, hid_in, hid_sum, hid_land, g_out, out_in, out_sum, out_land, vec, vec_land,
        sq_mine, sq_land, send_sem, recv_sem, own_sem, x_sem,
    ) = refs[25:64]
    bufs = refs[64:]
    at = Place(n_dp)
    links = Links(send_sem, recv_sem)
    span = at.span
    at.greet(at.dp_peers() + at.sub_peers())
    low = jnp.bfloat16
    rows, channels = x_ref.shape
    middle = one.shape[1]
    height = g_last.shape[3]
    mask = live_ref[...][:, :1]
    tile = rows // 4

    loads = {}
    for index, (name, source, target) in enumerate(
        (
            ("one", h_one, one), ("curve", h_curve, wide_low), ("normal", h_normal, x_ref),
            ("last", h_last, last_w), ("two", h_two, two), ("act", h_act, act_two), ("mid", h_mid, mid_w),
        )
    ):
        loads[name] = pltpu.make_async_copy(source, target, own_sem.at[index])
        loads[name].start()

    pair = [
        links(p_pool.at[2 * line + (1 - at.core)], pair_land.at[line], at.core_peer)
        for line in (1 - at.row, at.row)
    ]
    far_copies = [links(g_hid.at[:, 1 - at.far], hid_in, at.far_peer)]
    some = g_some.shape[0]
    block = g_out.at[pl.ds(at.sub * some, some)]
    own_out = pltpu.make_async_copy(g_some, block, own_sem.at[7])
    own_out.start()
    out_copies = [links(g_some, block, peer) for peer in at.sub_peers()]
    pair[0].wait()
    pair_sum[...] = plus(p_pool[2 * (1 - at.row) + at.core], pair_land[1 - at.row]).astype(low)
    over = links(pair_sum, row_land, at.row_peer)
    pair[1].wait()

    wholes = [(g_hid, hid_in, hid_sum, hid_land), (g_out, out_in, out_sum, out_land)]

    def whole_far(which):
        source, landed, summed, land = wholes[which]
        far_copies[which].wait()
        for near in range(span):
            summed[near] = plus(source[near, at.far], landed[near]).astype(low)
        return [
            links(summed.at[at.near_index(hop)], land.at[hop - 1], at.near_peer(hop))
            for hop in range(1, span)
        ]

    def whole_near(which, copies):
        source, landed, summed, land = wholes[which]
        wait_all(copies)
        value = summed[at.near].astype(jnp.float32)
        for hop in range(1, span):
            value = value + land[hop - 1].astype(jnp.float32)
        return value.astype(low)

    sq_mine[0] = jnp.zeros_like(sq_mine[0])

    def squares_of(matrix, value):
        value = value.astype(jnp.float32)
        line = jnp.sum(value * value, 0, keepdims=True)
        for lane in range(0, line.shape[1], LANES):
            sq_mine[0, pl.ds(matrix, 1), :] += line[:, lane : lane + LANES]

    pieces = piece_list(
        n_dp, height, g_mid.shape[3], ((g_first, o_first), (g_mid, o_mid), (g_last, o_last))
    )
    mine, beside = lanes_of(at.sub), lanes_of(at.row_sub)
    state = [0] * len(pieces)
    flight = [None] * len(pieces)

    def loop(count, body):
        def step(index, carry):
            body(index)
            return carry

        lax.fori_loop(0, count, step, 0)

    def go(index):
        source, target, start, taps, line, size, matrix = pieces[index]
        held, second, third, nears = bufs[4 * index : 4 * index + 4]
        stage = state[index]
        state[index] += 1
        row_first = index % 2 == 0
        lines, some = pl.ds(line, size), pl.ds(start, taps)
        if stage == 0:
            flight[index] = [
                links(
                    source.at[some, :, :, lines, lanes_of(2 * row + (1 - at.core))],
                    held.at[row],
                    at.core_peer,
                )
                for row in range(2)
            ]
            return
        wait_all(flight[index])
        if stage == 1:
            for row in range(2):
                cols = lanes_of(2 * row + at.core)

                def body(at_block):
                    tap, near, far = at_block // (2 * span), at_block // 2 % span, at_block % 2
                    held[row, tap, near, far] = plus(
                        source[start + tap, near, far, lines, cols], held[row, tap, near, far]
                    ).astype(low)

                loop(taps * span * 2, body)
            if row_first:
                flight[index] = [links(held.at[1 - at.row], second, at.row_peer)]
            else:
                flight[index] = [links(held.at[:, :, :, 1 - at.far], second, at.far_peer)]
        elif stage == 2:
            if row_first:

                def body(at_block):
                    tap, near, far = at_block // (2 * span), at_block // 2 % span, at_block % 2
                    second[tap, near, far] = plus(
                        held[at.row, tap, near, far], second[tap, near, far]
                    ).astype(low)

                loop(taps * span * 2, body)
                flight[index] = [links(second.at[:, :, 1 - at.far], third, at.far_peer)]
            else:

                def body(at_block):
                    row, tap, near = at_block // (taps * span), at_block // span % taps, at_block % span
                    second[row, tap, near] = plus(
                        held[row, tap, near, at.far], second[row, tap, near]
                    ).astype(low)

                loop(taps * span * 2, body)
                flight[index] = [links(second.at[1 - at.row], third, at.row_peer)]
        elif stage == 3:

            def body(at_block):
                tap, near = at_block // span, at_block % span
                part = second[tap, near, at.far] if row_first else second[at.row, tap, near]
                third[tap, near] = plus(part, third[tap, near]).astype(low)

            loop(taps * span, body)
            flight[index] = [
                links(third.at[:, at.near_index(hop)], nears.at[hop - 1], at.near_peer(hop))
                for hop in range(1, span)
            ]
        elif stage == 4:
            for tap in range(taps):
                value = third[tap, at.near].astype(jnp.float32)
                for hop in range(1, span):
                    value = value + nears[hop - 1, tap].astype(jnp.float32)
                value = value.astype(low)
                squares_of(matrix, value)
                target[start + tap, lines, mine] = value
            slab = target.at[some, lines, mine]
            flight[index] = [links(slab, slab, at.row_peer)]
        elif stage == 5:
            slabs = [target.at[some, lines, cols] for cols in (mine, beside)]
            flight[index] = [links(slab, slab, at.core_peer) for slab in slabs]

    def go_pair(number):
        go(2 * number)
        go(2 * number + 1)

    count_all = jnp.sum(lives_ref[...][:, :1, :1], 0) * float(rows // images)
    sums = GroupSums(at, links)

    def terms(start, wide):
        cols = pl.ds(start, wide)
        mean, inverse = stat_ref[pl.ds(0, 1), cols], stat_ref[pl.ds(1, 1), cols]
        scale = norm_ref[pl.ds(0, 1), cols] * inverse
        return mean * inverse, inverse, scale, norm_ref[pl.ds(1, 1), cols] - scale * mean

    def slope_of(pre):
        sigma = sigmoid_of(pre)
        return sigma + pre * sigma * (1.0 - sigma)

    def pack(target, wide):
        target[pl.ds(0, 1), :] = jnp.sum(total[0, :, :wide], 0, keepdims=True)
        target[pl.ds(1, 1), :] = jnp.sum(total[1, :, :wide], 0, keepdims=True)

    center_one, inverse_one, scale_one, shift_one = terms(0, middle)
    center_two, inverse_two, scale_two, shift_two = terms(middle, middle)
    scale_three = terms(2 * middle, channels)[2]
    loads["one"].wait()

    def step_act(index):
        span_rows = rows_at(index * tile, tile)
        pre = one[span_rows, :] * scale_one + shift_one
        act_one[span_rows, :] = (pre * sigmoid_of(pre)).astype(low)

    loop(4, step_act)
    own_out.wait()
    wait_all(out_copies)
    far_copies.append(links(g_out.at[:, 1 - at.far], out_in, at.far_peer))
    value = plus(p_pool[at.sub], pair_land[at.row])
    over.wait()
    value = value + row_land[...].astype(jnp.float32)
    big = NBIG * images
    grad_pool[pl.ds(0, big), :] = value[:big] * (1.0 / (BIG * BIG))
    grad_pool[pl.ds(big, NSMALL * images), :] = value[big:] * (1.0 / (SMALL * SMALL))
    for which in range(2):
        sums_c[pl.ds(which, 1), :] = jnp.sum(grad_pool[...] * slope_ref[which], 0, keepdims=True)
    sums.start(sums_c, land_c)
    loads["curve"].wait()
    loads["normal"].wait()
    both_three = sums.finish()
    vec[...] = extra_ref[...]
    vec[pl.ds(1, 1), :] = both_three[1:2]
    vec[pl.ds(3, 1), :] = both_three[0:1]
    both_three = both_three / count_all

    chunk = channels // 4
    for quarter in range(4):
        cols = pl.ds(quarter * chunk, chunk)
        here = slice(quarter * chunk, (quarter + 1) * chunk)
        base = 0
        for extent, crops in ((BIG, NBIG), (SMALL, NSMALL)):
            lines = crops * images
            into = pl.ds(0, lines) if extent == BIG else pl.ds(big, lines)

            def step_grad(index):
                span_rows = rows_at(base + index * extent * lines, extent * lines)
                curve = wide_low[span_rows, cols].astype(jnp.float32)
                grad = curve.reshape(extent, lines, chunk) * grad_pool[into, cols]
                normal = x_ref[span_rows, cols].astype(jnp.float32)
                back = both_three[0:1, here] + normal * both_three[1:2, here]
                back = back.reshape(extent * crops, images, chunk) * mask
                grad = grad.reshape(extent * crops, images, chunk) - back
                grad = grad.reshape(extent * lines, chunk) * scale_three[:, here]
                wide_low[span_rows, cols] = grad.astype(low)

            loop(extent, step_grad)
            base += extent * extent * lines
    x_copies = copy_rows(h_big, h_small, x_ref, x_sem)
    loads["last"].wait()

    near_hid, near_out = whole_far(0), whole_far(1)

    def norm_sums(grad, normal):
        total[0, :, :middle] += jnp.sum(grad.reshape(tile // 8, 8, middle), 0)
        total[1, :, :middle] += jnp.sum((grad * normal).reshape(tile // 8, 8, middle), 0)

    loads["two"].wait()
    loads["act"].wait()
    total[...] = jnp.zeros_like(total)

    def step_two(index):
        span_rows = rows_at(index * tile, tile)
        grad = jnp.dot(
            wide_low[span_rows, :],
            last_w[...].reshape(channels, middle),
            preferred_element_type=jnp.float32,
        )
        grad = grad * slope_of(two[span_rows, :] * scale_two + shift_two)
        work[span_rows, :] = grad
        norm_sums(grad, two[span_rows, :] * inverse_two - center_two)

    loop(4, step_two)
    pack(sums_a, middle)
    sums.start(sums_a, land_a)

    def weight_rows(target, left, right):
        part = 256
        shards = max(1, part // height)
        for index in range(channels // part):
            value = cross_rows(left[:, pl.ds(index * part, part)], right[...]).astype(low)
            if shards == 1:
                target[0, index // 2, index % 2] = value
            else:
                some = pl.ds(index * (shards // 2), shards // 2)
                target[0, some] = value.reshape(shards // 2, 2, height, middle)

    weight_rows(g_last, wide_low, act_two)
    go_pair(0)

    def settle_grad(source, center, inverse, scale, both):
        def step(index):
            span_rows = rows_at(index * tile, tile)
            normal = source[span_rows, :] * inverse - center
            back = both[0:1] + normal * both[1:2]
            back = (back.reshape(tile // 8, 8, middle) * mask).reshape(tile, middle)
            thin_low[span_rows, :] = ((work[span_rows, :] - back) * scale).astype(low)

        loop(4, step)

    both_two = sums.finish()
    settle_grad(two, center_two, inverse_two, scale_two, both_two / count_all)
    vec[pl.ds(0, 1), pl.ds(middle, middle)] = both_two[1:2]
    vec[pl.ds(0, 1), pl.ds(3 * middle, middle)] = both_two[0:1]
    go_pair(0)

    loads["mid"].wait()
    moves, zeros = tap_blocks(images, True)
    total[...] = jnp.zeros_like(total)
    for part in range(3):
        for slot in range(3):
            cols = pl.ds(slot * middle, middle)
            for target, start, size in moves[3 * part + slot]:
                wide_low[pl.ds(target, size), cols] = thin_low[pl.ds(start, size), :]
            for target, size in zeros[3 * part + slot]:
                wide_low[pl.ds(target, size), cols] = jnp.zeros((size, middle), low)

        def step_one(index):
            span_rows = rows_at(index * tile, tile)
            grad = against(
                wide_low[span_rows, pl.ds(0, middle)], mid_w[3 * part].reshape(middle, middle)
            )
            for slot in range(1, 3):
                grad = grad + against(
                    wide_low[span_rows, pl.ds(slot * middle, middle)],
                    mid_w[3 * part + slot].reshape(middle, middle),
                )
            if part:
                grad = grad + work[span_rows, :]
            if part == 2:
                grad = grad * slope_of(one[span_rows, :] * scale_one + shift_one)
                norm_sums(grad, one[span_rows, :] * inverse_one - center_one)
            work[span_rows, :] = grad

        loop(4, step_one)
        if part == 2:
            pack(sums_b, middle)
            sums.start(sums_b, land_b)
        for slot in range(3):
            value = cross_rows(act_one[...], wide_low[:, pl.ds(slot * middle, middle)]).astype(low)
            g_mid[3 * part + slot] = value.reshape(g_mid.shape[1:])
        if part == 0:
            go_pair(1)
            go_pair(0)
        elif part == 1:
            go_pair(2)
            go_pair(1)
            go_pair(0)
        else:
            go_pair(3)
            go_pair(4)
            go_pair(2)
            go_pair(1)
            go_pair(0)
            value = whole_near(0, near_hid)
            wide = g_hid.shape[3]
            squares_of(3, value)
            slabs = [o_hid.at[:, lanes_of(which, wide)] for which in (at.sub, at.row_sub)]
            o_hid[:, lanes_of(at.sub, wide)] = value
            hid_row = links(slabs[0], slabs[0], at.row_peer)
            value = whole_near(1, near_out)
            squares_of(4, value)
            o_out[...] = value

    both_one = sums.finish()
    settle_grad(one, center_one, inverse_one, scale_one, both_one / count_all)
    vec[pl.ds(0, 1), pl.ds(0, middle)] = both_one[1:2]
    vec[pl.ds(0, 1), pl.ds(2 * middle, middle)] = both_one[0:1]
    wide = vec.shape[1] // 4
    vec_cols = lanes_of(at.sub, wide)
    vec_copies = [
        links(vec.at[:, vec_cols], vec_land.at[hop], peer)
        for hop, peer in enumerate(at.dp_peers())
    ]
    go_pair(3)
    hid_row.wait()
    final = [links(slab, slab, at.core_peer) for slab in slabs]

    for copy in x_copies:
        copy.wait()
    weight_rows(g_first, x_ref, thin_low)
    go_pair(5)
    go_pair(6)

    numbers = range(len(pieces) // 2)
    tick = 0
    sent = False
    while min(state) < 6:
        for number in numbers:
            if state[2 * number] < 6 and tick >= max(0, number - 4):
                go_pair(number)
        if tick == 1:
            wait_all(vec_copies)
            value = vec[:, vec_cols]
            for hop in range(n_dp - 1):
                value = value + vec_land[hop]
            o_vec[:, vec_cols] = value
            vec_final = [
                links(o_vec.at[:, vec_cols], o_vec.at[:, vec_cols], peer)
                for peer in at.sub_peers()
            ]
        if not sent and min(state) >= 5:
            sent = True
            sq_copies = [
                links(sq_mine.at[0], sq_land.at[hop], peer)
                for hop, peer in enumerate(at.dp_peers())
            ]
        tick += 1
    wait_all(sq_copies)
    value = sq_mine[0]
    for hop in range(n_dp - 1):
        value = value + sq_land[hop]
    sq_mine[1] = value
    sq_copies = [
        links(sq_mine.at[1], sq_land.at[n_dp - 1 + hop], peer)
        for hop, peer in enumerate(at.sub_peers())
    ]
    wait_all(sq_copies)
    for hop in range(3):
        value = value + sq_land[n_dp - 1 + hop]
    o_sq[...] = value
    for copies in flight:
        wait_all(copies)
    wait_all(final)
    wait_all(vec_final)


def backward_trunk(
    n_dp, collective_id, images, pooled, slopes, stat, norms, live, lives, extra, hid, out, big, small,
    curve, normal, one, two, act, last, mid,
):
    span = n_dp // 2
    low, full = jnp.bfloat16, jnp.float32
    rows, channels = curve.shape
    middle = one.shape[1]
    height, mid_height = last.shape[2], mid.shape[3]
    narrow = out.shape[1]
    crops = CROPS * images
    some = jax.ShapeDtypeStruct
    bufs = []
    for index, piece in enumerate(piece_list(n_dp, height, mid_height, ((0, 0),) * 3)):
        taps, block = piece[3], (piece[5], LANES)
        bufs.append(pltpu.VMEM((2, taps, span, 2) + block, low))
        if index % 2 == 0:
            bufs.append(pltpu.VMEM((taps, span, 2) + block, low))
        else:
            bufs.append(pltpu.VMEM((2, taps, span) + block, low))
        bufs.append(pltpu.VMEM((taps, span) + block, low))
        bufs.append(pltpu.VMEM((span - 1, taps) + block, low))
    copies = 14 * (span + 6) + 2 * (span + 4) + 2 * n_dp + 40
    vmem, anywhere = pl.BlockSpec(memory_space=pltpu.VMEM), pl.BlockSpec(memory_space=pl.ANY)
    return pl.pallas_call(
        functools.partial(backward_kernel, n_dp, images),
        out_shape=(
            some((1, height, middle), low),
            some((TAPS, mid_height, middle), low),
            some((1, height, middle), low),
            some((height, 4 * hid.shape[1]), low),
            some((height, narrow), low),
            some(extra.shape, full),
            some((8, LANES), full),
        ),
        in_specs=[vmem] * 9 + [anywhere] * 9,
        out_specs=(vmem,) * 7,
        scratch_shapes=[
            pltpu.VMEM((rows, channels), low),
            pltpu.VMEM((rows, middle), full),
            pltpu.VMEM((rows, middle), full),
            pltpu.VMEM((rows, middle), low),
            pltpu.VMEM((span, 2, height, middle), low),
            pltpu.VMEM((TAPS, span, 2, mid_height, middle), low),
            pltpu.VMEM((rows, middle), low),
            pltpu.VMEM((rows, channels), low),
            pltpu.VMEM((rows, middle), full),
            pltpu.VMEM((rows, middle), low),
            pltpu.VMEM((1, span, 2, height, middle), low),
            pltpu.VMEM((TAPS, span, 2, mid_height, middle), low),
            pltpu.VMEM((1, span, 2, height, middle), low),
            pltpu.VMEM((2, 8, middle), full),
            pltpu.VMEM((2, crops, channels), low),
            pltpu.VMEM((crops, channels), low),
            pltpu.VMEM((crops, channels), low),
            pltpu.VMEM((crops, channels), full),
            pltpu.VMEM((2, middle), full),
            pltpu.VMEM((3, 2, middle), full),
            pltpu.VMEM((2, middle), full),
            pltpu.VMEM((3, 2, middle), full),
            pltpu.VMEM((2, channels), full),
            pltpu.VMEM((3, 2, channels), full),
            pltpu.VMEM((span, height, hid.shape[1]), low),
            pltpu.VMEM((span, height, hid.shape[1]), low),
            pltpu.VMEM((span - 1, height, hid.shape[1]), low),
            pltpu.VMEM((span, 2, height, narrow), low),
            pltpu.VMEM((span, height, narrow), low),
            pltpu.VMEM((span, height, narrow), low),
            pltpu.VMEM((span - 1, height, narrow), low),
            pltpu.VMEM(extra.shape, full),
            pltpu.VMEM((n_dp - 1, extra.shape[0], extra.shape[1] // 4), full),
            pltpu.VMEM((2, 8, LANES), full),
            pltpu.VMEM((n_dp + 2, 8, LANES), full),
            pltpu.SemaphoreType.DMA((copies,)),
            pltpu.SemaphoreType.DMA((copies,)),
            pltpu.SemaphoreType.DMA((8,)),
            pltpu.SemaphoreType.DMA((2,)),
        ]
        + bufs,
        compiler_params=pltpu.CompilerParams(
            collective_id=collective_id, has_side_effects=True, vmem_limit_bytes=62 * MIB
        ),
        name="backward_trunk",
    )(
        pooled,
        slopes,
        stat,
        norms,
        live,
        lives,
        extra,
        hid.reshape(span, 2, height, hid.shape[1]),
        out.reshape(span // 4, 2, height, narrow),
        big,
        small,
        curve,
        normal,
        one,
        two,
        act,
        last,
        mid,
    )


def sinkhorn_kernel(
    axis,
    count,
    protos,
    queue_ref,
    centers_ref,
    turned_ref,
    pooled_ref,
    hid_ref,
    out_ref,
    norm_ref,
    live_ref,
    lives_ref,
    weigh_ref,
    first_ref,
    proto_grad_ref,
    d_hid_ref,
    d_out_ref,
    back_ref,
    extra_ref,
    partial_ref,
    act,
    normal,
    grads,
    lows,
    embed_ref,
    four,
    four_land,
    grad,
    parts_land,
    kept,
    scores,
    mine,
    landed,
    shift,
    total,
    send_sem,
    recv_sem,
):
    me = lax.axis_index(axis)
    views, rows, _ = queue_ref.shape
    width = turned_ref.shape[1]
    images = live_ref.shape[0]
    tile = row_tile(rows)
    part = 512
    parts = range(0, width, part)
    mask = live_ref[...][:, :1]
    crops = CROPS * images
    share = hid_ref.shape[1]
    low = jnp.bfloat16
    greet(axis, count)

    slots = lax.broadcasted_iota(jnp.int32, (images, 1), 0).astype(jnp.float32)
    masks = [jnp.where(slots < lives_ref[member, :images, :1], 1.0, 0.0) for member in range(count)]
    live_group = sum(lives_ref[member, :1, :1] for member in range(count))
    count_crops = live_group * float(CROPS)

    def spread(values, member):
        return (values.reshape(CROPS, images, values.shape[1]) * masks[member]).reshape(values.shape)

    sums = jnp.zeros((1, share), jnp.float32)
    squares = jnp.zeros((1, share), jnp.float32)
    for member in range(count):
        value = jnp.dot(pooled_ref[member], hid_ref[...], preferred_element_type=jnp.float32)
        normal[member] = value
        masked = spread(value, member)
        sums = sums + jnp.sum(masked, 0, keepdims=True)
        squares = squares + jnp.sum(masked * value, 0, keepdims=True)
    mean = sums / count_crops
    inverse_four = lax.rsqrt(squares / count_crops - mean * mean + norm_eps)
    gain, bias = norm_ref[0:1, :], norm_ref[1:2, :]
    for member in range(count):
        value = (normal[member] - mean) * inverse_four
        normal[member] = value
        pre = value * gain + bias
        act[member] = (pre * sigmoid_of(pre)).astype(low)
        partial_ref[member] = jnp.dot(act[member], out_ref[...], preferred_element_type=jnp.float32)

    def start_group(turn, source, target):
        copies = []
        for hop in range(1, count):
            to = lax.rem(me + hop, count)
            copy = pltpu.make_async_remote_copy(
                src_ref=source(to),
                dst_ref=target(hop),
                send_sem=send_sem.at[turn, hop],
                recv_sem=recv_sem.at[turn, hop],
                device_id={axis: to},
                device_id_type=MESH,
            )
            copy.start()
            copies.append(copy)
        return copies

    def to_group(turn, source, target):
        for copy in start_group(turn, source, target):
            copy.wait()

    to_group(ITERS, lambda to: partial_ref.at[to], lambda hop: parts_land.at[hop])
    embedding = partial_ref[me]
    for hop in range(1, count):
        embedding = embedding + parts_land[hop]
    inverse = lax.rsqrt(jnp.sum(embedding * embedding, 1, keepdims=True) + unit_eps)
    unit = embedding * inverse
    unit_low = unit.astype(jnp.bfloat16)

    def sum_group(turn):
        copies = []
        for hop in range(1, count):
            copy = pltpu.make_async_remote_copy(
                src_ref=mine.at[turn],
                dst_ref=landed.at[turn, hop],
                send_sem=send_sem.at[turn, hop],
                recv_sem=recv_sem.at[turn, hop],
                device_id={axis: lax.rem(me + hop, count)},
                device_id_type=MESH,
            )
            copy.start()
            copies.append(copy)
        for copy in copies:
            copy.wait()
        whole = mine[turn]
        for hop in range(1, count):
            whole = whole + landed[turn, hop]
        return whole

    for start in parts:
        cols = pl.ds(start, part)
        scores[:, cols] = jnp.dot(
            unit_low, turned_ref[:, cols], preferred_element_type=jnp.float32
        )
        for view in range(views):
            lines = pl.ds(view * images, images)
            shares = jnp.exp2(scores[lines, cols] * SINK2) * mask
            mine[0, pl.ds(view, 1), cols] = first_ref[pl.ds(view, 1), cols] + jnp.sum(
                shares, 0, keepdims=True
            )
    real = lax.broadcasted_iota(jnp.int32, (1, width), 1) < protos
    first = sum_group(0)
    shift[...] = jnp.where(real, jnp.log2(first), 1e30)

    for turn in range(1, ITERS):
        for view in range(views):
            lines = pl.ds(view * images, images)
            row = pl.ds(view, 1)
            if turn == 1:
                own = jnp.exp2(scores[lines, :] * SINK2 - shift[row, :]) * mask
                weight = jnp.sum(own, 1, keepdims=True)
            else:
                own = jnp.exp2(scores[lines, :] * SINK2 - first_log[row, :]) * mask
                weight = jnp.sum(own * shift[row, :], 1, keepdims=True)
            total[...] = own / (weight + (1.0 - mask))

            def step(index, carry):
                span = pl.ds(index * tile, tile)
                if turn == 1:
                    lines = queue_ref[view, span, :]
                sums = jnp.zeros((tile, LANES), jnp.float32)
                for start in parts:
                    cols = pl.ds(start, part)
                    if turn == 1:
                        raw = jnp.dot(lines, turned_ref[:, cols], preferred_element_type=jnp.float32)
                        shares = jnp.exp2(raw * SINK2 - shift[row, cols])
                        kept[view, span, cols] = shares
                    else:
                        shares = kept[view, span, cols] * shift[row, cols]
                    for lane in range(0, part, LANES):
                        sums = sums + shares[:, lane : lane + LANES]
                scale = 1.0 / jnp.sum(sums, 1, keepdims=True)
                for start in parts:
                    cols = pl.ds(start, part)
                    scaled = kept[view, span, cols] * scale
                    total[:, cols] += jnp.sum(scaled.reshape(tile // 8, 8, part), 0)
                return carry

            lax.fori_loop(0, rows // tile, step, 0)
            mine[turn, row, :] = jnp.sum(total[...], 0, keepdims=True)
        if turn == 1:
            first_log = shift[...]
        whole = sum_group(turn)
        shift[...] = jnp.where(real, 1.0 / whole, 0.0)

    codes = []
    for view in range(views):
        lines = pl.ds(view * images, images)
        own = jnp.exp2(scores[lines, :] * SINK2 - first_log[view : view + 1, :]) * mask
        own = own * shift[pl.ds(view, 1), :]
        codes.append(own / (jnp.sum(own, 1, keepdims=True) + (1.0 - mask)))
    code_total = codes[0] + codes[1]
    loss = jnp.zeros((images, 1), jnp.float32)
    for crop in range(CROPS):
        lines = pl.ds(crop * images, images)
        raw = jnp.where(real, scores[lines, :] * SOFT2, -1e30)
        raw = raw - jnp.max(raw, 1, keepdims=True)
        powers = jnp.exp2(raw)
        norm = jnp.sum(powers, 1, keepdims=True)
        others = code_total - codes[crop] if crop < NBIG else code_total
        logs = jnp.where(real, (raw - jnp.log2(norm)) / LOG2E, 0.0)
        loss = loss - jnp.sum(others * logs, 1, keepdims=True)
        weight = (NBIG - 1.0 if crop < NBIG else float(NBIG)) * mask / norm
        grad[lines, :] = (weight * powers - others) / (PAIRS * softmax_temp)
    grad_unit = jnp.zeros(unit.shape, jnp.float32)
    for start in parts:
        cols = pl.ds(start, part)
        some = grad[:, cols].astype(jnp.bfloat16)
        grad_unit = grad_unit + jnp.dot(
            some, centers_ref[cols, :], preferred_element_type=jnp.float32
        )
        proto_grad_ref[cols, :] = cross_rows(some, unit_low)
    grad_embed = inverse * (
        grad_unit - unit * jnp.sum(unit * grad_unit, 1, keepdims=True)
    )
    embed_ref[me] = grad_embed.astype(jnp.bfloat16)
    to_group(ITERS + 1, lambda to: embed_ref.at[me], lambda hop: embed_ref.at[me])

    gain_sum = jnp.zeros((1, share), jnp.float32)
    bias_sum = jnp.zeros((1, share), jnp.float32)
    for member in range(count):
        value = against(embed_ref[member], out_ref[...])
        pre = normal[member] * gain + bias
        sigma = sigmoid_of(pre)
        value = value * (sigma + pre * sigma * (1.0 - sigma))
        grads[member] = value
        bias_sum = bias_sum + jnp.sum(value, 0, keepdims=True)
        gain_sum = gain_sum + jnp.sum(value * normal[member], 0, keepdims=True)
    four[pl.ds(0, 1), :] = gain_sum
    four[pl.ds(1, 1), :] = bias_sum
    four[pl.ds(2, 1), :] = jnp.broadcast_to(
        jnp.sum(loss, 0, keepdims=True) / PAIRS, (1, share)
    )
    copies = start_group(ITERS + 2, lambda to: four, lambda hop: four_land.at[hop])
    scale = gain * inverse_four
    for member in range(count):
        value = spread((bias_sum + normal[member] * gain_sum) / count_crops, member)
        lows[member] = ((grads[member] - value) * scale).astype(low)
    embeds = embed_ref[...].reshape(count * crops, embed_ref.shape[2])
    d_out_ref[...] = cross_rows(act[...].reshape(count * crops, share), embeds).astype(low)
    low_rows = lows[...].reshape(count * crops, share)
    for start in range(0, pooled_ref.shape[2], 256):
        left = pooled_ref[:, :, pl.ds(start, 256)].reshape(count * crops, 256)
        d_hid_ref[pl.ds(start, 256), :] = cross_rows(left, low_rows).astype(low)
        back = against(low_rows, hid_ref[pl.ds(start, 256), :]).astype(low)
        back_ref[:, :, pl.ds(start, 256)] = back.reshape(count, crops, 256)
    extra_ref[...] = jnp.zeros_like(extra_ref)
    for copy in copies:
        copy.wait()
    loss_group = jnp.zeros((1, 1), jnp.float32)
    for hop in range(count):
        source = (me + count - hop) % count
        value = four_land[hop] if hop else four[...]
        extra_ref[pl.ds(2, 1), lanes_of(source, share)] = value[0:1]
        extra_ref[pl.ds(4, 1), lanes_of(source, share)] = value[1:2]
        loss_group = loss_group + value[2:3, :1]
    lane = lax.broadcasted_iota(jnp.int32, (1, extra_ref.shape[1]), 1)
    line = jnp.where(lane == 0, loss_group, 0.0) + jnp.where(lane == 1, live_group, 0.0)
    for which in range(5):
        value = jnp.sum(weigh_ref[pl.ds(which, 1), :], 1, keepdims=True)
        line = line + jnp.where(lane == 2 + which, value, 0.0)
    extra_ref[pl.ds(5, 1), :] = line


def sinkhorn(
    sizes, collective_id, protos, queue, centers, turned, pooled, hid, out, norms, live, lives, weigh,
    first,
):
    count = sizes["sub"]
    views, rows, depth = queue.shape
    width = turned.shape[1]
    crops, channels = pooled.shape[1:]
    share = hid.shape[1]
    low, full = jnp.bfloat16, jnp.float32
    some = jax.ShapeDtypeStruct
    turns = ITERS + 3
    return pl.pallas_call(
        functools.partial(sinkhorn_kernel, "sub", count, protos),
        out_shape=(
            some((width, depth), full),
            some((channels, share), low),
            some((share, depth), low),
            some((count, crops, channels), low),
            some((8, count * share), full),
        ),
        in_specs=[pl.BlockSpec(memory_space=pltpu.VMEM)] * 11,
        out_specs=(pl.BlockSpec(memory_space=pltpu.VMEM),) * 5,
        scratch_shapes=[
            pltpu.VMEM((count, crops, depth), full),
            pltpu.VMEM((count, crops, share), low),
            pltpu.VMEM((count, crops, share), full),
            pltpu.VMEM((count, crops, share), full),
            pltpu.VMEM((count, crops, share), low),
            pltpu.VMEM((count, crops, depth), low),
            pltpu.VMEM((3, share), full),
            pltpu.VMEM((count, 3, share), full),
            pltpu.VMEM((crops, width), full),
            pltpu.VMEM((count, crops, depth), full),
            pltpu.VMEM((views, rows, width), full),
            pltpu.VMEM((crops, width), full),
            pltpu.VMEM((ITERS, views, width), full),
            pltpu.VMEM((ITERS, count, views, width), full),
            pltpu.VMEM((views, width), full),
            pltpu.VMEM((8, width), full),
            pltpu.SemaphoreType.DMA((turns, count)),
            pltpu.SemaphoreType.DMA((turns, count)),
        ],
        compiler_params=pltpu.CompilerParams(
            collective_id=collective_id, has_side_effects=True, vmem_limit_bytes=54 * MIB
        ),
        name="sinkhorn",
    )(queue, centers, turned, pooled, hid, out, norms, live, lives, weigh, first)


def advance(weight, gradient, moment, average, trust):
    step_now = trust * gradient
    moment_new = momentum_rate * moment + step_now
    weight_new = weight - learn_rate * (step_now + momentum_rate * moment_new)
    average_new = average_rate * average + (1.0 - average_rate) * weight_new
    return (weight_new, moment_new, average_new)


def update_kernel(protos, *refs):
    (
        g_first, g_mid, g_last, g_hid, g_out, vec, sq, centers,
        w_outer, w_mid, w_hid, w_out, w_proto, w_norm,
        m_outer, m_mid, m_hid, m_out, m_proto, m_norm,
        a_outer, a_mid, a_hid, a_out, a_proto, a_norm,
    ) = refs[:26]
    news, moments, averages, lows = refs[26:32], refs[32:38], refs[38:44], refs[44:48]
    proto_grad, norm_grad, square = refs[48:]
    middle = g_first.shape[2]

    def trust_of(weights, grads):
        return trust_rate * jnp.sqrt(weights) / (jnp.sqrt(grads) + 1e-12)

    def put(which, at, weight, grad, moment, average, trust):
        new, moment, average = advance(weight, grad.astype(jnp.float32), moment, average, trust)
        news[which][at] = new
        moments[which][at] = moment
        averages[which][at] = average
        if which < 4:
            lows[which][at] = new.astype(jnp.bfloat16)

    def matrix_trust(line, lane, share=1.0):
        grads = jnp.sum(sq[pl.ds(line, 1), :], 1, keepdims=True) * share
        return trust_of(vec[5:6, lane : lane + 1], grads)

    for which, (grad, line) in enumerate(((g_first, 0), (g_last, 2))):
        trust = matrix_trust(line, 2 + which)
        height = grad.shape[1] // 4
        for index in range(4):
            lines = pl.ds(index * height, height)
            at = (which, lines)
            put(0, at, w_outer[at], grad[0, lines], m_outer[at], a_outer[at], trust)
    trust_mid = matrix_trust(1, 4)

    def step_mid(index, carry):
        put(1, index, w_mid[index], g_mid[index], m_mid[index], a_mid[index], trust_mid)
        return carry

    lax.fori_loop(0, TAPS, step_mid, 0)
    trust_hid = matrix_trust(3, 5)
    height = w_hid.shape[0] // 8 if w_hid.shape[0] >= 64 else 8

    def step_hid(index, carry):
        at = pl.ds(pl.multiple_of(index * height, 8), height)
        put(2, at, w_hid[at], g_hid[at], m_hid[at], a_hid[at], trust_hid)
        return carry

    lax.fori_loop(0, w_hid.shape[0] // height, step_hid, 0)
    whole = slice(None)
    put(3, whole, w_out[...], g_out[...], m_out[...], a_out[...], matrix_trust(4, 6, 0.25))

    for row, lines in enumerate((((0, 0), 1, 2), ((0, 1), 3, 4))):
        (line, half), wide, last = lines
        start = 2 * middle * half
        norm_grad[pl.ds(row, 1), pl.ds(0, 2 * middle)] = vec[line : line + 1, start : start + 2 * middle]
        size = vec.shape[1]
        norm_grad[pl.ds(row, 1), pl.ds(2 * middle, size)] = vec[wide : wide + 1, :]
        norm_grad[pl.ds(row, 1), pl.ds(2 * middle + size, size)] = vec[last : last + 1, :]
    weight, grad = w_norm[...], norm_grad[...]
    trust = trust_of(
        jnp.sum(weight * weight, 1, keepdims=True), jnp.sum(grad * grad, 1, keepdims=True)
    )
    put(5, whole, weight, grad, m_norm[...], a_norm[...], trust)

    part = next(size for size in (600, 500, 400, 304, 200, 104, 40, 24, 8) if protos % size == 0)
    square[...] = jnp.zeros_like(square)

    def step_grad(index, carry):
        at = pl.ds(pl.multiple_of(index * part, 8), part)
        weight, value = w_proto[at], centers[at]
        inverse = lax.rsqrt(jnp.sum(weight * weight, 1, keepdims=True) + unit_eps)
        unit = weight * inverse
        grad = inverse * (value - unit * jnp.sum(unit * value, 1, keepdims=True))
        proto_grad[at] = grad
        weigh(square, 0, weight)
        weigh(square, 1, grad)
        return carry

    lax.fori_loop(0, protos // part, step_grad, 0)
    sums = jnp.sum(square[...], 1, keepdims=True)
    trust_proto = trust_of(sums[0:1], sums[1:2])

    def step_proto(index, carry):
        at = pl.ds(pl.multiple_of(index * part, 8), part)
        put(4, at, w_proto[at], proto_grad[at], m_proto[at], a_proto[at], trust_proto)
        return carry

    lax.fori_loop(0, protos // part, step_proto, 0)


def update(grads, vec, sq, centers, weights, moments, averages):
    some = jax.ShapeDtypeStruct
    protos = weights[4].shape[0]
    shapes = tuple(some(value.shape, value.dtype) for value in weights)
    lows = tuple(some(value.shape, jnp.bfloat16) for value in weights[:4])
    vmem = pl.BlockSpec(memory_space=pltpu.VMEM)
    results = pl.pallas_call(
        functools.partial(update_kernel, protos),
        out_shape=shapes * 3 + lows,
        in_specs=[vmem] * 26,
        out_specs=(vmem,) * 22,
        scratch_shapes=[
            pltpu.VMEM(weights[4].shape, jnp.float32),
            pltpu.VMEM(weights[5].shape, jnp.float32),
            pltpu.VMEM((8, LANES), jnp.float32),
        ],
        compiler_params=pltpu.CompilerParams(vmem_limit_bytes=56 * MIB),
        name="update",
    )(*grads, vec, sq, centers, *weights, *moments, *averages)
    return results


def per_device(
    sizes,
    big_maps,
    small_maps,
    live_counts,
    queue,
    bottleneck_outer,
    bottleneck_inner,
    proj_hidden,
    proj_out,
    prototypes,
    norm_params,
    mom_outer,
    mom_inner,
    mom_hidden,
    mom_out,
    mom_protos,
    mom_norms,
    avg_outer,
    avg_inner,
    avg_hidden,
    avg_out,
    avg_protos,
    avg_norms,
):
    n_dp, n_sub = sizes["dp"], sizes["sub"]
    exchange = Exchanger(sizes)
    images = big_maps.shape[0]
    channels = big_maps.shape[-1]
    middle = bottleneck_inner.shape[-1]
    hidden_width = proj_hidden.shape[1]
    out_width = proj_out.shape[1]
    proto_count = prototypes.shape[0]
    proto_width = -(-proto_count // 512) * 512
    here = lax.axis_index("sub")
    share = hidden_width // n_sub

    norm_start = 2 * middle + channels + here * share
    norm_four = lax.dynamic_slice(norm_params, (0, norm_start), (2, share))
    image_mask = (jnp.arange(images) < live_counts[0]).astype(jnp.float32)[:, None]
    live_tile = jnp.broadcast_to(image_mask, (images, LANES))
    big = jnp.transpose(big_maps, (2, 3, 1, 0, 4)).reshape(-1, channels)
    small = jnp.transpose(small_maps, (2, 3, 1, 0, 4)).reshape(-1, channels)

    (
        inner_low, last_w, hidden_low, out_low, hidden_one, hidden_two, act_two, curve, normal,
        trunk_stat, pooled_all, lives, slopes, weights_sq, centers_low, turned, first_sums,
    ) = forward_trunk(
        n_dp,
        exchange.next_id(),
        images,
        bottleneck_outer,
        bottleneck_inner,
        proj_hidden,
        proj_out,
        big,
        small,
        norm_params,
        live_tile,
        queue,
        prototypes,
        proto_width,
    )

    grad_centers, d_hidden, d_out, pooled_back, extra = sinkhorn(
        sizes,
        exchange.next_id(),
        proto_count,
        queue,
        centers_low,
        turned,
        pooled_all,
        hidden_low.reshape(channels, share),
        out_low.reshape(share, out_width),
        norm_four,
        live_tile,
        lives,
        weights_sq,
        first_sums,
    )
    centers_sum = lax.psum(grad_centers, ("dp", "sub"))

    shard_first, shard_inner, shard_last, shard_hidden, shard_out, vector, grad_sq = backward_trunk(
        n_dp,
        exchange.next_id(),
        images,
        pooled_back,
        slopes,
        trunk_stat,
        norm_params,
        live_tile,
        lives,
        extra,
        d_hidden,
        d_out,
        big,
        small,
        curve,
        normal,
        hidden_one,
        hidden_two,
        act_two,
        last_w,
        inner_low,
    )
    results = update(
        (shard_first, shard_inner, shard_last, shard_hidden, shard_out),
        vector,
        grad_sq,
        centers_sum,
        (bottleneck_outer, bottleneck_inner, proj_hidden, proj_out, prototypes, norm_params),
        (mom_outer, mom_inner, mom_hidden, mom_out, mom_protos, mom_norms),
        (avg_outer, avg_inner, avg_hidden, avg_out, avg_protos, avg_norms),
    )
    return (vector[5, 0], vector[5, 1]) + tuple(results)


def solution(mesh):
    data = P(("dp", "sub"), None, None, None, None)
    trees = (P(None, "dp", None), P(None, "dp", None), P("dp", None), P("dp", None), P(), P())
    in_specs = (data, data, P(("dp", "sub")), P(None, ("dp", "sub"), None)) + trees * 3
    out_specs = (P(), P()) + trees * 3 + trees[:4]
    sizes = {axis: mesh.shape[axis] for axis in ("dp", "sub")}
    return jax.shard_map(
        functools.partial(per_device, sizes),
        mesh=mesh,
        in_specs=in_specs,
        out_specs=out_specs,
        check_vma=False,
    )
```

```python
import functools
import math

import jax
import jax.numpy as jnp
from jax import lax
from jax.experimental import pallas as pl
from jax.experimental.pallas import tpu as pltpu
from jax.sharding import PartitionSpec as P

NBIG = 2
NSMALL = 6
CROPS = NBIG + NSMALL
BIG = 7
SMALL = 3
TAPS = 9
ITERS = 3
LANES = 128

sink_temp = 0.05
softmax_temp = 0.1
norm_eps = 1e-05
unit_eps = 1e-12
trust_rate = 0.5
learn_rate = 1.0
momentum_rate = 0.5
average_rate = 0.5

MESH = pl.DeviceIdType.MESH
MIB = 1 << 20
LOG2E = math.log2(math.e)
SINK2 = LOG2E / sink_temp
SOFT2 = LOG2E / softmax_temp
PAIRS = NBIG * (CROPS - 1)


def cross_rows(left, right):
    return lax.dot_general(
        left, right, (((0,), (0,)), ((), ())), preferred_element_type=jnp.float32
    )


def against(left, right):
    return lax.dot_general(
        left, right, (((1,), (1,)), ((), ())), preferred_element_type=jnp.float32
    )


def greet(axis, count):
    me = lax.axis_index(axis)
    barrier = pltpu.get_barrier_semaphore()
    for hop in range(1, count):
        pl.semaphore_signal(
            barrier, inc=1, device_id={axis: lax.rem(me + hop, count)}, device_id_type=MESH
        )
    pl.semaphore_wait(barrier, count - 1)


class Exchanger:
    def __init__(self, sizes):
        self.sizes = sizes
        self.used = 0

    def next_id(self):
        self.used += 1
        return self.used


class Links:
    def __init__(self, send_sem, recv_sem):
        self.send_sem = send_sem
        self.recv_sem = recv_sem
        self.used = 0

    def __call__(self, source, target, device):
        copy = pltpu.make_async_remote_copy(
            src_ref=source,
            dst_ref=target,
            send_sem=self.send_sem.at[self.used],
            recv_sem=self.recv_sem.at[self.used],
            device_id=device,
            device_id_type=MESH,
        )
        self.used += 1
        copy.start()
        return copy


def wait_all(copies):
    for copy in copies:
        copy.wait()


def lanes_of(index, width=LANES):
    return pl.ds(pl.multiple_of(index * width, LANES), width)


class Place:
    def __init__(self, n_dp):
        self.n_dp = n_dp
        self.span = n_dp // 2
        dp, self.sub = lax.axis_index("dp"), lax.axis_index("sub")
        self.dp = dp
        self.near, self.far = dp // 2, dp % 2
        row, core = self.sub // 2, self.sub % 2
        self.row, self.core = row, core
        self.row_sub = 2 * (1 - row) + core
        self.core_sub = 2 * row + (1 - core)
        self.far_peer = {"dp": self.near * 2 + (1 - self.far)}
        self.row_peer = {"sub": self.row_sub}
        self.core_peer = {"sub": self.core_sub}

    def near_index(self, hop):
        return (self.near + hop) % self.span

    def near_peer(self, hop):
        return {"dp": self.near_index(hop) * 2 + self.far}

    def dp_peers(self):
        return [{"dp": (self.dp + hop) % self.n_dp} for hop in range(1, self.n_dp)]

    def sub_peers(self):
        return [{"sub": (self.sub + hop) % 4} for hop in range(1, 4)]

    def greet(self, peers):
        barrier = pltpu.get_barrier_semaphore()
        for peer in peers:
            pl.semaphore_signal(barrier, inc=1, device_id=peer, device_id_type=MESH)
        pl.semaphore_wait(barrier, len(peers))


ALL = slice(None)


def sigmoid_of(values):
    return 0.5 * jnp.tanh(0.5 * values) + 0.5


def rows_at(start, size):
    return pl.ds(start if isinstance(start, int) else pl.multiple_of(start, 16), size)


def tap_blocks(images, flip):
    moves = [[] for _ in range(TAPS)]
    zeros = [[] for _ in range(TAPS)]
    base = 0
    for extent, lines in ((BIG, NBIG * images), (SMALL, NSMALL * images)):
        for tap in range(TAPS):
            down, right = tap // 3 - 1, tap % 3 - 1
            if flip:
                down, right = -down, -right
            for row in range(extent):
                start = base + row * extent * lines
                if not 0 <= row + down < extent:
                    zeros[tap].append((start, extent * lines))
                    continue
                left, stop = max(0, -right), min(extent, extent - right)
                moves[tap].append(
                    (
                        start + left * lines,
                        base + ((row + down) * extent + left + right) * lines,
                        (stop - left) * lines,
                    )
                )
                if left:
                    zeros[tap].append((start, left * lines))
                if stop < extent:
                    zeros[tap].append((start + stop * lines, (extent - stop) * lines))
        base += extent * extent * lines
    return moves, zeros


def fill_columns(columns, source, images, flip):
    wide = source.shape[1]
    moves, zeros = tap_blocks(images, flip)
    for tap in range(TAPS):
        cols = pl.ds(tap * wide, wide)
        for target, start, size in moves[tap]:
            columns[pl.ds(target, size), cols] = source[pl.ds(start, size), :]
        for target, size in zeros[tap]:
            columns[pl.ds(target, size), cols] = jnp.zeros((size, wide), columns.dtype)


def masked_sums(values, mask, total):
    rows, wide = values.shape
    blocks = values.reshape(rows // 8, 8, wide)
    masked = blocks * mask
    total[0] += jnp.sum(masked, 0)
    total[1] += jnp.sum(masked * blocks, 0)


def row_tile(rows):
    return next(size for size in (192, 160, 128, 96, 64, 48, 32, 24, 16, 8) if rows % size == 0)


def centers_of(proto_ref, centers_ref, turned_ref):
    protos, depth = proto_ref.shape
    part = 256
    for start in range(0, turned_ref.shape[1], part):
        here = max(0, min(part, protos - start))
        values = jnp.zeros((part, depth), jnp.float32)
        if here:
            values = proto_ref[pl.ds(start, here), :]
            values = values * lax.rsqrt(jnp.sum(values * values, 1, keepdims=True) + unit_eps)
        if 0 < here < part:
            values = jnp.concatenate([values, jnp.zeros((part - here, depth), jnp.float32)], 0)
        centers_ref[pl.ds(start, part), :] = values.astype(jnp.bfloat16)
        turned_ref[:, pl.ds(start, part)] = values.T.astype(jnp.bfloat16)


def queue_sums(queue_ref, turned_ref, o_ref, total, view):
    rows, width = queue_ref.shape[1], turned_ref.shape[1]
    tile, part = row_tile(rows), 256
    total[...] = jnp.zeros_like(total)

    def step(index, carry):
        lines = queue_ref[view, pl.ds(index * tile, tile), :]
        for start in range(0, width, part):
            cols = pl.ds(start, part)
            scores = jnp.dot(lines, turned_ref[:, cols], preferred_element_type=jnp.float32)
            shares = jnp.exp2(scores * SINK2)
            total[:, cols] += jnp.sum(shares.reshape(tile // 8, 8, part), 0)
        return carry

    lax.fori_loop(0, rows // tile, step, 0)
    o_ref[pl.ds(view, 1), :] = jnp.sum(total[...], 0, keepdims=True)


class GroupSums:
    def __init__(self, at, links):
        self.at, self.links = at, links

    def start(self, mine, land):
        self.mine, self.land = mine, land
        self.copies = [
            self.links(mine, land.at[hop], peer) for hop, peer in enumerate(self.at.sub_peers())
        ]

    def finish(self):
        wait_all(self.copies)
        value = self.mine[...]
        for hop in range(3):
            value = value + self.land[hop]
        return value


def copy_rows(big, small, target, sem):
    split = big.shape[0]
    copies = [
        pltpu.make_async_copy(big, target.at[pl.ds(0, split)], sem.at[0]),
        pltpu.make_async_copy(small, target.at[pl.ds(split, small.shape[0])], sem.at[1]),
    ]
    for copy in copies:
        copy.start()
    return copies


def weigh(target, line, values):
    sums = jnp.sum(values * values, 0, keepdims=True)
    for lane in range(0, sums.shape[1], LANES):
        target[pl.ds(line, 1), :] += sums[:, lane : lane + LANES]


def forward_kernel(n_dp, images, *refs):
    i_outer, i_mid, i_hid, i_out, h_big, h_small, norm_ref, live_ref, queue_ref, proto_ref = refs[:10]
    (
        o_mid, o_last, o_hid, o_out, o_one, o_two, o_act, o_curve, o_normal, o_stat, o_pooled, o_live,
        o_slope, o_weigh, o_centers, o_turned, o_queue,
    ) = refs[10:27]
    (
        x_ref, w_first, w_mid, w_last, w_hid, w_out, first_w, mid_w, last_w, out_w, columns, act_one,
        act_two, one, two, three, total, pool, sums_a, land_a, sums_b, land_b, sums_c, land_c, pooled,
        queue_total, send_sem, recv_sem, own_sem, x_sem,
    ) = refs[27:]
    at = Place(n_dp)
    links = Links(send_sem, recv_sem)
    x_copies = copy_rows(h_big, h_small, x_ref, x_sem)
    share = w_hid.shape[1]
    w_first[...] = i_outer[0].astype(w_first.dtype)
    at.greet(
        [at.near_peer(hop) for hop in range(1, at.span)] + [at.far_peer] + at.sub_peers()
    )
    low = jnp.bfloat16
    middle = first_w.shape[3]
    channels = x_ref.shape[1]
    rows = x_ref.shape[0]
    mask = live_ref[...][:, :1]
    half = middle // 2

    def flat(source, target, start, size, split):
        line = source.shape[0] // 4
        some = pl.ds(start * line, size * line)
        return (
            lambda cols: source.at[some, cols],
            lambda near, far, cols: target.at[near, far, some, cols],
            split,
        )

    def taps(start, size, split):
        some = pl.ds(start, size)
        return (
            lambda cols: w_mid.at[some, :, cols],
            lambda near, far, cols: mid_w.at[some, near, far, :, cols],
            split,
        )

    quarter = w_out.shape[0] // 4
    out_rows = pl.ds(at.sub * quarter, quarter)
    pieces = [flat(w_first, first_w, 0, 2, 4), flat(w_first, first_w, 2, 2, 4)]
    groups = (((0, 1, 2), (1, 2, 4)), ((3, 1, 4), (4, 1, 2), (5, 2, 4)), ((7, 1, 4), (8, 1, 2)))
    last_of = []
    for group in groups:
        pieces += [taps(*some) for some in group]
        last_of.append(len(pieces))
    pieces += [flat(w_last, last_w, 0, 2, 4), flat(w_last, last_w, 2, 1, 2), flat(w_last, last_w, 3, 1, 4)]
    trunk_pieces = len(pieces)
    pieces += [flat(w_hid, o_hid, part, 1, 1) for part in range(4)]
    pieces.append(
        (
            lambda cols: w_out.at[out_rows],
            lambda near, far, cols: out_w.at[near, far],
            1,
        )
    )
    count = len(pieces)
    mine = {4: lanes_of(at.sub), 2: lanes_of(at.core, half), 1: ALL}
    own, first, second, third, fourth = [], [], [], [], []

    def begin(index):
        if index < count:
            source, target, split = pieces[index]
            cols = mine[split]
            copy = pltpu.make_async_copy(
                source(cols), target(at.near, at.far, cols), own_sem.at[index]
            )
            copy.start()
            own.append(copy)
            first.append(
                [
                    links(source(cols), target(at.near, at.far, cols), at.near_peer(hop))
                    for hop in range(1, at.span)
                ]
            )

    begin(0)
    begin(1)

    def cast_tap(index, carry):
        w_mid[index] = i_mid[index].astype(w_mid.dtype)
        return carry

    lax.fori_loop(0, TAPS, cast_tap, 0)
    begin(2)
    w_last[...] = i_outer[1].astype(w_last.dtype)
    w_hid[...] = i_hid[:, lanes_of(at.sub, share)].astype(w_hid.dtype)
    w_out[...] = i_out[...].astype(w_out.dtype)
    lag = 2
    clock = [0]

    def pump(times=1):
        for _ in range(times):
            tick(clock[0])
            clock[0] += 1

    def need(index):
        while clock[0] <= index + 2 * lag:
            pump()
        wait_all(fourth[index])

    def tick(now):
        if now < count:
            source, target, split = pieces[now]
            own[now].wait()
            wait_all(first[now])
            begin(now + 3)
            slab = target(ALL, at.far, mine[split])
            second.append(links(slab, slab, at.far_peer))
        past = now - lag
        if 0 <= past < count:
            source, target, split = pieces[past]
            second[past].wait()
            slab = target(ALL, ALL, mine[split])
            third.append(links(slab, slab, at.row_peer) if split == 4 else None)
            fourth.append([links(slab, slab, at.core_peer)] if split == 2 else [])
        past = now - 2 * lag
        if 0 <= past < count and pieces[past][2] == 4:
            source, target, split = pieces[past]
            third[past].wait()
            slabs = [target(ALL, ALL, cols) for cols in (mine[4], lanes_of(at.row_sub))]
            fourth[past] = [links(slab, slab, at.core_peer) for slab in slabs]

    tile = rows // 4
    sums = GroupSums(at, links)

    def pack(target, wide):
        target[pl.ds(0, 1), :] = jnp.sum(total[0, :, :wide], 0, keepdims=True)
        target[pl.ds(1, 1), :] = jnp.sum(total[1, :, :wide], 0, keepdims=True)

    def settle(value, count_all, start, wide):
        mean = value[0:1] / count_all
        inverse = lax.rsqrt(value[1:2] / count_all - mean * mean + norm_eps)
        o_stat[pl.ds(0, 1), pl.ds(start, wide)] = mean
        o_stat[pl.ds(1, 1), pl.ds(start, wide)] = inverse
        scale = norm_ref[pl.ds(0, 1), pl.ds(start, wide)] * inverse
        return scale, norm_ref[pl.ds(1, 1), pl.ds(start, wide)] - scale * mean

    centers_of(proto_ref, o_centers, o_turned)
    pump()
    queue_sums(queue_ref, o_turned, o_queue, queue_total, 0)
    pump()
    queue_sums(queue_ref, o_turned, o_queue, queue_total, 1)
    pump()
    o_weigh[...] = jnp.zeros_like(o_weigh)
    weigh(o_weigh, 0, i_outer[0])
    weigh(o_weigh, 1, i_outer[1])
    weigh(o_weigh, 4, i_out[...])

    def weigh_tap(index, carry):
        weigh(o_weigh, 2, i_mid[index])
        return carry

    lax.fori_loop(0, TAPS, weigh_tap, 0)
    pump()

    def weigh_part(index, carry):
        weigh(o_weigh, 3, i_hid[:, lanes_of(index, 512)])
        return carry

    lax.fori_loop(0, i_hid.shape[1] // 512, weigh_part, 0)
    need(0)
    need(1)
    pump()
    for copy in x_copies:
        copy.wait()

    total[...] = jnp.zeros_like(total)

    def step_one(index, carry):
        span = rows_at(index * tile, tile)
        value = jnp.dot(
            x_ref[span, :],
            first_w[...].reshape(channels, middle),
            preferred_element_type=jnp.float32,
        )
        one[span, :] = value
        masked_sums(value, mask, total.at[:, :, pl.ds(0, middle)])
        return carry

    lax.fori_loop(0, 4, step_one, 0)
    pack(sums_a, middle)
    live = jnp.sum(mask, 0, keepdims=True)
    sums_a[pl.ds(2, 1), :] = jnp.broadcast_to(live, (1, middle))
    sums.start(sums_a, land_a)
    pump()
    value = sums.finish()
    per_image = rows // images
    lives = value[2:3, :1]
    count_all = lives * per_image
    o_live[at.sub] = jnp.broadcast_to(live, o_live.shape[1:])
    for hop in range(3):
        o_live[(at.sub + 3 - hop) % 4] = jnp.broadcast_to(land_a[hop, 2:3, :1], o_live.shape[1:])
    scale, shift = settle(value, count_all, 0, middle)

    def step_act(source, target):
        def step(index, carry):
            span = rows_at(index * tile, tile)
            pre = source[span, :] * scale + shift
            target[span, :] = (pre * sigmoid_of(pre)).astype(low)
            return carry

        lax.fori_loop(0, 4, step, 0)

    step_act(one, act_one)
    save = [pltpu.make_async_copy(one, o_one, own_sem.at[count])]
    save[-1].start()
    pump()
    fill_columns(columns, act_one, images, False)

    total[...] = jnp.zeros_like(total)
    for part in range(3):
        for index in range(last_of[part] - len(groups[part]), last_of[part]):
            need(index)

        def step_two(index, carry):
            span = rows_at(index * tile, tile)
            value = jnp.dot(
                columns[span, pl.ds(part * 3 * middle, 3 * middle)],
                mid_w[pl.ds(part * 3, 3)].reshape(3 * middle, middle),
                preferred_element_type=jnp.float32,
            )
            if part:
                value = value + two[span, :]
            two[span, :] = value
            if part == 2:
                masked_sums(value, mask, total.at[:, :, pl.ds(0, middle)])
            return carry

        lax.fori_loop(0, 4, step_two, 0)
    save.append(pltpu.make_async_copy(mid_w, o_mid, own_sem.at[count + 2]))
    save[-1].start()
    pack(sums_b, middle)
    sums.start(sums_b, land_b)
    scale, shift = settle(sums.finish(), count_all, middle, middle)
    step_act(two, act_two)
    save.append(pltpu.make_async_copy(two, o_two, own_sem.at[count + 3]))
    save[-1].start()
    save.append(pltpu.make_async_copy(act_two, o_act, own_sem.at[count + 4]))
    save[-1].start()

    for index in range(trunk_pieces - 3, trunk_pieces):
        need(index)
    save.append(pltpu.make_async_copy(last_w, o_last, own_sem.at[count + 5]))
    save[-1].start()
    total[...] = jnp.zeros_like(total)

    def step_three(index, carry):
        span = rows_at(index * tile, tile)
        for quarter in range(4):
            wide = channels // 4
            cols = pl.ds(quarter * wide, wide)
            weights = last_w[pl.ds(quarter * (at.span // 4), at.span // 4)].reshape(wide, middle)
            value = against(act_two[span, :], weights)
            three[span, cols] = value
            masked_sums(value, mask, total.at[:, :, cols])
        return carry

    lax.fori_loop(0, 4, step_three, 0)
    pack(sums_c, channels)
    sums.start(sums_c, land_c)
    pump()
    scale, shift = settle(sums.finish(), count_all, 2 * middle, channels)

    pool[...] = jnp.zeros_like(pool)
    o_slope[...] = jnp.zeros_like(o_slope)
    wide = pl.ds(2 * middle, channels)
    center = o_stat[pl.ds(0, 1), wide] * o_stat[pl.ds(1, 1), wide]
    base = 0
    for extent, crops in ((BIG, NBIG), (SMALL, NSMALL)):
        lines = crops * images
        into = pl.ds(0, lines) if extent == BIG else pl.ds(NBIG * images, lines)

        def step_out(index, carry):
            span = rows_at(base + index * extent * lines, extent * lines)
            for start in range(0, channels, 512):
                cols = pl.ds(start, 512)
                pre = three[span, cols] * scale[:, start : start + 512]
                pre = pre + shift[:, start : start + 512] + x_ref[span, cols].astype(jnp.float32)
                sigma = sigmoid_of(pre)
                value = pre * sigma
                slope = sigma + value * (1.0 - sigma)
                normal = three[span, cols] * o_stat[1:2, 2 * middle + start : 2 * middle + start + 512]
                normal = normal - center[:, start : start + 512]
                columns[span, cols] = slope.astype(low)
                columns[span, pl.ds(channels + start, 512)] = normal.astype(low)
                pool[into, cols] += jnp.sum(value.reshape(extent, lines, 512), 0)
                o_slope[0, into, cols] += jnp.sum(slope.reshape(extent, lines, 512), 0)
                slope = slope * normal
                o_slope[1, into, cols] += jnp.sum(slope.reshape(extent, lines, 512), 0)
            return carry

        lax.fori_loop(0, extent, step_out, 0)
        pump()
        pooled[into, :] = (pool[into, :] * (1.0 / (extent * extent))).astype(low)
        base += extent * extent * lines

    for index, target in enumerate((o_curve, o_normal)):
        some = columns.at[:, pl.ds(index * channels, channels)]
        save.append(pltpu.make_async_copy(some, target, x_sem.at[index]))
        save[-1].start()

    over = links(pooled, o_pooled.at[at.sub], at.row_peer)
    pair = links(pooled, o_pooled.at[at.sub], at.core_peer)
    o_pooled[at.sub] = pooled[...]
    pump()
    over.wait()
    last = links(o_pooled.at[at.row_sub], o_pooled.at[at.row_sub], at.core_peer)
    need(count - 1)
    some = at.span // 4
    out_own = out_w.at[pl.ds(at.sub * some, some)]
    into = o_out.at[:, :, out_rows]
    own.append(pltpu.make_async_copy(out_own, into, own_sem.at[count - 1]))
    own[-1].start()
    out_copies = [
        links(out_w.at[pl.ds(peer["sub"] * some, some)], into, peer) for peer in at.sub_peers()
    ]
    pair.wait()
    last.wait()
    own[-1].wait()
    wait_all(out_copies)
    for copy in save:
        copy.wait()


def forward_trunk(
    n_dp, collective_id, images, outer, mid, hid, out, big, small, norms, live, queue, prototypes, width
):
    span = n_dp // 2
    height, middle = outer.shape[1:]
    rows, channels = big.shape[0] + small.shape[0], big.shape[1]
    share, narrow = hid.shape[1] // 4, out.shape[1]
    some = jax.ShapeDtypeStruct
    low, full = jnp.bfloat16, jnp.float32
    copies = 17 * (span + 4) + 16
    vmem, anywhere = pl.BlockSpec(memory_space=pltpu.VMEM), pl.BlockSpec(memory_space=pl.ANY)
    return pl.pallas_call(
        functools.partial(forward_kernel, n_dp, images),
        out_shape=(
            some((TAPS, span, 2, mid.shape[1], middle), low),
            some((span, 2, height, middle), low),
            some((span, 2, height, share), low),
            some((span // 4, 2, height, narrow), low),
            some((rows, middle), full),
            some((rows, middle), full),
            some((rows, middle), low),
            some((rows, channels), low),
            some((rows, channels), low),
            some((2, 2 * middle + channels), full),
            some((4, CROPS * images, channels), low),
            some((4, 8, LANES), full),
            some((2, CROPS * images, channels), full),
            some((8, LANES), full),
            some((width, prototypes.shape[1]), low),
            some((prototypes.shape[1], width), low),
            some((queue.shape[0], width), full),
        ),
        in_specs=[vmem] * 4 + [anywhere] * 2 + [vmem] * 4,
        out_specs=(anywhere,) * 9 + (vmem,) * 8,
        scratch_shapes=[
            pltpu.VMEM((rows, channels), low),
            pltpu.VMEM((height, middle), low),
            pltpu.VMEM(mid.shape, low),
            pltpu.VMEM((height, middle), low),
            pltpu.VMEM((height, share), low),
            pltpu.VMEM((height, narrow), low),
            pltpu.VMEM((span, 2, height, middle), low),
            pltpu.VMEM((TAPS, span, 2, mid.shape[1], middle), low),
            pltpu.VMEM((span, 2, height, middle), low),
            pltpu.VMEM((span, 2, height // 4, narrow), low),
            pltpu.VMEM((rows, TAPS * middle), low),
            pltpu.VMEM((rows, middle), low),
            pltpu.VMEM((rows, middle), low),
            pltpu.VMEM((rows, middle), full),
            pltpu.VMEM((rows, middle), full),
            pltpu.VMEM((rows, channels), full),
            pltpu.VMEM((2, 8, channels), full),
            pltpu.VMEM((CROPS * images, channels), full),
            pltpu.VMEM((3, middle), full),
            pltpu.VMEM((3, 3, middle), full),
            pltpu.VMEM((2, middle), full),
            pltpu.VMEM((3, 2, middle), full),
            pltpu.VMEM((2, channels), full),
            pltpu.VMEM((3, 2, channels), full),
            pltpu.VMEM((CROPS * images, channels), low),
            pltpu.VMEM((8, width), full),
            pltpu.SemaphoreType.DMA((copies,)),
            pltpu.SemaphoreType.DMA((copies,)),
            pltpu.SemaphoreType.DMA((17 + 6,)),
            pltpu.SemaphoreType.DMA((2,)),
        ],
        compiler_params=pltpu.CompilerParams(
            collective_id=collective_id, has_side_effects=True, vmem_limit_bytes=62 * MIB
        ),
        name="forward_trunk",
    )(outer, mid, hid, out, big, small, norms, live, queue, prototypes)


def plus(left, right):
    return left.astype(jnp.float32) + right.astype(jnp.float32)


def piece_list(n_dp, height, mid_height, refs):
    first, mid, last = refs
    half, quarter = height // 2, height // 4
    pieces = [last + (0, 1, part * half, half, 2) for part in range(2)]
    for start, taps in ((0, 1), (1, 1), (2, 1), (3, 1), (4, 1), (5, 1), (6, 1), (7, 2)):
        pieces.append(mid + (start, taps, 0, mid_height, 1))
    return pieces + [first + (0, 1, part * quarter, quarter, 0) for part in range(4)]


def backward_kernel(n_dp, images, *refs):
    p_pool, slope_ref, stat_ref, norm_ref, live_ref, lives_ref, extra_ref, g_hid, g_some = refs[:9]
    h_big, h_small, h_curve, h_normal, h_one, h_two, h_act, h_last, h_mid = refs[9:18]
    o_first, o_mid, o_last, o_hid, o_out, o_vec, o_sq = refs[18:25]
    (
        x_ref, one, two, act_two, last_w, mid_w, act_one, wide_low, work, thin_low, g_first, g_mid,
        g_last, total, pair_land, pair_sum, row_land, grad_pool, sums_a, land_a, sums_b, land_b,
        sums_c, land_c, hid_in, hid_sum, hid_land, g_out, out_in, out_sum, out_land, vec, vec_land,
        sq_mine, sq_land, send_sem, recv_sem, own_sem, x_sem,
    ) = refs[25:64]
    bufs = refs[64:]
    at = Place(n_dp)
    links = Links(send_sem, recv_sem)
    span = at.span
    at.greet(at.dp_peers() + at.sub_peers())
    low = jnp.bfloat16
    rows, channels = x_ref.shape
    middle = one.shape[1]
    height = g_last.shape[3]
    mask = live_ref[...][:, :1]
    tile = rows // 4

    loads = {}
    for index, (name, source, target) in enumerate(
        (
            ("one", h_one, one), ("curve", h_curve, wide_low), ("normal", h_normal, x_ref),
            ("last", h_last, last_w), ("two", h_two, two), ("act", h_act, act_two), ("mid", h_mid, mid_w),
        )
    ):
        loads[name] = pltpu.make_async_copy(source, target, own_sem.at[index])
        loads[name].start()

    pair = [
        links(p_pool.at[2 * line + (1 - at.core)], pair_land.at[line], at.core_peer)
        for line in (1 - at.row, at.row)
    ]
    far_copies = [links(g_hid.at[:, 1 - at.far], hid_in, at.far_peer)]
    some = g_some.shape[0]
    block = g_out.at[pl.ds(at.sub * some, some)]
    own_out = pltpu.make_async_copy(g_some, block, own_sem.at[7])
    own_out.start()
    out_copies = [links(g_some, block, peer) for peer in at.sub_peers()]
    pair[0].wait()
    pair_sum[...] = plus(p_pool[2 * (1 - at.row) + at.core], pair_land[1 - at.row]).astype(low)
    over = links(pair_sum, row_land, at.row_peer)
    pair[1].wait()

    wholes = [(g_hid, hid_in, hid_sum, hid_land), (g_out, out_in, out_sum, out_land)]

    def whole_far(which):
        source, landed, summed, land = wholes[which]
        far_copies[which].wait()
        for near in range(span):
            summed[near] = plus(source[near, at.far], landed[near]).astype(low)
        return [
            links(summed.at[at.near_index(hop)], land.at[hop - 1], at.near_peer(hop))
            for hop in range(1, span)
        ]

    def whole_near(which, copies):
        source, landed, summed, land = wholes[which]
        wait_all(copies)
        value = summed[at.near].astype(jnp.float32)
        for hop in range(1, span):
            value = value + land[hop - 1].astype(jnp.float32)
        return value.astype(low)

    sq_mine[0] = jnp.zeros_like(sq_mine[0])

    def squares_of(matrix, value):
        value = value.astype(jnp.float32)
        line = jnp.sum(value * value, 0, keepdims=True)
        for lane in range(0, line.shape[1], LANES):
            sq_mine[0, pl.ds(matrix, 1), :] += line[:, lane : lane + LANES]

    pieces = piece_list(
        n_dp, height, g_mid.shape[3], ((g_first, o_first), (g_mid, o_mid), (g_last, o_last))
    )
    mine, beside = lanes_of(at.sub), lanes_of(at.row_sub)
    state = [0] * len(pieces)
    flight = [None] * len(pieces)

    def loop(count, body):
        def step(index, carry):
            body(index)
            return carry

        lax.fori_loop(0, count, step, 0)

    def go(index):
        source, target, start, taps, line, size, matrix = pieces[index]
        held, second, third, nears = bufs[4 * index : 4 * index + 4]
        stage = state[index]
        state[index] += 1
        row_first = index % 2 == 0
        lines, some = pl.ds(line, size), pl.ds(start, taps)
        if stage == 0:
            flight[index] = [
                links(
                    source.at[some, :, :, lines, lanes_of(2 * row + (1 - at.core))],
                    held.at[row],
                    at.core_peer,
                )
                for row in range(2)
            ]
            return
        wait_all(flight[index])
        if stage == 1:
            for row in range(2):
                cols = lanes_of(2 * row + at.core)

                def body(at_block):
                    tap, near, far = at_block // (2 * span), at_block // 2 % span, at_block % 2
                    held[row, tap, near, far] = plus(
                        source[start + tap, near, far, lines, cols], held[row, tap, near, far]
                    ).astype(low)

                loop(taps * span * 2, body)
            if row_first:
                flight[index] = [links(held.at[1 - at.row], second, at.row_peer)]
            else:
                flight[index] = [links(held.at[:, :, :, 1 - at.far], second, at.far_peer)]
        elif stage == 2:
            if row_first:

                def body(at_block):
                    tap, near, far = at_block // (2 * span), at_block // 2 % span, at_block % 2
                    second[tap, near, far] = plus(
                        held[at.row, tap, near, far], second[tap, near, far]
                    ).astype(low)

                loop(taps * span * 2, body)
                flight[index] = [links(second.at[:, :, 1 - at.far], third, at.far_peer)]
            else:

                def body(at_block):
                    row, tap, near = at_block // (taps * span), at_block // span % taps, at_block % span
                    second[row, tap, near] = plus(
                        held[row, tap, near, at.far], second[row, tap, near]
                    ).astype(low)

                loop(taps * span * 2, body)
                flight[index] = [links(second.at[1 - at.row], third, at.row_peer)]
        elif stage == 3:

            def body(at_block):
                tap, near = at_block // span, at_block % span
                part = second[tap, near, at.far] if row_first else second[at.row, tap, near]
                third[tap, near] = plus(part, third[tap, near]).astype(low)

            loop(taps * span, body)
            flight[index] = [
                links(third.at[:, at.near_index(hop)], nears.at[hop - 1], at.near_peer(hop))
                for hop in range(1, span)
            ]
        elif stage == 4:
            for tap in range(taps):
                value = third[tap, at.near].astype(jnp.float32)
                for hop in range(1, span):
                    value = value + nears[hop - 1, tap].astype(jnp.float32)
                value = value.astype(low)
                squares_of(matrix, value)
                target[start + tap, lines, mine] = value
            slab = target.at[some, lines, mine]
            flight[index] = [links(slab, slab, at.row_peer)]
        elif stage == 5:
            slabs = [target.at[some, lines, cols] for cols in (mine, beside)]
            flight[index] = [links(slab, slab, at.core_peer) for slab in slabs]

    def go_pair(number):
        go(2 * number)
        go(2 * number + 1)

    count_all = jnp.sum(lives_ref[...][:, :1, :1], 0) * float(rows // images)
    sums = GroupSums(at, links)

    def terms(start, wide):
        cols = pl.ds(start, wide)
        mean, inverse = stat_ref[pl.ds(0, 1), cols], stat_ref[pl.ds(1, 1), cols]
        scale = norm_ref[pl.ds(0, 1), cols] * inverse
        return mean * inverse, inverse, scale, norm_ref[pl.ds(1, 1), cols] - scale * mean

    def slope_of(pre):
        sigma = sigmoid_of(pre)
        return sigma + pre * sigma * (1.0 - sigma)

    def pack(target, wide):
        target[pl.ds(0, 1), :] = jnp.sum(total[0, :, :wide], 0, keepdims=True)
        target[pl.ds(1, 1), :] = jnp.sum(total[1, :, :wide], 0, keepdims=True)

    center_one, inverse_one, scale_one, shift_one = terms(0, middle)
    center_two, inverse_two, scale_two, shift_two = terms(middle, middle)
    scale_three = terms(2 * middle, channels)[2]
    loads["one"].wait()

    def step_act(index):
        span_rows = rows_at(index * tile, tile)
        pre = one[span_rows, :] * scale_one + shift_one
        act_one[span_rows, :] = (pre * sigmoid_of(pre)).astype(low)

    loop(4, step_act)
    own_out.wait()
    wait_all(out_copies)
    far_copies.append(links(g_out.at[:, 1 - at.far], out_in, at.far_peer))
    value = plus(p_pool[at.sub], pair_land[at.row])
    over.wait()
    value = value + row_land[...].astype(jnp.float32)
    big = NBIG * images
    grad_pool[pl.ds(0, big), :] = value[:big] * (1.0 / (BIG * BIG))
    grad_pool[pl.ds(big, NSMALL * images), :] = value[big:] * (1.0 / (SMALL * SMALL))
    for which in range(2):
        sums_c[pl.ds(which, 1), :] = jnp.sum(grad_pool[...] * slope_ref[which], 0, keepdims=True)
    sums.start(sums_c, land_c)
    loads["curve"].wait()
    loads["normal"].wait()
    both_three = sums.finish()
    vec[...] = extra_ref[...]
    vec[pl.ds(1, 1), :] = both_three[1:2]
    vec[pl.ds(3, 1), :] = both_three[0:1]
    both_three = both_three / count_all

    chunk = channels // 4
    for quarter in range(4):
        cols = pl.ds(quarter * chunk, chunk)
        here = slice(quarter * chunk, (quarter + 1) * chunk)
        base = 0
        for extent, crops in ((BIG, NBIG), (SMALL, NSMALL)):
            lines = crops * images
            into = pl.ds(0, lines) if extent == BIG else pl.ds(big, lines)

            def step_grad(index):
                span_rows = rows_at(base + index * extent * lines, extent * lines)
                curve = wide_low[span_rows, cols].astype(jnp.float32)
                grad = curve.reshape(extent, lines, chunk) * grad_pool[into, cols]
                normal = x_ref[span_rows, cols].astype(jnp.float32)
                back = both_three[0:1, here] + normal * both_three[1:2, here]
                back = back.reshape(extent * crops, images, chunk) * mask
                grad = grad.reshape(extent * crops, images, chunk) - back
                grad = grad.reshape(extent * lines, chunk) * scale_three[:, here]
                wide_low[span_rows, cols] = grad.astype(low)

            loop(extent, step_grad)
            base += extent * extent * lines
    x_copies = copy_rows(h_big, h_small, x_ref, x_sem)
    loads["last"].wait()

    near_hid, near_out = whole_far(0), whole_far(1)

    def norm_sums(grad, normal):
        total[0, :, :middle] += jnp.sum(grad.reshape(tile // 8, 8, middle), 0)
        total[1, :, :middle] += jnp.sum((grad * normal).reshape(tile // 8, 8, middle), 0)

    loads["two"].wait()
    loads["act"].wait()
    total[...] = jnp.zeros_like(total)

    def step_two(index):
        span_rows = rows_at(index * tile, tile)
        grad = jnp.dot(
            wide_low[span_rows, :],
            last_w[...].reshape(channels, middle),
            preferred_element_type=jnp.float32,
        )
        grad = grad * slope_of(two[span_rows, :] * scale_two + shift_two)
        work[span_rows, :] = grad
        norm_sums(grad, two[span_rows, :] * inverse_two - center_two)

    loop(4, step_two)
    pack(sums_a, middle)
    sums.start(sums_a, land_a)

    def weight_rows(target, left, right):
        part = 256
        shards = max(1, part // height)
        for index in range(channels // part):
            value = cross_rows(left[:, pl.ds(index * part, part)], right[...]).astype(low)
            if shards == 1:
                target[0, index // 2, index % 2] = value
            else:
                some = pl.ds(index * (shards // 2), shards // 2)
                target[0, some] = value.reshape(shards // 2, 2, height, middle)

    weight_rows(g_last, wide_low, act_two)
    go_pair(0)

    def settle_grad(source, center, inverse, scale, both):
        def step(index):
            span_rows = rows_at(index * tile, tile)
            normal = source[span_rows, :] * inverse - center
            back = both[0:1] + normal * both[1:2]
            back = (back.reshape(tile // 8, 8, middle) * mask).reshape(tile, middle)
            thin_low[span_rows, :] = ((work[span_rows, :] - back) * scale).astype(low)

        loop(4, step)

    both_two = sums.finish()
    settle_grad(two, center_two, inverse_two, scale_two, both_two / count_all)
    vec[pl.ds(0, 1), pl.ds(middle, middle)] = both_two[1:2]
    vec[pl.ds(0, 1), pl.ds(3 * middle, middle)] = both_two[0:1]
    go_pair(0)

    loads["mid"].wait()
    moves, zeros = tap_blocks(images, True)
    total[...] = jnp.zeros_like(total)
    for part in range(3):
        for slot in range(3):
            cols = pl.ds(slot * middle, middle)
            for target, start, size in moves[3 * part + slot]:
                wide_low[pl.ds(target, size), cols] = thin_low[pl.ds(start, size), :]
            for target, size in zeros[3 * part + slot]:
                wide_low[pl.ds(target, size), cols] = jnp.zeros((size, middle), low)

        for slot in range(3):
            value = cross_rows(act_one[...], wide_low[:, pl.ds(slot * middle, middle)]).astype(low)
            g_mid[3 * part + slot] = value.reshape(g_mid.shape[1:])
        for number in ((1,), (2, 3), (4,))[part]:
            go_pair(number)

        def step_one(index):
            span_rows = rows_at(index * tile, tile)
            grad = against(
                wide_low[span_rows, pl.ds(0, middle)], mid_w[3 * part].reshape(middle, middle)
            )
            for slot in range(1, 3):
                grad = grad + against(
                    wide_low[span_rows, pl.ds(slot * middle, middle)],
                    mid_w[3 * part + slot].reshape(middle, middle),
                )
            if part:
                grad = grad + work[span_rows, :]
            if part == 2:
                grad = grad * slope_of(one[span_rows, :] * scale_one + shift_one)
                norm_sums(grad, one[span_rows, :] * inverse_one - center_one)
            work[span_rows, :] = grad

        loop(4, step_one)
        if part == 2:
            pack(sums_b, middle)
            sums.start(sums_b, land_b)
        for number in ((0, 1), (0, 1, 2, 3), (0, 1, 2, 3, 4))[part]:
            go_pair(number)
    value = whole_near(0, near_hid)
    wide = g_hid.shape[3]
    squares_of(3, value)
    slabs = [o_hid.at[:, lanes_of(which, wide)] for which in (at.sub, at.row_sub)]
    o_hid[:, lanes_of(at.sub, wide)] = value
    hid_row = links(slabs[0], slabs[0], at.row_peer)
    value = whole_near(1, near_out)
    squares_of(4, value)
    o_out[...] = value

    both_one = sums.finish()
    settle_grad(one, center_one, inverse_one, scale_one, both_one / count_all)
    vec[pl.ds(0, 1), pl.ds(0, middle)] = both_one[1:2]
    vec[pl.ds(0, 1), pl.ds(2 * middle, middle)] = both_one[0:1]
    wide = vec.shape[1] // 4
    vec_cols = lanes_of(at.sub, wide)
    vec_copies = [
        links(vec.at[:, vec_cols], vec_land.at[hop], peer)
        for hop, peer in enumerate(at.dp_peers())
    ]
    for number in range(1, 5):
        go_pair(number)
    hid_row.wait()
    final = [links(slab, slab, at.core_peer) for slab in slabs]

    for copy in x_copies:
        copy.wait()
    weight_rows(g_first, x_ref, thin_low)
    go_pair(5)
    go_pair(6)

    numbers = range(len(pieces) // 2)
    tick = 0
    sent = False
    while min(state) < 6:
        for number in numbers:
            if state[2 * number] < 6:
                go_pair(number)
        if tick == 1:
            wait_all(vec_copies)
            value = vec[:, vec_cols]
            for hop in range(n_dp - 1):
                value = value + vec_land[hop]
            o_vec[:, vec_cols] = value
            vec_final = [
                links(o_vec.at[:, vec_cols], o_vec.at[:, vec_cols], peer)
                for peer in at.sub_peers()
            ]
        if not sent and min(state) >= 5:
            sent = True
            sq_copies = [
                links(sq_mine.at[0], sq_land.at[hop], peer)
                for hop, peer in enumerate(at.dp_peers())
            ]
        tick += 1
    wait_all(sq_copies)
    value = sq_mine[0]
    for hop in range(n_dp - 1):
        value = value + sq_land[hop]
    sq_mine[1] = value
    sq_copies = [
        links(sq_mine.at[1], sq_land.at[n_dp - 1 + hop], peer)
        for hop, peer in enumerate(at.sub_peers())
    ]
    wait_all(sq_copies)
    for hop in range(3):
        value = value + sq_land[n_dp - 1 + hop]
    o_sq[...] = value
    for copies in flight:
        wait_all(copies)
    wait_all(final)
    wait_all(vec_final)


def backward_trunk(
    n_dp, collective_id, images, pooled, slopes, stat, norms, live, lives, extra, hid, out, big, small,
    curve, normal, one, two, act, last, mid,
):
    span = n_dp // 2
    low, full = jnp.bfloat16, jnp.float32
    rows, channels = curve.shape
    middle = one.shape[1]
    height, mid_height = last.shape[2], mid.shape[3]
    narrow = out.shape[1]
    crops = CROPS * images
    some = jax.ShapeDtypeStruct
    bufs = []
    for index, piece in enumerate(piece_list(n_dp, height, mid_height, ((0, 0),) * 3)):
        taps, block = piece[3], (piece[5], LANES)
        bufs.append(pltpu.VMEM((2, taps, span, 2) + block, low))
        if index % 2 == 0:
            bufs.append(pltpu.VMEM((taps, span, 2) + block, low))
        else:
            bufs.append(pltpu.VMEM((2, taps, span) + block, low))
        bufs.append(pltpu.VMEM((taps, span) + block, low))
        bufs.append(pltpu.VMEM((span - 1, taps) + block, low))
    copies = 14 * (span + 6) + 2 * (span + 4) + 2 * n_dp + 40
    vmem, anywhere = pl.BlockSpec(memory_space=pltpu.VMEM), pl.BlockSpec(memory_space=pl.ANY)
    return pl.pallas_call(
        functools.partial(backward_kernel, n_dp, images),
        out_shape=(
            some((1, height, middle), low),
            some((TAPS, mid_height, middle), low),
            some((1, height, middle), low),
            some((height, 4 * hid.shape[1]), low),
            some((height, narrow), low),
            some(extra.shape, full),
            some((8, LANES), full),
        ),
        in_specs=[vmem] * 9 + [anywhere] * 9,
        out_specs=(vmem,) * 7,
        scratch_shapes=[
            pltpu.VMEM((rows, channels), low),
            pltpu.VMEM((rows, middle), full),
            pltpu.VMEM((rows, middle), full),
            pltpu.VMEM((rows, middle), low),
            pltpu.VMEM((span, 2, height, middle), low),
            pltpu.VMEM((TAPS, span, 2, mid_height, middle), low),
            pltpu.VMEM((rows, middle), low),
            pltpu.VMEM((rows, channels), low),
            pltpu.VMEM((rows, middle), full),
            pltpu.VMEM((rows, middle), low),
            pltpu.VMEM((1, span, 2, height, middle), low),
            pltpu.VMEM((TAPS, span, 2, mid_height, middle), low),
            pltpu.VMEM((1, span, 2, height, middle), low),
            pltpu.VMEM((2, 8, middle), full),
            pltpu.VMEM((2, crops, channels), low),
            pltpu.VMEM((crops, channels), low),
            pltpu.VMEM((crops, channels), low),
            pltpu.VMEM((crops, channels), full),
            pltpu.VMEM((2, middle), full),
            pltpu.VMEM((3, 2, middle), full),
            pltpu.VMEM((2, middle), full),
            pltpu.VMEM((3, 2, middle), full),
            pltpu.VMEM((2, channels), full),
            pltpu.VMEM((3, 2, channels), full),
            pltpu.VMEM((span, height, hid.shape[1]), low),
            pltpu.VMEM((span, height, hid.shape[1]), low),
            pltpu.VMEM((span - 1, height, hid.shape[1]), low),
            pltpu.VMEM((span, 2, height, narrow), low),
            pltpu.VMEM((span, height, narrow), low),
            pltpu.VMEM((span, height, narrow), low),
            pltpu.VMEM((span - 1, height, narrow), low),
            pltpu.VMEM(extra.shape, full),
            pltpu.VMEM((n_dp - 1, extra.shape[0], extra.shape[1] // 4), full),
            pltpu.VMEM((2, 8, LANES), full),
            pltpu.VMEM((n_dp + 2, 8, LANES), full),
            pltpu.SemaphoreType.DMA((copies,)),
            pltpu.SemaphoreType.DMA((copies,)),
            pltpu.SemaphoreType.DMA((8,)),
            pltpu.SemaphoreType.DMA((2,)),
        ]
        + bufs,
        compiler_params=pltpu.CompilerParams(
            collective_id=collective_id, has_side_effects=True, vmem_limit_bytes=62 * MIB
        ),
        name="backward_trunk",
    )(
        pooled,
        slopes,
        stat,
        norms,
        live,
        lives,
        extra,
        hid.reshape(span, 2, height, hid.shape[1]),
        out.reshape(span // 4, 2, height, narrow),
        big,
        small,
        curve,
        normal,
        one,
        two,
        act,
        last,
        mid,
    )


def sinkhorn_kernel(
    axis,
    count,
    protos,
    queue_ref,
    centers_ref,
    turned_ref,
    pooled_ref,
    hid_ref,
    out_ref,
    norm_ref,
    live_ref,
    lives_ref,
    weigh_ref,
    first_ref,
    proto_grad_ref,
    d_hid_ref,
    d_out_ref,
    back_ref,
    extra_ref,
    partial_ref,
    act,
    normal,
    grads,
    lows,
    embed_ref,
    four,
    four_land,
    grad,
    parts_land,
    kept,
    scores,
    mine,
    landed,
    shift,
    total,
    send_sem,
    recv_sem,
):
    me = lax.axis_index(axis)
    views, rows, _ = queue_ref.shape
    width = turned_ref.shape[1]
    images = live_ref.shape[0]
    tile = row_tile(rows)
    part = 512
    parts = range(0, width, part)
    mask = live_ref[...][:, :1]
    crops = CROPS * images
    share = hid_ref.shape[1]
    low = jnp.bfloat16
    greet(axis, count)

    slots = lax.broadcasted_iota(jnp.int32, (images, 1), 0).astype(jnp.float32)
    masks = [jnp.where(slots < lives_ref[member, :images, :1], 1.0, 0.0) for member in range(count)]
    live_group = sum(lives_ref[member, :1, :1] for member in range(count))
    count_crops = live_group * float(CROPS)

    def spread(values, member):
        return (values.reshape(CROPS, images, values.shape[1]) * masks[member]).reshape(values.shape)

    sums = jnp.zeros((1, share), jnp.float32)
    squares = jnp.zeros((1, share), jnp.float32)
    for member in range(count):
        value = jnp.dot(pooled_ref[member], hid_ref[...], preferred_element_type=jnp.float32)
        normal[member] = value
        masked = spread(value, member)
        sums = sums + jnp.sum(masked, 0, keepdims=True)
        squares = squares + jnp.sum(masked * value, 0, keepdims=True)
    mean = sums / count_crops
    inverse_four = lax.rsqrt(squares / count_crops - mean * mean + norm_eps)
    gain, bias = norm_ref[0:1, :], norm_ref[1:2, :]
    for member in range(count):
        value = (normal[member] - mean) * inverse_four
        normal[member] = value
        pre = value * gain + bias
        act[member] = (pre * sigmoid_of(pre)).astype(low)
        partial_ref[member] = jnp.dot(act[member], out_ref[...], preferred_element_type=jnp.float32)

    def start_group(turn, source, target):
        copies = []
        for hop in range(1, count):
            to = lax.rem(me + hop, count)
            copy = pltpu.make_async_remote_copy(
                src_ref=source(to),
                dst_ref=target(hop),
                send_sem=send_sem.at[turn, hop],
                recv_sem=recv_sem.at[turn, hop],
                device_id={axis: to},
                device_id_type=MESH,
            )
            copy.start()
            copies.append(copy)
        return copies

    def to_group(turn, source, target):
        for copy in start_group(turn, source, target):
            copy.wait()

    to_group(ITERS, lambda to: partial_ref.at[to], lambda hop: parts_land.at[hop])
    embedding = partial_ref[me]
    for hop in range(1, count):
        embedding = embedding + parts_land[hop]
    inverse = lax.rsqrt(jnp.sum(embedding * embedding, 1, keepdims=True) + unit_eps)
    unit = embedding * inverse
    unit_low = unit.astype(jnp.bfloat16)

    def sum_group(turn):
        copies = []
        for hop in range(1, count):
            copy = pltpu.make_async_remote_copy(
                src_ref=mine.at[turn],
                dst_ref=landed.at[turn, hop],
                send_sem=send_sem.at[turn, hop],
                recv_sem=recv_sem.at[turn, hop],
                device_id={axis: lax.rem(me + hop, count)},
                device_id_type=MESH,
            )
            copy.start()
            copies.append(copy)
        for copy in copies:
            copy.wait()
        whole = mine[turn]
        for hop in range(1, count):
            whole = whole + landed[turn, hop]
        return whole

    for start in parts:
        cols = pl.ds(start, part)
        scores[:, cols] = jnp.dot(
            unit_low, turned_ref[:, cols], preferred_element_type=jnp.float32
        )
        for view in range(views):
            lines = pl.ds(view * images, images)
            shares = jnp.exp2(scores[lines, cols] * SINK2) * mask
            mine[0, pl.ds(view, 1), cols] = first_ref[pl.ds(view, 1), cols] + jnp.sum(
                shares, 0, keepdims=True
            )
    real = lax.broadcasted_iota(jnp.int32, (1, width), 1) < protos
    first = sum_group(0)
    shift[...] = jnp.where(real, jnp.log2(first), 1e30)

    for turn in range(1, ITERS):
        for view in range(views):
            lines = pl.ds(view * images, images)
            row = pl.ds(view, 1)
            if turn == 1:
                own = jnp.exp2(scores[lines, :] * SINK2 - shift[row, :]) * mask
                weight = jnp.sum(own, 1, keepdims=True)
            else:
                own = jnp.exp2(scores[lines, :] * SINK2 - first_log[row, :]) * mask
                weight = jnp.sum(own * shift[row, :], 1, keepdims=True)
            total[...] = own / (weight + (1.0 - mask))

            def step(index, carry):
                span = pl.ds(index * tile, tile)
                if turn == 1:
                    lines = queue_ref[view, span, :]
                sums = jnp.zeros((tile, LANES), jnp.float32)
                for start in parts:
                    cols = pl.ds(start, part)
                    if turn == 1:
                        raw = jnp.dot(lines, turned_ref[:, cols], preferred_element_type=jnp.float32)
                        shares = jnp.exp2(raw * SINK2 - shift[row, cols])
                        kept[view, span, cols] = shares
                    else:
                        shares = kept[view, span, cols] * shift[row, cols]
                    for lane in range(0, part, LANES):
                        sums = sums + shares[:, lane : lane + LANES]
                scale = 1.0 / jnp.sum(sums, 1, keepdims=True)
                for start in parts:
                    cols = pl.ds(start, part)
                    scaled = kept[view, span, cols] * scale
                    total[:, cols] += jnp.sum(scaled.reshape(tile // 8, 8, part), 0)
                return carry

            lax.fori_loop(0, rows // tile, step, 0)
            mine[turn, row, :] = jnp.sum(total[...], 0, keepdims=True)
        if turn == 1:
            first_log = shift[...]
        whole = sum_group(turn)
        shift[...] = jnp.where(real, 1.0 / whole, 0.0)

    codes = []
    for view in range(views):
        lines = pl.ds(view * images, images)
        own = jnp.exp2(scores[lines, :] * SINK2 - first_log[view : view + 1, :]) * mask
        own = own * shift[pl.ds(view, 1), :]
        codes.append(own / (jnp.sum(own, 1, keepdims=True) + (1.0 - mask)))
    code_total = codes[0] + codes[1]
    loss = jnp.zeros((images, 1), jnp.float32)
    for crop in range(CROPS):
        lines = pl.ds(crop * images, images)
        raw = jnp.where(real, scores[lines, :] * SOFT2, -1e30)
        raw = raw - jnp.max(raw, 1, keepdims=True)
        powers = jnp.exp2(raw)
        norm = jnp.sum(powers, 1, keepdims=True)
        others = code_total - codes[crop] if crop < NBIG else code_total
        logs = jnp.where(real, (raw - jnp.log2(norm)) / LOG2E, 0.0)
        loss = loss - jnp.sum(others * logs, 1, keepdims=True)
        weight = (NBIG - 1.0 if crop < NBIG else float(NBIG)) * mask / norm
        grad[lines, :] = (weight * powers - others) / (PAIRS * softmax_temp)
    grad_unit = jnp.zeros(unit.shape, jnp.float32)
    for start in parts:
        cols = pl.ds(start, part)
        some = grad[:, cols].astype(jnp.bfloat16)
        grad_unit = grad_unit + jnp.dot(
            some, centers_ref[cols, :], preferred_element_type=jnp.float32
        )
        proto_grad_ref[cols, :] = cross_rows(some, unit_low).astype(low)
    grad_embed = inverse * (
        grad_unit - unit * jnp.sum(unit * grad_unit, 1, keepdims=True)
    )
    embed_ref[me] = grad_embed.astype(jnp.bfloat16)
    to_group(ITERS + 1, lambda to: embed_ref.at[me], lambda hop: embed_ref.at[me])

    gain_sum = jnp.zeros((1, share), jnp.float32)
    bias_sum = jnp.zeros((1, share), jnp.float32)
    for member in range(count):
        value = against(embed_ref[member], out_ref[...])
        pre = normal[member] * gain + bias
        sigma = sigmoid_of(pre)
        value = value * (sigma + pre * sigma * (1.0 - sigma))
        grads[member] = value
        bias_sum = bias_sum + jnp.sum(value, 0, keepdims=True)
        gain_sum = gain_sum + jnp.sum(value * normal[member], 0, keepdims=True)
    four[pl.ds(0, 1), :] = gain_sum
    four[pl.ds(1, 1), :] = bias_sum
    four[pl.ds(2, 1), :] = jnp.broadcast_to(
        jnp.sum(loss, 0, keepdims=True) / PAIRS, (1, share)
    )
    copies = start_group(ITERS + 2, lambda to: four, lambda hop: four_land.at[hop])
    scale = gain * inverse_four
    for member in range(count):
        value = spread((bias_sum + normal[member] * gain_sum) / count_crops, member)
        lows[member] = ((grads[member] - value) * scale).astype(low)
    embeds = embed_ref[...].reshape(count * crops, embed_ref.shape[2])
    d_out_ref[...] = cross_rows(act[...].reshape(count * crops, share), embeds).astype(low)
    low_rows = lows[...].reshape(count * crops, share)
    for start in range(0, pooled_ref.shape[2], 256):
        left = pooled_ref[:, :, pl.ds(start, 256)].reshape(count * crops, 256)
        d_hid_ref[pl.ds(start, 256), :] = cross_rows(left, low_rows).astype(low)
        back = against(low_rows, hid_ref[pl.ds(start, 256), :]).astype(low)
        back_ref[:, :, pl.ds(start, 256)] = back.reshape(count, crops, 256)
    extra_ref[...] = jnp.zeros_like(extra_ref)
    for copy in copies:
        copy.wait()
    loss_group = jnp.zeros((1, 1), jnp.float32)
    for hop in range(count):
        source = (me + count - hop) % count
        value = four_land[hop] if hop else four[...]
        extra_ref[pl.ds(2, 1), lanes_of(source, share)] = value[0:1]
        extra_ref[pl.ds(4, 1), lanes_of(source, share)] = value[1:2]
        loss_group = loss_group + value[2:3, :1]
    lane = lax.broadcasted_iota(jnp.int32, (1, extra_ref.shape[1]), 1)
    line = jnp.where(lane == 0, loss_group, 0.0) + jnp.where(lane == 1, live_group, 0.0)
    for which in range(5):
        value = jnp.sum(weigh_ref[pl.ds(which, 1), :], 1, keepdims=True)
        line = line + jnp.where(lane == 2 + which, value, 0.0)
    extra_ref[pl.ds(5, 1), :] = line


def sinkhorn(
    sizes, collective_id, protos, queue, centers, turned, pooled, hid, out, norms, live, lives, weigh,
    first,
):
    count = sizes["sub"]
    views, rows, depth = queue.shape
    width = turned.shape[1]
    crops, channels = pooled.shape[1:]
    share = hid.shape[1]
    low, full = jnp.bfloat16, jnp.float32
    some = jax.ShapeDtypeStruct
    turns = ITERS + 3
    return pl.pallas_call(
        functools.partial(sinkhorn_kernel, "sub", count, protos),
        out_shape=(
            some((width, depth), low),
            some((channels, share), low),
            some((share, depth), low),
            some((count, crops, channels), low),
            some((8, count * share), full),
        ),
        in_specs=[pl.BlockSpec(memory_space=pltpu.VMEM)] * 11,
        out_specs=(pl.BlockSpec(memory_space=pltpu.VMEM),) * 5,
        scratch_shapes=[
            pltpu.VMEM((count, crops, depth), full),
            pltpu.VMEM((count, crops, share), low),
            pltpu.VMEM((count, crops, share), full),
            pltpu.VMEM((count, crops, share), full),
            pltpu.VMEM((count, crops, share), low),
            pltpu.VMEM((count, crops, depth), low),
            pltpu.VMEM((3, share), full),
            pltpu.VMEM((count, 3, share), full),
            pltpu.VMEM((crops, width), full),
            pltpu.VMEM((count, crops, depth), full),
            pltpu.VMEM((views, rows, width), full),
            pltpu.VMEM((crops, width), full),
            pltpu.VMEM((ITERS, views, width), full),
            pltpu.VMEM((ITERS, count, views, width), full),
            pltpu.VMEM((views, width), full),
            pltpu.VMEM((8, width), full),
            pltpu.SemaphoreType.DMA((turns, count)),
            pltpu.SemaphoreType.DMA((turns, count)),
        ],
        compiler_params=pltpu.CompilerParams(
            collective_id=collective_id, has_side_effects=True, vmem_limit_bytes=54 * MIB
        ),
        name="sinkhorn",
    )(queue, centers, turned, pooled, hid, out, norms, live, lives, weigh, first)


def advance(weight, gradient, moment, average, trust):
    step_now = trust * gradient
    moment_new = momentum_rate * moment + step_now
    weight_new = weight - learn_rate * (step_now + momentum_rate * moment_new)
    average_new = average_rate * average + (1.0 - average_rate) * weight_new
    return (weight_new, moment_new, average_new)


def update_kernel(protos, *refs):
    g_first, g_mid, g_last, g_hid, g_out, vec, sq, centers = refs[:8]
    sources, targets = refs[8:26], refs[26:48]
    held, lows = refs[48:66], refs[66:70]
    proto_grad, norm_grad, square, load_sem, save_sem = refs[70:]
    weights, moments, averages = held[:6], held[6:12], held[12:]
    w_outer, w_mid, w_hid, w_out, w_proto, w_norm = weights
    middle = g_first.shape[2]
    loads, saves = {}, []
    for which in (2, 1, 0, 3, 5, 4):
        loads[which] = []
        for part in range(3):
            index = 6 * part + which
            copy = pltpu.make_async_copy(sources[index], held[index], load_sem.at[index])
            copy.start()
            loads[which].append(copy)

    def trust_of(weights, grads):
        return trust_rate * jnp.sqrt(weights) / (jnp.sqrt(grads) + 1e-12)

    def put(which, at, grad, trust):
        new, moment, average = advance(
            weights[which][at],
            grad.astype(jnp.float32),
            moments[which][at],
            averages[which][at],
            trust,
        )
        weights[which][at] = new
        moments[which][at] = moment
        averages[which][at] = average
        if which < 4:
            lows[which][at] = new.astype(jnp.bfloat16)

    def load(which):
        for copy in loads[which]:
            copy.wait()

    def save(which):
        parts = [(held[6 * part + which], 6 * part + which) for part in range(3)]
        if which < 4:
            parts.append((lows[which], 18 + which))
        for source, index in parts:
            copy = pltpu.make_async_copy(source, targets[index], save_sem.at[index])
            copy.start()
            saves.append(copy)

    def matrix_trust(line, lane, share=1.0):
        grads = jnp.sum(sq[pl.ds(line, 1), :], 1, keepdims=True) * share
        return trust_of(vec[5:6, lane : lane + 1], grads)

    trust_hid = matrix_trust(3, 5)
    height = w_hid.shape[0] // 8 if w_hid.shape[0] >= 64 else 8
    load(2)

    def step_hid(index, carry):
        at = pl.ds(pl.multiple_of(index * height, 8), height)
        put(2, at, g_hid[at], trust_hid)
        return carry

    lax.fori_loop(0, w_hid.shape[0] // height, step_hid, 0)
    save(2)
    trust_mid = matrix_trust(1, 4)
    load(1)

    def step_mid(index, carry):
        put(1, index, g_mid[index], trust_mid)
        return carry

    lax.fori_loop(0, TAPS, step_mid, 0)
    save(1)
    load(0)
    for which, (grad, line) in enumerate(((g_first, 0), (g_last, 2))):
        trust = matrix_trust(line, 2 + which)
        height = grad.shape[1] // 4
        for index in range(4):
            lines = pl.ds(index * height, height)
            put(0, (which, lines), grad[0, lines], trust)
    save(0)
    load(3)
    whole = slice(None)
    put(3, whole, g_out[...], matrix_trust(4, 6, 0.25))
    save(3)

    for row, lines in enumerate((((0, 0), 1, 2), ((0, 1), 3, 4))):
        (line, half), wide, last = lines
        start = 2 * middle * half
        norm_grad[pl.ds(row, 1), pl.ds(0, 2 * middle)] = vec[line : line + 1, start : start + 2 * middle]
        size = vec.shape[1]
        norm_grad[pl.ds(row, 1), pl.ds(2 * middle, size)] = vec[wide : wide + 1, :]
        norm_grad[pl.ds(row, 1), pl.ds(2 * middle + size, size)] = vec[last : last + 1, :]
    load(5)
    weight, grad = w_norm[...], norm_grad[...]
    trust = trust_of(
        jnp.sum(weight * weight, 1, keepdims=True), jnp.sum(grad * grad, 1, keepdims=True)
    )
    put(5, whole, grad, trust)
    save(5)

    part = next(size for size in (600, 500, 400, 304, 200, 104, 40, 24, 8) if protos % size == 0)
    square[...] = jnp.zeros_like(square)
    load(4)

    def step_grad(index, carry):
        at = pl.ds(pl.multiple_of(index * part, 8), part)
        weight, value = w_proto[at], centers[at].astype(jnp.float32)
        inverse = lax.rsqrt(jnp.sum(weight * weight, 1, keepdims=True) + unit_eps)
        unit = weight * inverse
        grad = inverse * (value - unit * jnp.sum(unit * value, 1, keepdims=True))
        proto_grad[at] = grad
        weigh(square, 0, weight)
        weigh(square, 1, grad)
        return carry

    lax.fori_loop(0, protos // part, step_grad, 0)
    sums = jnp.sum(square[...], 1, keepdims=True)
    trust_proto = trust_of(sums[0:1], sums[1:2])

    def step_proto(index, carry):
        at = pl.ds(pl.multiple_of(index * part, 8), part)
        put(4, at, proto_grad[at], trust_proto)
        return carry

    lax.fori_loop(0, protos // part, step_proto, 0)
    save(4)
    for copy in saves:
        copy.wait()


def update(grads, vec, sq, centers, weights, moments, averages):
    some = jax.ShapeDtypeStruct
    protos = weights[4].shape[0]
    shapes = tuple(some(value.shape, value.dtype) for value in weights)
    lows = tuple(some(value.shape, jnp.bfloat16) for value in weights[:4])
    vmem, anywhere = pl.BlockSpec(memory_space=pltpu.VMEM), pl.BlockSpec(memory_space=pl.ANY)
    results = pl.pallas_call(
        functools.partial(update_kernel, protos),
        out_shape=shapes * 3 + lows,
        in_specs=[vmem] * 8 + [anywhere] * 18,
        out_specs=(anywhere,) * 22,
        scratch_shapes=[pltpu.VMEM(value.shape, value.dtype) for value in shapes * 3 + lows]
        + [
            pltpu.VMEM(weights[4].shape, jnp.float32),
            pltpu.VMEM(weights[5].shape, jnp.float32),
            pltpu.VMEM((8, LANES), jnp.float32),
            pltpu.SemaphoreType.DMA((18,)),
            pltpu.SemaphoreType.DMA((22,)),
        ],
        compiler_params=pltpu.CompilerParams(vmem_limit_bytes=56 * MIB),
        name="update",
    )(*grads, vec, sq, centers, *weights, *moments, *averages)
    return results


def per_device(
    sizes,
    big_maps,
    small_maps,
    live_counts,
    queue,
    bottleneck_outer,
    bottleneck_inner,
    proj_hidden,
    proj_out,
    prototypes,
    norm_params,
    mom_outer,
    mom_inner,
    mom_hidden,
    mom_out,
    mom_protos,
    mom_norms,
    avg_outer,
    avg_inner,
    avg_hidden,
    avg_out,
    avg_protos,
    avg_norms,
):
    n_dp, n_sub = sizes["dp"], sizes["sub"]
    exchange = Exchanger(sizes)
    images = big_maps.shape[0]
    channels = big_maps.shape[-1]
    middle = bottleneck_inner.shape[-1]
    hidden_width = proj_hidden.shape[1]
    out_width = proj_out.shape[1]
    proto_count = prototypes.shape[0]
    proto_width = -(-proto_count // 512) * 512
    here = lax.axis_index("sub")
    share = hidden_width // n_sub

    norm_start = 2 * middle + channels + here * share
    norm_four = lax.dynamic_slice(norm_params, (0, norm_start), (2, share))
    image_mask = (jnp.arange(images) < live_counts[0]).astype(jnp.float32)[:, None]
    live_tile = jnp.broadcast_to(image_mask, (images, LANES))
    big = jnp.transpose(big_maps, (2, 3, 1, 0, 4)).reshape(-1, channels)
    small = jnp.transpose(small_maps, (2, 3, 1, 0, 4)).reshape(-1, channels)

    (
        inner_low, last_w, hidden_low, out_low, hidden_one, hidden_two, act_two, curve, normal,
        trunk_stat, pooled_all, lives, slopes, weights_sq, centers_low, turned, first_sums,
    ) = forward_trunk(
        n_dp,
        exchange.next_id(),
        images,
        bottleneck_outer,
        bottleneck_inner,
        proj_hidden,
        proj_out,
        big,
        small,
        norm_params,
        live_tile,
        queue,
        prototypes,
        proto_width,
    )

    grad_centers, d_hidden, d_out, pooled_back, extra = sinkhorn(
        sizes,
        exchange.next_id(),
        proto_count,
        queue,
        centers_low,
        turned,
        pooled_all,
        hidden_low.reshape(channels, share),
        out_low.reshape(share, out_width),
        norm_four,
        live_tile,
        lives,
        weights_sq,
        first_sums,
    )
    centers_sum = lax.psum(grad_centers, ("dp", "sub"))

    shard_first, shard_inner, shard_last, shard_hidden, shard_out, vector, grad_sq = backward_trunk(
        n_dp,
        exchange.next_id(),
        images,
        pooled_back,
        slopes,
        trunk_stat,
        norm_params,
        live_tile,
        lives,
        extra,
        d_hidden,
        d_out,
        big,
        small,
        curve,
        normal,
        hidden_one,
        hidden_two,
        act_two,
        last_w,
        inner_low,
    )
    results = update(
        (shard_first, shard_inner, shard_last, shard_hidden, shard_out),
        vector,
        grad_sq,
        centers_sum,
        (bottleneck_outer, bottleneck_inner, proj_hidden, proj_out, prototypes, norm_params),
        (mom_outer, mom_inner, mom_hidden, mom_out, mom_protos, mom_norms),
        (avg_outer, avg_inner, avg_hidden, avg_out, avg_protos, avg_norms),
    )
    return (vector[5, 0], vector[5, 1]) + tuple(results)


def solution(mesh):
    data = P(("dp", "sub"), None, None, None, None)
    trees = (P(None, "dp", None), P(None, "dp", None), P("dp", None), P("dp", None), P(), P())
    in_specs = (data, data, P(("dp", "sub")), P(None, ("dp", "sub"), None)) + trees * 3
    out_specs = (P(), P()) + trees * 3 + trees[:4]
    sizes = {axis: mesh.shape[axis] for axis in ("dp", "sub")}
    return jax.shard_map(
        functools.partial(per_device, sizes),
        mesh=mesh,
        in_specs=in_specs,
        out_specs=out_specs,
        check_vma=False,
    )
```

```python
import functools
import math

import jax
import jax.numpy as jnp
from jax import lax
from jax.experimental import pallas as pl
from jax.experimental.pallas import tpu as pltpu
from jax.sharding import PartitionSpec as P

NBIG = 2
NSMALL = 6
CROPS = NBIG + NSMALL
BIG = 7
SMALL = 3
TAPS = 9
ITERS = 3
LANES = 128

sink_temp = 0.05
softmax_temp = 0.1
norm_eps = 1e-05
unit_eps = 1e-12
trust_rate = 0.5
learn_rate = 1.0
momentum_rate = 0.5
average_rate = 0.5

MESH = pl.DeviceIdType.MESH
MIB = 1 << 20
LOG2E = math.log2(math.e)
SINK2 = LOG2E / sink_temp
SOFT2 = LOG2E / softmax_temp
PAIRS = NBIG * (CROPS - 1)


def cross_rows(left, right):
    return lax.dot_general(
        left, right, (((0,), (0,)), ((), ())), preferred_element_type=jnp.float32
    )


def against(left, right):
    return lax.dot_general(
        left, right, (((1,), (1,)), ((), ())), preferred_element_type=jnp.float32
    )


def greet(axis, count):
    me = lax.axis_index(axis)
    barrier = pltpu.get_barrier_semaphore()
    for hop in range(1, count):
        pl.semaphore_signal(
            barrier, inc=1, device_id={axis: lax.rem(me + hop, count)}, device_id_type=MESH
        )
    pl.semaphore_wait(barrier, count - 1)


class Exchanger:
    def __init__(self, sizes):
        self.sizes = sizes
        self.used = 0

    def next_id(self):
        self.used += 1
        return self.used


class Links:
    def __init__(self, send_sem, recv_sem):
        self.send_sem = send_sem
        self.recv_sem = recv_sem
        self.used = 0

    def __call__(self, source, target, device):
        copy = pltpu.make_async_remote_copy(
            src_ref=source,
            dst_ref=target,
            send_sem=self.send_sem.at[self.used],
            recv_sem=self.recv_sem.at[self.used],
            device_id=device,
            device_id_type=MESH,
        )
        self.used += 1
        copy.start()
        return copy


def wait_all(copies):
    for copy in copies:
        copy.wait()


def lanes_of(index, width=LANES):
    return pl.ds(pl.multiple_of(index * width, LANES), width)


class Place:
    def __init__(self, n_dp):
        self.n_dp = n_dp
        self.span = n_dp // 2
        dp, self.sub = lax.axis_index("dp"), lax.axis_index("sub")
        self.dp = dp
        self.near, self.far = dp // 2, dp % 2
        row, core = self.sub // 2, self.sub % 2
        self.row, self.core = row, core
        self.row_sub = 2 * (1 - row) + core
        self.core_sub = 2 * row + (1 - core)
        self.far_peer = {"dp": self.near * 2 + (1 - self.far)}
        self.row_peer = {"sub": self.row_sub}
        self.core_peer = {"sub": self.core_sub}

    def near_index(self, hop):
        return (self.near + hop) % self.span

    def near_peer(self, hop):
        return {"dp": self.near_index(hop) * 2 + self.far}

    def dp_peers(self):
        return [{"dp": (self.dp + hop) % self.n_dp} for hop in range(1, self.n_dp)]

    def sub_peers(self):
        return [{"sub": (self.sub + hop) % 4} for hop in range(1, 4)]

    def greet(self, peers):
        barrier = pltpu.get_barrier_semaphore()
        for peer in peers:
            pl.semaphore_signal(barrier, inc=1, device_id=peer, device_id_type=MESH)
        pl.semaphore_wait(barrier, len(peers))


ALL = slice(None)


def sigmoid_of(values):
    return 0.5 * jnp.tanh(0.5 * values) + 0.5


def rows_at(start, size):
    return pl.ds(start if isinstance(start, int) else pl.multiple_of(start, 16), size)


def tap_blocks(images, flip):
    moves = [[] for _ in range(TAPS)]
    zeros = [[] for _ in range(TAPS)]
    base = 0
    for extent, lines in ((BIG, NBIG * images), (SMALL, NSMALL * images)):
        for tap in range(TAPS):
            down, right = tap // 3 - 1, tap % 3 - 1
            if flip:
                down, right = -down, -right
            for row in range(extent):
                start = base + row * extent * lines
                if not 0 <= row + down < extent:
                    zeros[tap].append((start, extent * lines))
                    continue
                left, stop = max(0, -right), min(extent, extent - right)
                moves[tap].append(
                    (
                        start + left * lines,
                        base + ((row + down) * extent + left + right) * lines,
                        (stop - left) * lines,
                    )
                )
                if left:
                    zeros[tap].append((start, left * lines))
                if stop < extent:
                    zeros[tap].append((start + stop * lines, (extent - stop) * lines))
        base += extent * extent * lines
    return moves, zeros


def fill_columns(columns, source, images, flip):
    wide = source.shape[1]
    moves, zeros = tap_blocks(images, flip)
    for tap in range(TAPS):
        cols = pl.ds(tap * wide, wide)
        for target, start, size in moves[tap]:
            columns[pl.ds(target, size), cols] = source[pl.ds(start, size), :]
        for target, size in zeros[tap]:
            columns[pl.ds(target, size), cols] = jnp.zeros((size, wide), columns.dtype)


def masked_sums(values, mask, total):
    rows, wide = values.shape
    blocks = values.reshape(rows // 8, 8, wide)
    masked = blocks * mask
    total[0] += jnp.sum(masked, 0)
    total[1] += jnp.sum(masked * blocks, 0)


def row_tile(rows):
    return next(size for size in (192, 160, 128, 96, 64, 48, 32, 24, 16, 8) if rows % size == 0)


def centers_of(proto_ref, centers_ref, turned_ref):
    protos, depth = proto_ref.shape
    part = 256
    for start in range(0, turned_ref.shape[1], part):
        here = max(0, min(part, protos - start))
        values = jnp.zeros((part, depth), jnp.float32)
        if here:
            values = proto_ref[pl.ds(start, here), :]
            values = values * lax.rsqrt(jnp.sum(values * values, 1, keepdims=True) + unit_eps)
        if 0 < here < part:
            values = jnp.concatenate([values, jnp.zeros((part - here, depth), jnp.float32)], 0)
        centers_ref[pl.ds(start, part), :] = values.astype(jnp.bfloat16)
        turned_ref[:, pl.ds(start, part)] = values.T.astype(jnp.bfloat16)


def queue_sums(queue_ref, turned_ref, o_ref, total, view):
    rows, width = queue_ref.shape[1], turned_ref.shape[1]
    tile, part = row_tile(rows), 256
    total[...] = jnp.zeros_like(total)

    def step(index, carry):
        lines = queue_ref[view, pl.ds(index * tile, tile), :]
        for start in range(0, width, part):
            cols = pl.ds(start, part)
            scores = jnp.dot(lines, turned_ref[:, cols], preferred_element_type=jnp.float32)
            shares = jnp.exp2(scores * SINK2)
            total[:, cols] += jnp.sum(shares.reshape(tile // 8, 8, part), 0)
        return carry

    lax.fori_loop(0, rows // tile, step, 0)
    o_ref[pl.ds(view, 1), :] = jnp.sum(total[...], 0, keepdims=True)


class GroupSums:
    def __init__(self, at, links):
        self.at, self.links = at, links

    def start(self, mine, land):
        self.mine, self.land = mine, land
        self.copies = [
            self.links(mine, land.at[hop], peer) for hop, peer in enumerate(self.at.sub_peers())
        ]

    def finish(self):
        wait_all(self.copies)
        value = self.mine[...]
        for hop in range(3):
            value = value + self.land[hop]
        return value


def copy_rows(big, small, target, sem):
    split = big.shape[0]
    copies = [
        pltpu.make_async_copy(big, target.at[pl.ds(0, split)], sem.at[0]),
        pltpu.make_async_copy(small, target.at[pl.ds(split, small.shape[0])], sem.at[1]),
    ]
    for copy in copies:
        copy.start()
    return copies


def weigh(target, line, values):
    sums = jnp.sum(values * values, 0, keepdims=True)
    for lane in range(0, sums.shape[1], LANES):
        target[pl.ds(line, 1), :] += sums[:, lane : lane + LANES]


def forward_kernel(n_dp, images, *refs):
    i_outer, i_mid, i_hid, i_out, h_big, h_small, norm_ref, live_ref, queue_ref, proto_ref = refs[:10]
    (
        o_mid, o_last, o_hid, o_out, o_one, o_two, o_act, o_curve, o_normal, o_stat, o_pooled, o_live,
        o_slope, o_weigh, o_centers, o_turned, o_queue,
    ) = refs[10:27]
    (
        x_ref, w_first, w_mid, w_last, w_hid, w_out, first_w, mid_w, last_w, out_w, columns, act_one,
        act_two, one, two, three, total, pool, sums_a, land_a, sums_b, land_b, sums_c, land_c, pooled,
        queue_total, send_sem, recv_sem, own_sem, x_sem,
    ) = refs[27:]
    at = Place(n_dp)
    links = Links(send_sem, recv_sem)
    x_copies = copy_rows(h_big, h_small, x_ref, x_sem)
    share = w_hid.shape[1]
    w_first[...] = i_outer[0].astype(w_first.dtype)
    at.greet(
        [at.near_peer(hop) for hop in range(1, at.span)] + [at.far_peer] + at.sub_peers()
    )
    low = jnp.bfloat16
    middle = first_w.shape[3]
    channels = x_ref.shape[1]
    rows = x_ref.shape[0]
    mask = live_ref[...][:, :1]
    half = middle // 2

    def flat(source, target, start, size, split):
        line = source.shape[0] // 4
        some = pl.ds(start * line, size * line)
        return (
            lambda cols: source.at[some, cols],
            lambda near, far, cols: target.at[near, far, some, cols],
            split,
        )

    def taps(start, size, split):
        some = pl.ds(start, size)
        return (
            lambda cols: w_mid.at[some, :, cols],
            lambda near, far, cols: mid_w.at[some, near, far, :, cols],
            split,
        )

    quarter = w_out.shape[0] // 4
    out_rows = pl.ds(at.sub * quarter, quarter)
    pieces = [flat(w_first, first_w, 0, 2, 4), flat(w_first, first_w, 2, 2, 4)]
    groups = (((0, 1, 2), (1, 2, 4)), ((3, 1, 4), (4, 1, 2), (5, 2, 4)), ((7, 1, 4), (8, 1, 2)))
    last_of = []
    for group in groups:
        pieces += [taps(*some) for some in group]
        last_of.append(len(pieces))
    pieces += [flat(w_last, last_w, 0, 2, 4), flat(w_last, last_w, 2, 1, 2), flat(w_last, last_w, 3, 1, 4)]
    trunk_pieces = len(pieces)
    pieces += [flat(w_hid, o_hid, part, 1, 1) for part in range(4)]
    pieces.append(
        (
            lambda cols: w_out.at[out_rows],
            lambda near, far, cols: out_w.at[near, far],
            1,
        )
    )
    count = len(pieces)
    mine = {4: lanes_of(at.sub), 2: lanes_of(at.core, half), 1: ALL}
    own, first, second, third, fourth = [], [], [], [], []

    def begin(index):
        if index < count:
            source, target, split = pieces[index]
            cols = mine[split]
            copy = pltpu.make_async_copy(
                source(cols), target(at.near, at.far, cols), own_sem.at[index]
            )
            copy.start()
            own.append(copy)
            first.append(
                [
                    links(source(cols), target(at.near, at.far, cols), at.near_peer(hop))
                    for hop in range(1, at.span)
                ]
            )

    begin(0)
    begin(1)

    def cast_tap(index, carry):
        w_mid[index] = i_mid[index].astype(w_mid.dtype)
        return carry

    lax.fori_loop(0, TAPS, cast_tap, 0)
    begin(2)
    w_last[...] = i_outer[1].astype(w_last.dtype)
    w_hid[...] = i_hid[:, lanes_of(at.sub, share)].astype(w_hid.dtype)
    w_out[...] = i_out[...].astype(w_out.dtype)
    lag = 2
    clock = [0]

    def pump(times=1):
        for _ in range(times):
            tick(clock[0])
            clock[0] += 1

    def need(index):
        while clock[0] <= index + 2 * lag:
            pump()
        wait_all(fourth[index])

    def tick(now):
        if now < count:
            source, target, split = pieces[now]
            own[now].wait()
            wait_all(first[now])
            begin(now + 3)
            slab = target(ALL, at.far, mine[split])
            second.append(links(slab, slab, at.far_peer))
        past = now - lag
        if 0 <= past < count:
            source, target, split = pieces[past]
            second[past].wait()
            slab = target(ALL, ALL, mine[split])
            third.append(links(slab, slab, at.row_peer) if split == 4 else None)
            fourth.append([links(slab, slab, at.core_peer)] if split == 2 else [])
        past = now - 2 * lag
        if 0 <= past < count and pieces[past][2] == 4:
            source, target, split = pieces[past]
            third[past].wait()
            slabs = [target(ALL, ALL, cols) for cols in (mine[4], lanes_of(at.row_sub))]
            fourth[past] = [links(slab, slab, at.core_peer) for slab in slabs]

    tile = rows // 4
    sums = GroupSums(at, links)

    def pack(target, wide):
        target[pl.ds(0, 1), :] = jnp.sum(total[0, :, :wide], 0, keepdims=True)
        target[pl.ds(1, 1), :] = jnp.sum(total[1, :, :wide], 0, keepdims=True)

    def settle(value, count_all, start, wide):
        mean = value[0:1] / count_all
        inverse = lax.rsqrt(value[1:2] / count_all - mean * mean + norm_eps)
        o_stat[pl.ds(0, 1), pl.ds(start, wide)] = mean
        o_stat[pl.ds(1, 1), pl.ds(start, wide)] = inverse
        scale = norm_ref[pl.ds(0, 1), pl.ds(start, wide)] * inverse
        return scale, norm_ref[pl.ds(1, 1), pl.ds(start, wide)] - scale * mean

    centers_of(proto_ref, o_centers, o_turned)
    pump()
    queue_sums(queue_ref, o_turned, o_queue, queue_total, 0)
    pump()
    queue_sums(queue_ref, o_turned, o_queue, queue_total, 1)
    pump()
    o_weigh[...] = jnp.zeros_like(o_weigh)
    weigh(o_weigh, 0, i_outer[0])
    weigh(o_weigh, 1, i_outer[1])
    weigh(o_weigh, 4, i_out[...])

    def weigh_tap(index, carry):
        weigh(o_weigh, 2, i_mid[index])
        return carry

    lax.fori_loop(0, TAPS, weigh_tap, 0)
    pump()

    def weigh_part(index, carry):
        weigh(o_weigh, 3, i_hid[:, lanes_of(index, 512)])
        return carry

    lax.fori_loop(0, i_hid.shape[1] // 512, weigh_part, 0)
    need(0)
    need(1)
    pump()
    for copy in x_copies:
        copy.wait()

    total[...] = jnp.zeros_like(total)

    def step_one(index, carry):
        span = rows_at(index * tile, tile)
        value = jnp.dot(
            x_ref[span, :],
            first_w[...].reshape(channels, middle),
            preferred_element_type=jnp.float32,
        )
        one[span, :] = value
        masked_sums(value, mask, total.at[:, :, pl.ds(0, middle)])
        return carry

    lax.fori_loop(0, 4, step_one, 0)
    pack(sums_a, middle)
    live = jnp.sum(mask, 0, keepdims=True)
    sums_a[pl.ds(2, 1), :] = jnp.broadcast_to(live, (1, middle))
    sums.start(sums_a, land_a)
    pump()
    value = sums.finish()
    per_image = rows // images
    lives = value[2:3, :1]
    count_all = lives * per_image
    o_live[at.sub] = jnp.broadcast_to(live, o_live.shape[1:])
    for hop in range(3):
        o_live[(at.sub + 3 - hop) % 4] = jnp.broadcast_to(land_a[hop, 2:3, :1], o_live.shape[1:])
    scale, shift = settle(value, count_all, 0, middle)

    def step_act(source, target):
        def step(index, carry):
            span = rows_at(index * tile, tile)
            pre = source[span, :] * scale + shift
            target[span, :] = (pre * sigmoid_of(pre)).astype(low)
            return carry

        lax.fori_loop(0, 4, step, 0)

    step_act(one, act_one)
    save = [pltpu.make_async_copy(one, o_one, own_sem.at[count])]
    save[-1].start()
    pump()
    fill_columns(columns, act_one, images, False)

    total[...] = jnp.zeros_like(total)
    for part in range(3):
        for index in range(last_of[part] - len(groups[part]), last_of[part]):
            need(index)

        def step_two(index, carry):
            span = rows_at(index * tile, tile)
            value = jnp.dot(
                columns[span, pl.ds(part * 3 * middle, 3 * middle)],
                mid_w[pl.ds(part * 3, 3)].reshape(3 * middle, middle),
                preferred_element_type=jnp.float32,
            )
            if part:
                value = value + two[span, :]
            two[span, :] = value
            if part == 2:
                masked_sums(value, mask, total.at[:, :, pl.ds(0, middle)])
            return carry

        lax.fori_loop(0, 4, step_two, 0)
    save.append(pltpu.make_async_copy(mid_w, o_mid, own_sem.at[count + 2]))
    save[-1].start()
    pack(sums_b, middle)
    sums.start(sums_b, land_b)
    scale, shift = settle(sums.finish(), count_all, middle, middle)
    step_act(two, act_two)
    save.append(pltpu.make_async_copy(two, o_two, own_sem.at[count + 3]))
    save[-1].start()
    save.append(pltpu.make_async_copy(act_two, o_act, own_sem.at[count + 4]))
    save[-1].start()

    for index in range(trunk_pieces - 3, trunk_pieces):
        need(index)
    save.append(pltpu.make_async_copy(last_w, o_last, own_sem.at[count + 5]))
    save[-1].start()
    total[...] = jnp.zeros_like(total)

    def step_three(index, carry):
        span = rows_at(index * tile, tile)
        for quarter in range(4):
            wide = channels // 4
            cols = pl.ds(quarter * wide, wide)
            weights = last_w[pl.ds(quarter * (at.span // 4), at.span // 4)].reshape(wide, middle)
            value = against(act_two[span, :], weights)
            three[span, cols] = value
            masked_sums(value, mask, total.at[:, :, cols])
        return carry

    lax.fori_loop(0, 4, step_three, 0)
    pack(sums_c, channels)
    sums.start(sums_c, land_c)
    pump()
    scale, shift = settle(sums.finish(), count_all, 2 * middle, channels)

    pool[...] = jnp.zeros_like(pool)
    o_slope[...] = jnp.zeros_like(o_slope)
    wide = pl.ds(2 * middle, channels)
    center = o_stat[pl.ds(0, 1), wide] * o_stat[pl.ds(1, 1), wide]
    base = 0
    for extent, crops in ((BIG, NBIG), (SMALL, NSMALL)):
        lines = crops * images
        into = pl.ds(0, lines) if extent == BIG else pl.ds(NBIG * images, lines)

        def step_out(index, carry):
            span = rows_at(base + index * extent * lines, extent * lines)
            for start in range(0, channels, 512):
                cols = pl.ds(start, 512)
                pre = three[span, cols] * scale[:, start : start + 512]
                pre = pre + shift[:, start : start + 512] + x_ref[span, cols].astype(jnp.float32)
                sigma = sigmoid_of(pre)
                value = pre * sigma
                slope = sigma + value * (1.0 - sigma)
                normal = three[span, cols] * o_stat[1:2, 2 * middle + start : 2 * middle + start + 512]
                normal = normal - center[:, start : start + 512]
                columns[span, cols] = slope.astype(low)
                columns[span, pl.ds(channels + start, 512)] = normal.astype(low)
                pool[into, cols] += jnp.sum(value.reshape(extent, lines, 512), 0)
                o_slope[0, into, cols] += jnp.sum(slope.reshape(extent, lines, 512), 0)
                slope = slope * normal
                o_slope[1, into, cols] += jnp.sum(slope.reshape(extent, lines, 512), 0)
            return carry

        lax.fori_loop(0, extent, step_out, 0)
        pump()
        pooled[into, :] = (pool[into, :] * (1.0 / (extent * extent))).astype(low)
        base += extent * extent * lines

    for index, target in enumerate((o_curve, o_normal)):
        some = columns.at[:, pl.ds(index * channels, channels)]
        save.append(pltpu.make_async_copy(some, target, x_sem.at[index]))
        save[-1].start()

    over = links(pooled, o_pooled.at[at.sub], at.row_peer)
    pair = links(pooled, o_pooled.at[at.sub], at.core_peer)
    o_pooled[at.sub] = pooled[...]
    pump()
    over.wait()
    last = links(o_pooled.at[at.row_sub], o_pooled.at[at.row_sub], at.core_peer)
    need(count - 1)
    some = at.span // 4
    out_own = out_w.at[pl.ds(at.sub * some, some)]
    into = o_out.at[:, :, out_rows]
    own.append(pltpu.make_async_copy(out_own, into, own_sem.at[count - 1]))
    own[-1].start()
    out_copies = [
        links(out_w.at[pl.ds(peer["sub"] * some, some)], into, peer) for peer in at.sub_peers()
    ]
    pair.wait()
    last.wait()
    own[-1].wait()
    wait_all(out_copies)
    for copy in save:
        copy.wait()


def forward_trunk(
    n_dp, collective_id, images, outer, mid, hid, out, big, small, norms, live, queue, prototypes, width
):
    span = n_dp // 2
    height, middle = outer.shape[1:]
    rows, channels = big.shape[0] + small.shape[0], big.shape[1]
    share, narrow = hid.shape[1] // 4, out.shape[1]
    some = jax.ShapeDtypeStruct
    low, full = jnp.bfloat16, jnp.float32
    copies = 17 * (span + 4) + 16
    vmem, anywhere = pl.BlockSpec(memory_space=pltpu.VMEM), pl.BlockSpec(memory_space=pl.ANY)
    return pl.pallas_call(
        functools.partial(forward_kernel, n_dp, images),
        out_shape=(
            some((TAPS, span, 2, mid.shape[1], middle), low),
            some((span, 2, height, middle), low),
            some((span, 2, height, share), low),
            some((span // 4, 2, height, narrow), low),
            some((rows, middle), full),
            some((rows, middle), full),
            some((rows, middle), low),
            some((rows, channels), low),
            some((rows, channels), low),
            some((2, 2 * middle + channels), full),
            some((4, CROPS * images, channels), low),
            some((4, 8, LANES), full),
            some((2, CROPS * images, channels), full),
            some((8, LANES), full),
            some((width, prototypes.shape[1]), low),
            some((prototypes.shape[1], width), low),
            some((queue.shape[0], width), full),
        ),
        in_specs=[vmem] * 4 + [anywhere] * 2 + [vmem] * 4,
        out_specs=(anywhere,) * 9 + (vmem,) * 8,
        scratch_shapes=[
            pltpu.VMEM((rows, channels), low),
            pltpu.VMEM((height, middle), low),
            pltpu.VMEM(mid.shape, low),
            pltpu.VMEM((height, middle), low),
            pltpu.VMEM((height, share), low),
            pltpu.VMEM((height, narrow), low),
            pltpu.VMEM((span, 2, height, middle), low),
            pltpu.VMEM((TAPS, span, 2, mid.shape[1], middle), low),
            pltpu.VMEM((span, 2, height, middle), low),
            pltpu.VMEM((span, 2, height // 4, narrow), low),
            pltpu.VMEM((rows, TAPS * middle), low),
            pltpu.VMEM((rows, middle), low),
            pltpu.VMEM((rows, middle), low),
            pltpu.VMEM((rows, middle), full),
            pltpu.VMEM((rows, middle), full),
            pltpu.VMEM((rows, channels), full),
            pltpu.VMEM((2, 8, channels), full),
            pltpu.VMEM((CROPS * images, channels), full),
            pltpu.VMEM((3, middle), full),
            pltpu.VMEM((3, 3, middle), full),
            pltpu.VMEM((2, middle), full),
            pltpu.VMEM((3, 2, middle), full),
            pltpu.VMEM((2, channels), full),
            pltpu.VMEM((3, 2, channels), full),
            pltpu.VMEM((CROPS * images, channels), low),
            pltpu.VMEM((8, width), full),
            pltpu.SemaphoreType.DMA((copies,)),
            pltpu.SemaphoreType.DMA((copies,)),
            pltpu.SemaphoreType.DMA((17 + 6,)),
            pltpu.SemaphoreType.DMA((2,)),
        ],
        compiler_params=pltpu.CompilerParams(
            collective_id=collective_id, has_side_effects=True, vmem_limit_bytes=62 * MIB
        ),
        name="forward_trunk",
    )(outer, mid, hid, out, big, small, norms, live, queue, prototypes)


def plus(left, right):
    return left.astype(jnp.float32) + right.astype(jnp.float32)


def piece_list(height, mid_height, proto_height, refs):
    first, mid, last, proto = refs
    half, quarter = height // 2, height // 4
    pieces = [last + (0, 1, part * half, half, 2) for part in range(2)]
    for start, taps in ((0, 1), (1, 1), (2, 1), (3, 1), (4, 1), (5, 1), (6, 1), (7, 2)):
        pieces.append(mid + (start, taps, 0, mid_height, 1))
    pieces += [first + (0, 1, part * quarter, quarter, 0) for part in range(4)]
    return pieces + [proto + (0, 1, 0, proto_height, 5)]


def backward_kernel(n_dp, images, *refs):
    p_pool, slope_ref, stat_ref, norm_ref, live_ref, lives_ref, extra_ref, g_hid, g_some, g_proto = refs[:10]
    h_big, h_small, h_curve, h_normal, h_one, h_two, h_act, h_last, h_mid = refs[10:19]
    o_first, o_mid, o_last, o_hid, o_out, o_proto, o_vec, o_sq = refs[19:27]
    (
        x_ref, one, two, act_two, last_w, mid_w, act_one, wide_low, work, thin_low, g_first, g_mid,
        g_last, total, pair_land, pair_sum, row_land, grad_pool, sums_a, land_a, sums_b, land_b,
        sums_c, land_c, hid_in, hid_sum, hid_land, g_out, out_in, out_sum, out_land, vec, vec_land,
        sq_mine, sq_land, proto_own, send_sem, recv_sem, own_sem, x_sem,
    ) = refs[27:67]
    bufs = refs[67:]
    at = Place(n_dp)
    links = Links(send_sem, recv_sem)
    span = at.span
    at.greet(at.dp_peers() + at.sub_peers())
    low = jnp.bfloat16
    rows, channels = x_ref.shape
    middle = one.shape[1]
    height = g_last.shape[3]
    mask = live_ref[...][:, :1]
    tile = rows // 4

    loads = {}
    for index, (name, source, target) in enumerate(
        (
            ("one", h_one, one), ("curve", h_curve, wide_low), ("normal", h_normal, x_ref),
            ("last", h_last, last_w), ("two", h_two, two), ("act", h_act, act_two), ("mid", h_mid, mid_w),
        )
    ):
        loads[name] = pltpu.make_async_copy(source, target, own_sem.at[index])
        loads[name].start()

    pair = [
        links(p_pool.at[2 * line + (1 - at.core)], pair_land.at[line], at.core_peer)
        for line in (1 - at.row, at.row)
    ]
    far_copies = [links(g_hid.at[:, 1 - at.far], hid_in, at.far_peer)]
    some = g_some.shape[0]
    block = g_out.at[pl.ds(at.sub * some, some)]
    own_out = pltpu.make_async_copy(g_some, block, own_sem.at[7])
    own_out.start()
    out_copies = [links(g_some, block, peer) for peer in at.sub_peers()]
    pair[0].wait()
    pair_sum[...] = plus(p_pool[2 * (1 - at.row) + at.core], pair_land[1 - at.row]).astype(low)
    over = links(pair_sum, row_land, at.row_peer)
    pair[1].wait()

    wholes = [(g_hid, hid_in, hid_sum, hid_land), (g_out, out_in, out_sum, out_land)]

    def whole_far(which):
        source, landed, summed, land = wholes[which]
        far_copies[which].wait()
        for near in range(span):
            summed[near] = plus(source[near, at.far], landed[near]).astype(low)
        return [
            links(summed.at[at.near_index(hop)], land.at[hop - 1], at.near_peer(hop))
            for hop in range(1, span)
        ]

    def whole_near(which, copies):
        source, landed, summed, land = wholes[which]
        wait_all(copies)
        value = summed[at.near].astype(jnp.float32)
        for hop in range(1, span):
            value = value + land[hop - 1].astype(jnp.float32)
        return value.astype(low)

    sq_mine[0] = jnp.zeros_like(sq_mine[0])

    def squares_of(matrix, value):
        value = value.astype(jnp.float32)
        line = jnp.sum(value * value, 0, keepdims=True)
        for lane in range(0, line.shape[1], LANES):
            sq_mine[0, pl.ds(matrix, 1), :] += line[:, lane : lane + LANES]

    pieces = piece_list(
        height,
        g_mid.shape[3],
        g_proto.shape[3],
        ((g_first, o_first), (g_mid, o_mid), (g_last, o_last), (g_proto, proto_own)),
    )
    proto = len(pieces) - 1
    mine, beside = lanes_of(at.sub), lanes_of(at.row_sub)
    state = [0] * len(pieces)
    flight = [None] * len(pieces)

    def loop(count, body):
        def step(index, carry):
            body(index)
            return carry

        lax.fori_loop(0, count, step, 0)

    def go(index):
        source, target, start, taps, line, size, matrix = pieces[index]
        held, second, third, nears = bufs[4 * index : 4 * index + 4]
        stage = state[index]
        state[index] += 1
        row_first = index % 2 == 0
        lines, some = pl.ds(line, size), pl.ds(start, taps)
        if stage == 0:
            flight[index] = [
                links(
                    source.at[some, :, :, lines, lanes_of(2 * row + (1 - at.core))],
                    held.at[row],
                    at.core_peer,
                )
                for row in range(2)
            ]
            return
        wait_all(flight[index])
        if stage == 1:
            for row in range(2):
                cols = lanes_of(2 * row + at.core)

                def body(at_block):
                    tap, near, far = at_block // (2 * span), at_block // 2 % span, at_block % 2
                    held[row, tap, near, far] = plus(
                        source[start + tap, near, far, lines, cols], held[row, tap, near, far]
                    ).astype(low)

                loop(taps * span * 2, body)
            if row_first:
                flight[index] = [links(held.at[1 - at.row], second, at.row_peer)]
            else:
                flight[index] = [links(held.at[:, :, :, 1 - at.far], second, at.far_peer)]
        elif stage == 2:
            if row_first:

                def body(at_block):
                    tap, near, far = at_block // (2 * span), at_block // 2 % span, at_block % 2
                    second[tap, near, far] = plus(
                        held[at.row, tap, near, far], second[tap, near, far]
                    ).astype(low)

                loop(taps * span * 2, body)
                flight[index] = [links(second.at[:, :, 1 - at.far], third, at.far_peer)]
            else:

                def body(at_block):
                    row, tap, near = at_block // (taps * span), at_block // span % taps, at_block % span
                    second[row, tap, near] = plus(
                        held[row, tap, near, at.far], second[row, tap, near]
                    ).astype(low)

                loop(taps * span * 2, body)
                flight[index] = [links(second.at[1 - at.row], third, at.row_peer)]
        elif stage == 3:

            def body(at_block):
                tap, near = at_block // span, at_block % span
                part = second[tap, near, at.far] if row_first else second[at.row, tap, near]
                third[tap, near] = plus(part, third[tap, near]).astype(low)

            loop(taps * span, body)
            flight[index] = [
                links(third.at[:, at.near_index(hop)], nears.at[hop - 1], at.near_peer(hop))
                for hop in range(1, span)
            ]
        elif stage == 4:
            for tap in range(taps):
                value = third[tap, at.near].astype(jnp.float32)
                for hop in range(1, span):
                    value = value + nears[hop - 1, tap].astype(jnp.float32)
                value = value.astype(low)
                squares_of(matrix, value)
                target[start + tap, lines, mine] = value
            slab = target.at[some, lines, mine]
            flight[index] = [links(slab, slab, at.row_peer)]
        elif stage == 5:
            slabs = [target.at[some, lines, cols] for cols in (mine, beside)]
            flight[index] = [links(slab, slab, at.core_peer) for slab in slabs]

    go(proto)

    def go_pair(number):
        go(2 * number)
        go(2 * number + 1)

    count_all = jnp.sum(lives_ref[...][:, :1, :1], 0) * float(rows // images)
    sums = GroupSums(at, links)

    def terms(start, wide):
        cols = pl.ds(start, wide)
        mean, inverse = stat_ref[pl.ds(0, 1), cols], stat_ref[pl.ds(1, 1), cols]
        scale = norm_ref[pl.ds(0, 1), cols] * inverse
        return mean * inverse, inverse, scale, norm_ref[pl.ds(1, 1), cols] - scale * mean

    def slope_of(pre):
        sigma = sigmoid_of(pre)
        return sigma + pre * sigma * (1.0 - sigma)

    def pack(target, wide):
        target[pl.ds(0, 1), :] = jnp.sum(total[0, :, :wide], 0, keepdims=True)
        target[pl.ds(1, 1), :] = jnp.sum(total[1, :, :wide], 0, keepdims=True)

    center_one, inverse_one, scale_one, shift_one = terms(0, middle)
    center_two, inverse_two, scale_two, shift_two = terms(middle, middle)
    scale_three = terms(2 * middle, channels)[2]
    loads["one"].wait()

    def step_act(index):
        span_rows = rows_at(index * tile, tile)
        pre = one[span_rows, :] * scale_one + shift_one
        act_one[span_rows, :] = (pre * sigmoid_of(pre)).astype(low)

    loop(4, step_act)
    go(proto)
    own_out.wait()
    wait_all(out_copies)
    far_copies.append(links(g_out.at[:, 1 - at.far], out_in, at.far_peer))
    value = plus(p_pool[at.sub], pair_land[at.row])
    over.wait()
    value = value + row_land[...].astype(jnp.float32)
    big = NBIG * images
    grad_pool[pl.ds(0, big), :] = value[:big] * (1.0 / (BIG * BIG))
    grad_pool[pl.ds(big, NSMALL * images), :] = value[big:] * (1.0 / (SMALL * SMALL))
    for which in range(2):
        sums_c[pl.ds(which, 1), :] = jnp.sum(grad_pool[...] * slope_ref[which], 0, keepdims=True)
    sums.start(sums_c, land_c)
    loads["curve"].wait()
    loads["normal"].wait()
    both_three = sums.finish()
    vec[...] = extra_ref[...]
    vec[pl.ds(1, 1), :] = both_three[1:2]
    vec[pl.ds(3, 1), :] = both_three[0:1]
    both_three = both_three / count_all

    chunk = channels // 4
    for quarter in range(4):
        cols = pl.ds(quarter * chunk, chunk)
        here = slice(quarter * chunk, (quarter + 1) * chunk)
        base = 0
        for extent, crops in ((BIG, NBIG), (SMALL, NSMALL)):
            lines = crops * images
            into = pl.ds(0, lines) if extent == BIG else pl.ds(big, lines)

            def step_grad(index):
                span_rows = rows_at(base + index * extent * lines, extent * lines)
                curve = wide_low[span_rows, cols].astype(jnp.float32)
                grad = curve.reshape(extent, lines, chunk) * grad_pool[into, cols]
                normal = x_ref[span_rows, cols].astype(jnp.float32)
                back = both_three[0:1, here] + normal * both_three[1:2, here]
                back = back.reshape(extent * crops, images, chunk) * mask
                grad = grad.reshape(extent * crops, images, chunk) - back
                grad = grad.reshape(extent * lines, chunk) * scale_three[:, here]
                wide_low[span_rows, cols] = grad.astype(low)

            loop(extent, step_grad)
            base += extent * extent * lines
    x_copies = copy_rows(h_big, h_small, x_ref, x_sem)
    loads["last"].wait()

    go(proto)
    near_hid, near_out = whole_far(0), whole_far(1)

    def norm_sums(grad, normal):
        total[0, :, :middle] += jnp.sum(grad.reshape(tile // 8, 8, middle), 0)
        total[1, :, :middle] += jnp.sum((grad * normal).reshape(tile // 8, 8, middle), 0)

    loads["two"].wait()
    loads["act"].wait()
    total[...] = jnp.zeros_like(total)

    def step_two(index):
        span_rows = rows_at(index * tile, tile)
        grad = jnp.dot(
            wide_low[span_rows, :],
            last_w[...].reshape(channels, middle),
            preferred_element_type=jnp.float32,
        )
        grad = grad * slope_of(two[span_rows, :] * scale_two + shift_two)
        work[span_rows, :] = grad
        norm_sums(grad, two[span_rows, :] * inverse_two - center_two)

    loop(4, step_two)
    pack(sums_a, middle)
    sums.start(sums_a, land_a)

    def weight_rows(target, left, right):
        part = 256
        shards = max(1, part // height)
        for index in range(channels // part):
            value = cross_rows(left[:, pl.ds(index * part, part)], right[...]).astype(low)
            if shards == 1:
                target[0, index // 2, index % 2] = value
            else:
                some = pl.ds(index * (shards // 2), shards // 2)
                target[0, some] = value.reshape(shards // 2, 2, height, middle)

    weight_rows(g_last, wide_low, act_two)
    go_pair(0)
    go(proto)

    def settle_grad(source, center, inverse, scale, both):
        def step(index):
            span_rows = rows_at(index * tile, tile)
            normal = source[span_rows, :] * inverse - center
            back = both[0:1] + normal * both[1:2]
            back = (back.reshape(tile // 8, 8, middle) * mask).reshape(tile, middle)
            thin_low[span_rows, :] = ((work[span_rows, :] - back) * scale).astype(low)

        loop(4, step)

    both_two = sums.finish()
    settle_grad(two, center_two, inverse_two, scale_two, both_two / count_all)
    vec[pl.ds(0, 1), pl.ds(middle, middle)] = both_two[1:2]
    vec[pl.ds(0, 1), pl.ds(3 * middle, middle)] = both_two[0:1]
    go_pair(0)

    go(proto)

    loads["mid"].wait()
    moves, zeros = tap_blocks(images, True)
    total[...] = jnp.zeros_like(total)
    for part in range(3):
        for slot in range(3):
            cols = pl.ds(slot * middle, middle)
            for target, start, size in moves[3 * part + slot]:
                wide_low[pl.ds(target, size), cols] = thin_low[pl.ds(start, size), :]
            for target, size in zeros[3 * part + slot]:
                wide_low[pl.ds(target, size), cols] = jnp.zeros((size, middle), low)

        for slot in range(3):
            value = cross_rows(act_one[...], wide_low[:, pl.ds(slot * middle, middle)]).astype(low)
            g_mid[3 * part + slot] = value.reshape(g_mid.shape[1:])
        for number in ((1,), (2, 3), (4,))[part]:
            go_pair(number)

        def step_one(index):
            span_rows = rows_at(index * tile, tile)
            grad = against(
                wide_low[span_rows, pl.ds(0, middle)], mid_w[3 * part].reshape(middle, middle)
            )
            for slot in range(1, 3):
                grad = grad + against(
                    wide_low[span_rows, pl.ds(slot * middle, middle)],
                    mid_w[3 * part + slot].reshape(middle, middle),
                )
            if part:
                grad = grad + work[span_rows, :]
            if part == 2:
                grad = grad * slope_of(one[span_rows, :] * scale_one + shift_one)
                norm_sums(grad, one[span_rows, :] * inverse_one - center_one)
            work[span_rows, :] = grad

        loop(4, step_one)
        if part == 2:
            pack(sums_b, middle)
            sums.start(sums_b, land_b)
        for number in ((0, 1), (0, 1, 2, 3), (0, 1, 2, 3, 4))[part]:
            go_pair(number)
        if part == 0:
            go(proto)
        elif part == 1:
            wait_all(flight[proto])
            flight[proto] = []
            own_rows = o_proto.at[at.near, at.far]
            o_proto[at.near, at.far] = proto_own[0]
            proto_copies = [
                links(proto_own.at[0], own_rows, at.near_peer(hop)) for hop in range(1, span)
            ]
        else:
            wait_all(proto_copies)
            slab = o_proto.at[:, at.far]
            proto_copies = [links(slab, slab, at.far_peer)]
    value = whole_near(0, near_hid)
    wide = g_hid.shape[3]
    squares_of(3, value)
    slabs = [o_hid.at[:, lanes_of(which, wide)] for which in (at.sub, at.row_sub)]
    o_hid[:, lanes_of(at.sub, wide)] = value
    hid_row = links(slabs[0], slabs[0], at.row_peer)
    value = whole_near(1, near_out)
    squares_of(4, value)
    o_out[...] = value

    both_one = sums.finish()
    settle_grad(one, center_one, inverse_one, scale_one, both_one / count_all)
    vec[pl.ds(0, 1), pl.ds(0, middle)] = both_one[1:2]
    vec[pl.ds(0, 1), pl.ds(2 * middle, middle)] = both_one[0:1]
    wide = vec.shape[1] // 4
    vec_cols = lanes_of(at.sub, wide)
    vec_copies = [
        links(vec.at[:, vec_cols], vec_land.at[hop], peer)
        for hop, peer in enumerate(at.dp_peers())
    ]
    for number in range(1, 5):
        go_pair(number)
    hid_row.wait()
    final = [links(slab, slab, at.core_peer) for slab in slabs]

    for copy in x_copies:
        copy.wait()
    weight_rows(g_first, x_ref, thin_low)
    go_pair(5)
    go_pair(6)

    numbers = range(len(pieces) // 2)
    tick = 0
    sent = False
    while min(state[:proto]) < 6:
        for number in numbers:
            if state[2 * number] < 6:
                go_pair(number)
        if tick == 1:
            wait_all(vec_copies)
            value = vec[:, vec_cols]
            for hop in range(n_dp - 1):
                value = value + vec_land[hop]
            o_vec[:, vec_cols] = value
            vec_final = [
                links(o_vec.at[:, vec_cols], o_vec.at[:, vec_cols], peer)
                for peer in at.sub_peers()
            ]
        if not sent and min(state[:proto]) >= 5:
            sent = True
            sq_copies = [
                links(sq_mine.at[0], sq_land.at[hop], peer)
                for hop, peer in enumerate(at.dp_peers())
            ]
        tick += 1
    wait_all(sq_copies)
    value = sq_mine[0]
    for hop in range(n_dp - 1):
        value = value + sq_land[hop]
    sq_mine[1] = value
    sq_copies = [
        links(sq_mine.at[1], sq_land.at[n_dp - 1 + hop], peer)
        for hop, peer in enumerate(at.sub_peers())
    ]
    wait_all(sq_copies)
    for hop in range(3):
        value = value + sq_land[n_dp - 1 + hop]
    o_sq[...] = value
    for copies in flight:
        wait_all(copies)
    wait_all(final)
    wait_all(vec_final)
    wait_all(proto_copies)


def backward_trunk(
    n_dp, collective_id, images, pooled, slopes, stat, norms, live, lives, extra, hid, out, proto, big,
    small, curve, normal, one, two, act, last, mid,
):
    span = n_dp // 2
    low, full = jnp.bfloat16, jnp.float32
    rows, channels = curve.shape
    middle = one.shape[1]
    height, mid_height = last.shape[2], mid.shape[3]
    narrow = out.shape[1]
    crops = CROPS * images
    some = jax.ShapeDtypeStruct
    bufs = []
    for index, piece in enumerate(piece_list(height, mid_height, proto.shape[0] // n_dp, ((0, 0),) * 4)):
        taps, block = piece[3], (piece[5], LANES)
        bufs.append(pltpu.VMEM((2, taps, span, 2) + block, low))
        if index % 2 == 0:
            bufs.append(pltpu.VMEM((taps, span, 2) + block, low))
        else:
            bufs.append(pltpu.VMEM((2, taps, span) + block, low))
        bufs.append(pltpu.VMEM((taps, span) + block, low))
        bufs.append(pltpu.VMEM((span - 1, taps) + block, low))
    copies = 15 * (span + 6) + 3 * (span + 4) + 2 * n_dp + 40
    vmem, anywhere = pl.BlockSpec(memory_space=pltpu.VMEM), pl.BlockSpec(memory_space=pl.ANY)
    return pl.pallas_call(
        functools.partial(backward_kernel, n_dp, images),
        out_shape=(
            some((1, height, middle), low),
            some((TAPS, mid_height, middle), low),
            some((1, height, middle), low),
            some((height, 4 * hid.shape[1]), low),
            some((height, narrow), low),
            some((span, 2, proto.shape[0] // n_dp, proto.shape[1]), low),
            some(extra.shape, full),
            some((8, LANES), full),
        ),
        in_specs=[vmem] * 10 + [anywhere] * 9,
        out_specs=(vmem,) * 8,
        scratch_shapes=[
            pltpu.VMEM((rows, channels), low),
            pltpu.VMEM((rows, middle), full),
            pltpu.VMEM((rows, middle), full),
            pltpu.VMEM((rows, middle), low),
            pltpu.VMEM((span, 2, height, middle), low),
            pltpu.VMEM((TAPS, span, 2, mid_height, middle), low),
            pltpu.VMEM((rows, middle), low),
            pltpu.VMEM((rows, channels), low),
            pltpu.VMEM((rows, middle), full),
            pltpu.VMEM((rows, middle), low),
            pltpu.VMEM((1, span, 2, height, middle), low),
            pltpu.VMEM((TAPS, span, 2, mid_height, middle), low),
            pltpu.VMEM((1, span, 2, height, middle), low),
            pltpu.VMEM((2, 8, middle), full),
            pltpu.VMEM((2, crops, channels), low),
            pltpu.VMEM((crops, channels), low),
            pltpu.VMEM((crops, channels), low),
            pltpu.VMEM((crops, channels), full),
            pltpu.VMEM((2, middle), full),
            pltpu.VMEM((3, 2, middle), full),
            pltpu.VMEM((2, middle), full),
            pltpu.VMEM((3, 2, middle), full),
            pltpu.VMEM((2, channels), full),
            pltpu.VMEM((3, 2, channels), full),
            pltpu.VMEM((span, height, hid.shape[1]), low),
            pltpu.VMEM((span, height, hid.shape[1]), low),
            pltpu.VMEM((span - 1, height, hid.shape[1]), low),
            pltpu.VMEM((span, 2, height, narrow), low),
            pltpu.VMEM((span, height, narrow), low),
            pltpu.VMEM((span, height, narrow), low),
            pltpu.VMEM((span - 1, height, narrow), low),
            pltpu.VMEM(extra.shape, full),
            pltpu.VMEM((n_dp - 1, extra.shape[0], extra.shape[1] // 4), full),
            pltpu.VMEM((2, 8, LANES), full),
            pltpu.VMEM((n_dp + 2, 8, LANES), full),
            pltpu.VMEM((1, proto.shape[0] // n_dp, proto.shape[1]), low),
            pltpu.SemaphoreType.DMA((copies,)),
            pltpu.SemaphoreType.DMA((copies,)),
            pltpu.SemaphoreType.DMA((8,)),
            pltpu.SemaphoreType.DMA((2,)),
        ]
        + bufs,
        compiler_params=pltpu.CompilerParams(
            collective_id=collective_id, has_side_effects=True, vmem_limit_bytes=62 * MIB
        ),
        name="backward_trunk",
    )(
        pooled,
        slopes,
        stat,
        norms,
        live,
        lives,
        extra,
        hid.reshape(span, 2, height, hid.shape[1]),
        out.reshape(span // 4, 2, height, narrow),
        proto.reshape(1, span, 2, proto.shape[0] // n_dp, proto.shape[1]),
        big,
        small,
        curve,
        normal,
        one,
        two,
        act,
        last,
        mid,
    )


def sinkhorn_kernel(
    axis,
    count,
    protos,
    queue_ref,
    centers_ref,
    turned_ref,
    pooled_ref,
    hid_ref,
    out_ref,
    norm_ref,
    live_ref,
    lives_ref,
    weigh_ref,
    first_ref,
    proto_grad_ref,
    d_hid_ref,
    d_out_ref,
    back_ref,
    extra_ref,
    partial_ref,
    act,
    normal,
    grads,
    lows,
    embed_ref,
    four,
    four_land,
    grad,
    parts_land,
    kept,
    scores,
    mine,
    landed,
    shift,
    total,
    send_sem,
    recv_sem,
):
    me = lax.axis_index(axis)
    views, rows, _ = queue_ref.shape
    width = turned_ref.shape[1]
    images = live_ref.shape[0]
    tile = row_tile(rows)
    part = 512
    parts = range(0, width, part)
    mask = live_ref[...][:, :1]
    crops = CROPS * images
    share = hid_ref.shape[1]
    low = jnp.bfloat16
    greet(axis, count)

    slots = lax.broadcasted_iota(jnp.int32, (images, 1), 0).astype(jnp.float32)
    masks = [jnp.where(slots < lives_ref[member, :images, :1], 1.0, 0.0) for member in range(count)]
    live_group = sum(lives_ref[member, :1, :1] for member in range(count))
    count_crops = live_group * float(CROPS)

    def spread(values, member):
        return (values.reshape(CROPS, images, values.shape[1]) * masks[member]).reshape(values.shape)

    sums = jnp.zeros((1, share), jnp.float32)
    squares = jnp.zeros((1, share), jnp.float32)
    for member in range(count):
        value = jnp.dot(pooled_ref[member], hid_ref[...], preferred_element_type=jnp.float32)
        normal[member] = value
        masked = spread(value, member)
        sums = sums + jnp.sum(masked, 0, keepdims=True)
        squares = squares + jnp.sum(masked * value, 0, keepdims=True)
    mean = sums / count_crops
    inverse_four = lax.rsqrt(squares / count_crops - mean * mean + norm_eps)
    gain, bias = norm_ref[0:1, :], norm_ref[1:2, :]
    for member in range(count):
        value = (normal[member] - mean) * inverse_four
        normal[member] = value
        pre = value * gain + bias
        act[member] = (pre * sigmoid_of(pre)).astype(low)
        partial_ref[member] = jnp.dot(act[member], out_ref[...], preferred_element_type=jnp.float32)

    def start_group(turn, source, target):
        copies = []
        for hop in range(1, count):
            to = lax.rem(me + hop, count)
            copy = pltpu.make_async_remote_copy(
                src_ref=source(to),
                dst_ref=target(hop),
                send_sem=send_sem.at[turn, hop],
                recv_sem=recv_sem.at[turn, hop],
                device_id={axis: to},
                device_id_type=MESH,
            )
            copy.start()
            copies.append(copy)
        return copies

    def to_group(turn, source, target):
        for copy in start_group(turn, source, target):
            copy.wait()

    to_group(ITERS, lambda to: partial_ref.at[to], lambda hop: parts_land.at[hop])
    embedding = partial_ref[me]
    for hop in range(1, count):
        embedding = embedding + parts_land[hop]
    inverse = lax.rsqrt(jnp.sum(embedding * embedding, 1, keepdims=True) + unit_eps)
    unit = embedding * inverse
    unit_low = unit.astype(jnp.bfloat16)

    def sum_group(turn):
        copies = []
        for hop in range(1, count):
            copy = pltpu.make_async_remote_copy(
                src_ref=mine.at[turn],
                dst_ref=landed.at[turn, hop],
                send_sem=send_sem.at[turn, hop],
                recv_sem=recv_sem.at[turn, hop],
                device_id={axis: lax.rem(me + hop, count)},
                device_id_type=MESH,
            )
            copy.start()
            copies.append(copy)
        for copy in copies:
            copy.wait()
        whole = mine[turn]
        for hop in range(1, count):
            whole = whole + landed[turn, hop]
        return whole

    for start in parts:
        cols = pl.ds(start, part)
        scores[:, cols] = jnp.dot(
            unit_low, turned_ref[:, cols], preferred_element_type=jnp.float32
        )
        for view in range(views):
            lines = pl.ds(view * images, images)
            shares = jnp.exp2(scores[lines, cols] * SINK2) * mask
            mine[0, pl.ds(view, 1), cols] = first_ref[pl.ds(view, 1), cols] + jnp.sum(
                shares, 0, keepdims=True
            )
    real = lax.broadcasted_iota(jnp.int32, (1, width), 1) < protos
    first = sum_group(0)
    shift[...] = jnp.where(real, jnp.log2(first), 1e30)

    for turn in range(1, ITERS):
        for view in range(views):
            lines = pl.ds(view * images, images)
            row = pl.ds(view, 1)
            if turn == 1:
                own = jnp.exp2(scores[lines, :] * SINK2 - shift[row, :]) * mask
                weight = jnp.sum(own, 1, keepdims=True)
            else:
                own = jnp.exp2(scores[lines, :] * SINK2 - first_log[row, :]) * mask
                weight = jnp.sum(own * shift[row, :], 1, keepdims=True)
            total[...] = own / (weight + (1.0 - mask))

            def step(index, carry):
                span = pl.ds(index * tile, tile)
                if turn == 1:
                    lines = queue_ref[view, span, :]
                sums = jnp.zeros((tile, LANES), jnp.float32)
                for start in parts:
                    cols = pl.ds(start, part)
                    if turn == 1:
                        raw = jnp.dot(lines, turned_ref[:, cols], preferred_element_type=jnp.float32)
                        shares = jnp.exp2(raw * SINK2 - shift[row, cols])
                        kept[view, span, cols] = shares
                    else:
                        shares = kept[view, span, cols] * shift[row, cols]
                    for lane in range(0, part, LANES):
                        sums = sums + shares[:, lane : lane + LANES]
                scale = 1.0 / jnp.sum(sums, 1, keepdims=True)
                for start in parts:
                    cols = pl.ds(start, part)
                    scaled = kept[view, span, cols] * scale
                    total[:, cols] += jnp.sum(scaled.reshape(tile // 8, 8, part), 0)
                return carry

            lax.fori_loop(0, rows // tile, step, 0)
            mine[turn, row, :] = jnp.sum(total[...], 0, keepdims=True)
        if turn == 1:
            first_log = shift[...]
        whole = sum_group(turn)
        shift[...] = jnp.where(real, 1.0 / whole, 0.0)

    codes = []
    for view in range(views):
        lines = pl.ds(view * images, images)
        own = jnp.exp2(scores[lines, :] * SINK2 - first_log[view : view + 1, :]) * mask
        own = own * shift[pl.ds(view, 1), :]
        codes.append(own / (jnp.sum(own, 1, keepdims=True) + (1.0 - mask)))
    code_total = codes[0] + codes[1]
    loss = jnp.zeros((images, 1), jnp.float32)
    for crop in range(CROPS):
        lines = pl.ds(crop * images, images)
        raw = jnp.where(real, scores[lines, :] * SOFT2, -1e30)
        raw = raw - jnp.max(raw, 1, keepdims=True)
        powers = jnp.exp2(raw)
        norm = jnp.sum(powers, 1, keepdims=True)
        others = code_total - codes[crop] if crop < NBIG else code_total
        logs = jnp.where(real, (raw - jnp.log2(norm)) / LOG2E, 0.0)
        loss = loss - jnp.sum(others * logs, 1, keepdims=True)
        weight = (NBIG - 1.0 if crop < NBIG else float(NBIG)) * mask / norm
        grad[lines, :] = (weight * powers - others) / (PAIRS * softmax_temp)
    grad_unit = jnp.zeros(unit.shape, jnp.float32)
    for start in parts:
        cols = pl.ds(start, part)
        some = grad[:, cols].astype(jnp.bfloat16)
        grad_unit = grad_unit + jnp.dot(
            some, centers_ref[cols, :], preferred_element_type=jnp.float32
        )
        for first in range(start, start + part, 256):
            value = cross_rows(grad[:, pl.ds(first, 256)].astype(jnp.bfloat16), unit_low)
            lines = pl.ds(first % (width // 4), 256)
            proto_grad_ref[lines, pl.ds(first // (width // 4) * LANES, LANES)] = value.astype(low)
    grad_embed = inverse * (
        grad_unit - unit * jnp.sum(unit * grad_unit, 1, keepdims=True)
    )
    embed_ref[me] = grad_embed.astype(jnp.bfloat16)
    to_group(ITERS + 1, lambda to: embed_ref.at[me], lambda hop: embed_ref.at[me])

    gain_sum = jnp.zeros((1, share), jnp.float32)
    bias_sum = jnp.zeros((1, share), jnp.float32)
    for member in range(count):
        value = against(embed_ref[member], out_ref[...])
        pre = normal[member] * gain + bias
        sigma = sigmoid_of(pre)
        value = value * (sigma + pre * sigma * (1.0 - sigma))
        grads[member] = value
        bias_sum = bias_sum + jnp.sum(value, 0, keepdims=True)
        gain_sum = gain_sum + jnp.sum(value * normal[member], 0, keepdims=True)
    four[pl.ds(0, 1), :] = gain_sum
    four[pl.ds(1, 1), :] = bias_sum
    four[pl.ds(2, 1), :] = jnp.broadcast_to(
        jnp.sum(loss, 0, keepdims=True) / PAIRS, (1, share)
    )
    copies = start_group(ITERS + 2, lambda to: four, lambda hop: four_land.at[hop])
    scale = gain * inverse_four
    for member in range(count):
        value = spread((bias_sum + normal[member] * gain_sum) / count_crops, member)
        lows[member] = ((grads[member] - value) * scale).astype(low)
    embeds = embed_ref[...].reshape(count * crops, embed_ref.shape[2])
    d_out_ref[...] = cross_rows(act[...].reshape(count * crops, share), embeds).astype(low)
    low_rows = lows[...].reshape(count * crops, share)
    for start in range(0, pooled_ref.shape[2], 256):
        left = pooled_ref[:, :, pl.ds(start, 256)].reshape(count * crops, 256)
        d_hid_ref[pl.ds(start, 256), :] = cross_rows(left, low_rows).astype(low)
        back = against(low_rows, hid_ref[pl.ds(start, 256), :]).astype(low)
        back_ref[:, :, pl.ds(start, 256)] = back.reshape(count, crops, 256)
    extra_ref[...] = jnp.zeros_like(extra_ref)
    for copy in copies:
        copy.wait()
    loss_group = jnp.zeros((1, 1), jnp.float32)
    for hop in range(count):
        source = (me + count - hop) % count
        value = four_land[hop] if hop else four[...]
        extra_ref[pl.ds(2, 1), lanes_of(source, share)] = value[0:1]
        extra_ref[pl.ds(4, 1), lanes_of(source, share)] = value[1:2]
        loss_group = loss_group + value[2:3, :1]
    lane = lax.broadcasted_iota(jnp.int32, (1, extra_ref.shape[1]), 1)
    line = jnp.where(lane == 0, loss_group, 0.0) + jnp.where(lane == 1, live_group, 0.0)
    for which in range(5):
        value = jnp.sum(weigh_ref[pl.ds(which, 1), :], 1, keepdims=True)
        line = line + jnp.where(lane == 2 + which, value, 0.0)
    extra_ref[pl.ds(5, 1), :] = line


def sinkhorn(
    sizes, collective_id, protos, queue, centers, turned, pooled, hid, out, norms, live, lives, weigh,
    first,
):
    count = sizes["sub"]
    views, rows, depth = queue.shape
    width = turned.shape[1]
    crops, channels = pooled.shape[1:]
    share = hid.shape[1]
    low, full = jnp.bfloat16, jnp.float32
    some = jax.ShapeDtypeStruct
    turns = ITERS + 3
    return pl.pallas_call(
        functools.partial(sinkhorn_kernel, "sub", count, protos),
        out_shape=(
            some((width // 4, 4 * depth), low),
            some((channels, share), low),
            some((share, depth), low),
            some((count, crops, channels), low),
            some((8, count * share), full),
        ),
        in_specs=[pl.BlockSpec(memory_space=pltpu.VMEM)] * 11,
        out_specs=(pl.BlockSpec(memory_space=pltpu.VMEM),) * 5,
        scratch_shapes=[
            pltpu.VMEM((count, crops, depth), full),
            pltpu.VMEM((count, crops, share), low),
            pltpu.VMEM((count, crops, share), full),
            pltpu.VMEM((count, crops, share), full),
            pltpu.VMEM((count, crops, share), low),
            pltpu.VMEM((count, crops, depth), low),
            pltpu.VMEM((3, share), full),
            pltpu.VMEM((count, 3, share), full),
            pltpu.VMEM((crops, width), full),
            pltpu.VMEM((count, crops, depth), full),
            pltpu.VMEM((views, rows, width), full),
            pltpu.VMEM((crops, width), full),
            pltpu.VMEM((ITERS, views, width), full),
            pltpu.VMEM((ITERS, count, views, width), full),
            pltpu.VMEM((views, width), full),
            pltpu.VMEM((8, width), full),
            pltpu.SemaphoreType.DMA((turns, count)),
            pltpu.SemaphoreType.DMA((turns, count)),
        ],
        compiler_params=pltpu.CompilerParams(
            collective_id=collective_id, has_side_effects=True, vmem_limit_bytes=54 * MIB
        ),
        name="sinkhorn",
    )(queue, centers, turned, pooled, hid, out, norms, live, lives, weigh, first)


def advance(weight, gradient, moment, average, trust):
    step_now = trust * gradient
    moment_new = momentum_rate * moment + step_now
    weight_new = weight - learn_rate * (step_now + momentum_rate * moment_new)
    average_new = average_rate * average + (1.0 - average_rate) * weight_new
    return (weight_new, moment_new, average_new)


def update_kernel(protos, *refs):
    g_first, g_mid, g_last, g_hid, g_out, vec, sq, centers = refs[:8]
    sources, targets = refs[8:26], refs[26:48]
    held, lows = refs[48:66], refs[66:70]
    proto_grad, norm_grad, square, load_sem, save_sem = refs[70:]
    weights, moments, averages = held[:6], held[6:12], held[12:]
    w_outer, w_mid, w_hid, w_out, w_proto, w_norm = weights
    middle = g_first.shape[2]
    loads, saves = {}, []
    for which in (2, 1, 0, 3, 5, 4):
        loads[which] = []
        for part in range(3):
            index = 6 * part + which
            copy = pltpu.make_async_copy(sources[index], held[index], load_sem.at[index])
            copy.start()
            loads[which].append(copy)

    def trust_of(weights, grads):
        return trust_rate * jnp.sqrt(weights) / (jnp.sqrt(grads) + 1e-12)

    def put(which, at, grad, trust):
        new, moment, average = advance(
            weights[which][at],
            grad.astype(jnp.float32),
            moments[which][at],
            averages[which][at],
            trust,
        )
        weights[which][at] = new
        moments[which][at] = moment
        averages[which][at] = average
        if which < 4:
            lows[which][at] = new.astype(jnp.bfloat16)

    def load(which):
        for copy in loads[which]:
            copy.wait()

    def save(which):
        parts = [(held[6 * part + which], 6 * part + which) for part in range(3)]
        if which < 4:
            parts.append((lows[which], 18 + which))
        for source, index in parts:
            copy = pltpu.make_async_copy(source, targets[index], save_sem.at[index])
            copy.start()
            saves.append(copy)

    def matrix_trust(line, lane, share=1.0):
        grads = jnp.sum(sq[pl.ds(line, 1), :], 1, keepdims=True) * share
        return trust_of(vec[5:6, lane : lane + 1], grads)

    trust_hid = matrix_trust(3, 5)
    height = w_hid.shape[0] // 8 if w_hid.shape[0] >= 64 else 8
    load(2)

    def step_hid(index, carry):
        at = pl.ds(pl.multiple_of(index * height, 8), height)
        put(2, at, g_hid[at], trust_hid)
        return carry

    lax.fori_loop(0, w_hid.shape[0] // height, step_hid, 0)
    save(2)
    trust_mid = matrix_trust(1, 4)
    load(1)

    def step_mid(index, carry):
        put(1, index, g_mid[index], trust_mid)
        return carry

    lax.fori_loop(0, TAPS, step_mid, 0)
    save(1)
    load(0)
    for which, (grad, line) in enumerate(((g_first, 0), (g_last, 2))):
        trust = matrix_trust(line, 2 + which)
        height = grad.shape[1] // 4
        for index in range(4):
            lines = pl.ds(index * height, height)
            put(0, (which, lines), grad[0, lines], trust)
    save(0)
    load(3)
    whole = slice(None)
    put(3, whole, g_out[...], matrix_trust(4, 6, 0.25))
    save(3)

    for row, lines in enumerate((((0, 0), 1, 2), ((0, 1), 3, 4))):
        (line, half), wide, last = lines
        start = 2 * middle * half
        norm_grad[pl.ds(row, 1), pl.ds(0, 2 * middle)] = vec[line : line + 1, start : start + 2 * middle]
        size = vec.shape[1]
        norm_grad[pl.ds(row, 1), pl.ds(2 * middle, size)] = vec[wide : wide + 1, :]
        norm_grad[pl.ds(row, 1), pl.ds(2 * middle + size, size)] = vec[last : last + 1, :]
    load(5)
    weight, grad = w_norm[...], norm_grad[...]
    trust = trust_of(
        jnp.sum(weight * weight, 1, keepdims=True), jnp.sum(grad * grad, 1, keepdims=True)
    )
    put(5, whole, grad, trust)
    save(5)

    square[...] = jnp.zeros_like(square)
    load(4)
    fold = centers.shape[0]
    chunks = []
    for quarter in range(4):
        for start in range(0, fold, 256):
            here = quarter * fold + start
            size = min(256, fold - start, protos - here)
            if size > 0:
                chunks.append((pl.ds(here, size), pl.ds(start, size), pl.ds(quarter * LANES, LANES)))
    for at, lines, cols in chunks:
        weight, value = w_proto[at], centers[lines, cols].astype(jnp.float32)
        inverse = lax.rsqrt(jnp.sum(weight * weight, 1, keepdims=True) + unit_eps)
        unit = weight * inverse
        grad = inverse * (value - unit * jnp.sum(unit * value, 1, keepdims=True))
        proto_grad[at] = grad
        weigh(square, 0, weight)
        weigh(square, 1, grad)
    sums = jnp.sum(square[...], 1, keepdims=True)
    trust_proto = trust_of(sums[0:1], sums[1:2])
    for at, lines, cols in chunks:
        put(4, at, proto_grad[at], trust_proto)
    save(4)
    for copy in saves:
        copy.wait()


def update(grads, vec, sq, centers, weights, moments, averages):
    some = jax.ShapeDtypeStruct
    protos = weights[4].shape[0]
    shapes = tuple(some(value.shape, value.dtype) for value in weights)
    lows = tuple(some(value.shape, jnp.bfloat16) for value in weights[:4])
    vmem, anywhere = pl.BlockSpec(memory_space=pltpu.VMEM), pl.BlockSpec(memory_space=pl.ANY)
    results = pl.pallas_call(
        functools.partial(update_kernel, protos),
        out_shape=shapes * 3 + lows,
        in_specs=[vmem] * 8 + [anywhere] * 18,
        out_specs=(anywhere,) * 22,
        scratch_shapes=[pltpu.VMEM(value.shape, value.dtype) for value in shapes * 3 + lows]
        + [
            pltpu.VMEM(weights[4].shape, jnp.float32),
            pltpu.VMEM(weights[5].shape, jnp.float32),
            pltpu.VMEM((8, LANES), jnp.float32),
            pltpu.SemaphoreType.DMA((18,)),
            pltpu.SemaphoreType.DMA((22,)),
        ],
        compiler_params=pltpu.CompilerParams(vmem_limit_bytes=56 * MIB),
        name="update",
    )(*grads, vec, sq, centers, *weights, *moments, *averages)
    return results


def per_device(
    sizes,
    big_maps,
    small_maps,
    live_counts,
    queue,
    bottleneck_outer,
    bottleneck_inner,
    proj_hidden,
    proj_out,
    prototypes,
    norm_params,
    mom_outer,
    mom_inner,
    mom_hidden,
    mom_out,
    mom_protos,
    mom_norms,
    avg_outer,
    avg_inner,
    avg_hidden,
    avg_out,
    avg_protos,
    avg_norms,
):
    n_dp, n_sub = sizes["dp"], sizes["sub"]
    exchange = Exchanger(sizes)
    images = big_maps.shape[0]
    channels = big_maps.shape[-1]
    middle = bottleneck_inner.shape[-1]
    hidden_width = proj_hidden.shape[1]
    out_width = proj_out.shape[1]
    proto_count = prototypes.shape[0]
    unit = max(512, 64 * n_dp)
    proto_width = -(-proto_count // unit) * unit
    here = lax.axis_index("sub")
    share = hidden_width // n_sub

    norm_start = 2 * middle + channels + here * share
    norm_four = lax.dynamic_slice(norm_params, (0, norm_start), (2, share))
    image_mask = (jnp.arange(images) < live_counts[0]).astype(jnp.float32)[:, None]
    live_tile = jnp.broadcast_to(image_mask, (images, LANES))
    big = jnp.transpose(big_maps, (2, 3, 1, 0, 4)).reshape(-1, channels)
    small = jnp.transpose(small_maps, (2, 3, 1, 0, 4)).reshape(-1, channels)

    (
        inner_low, last_w, hidden_low, out_low, hidden_one, hidden_two, act_two, curve, normal,
        trunk_stat, pooled_all, lives, slopes, weights_sq, centers_low, turned, first_sums,
    ) = forward_trunk(
        n_dp,
        exchange.next_id(),
        images,
        bottleneck_outer,
        bottleneck_inner,
        proj_hidden,
        proj_out,
        big,
        small,
        norm_params,
        live_tile,
        queue,
        prototypes,
        proto_width,
    )

    grad_centers, d_hidden, d_out, pooled_back, extra = sinkhorn(
        sizes,
        exchange.next_id(),
        proto_count,
        queue,
        centers_low,
        turned,
        pooled_all,
        hidden_low.reshape(channels, share),
        out_low.reshape(share, out_width),
        norm_four,
        live_tile,
        lives,
        weights_sq,
        first_sums,
    )

    (
        shard_first, shard_inner, shard_last, shard_hidden, shard_out, centers_sum, vector, grad_sq,
    ) = backward_trunk(
        n_dp,
        exchange.next_id(),
        images,
        pooled_back,
        slopes,
        trunk_stat,
        norm_params,
        live_tile,
        lives,
        extra,
        d_hidden,
        d_out,
        grad_centers,
        big,
        small,
        curve,
        normal,
        hidden_one,
        hidden_two,
        act_two,
        last_w,
        inner_low,
    )
    results = update(
        (shard_first, shard_inner, shard_last, shard_hidden, shard_out),
        vector,
        grad_sq,
        centers_sum.reshape(proto_width // 4, 4 * out_width),
        (bottleneck_outer, bottleneck_inner, proj_hidden, proj_out, prototypes, norm_params),
        (mom_outer, mom_inner, mom_hidden, mom_out, mom_protos, mom_norms),
        (avg_outer, avg_inner, avg_hidden, avg_out, avg_protos, avg_norms),
    )
    return (vector[5, 0], vector[5, 1]) + tuple(results)


def solution(mesh):
    data = P(("dp", "sub"), None, None, None, None)
    trees = (P(None, "dp", None), P(None, "dp", None), P("dp", None), P("dp", None), P(), P())
    in_specs = (data, data, P(("dp", "sub")), P(None, ("dp", "sub"), None)) + trees * 3
    out_specs = (P(), P()) + trees * 3 + trees[:4]
    sizes = {axis: mesh.shape[axis] for axis in ("dp", "sub")}
    return jax.shard_map(
        functools.partial(per_device, sizes),
        mesh=mesh,
        in_specs=in_specs,
        out_specs=out_specs,
        check_vma=False,
    )
```

```python
import functools
import math

import jax
import jax.numpy as jnp
from jax import lax
from jax.experimental import pallas as pl
from jax.experimental.pallas import tpu as pltpu
from jax.sharding import PartitionSpec as P

NBIG = 2
NSMALL = 6
CROPS = NBIG + NSMALL
BIG = 7
SMALL = 3
TAPS = 9
ITERS = 3
LANES = 128

sink_temp = 0.05
softmax_temp = 0.1
norm_eps = 1e-05
unit_eps = 1e-12
trust_rate = 0.5
learn_rate = 1.0
momentum_rate = 0.5
average_rate = 0.5

MESH = pl.DeviceIdType.MESH
MIB = 1 << 20
LOG2E = math.log2(math.e)
SINK2 = LOG2E / sink_temp
SOFT2 = LOG2E / softmax_temp
PAIRS = NBIG * (CROPS - 1)


def cross_rows(left, right):
    return lax.dot_general(
        left, right, (((0,), (0,)), ((), ())), preferred_element_type=jnp.float32
    )


def against(left, right):
    return lax.dot_general(
        left, right, (((1,), (1,)), ((), ())), preferred_element_type=jnp.float32
    )


def greet(axis, count):
    me = lax.axis_index(axis)
    barrier = pltpu.get_barrier_semaphore()
    for hop in range(1, count):
        pl.semaphore_signal(
            barrier, inc=1, device_id={axis: lax.rem(me + hop, count)}, device_id_type=MESH
        )
    pl.semaphore_wait(barrier, count - 1)


class Exchanger:
    def __init__(self, sizes):
        self.sizes = sizes
        self.used = 0

    def next_id(self):
        self.used += 1
        return self.used


class Links:
    def __init__(self, send_sem, recv_sem):
        self.send_sem = send_sem
        self.recv_sem = recv_sem
        self.used = 0

    def __call__(self, source, target, device):
        copy = pltpu.make_async_remote_copy(
            src_ref=source,
            dst_ref=target,
            send_sem=self.send_sem.at[self.used],
            recv_sem=self.recv_sem.at[self.used],
            device_id=device,
            device_id_type=MESH,
        )
        self.used += 1
        copy.start()
        return copy


def wait_all(copies):
    for copy in copies:
        copy.wait()


def lanes_of(index, width=LANES):
    return pl.ds(pl.multiple_of(index * width, LANES), width)


class Place:
    def __init__(self, n_dp):
        self.n_dp = n_dp
        self.span = n_dp // 2
        dp, self.sub = lax.axis_index("dp"), lax.axis_index("sub")
        self.dp = dp
        self.near, self.far = dp // 2, dp % 2
        row, core = self.sub // 2, self.sub % 2
        self.row, self.core = row, core
        self.row_sub = 2 * (1 - row) + core
        self.core_sub = 2 * row + (1 - core)
        self.far_peer = {"dp": self.near * 2 + (1 - self.far)}
        self.row_peer = {"sub": self.row_sub}
        self.core_peer = {"sub": self.core_sub}

    def near_index(self, hop):
        return (self.near + hop) % self.span

    def near_peer(self, hop):
        return {"dp": self.near_index(hop) * 2 + self.far}

    def dp_peers(self):
        return [{"dp": (self.dp + hop) % self.n_dp} for hop in range(1, self.n_dp)]

    def sub_peers(self):
        return [{"sub": (self.sub + hop) % 4} for hop in range(1, 4)]

    def greet(self, peers):
        barrier = pltpu.get_barrier_semaphore()
        for peer in peers:
            pl.semaphore_signal(barrier, inc=1, device_id=peer, device_id_type=MESH)
        pl.semaphore_wait(barrier, len(peers))


ALL = slice(None)


def sigmoid_of(values):
    return 0.5 * jnp.tanh(0.5 * values) + 0.5


def rows_at(start, size):
    return pl.ds(start if isinstance(start, int) else pl.multiple_of(start, 16), size)


def tap_blocks(images, flip):
    moves = [[] for _ in range(TAPS)]
    zeros = [[] for _ in range(TAPS)]
    base = 0
    for extent, lines in ((BIG, NBIG * images), (SMALL, NSMALL * images)):
        for tap in range(TAPS):
            down, right = tap // 3 - 1, tap % 3 - 1
            if flip:
                down, right = -down, -right
            for row in range(extent):
                start = base + row * extent * lines
                if not 0 <= row + down < extent:
                    zeros[tap].append((start, extent * lines))
                    continue
                left, stop = max(0, -right), min(extent, extent - right)
                moves[tap].append(
                    (
                        start + left * lines,
                        base + ((row + down) * extent + left + right) * lines,
                        (stop - left) * lines,
                    )
                )
                if left:
                    zeros[tap].append((start, left * lines))
                if stop < extent:
                    zeros[tap].append((start + stop * lines, (extent - stop) * lines))
        base += extent * extent * lines
    return moves, zeros


def fill_columns(columns, source, images, flip):
    wide = source.shape[1]
    moves, zeros = tap_blocks(images, flip)
    for tap in range(TAPS):
        cols = pl.ds(tap * wide, wide)
        for target, start, size in moves[tap]:
            columns[pl.ds(target, size), cols] = source[pl.ds(start, size), :]
        for target, size in zeros[tap]:
            columns[pl.ds(target, size), cols] = jnp.zeros((size, wide), columns.dtype)


def masked_sums(values, mask, total):
    rows, wide = values.shape
    blocks = values.reshape(rows // 8, 8, wide)
    masked = blocks * mask
    total[0] += jnp.sum(masked, 0)
    total[1] += jnp.sum(masked * blocks, 0)


def row_tile(rows):
    return next(size for size in (192, 160, 128, 96, 64, 48, 32, 24, 16, 8) if rows % size == 0)


def centers_of(proto_ref, centers_ref, turned_ref):
    protos, depth = proto_ref.shape
    part = 256
    for start in range(0, turned_ref.shape[1], part):
        here = max(0, min(part, protos - start))
        values = jnp.zeros((part, depth), jnp.float32)
        if here:
            values = proto_ref[pl.ds(start, here), :]
            values = values * lax.rsqrt(jnp.sum(values * values, 1, keepdims=True) + unit_eps)
        if 0 < here < part:
            values = jnp.concatenate([values, jnp.zeros((part - here, depth), jnp.float32)], 0)
        centers_ref[pl.ds(start, part), :] = values.astype(jnp.bfloat16)
        turned_ref[:, pl.ds(start, part)] = values.T.astype(jnp.bfloat16)


def queue_sums(queue_ref, turned_ref, o_ref, total, view):
    rows, width = queue_ref.shape[1], turned_ref.shape[1]
    tile, part = row_tile(rows), 256
    total[...] = jnp.zeros_like(total)

    def step(index, carry):
        lines = queue_ref[view, pl.ds(index * tile, tile), :]
        for start in range(0, width, part):
            cols = pl.ds(start, part)
            scores = jnp.dot(lines, turned_ref[:, cols], preferred_element_type=jnp.float32)
            shares = jnp.exp2(scores * SINK2)
            total[:, cols] += jnp.sum(shares.reshape(tile // 8, 8, part), 0)
        return carry

    lax.fori_loop(0, rows // tile, step, 0)
    o_ref[pl.ds(view, 1), :] = jnp.sum(total[...], 0, keepdims=True)


class GroupSums:
    def __init__(self, at, links):
        self.at, self.links = at, links

    def start(self, mine, land):
        self.mine, self.land = mine, land
        self.copies = [
            self.links(mine, land.at[hop], peer) for hop, peer in enumerate(self.at.sub_peers())
        ]

    def finish(self):
        wait_all(self.copies)
        value = self.mine[...]
        for hop in range(3):
            value = value + self.land[hop]
        return value


def copy_rows(big, small, target, sem):
    split = big.shape[0]
    copies = [
        pltpu.make_async_copy(big, target.at[pl.ds(0, split)], sem.at[0]),
        pltpu.make_async_copy(small, target.at[pl.ds(split, small.shape[0])], sem.at[1]),
    ]
    for copy in copies:
        copy.start()
    return copies


def weigh(target, line, values):
    sums = jnp.sum(values * values, 0, keepdims=True)
    for lane in range(0, sums.shape[1], LANES):
        target[pl.ds(line, 1), :] += sums[:, lane : lane + LANES]


def forward_kernel(n_dp, images, *refs):
    i_outer, i_mid, i_hid, i_out, h_big, h_small, norm_ref, live_ref, queue_ref, proto_ref = refs[:10]
    (
        o_mid, o_last, o_hid, o_out, o_one, o_two, o_act, o_curve, o_normal, o_stat, o_pooled, o_live,
        o_slope, o_weigh, o_centers, o_turned, o_queue,
    ) = refs[10:27]
    (
        x_ref, w_first, w_mid, w_last, w_hid, w_out, first_w, mid_w, last_w, out_w, columns, act_one,
        act_two, one, two, three, total, pool, sums_a, land_a, sums_b, land_b, sums_c, land_c, pooled,
        queue_total, send_sem, recv_sem, own_sem, x_sem,
    ) = refs[27:]
    at = Place(n_dp)
    links = Links(send_sem, recv_sem)
    x_copies = copy_rows(h_big, h_small, x_ref, x_sem)
    share = w_hid.shape[1]
    w_first[...] = i_outer[0].astype(w_first.dtype)
    at.greet(
        [at.near_peer(hop) for hop in range(1, at.span)] + [at.far_peer] + at.sub_peers()
    )
    low = jnp.bfloat16
    middle = first_w.shape[3]
    channels = x_ref.shape[1]
    rows = x_ref.shape[0]
    mask = live_ref[...][:, :1]
    half = middle // 2

    def flat(source, target, start, size, split):
        line = source.shape[0] // 4
        some = pl.ds(start * line, size * line)
        return (
            lambda cols: source.at[some, cols],
            lambda near, far, cols: target.at[near, far, some, cols],
            split,
        )

    def taps(start, size, split):
        some = pl.ds(start, size)
        return (
            lambda cols: w_mid.at[some, :, cols],
            lambda near, far, cols: mid_w.at[some, near, far, :, cols],
            split,
        )

    quarter = w_out.shape[0] // 4
    out_rows = pl.ds(at.sub * quarter, quarter)
    pieces = [flat(w_first, first_w, 0, 2, 4), flat(w_first, first_w, 2, 2, 4)]
    groups = (((0, 1, 2), (1, 2, 4)), ((3, 1, 4), (4, 1, 2), (5, 2, 4)), ((7, 1, 4), (8, 1, 2)))
    last_of = []
    for group in groups:
        pieces += [taps(*some) for some in group]
        last_of.append(len(pieces))
    pieces += [flat(w_last, last_w, 0, 2, 4), flat(w_last, last_w, 2, 1, 2), flat(w_last, last_w, 3, 1, 4)]
    trunk_pieces = len(pieces)
    pieces += [flat(w_hid, o_hid, part, 1, 1) for part in range(4)]
    pieces.append(
        (
            lambda cols: w_out.at[out_rows],
            lambda near, far, cols: out_w.at[near, far],
            1,
        )
    )
    count = len(pieces)
    mine = {4: lanes_of(at.sub), 2: lanes_of(at.core, half), 1: ALL}
    own, first, second, third, fourth = [], [], [], [], []

    def begin(index):
        if index < count:
            source, target, split = pieces[index]
            cols = mine[split]
            copy = pltpu.make_async_copy(
                source(cols), target(at.near, at.far, cols), own_sem.at[index]
            )
            copy.start()
            own.append(copy)
            first.append(
                [
                    links(source(cols), target(at.near, at.far, cols), at.near_peer(hop))
                    for hop in range(1, at.span)
                ]
            )

    begin(0)
    begin(1)

    def cast_tap(index, carry):
        w_mid[index] = i_mid[index].astype(w_mid.dtype)
        return carry

    lax.fori_loop(0, TAPS, cast_tap, 0)
    begin(2)
    w_last[...] = i_outer[1].astype(w_last.dtype)
    w_hid[...] = i_hid[:, lanes_of(at.sub, share)].astype(w_hid.dtype)
    w_out[...] = i_out[...].astype(w_out.dtype)
    lag = 2
    clock = [0]

    def pump(times=1):
        for _ in range(times):
            tick(clock[0])
            clock[0] += 1

    def need(index):
        while clock[0] <= index + 2 * lag:
            pump()
        wait_all(fourth[index])

    def tick(now):
        if now < count:
            source, target, split = pieces[now]
            own[now].wait()
            wait_all(first[now])
            begin(now + 3)
            slab = target(ALL, at.far, mine[split])
            second.append(links(slab, slab, at.far_peer))
        past = now - lag
        if 0 <= past < count:
            source, target, split = pieces[past]
            second[past].wait()
            slab = target(ALL, ALL, mine[split])
            third.append(links(slab, slab, at.row_peer) if split == 4 else None)
            fourth.append([links(slab, slab, at.core_peer)] if split == 2 else [])
        past = now - 2 * lag
        if 0 <= past < count and pieces[past][2] == 4:
            source, target, split = pieces[past]
            third[past].wait()
            slabs = [target(ALL, ALL, cols) for cols in (mine[4], lanes_of(at.row_sub))]
            fourth[past] = [links(slab, slab, at.core_peer) for slab in slabs]

    tile = rows // 4
    sums = GroupSums(at, links)

    def pack(target, wide):
        target[pl.ds(0, 1), :] = jnp.sum(total[0, :, :wide], 0, keepdims=True)
        target[pl.ds(1, 1), :] = jnp.sum(total[1, :, :wide], 0, keepdims=True)

    def settle(value, count_all, start, wide):
        mean = value[0:1] / count_all
        inverse = lax.rsqrt(value[1:2] / count_all - mean * mean + norm_eps)
        o_stat[pl.ds(0, 1), pl.ds(start, wide)] = mean
        o_stat[pl.ds(1, 1), pl.ds(start, wide)] = inverse
        scale = norm_ref[pl.ds(0, 1), pl.ds(start, wide)] * inverse
        return scale, norm_ref[pl.ds(1, 1), pl.ds(start, wide)] - scale * mean

    centers_of(proto_ref, o_centers, o_turned)
    pump()
    queue_sums(queue_ref, o_turned, o_queue, queue_total, 0)
    pump()
    queue_sums(queue_ref, o_turned, o_queue, queue_total, 1)
    pump()
    o_weigh[...] = jnp.zeros_like(o_weigh)
    weigh(o_weigh, 0, i_outer[0])
    weigh(o_weigh, 1, i_outer[1])
    weigh(o_weigh, 4, i_out[...])

    def weigh_tap(index, carry):
        weigh(o_weigh, 2, i_mid[index])
        return carry

    lax.fori_loop(0, TAPS, weigh_tap, 0)
    pump()

    def weigh_part(index, carry):
        weigh(o_weigh, 3, i_hid[:, lanes_of(index, 512)])
        return carry

    lax.fori_loop(0, i_hid.shape[1] // 512, weigh_part, 0)
    need(0)
    need(1)
    pump()
    for copy in x_copies:
        copy.wait()

    total[...] = jnp.zeros_like(total)

    def step_one(index, carry):
        span = rows_at(index * tile, tile)
        value = jnp.dot(
            x_ref[span, :],
            first_w[...].reshape(channels, middle),
            preferred_element_type=jnp.float32,
        )
        one[span, :] = value
        masked_sums(value, mask, total.at[:, :, pl.ds(0, middle)])
        return carry

    lax.fori_loop(0, 4, step_one, 0)
    pack(sums_a, middle)
    live = jnp.sum(mask, 0, keepdims=True)
    sums_a[pl.ds(2, 1), :] = jnp.broadcast_to(live, (1, middle))
    sums.start(sums_a, land_a)
    pump()
    value = sums.finish()
    per_image = rows // images
    lives = value[2:3, :1]
    count_all = lives * per_image
    o_live[at.sub] = jnp.broadcast_to(live, o_live.shape[1:])
    for hop in range(3):
        o_live[(at.sub + 3 - hop) % 4] = jnp.broadcast_to(land_a[hop, 2:3, :1], o_live.shape[1:])
    scale, shift = settle(value, count_all, 0, middle)

    def step_act(source, target):
        def step(index, carry):
            span = rows_at(index * tile, tile)
            pre = source[span, :] * scale + shift
            target[span, :] = (pre * sigmoid_of(pre)).astype(low)
            return carry

        lax.fori_loop(0, 4, step, 0)

    step_act(one, act_one)
    save = [pltpu.make_async_copy(one, o_one, own_sem.at[count])]
    save[-1].start()
    pump()
    fill_columns(columns, act_one, images, False)

    total[...] = jnp.zeros_like(total)
    for part in range(3):
        for index in range(last_of[part] - len(groups[part]), last_of[part]):
            need(index)

        def step_two(index, carry):
            span = rows_at(index * tile, tile)
            value = jnp.dot(
                columns[span, pl.ds(part * 3 * middle, 3 * middle)],
                mid_w[pl.ds(part * 3, 3)].reshape(3 * middle, middle),
                preferred_element_type=jnp.float32,
            )
            if part:
                value = value + two[span, :]
            two[span, :] = value
            if part == 2:
                masked_sums(value, mask, total.at[:, :, pl.ds(0, middle)])
            return carry

        lax.fori_loop(0, 4, step_two, 0)
    save.append(pltpu.make_async_copy(mid_w, o_mid, own_sem.at[count + 2]))
    save[-1].start()
    pack(sums_b, middle)
    sums.start(sums_b, land_b)
    scale, shift = settle(sums.finish(), count_all, middle, middle)
    step_act(two, act_two)
    save.append(pltpu.make_async_copy(two, o_two, own_sem.at[count + 3]))
    save[-1].start()
    save.append(pltpu.make_async_copy(act_two, o_act, own_sem.at[count + 4]))
    save[-1].start()

    for index in range(trunk_pieces - 3, trunk_pieces):
        need(index)
    save.append(pltpu.make_async_copy(last_w, o_last, own_sem.at[count + 5]))
    save[-1].start()
    total[...] = jnp.zeros_like(total)

    def step_three(index, carry):
        span = rows_at(index * tile, tile)
        for quarter in range(4):
            wide = channels // 4
            cols = pl.ds(quarter * wide, wide)
            weights = last_w[pl.ds(quarter * (at.span // 4), at.span // 4)].reshape(wide, middle)
            value = against(act_two[span, :], weights)
            three[span, cols] = value
            masked_sums(value, mask, total.at[:, :, cols])
        return carry

    lax.fori_loop(0, 4, step_three, 0)
    pack(sums_c, channels)
    sums.start(sums_c, land_c)
    pump()
    scale, shift = settle(sums.finish(), count_all, 2 * middle, channels)

    pool[...] = jnp.zeros_like(pool)
    o_slope[...] = jnp.zeros_like(o_slope)
    wide = pl.ds(2 * middle, channels)
    center = o_stat[pl.ds(0, 1), wide] * o_stat[pl.ds(1, 1), wide]
    base = 0
    for extent, crops in ((BIG, NBIG), (SMALL, NSMALL)):
        lines = crops * images
        into = pl.ds(0, lines) if extent == BIG else pl.ds(NBIG * images, lines)

        def step_out(index, carry):
            span = rows_at(base + index * extent * lines, extent * lines)
            for start in range(0, channels, 512):
                cols = pl.ds(start, 512)
                pre = three[span, cols] * scale[:, start : start + 512]
                pre = pre + shift[:, start : start + 512] + x_ref[span, cols].astype(jnp.float32)
                sigma = sigmoid_of(pre)
                value = pre * sigma
                slope = sigma + value * (1.0 - sigma)
                normal = three[span, cols] * o_stat[1:2, 2 * middle + start : 2 * middle + start + 512]
                normal = normal - center[:, start : start + 512]
                columns[span, cols] = slope.astype(low)
                columns[span, pl.ds(channels + start, 512)] = normal.astype(low)
                pool[into, cols] += jnp.sum(value.reshape(extent, lines, 512), 0)
                o_slope[0, into, cols] += jnp.sum(slope.reshape(extent, lines, 512), 0)
                slope = slope * normal
                o_slope[1, into, cols] += jnp.sum(slope.reshape(extent, lines, 512), 0)
            return carry

        lax.fori_loop(0, extent, step_out, 0)
        pump()
        pooled[into, :] = (pool[into, :] * (1.0 / (extent * extent))).astype(low)
        base += extent * extent * lines

    for index, target in enumerate((o_curve, o_normal)):
        some = columns.at[:, pl.ds(index * channels, channels)]
        save.append(pltpu.make_async_copy(some, target, x_sem.at[index]))
        save[-1].start()

    over = links(pooled, o_pooled.at[at.sub], at.row_peer)
    pair = links(pooled, o_pooled.at[at.sub], at.core_peer)
    o_pooled[at.sub] = pooled[...]
    pump()
    over.wait()
    last = links(o_pooled.at[at.row_sub], o_pooled.at[at.row_sub], at.core_peer)
    need(count - 1)
    some = at.span // 4
    out_own = out_w.at[pl.ds(at.sub * some, some)]
    into = o_out.at[:, :, out_rows]
    own.append(pltpu.make_async_copy(out_own, into, own_sem.at[count - 1]))
    own[-1].start()
    out_copies = [
        links(out_w.at[pl.ds(peer["sub"] * some, some)], into, peer) for peer in at.sub_peers()
    ]
    pair.wait()
    last.wait()
    own[-1].wait()
    wait_all(out_copies)
    for copy in save:
        copy.wait()


def forward_trunk(
    n_dp, collective_id, images, outer, mid, hid, out, big, small, norms, live, queue, prototypes, width
):
    span = n_dp // 2
    height, middle = outer.shape[1:]
    rows, channels = big.shape[0] + small.shape[0], big.shape[1]
    share, narrow = hid.shape[1] // 4, out.shape[1]
    some = jax.ShapeDtypeStruct
    low, full = jnp.bfloat16, jnp.float32
    copies = 17 * (span + 4) + 16
    vmem, anywhere = pl.BlockSpec(memory_space=pltpu.VMEM), pl.BlockSpec(memory_space=pl.ANY)
    return pl.pallas_call(
        functools.partial(forward_kernel, n_dp, images),
        out_shape=(
            some((TAPS, span, 2, mid.shape[1], middle), low),
            some((span, 2, height, middle), low),
            some((span, 2, height, share), low),
            some((span // 4, 2, height, narrow), low),
            some((rows, middle), full),
            some((rows, middle), full),
            some((rows, middle), low),
            some((rows, channels), low),
            some((rows, channels), low),
            some((2, 2 * middle + channels), full),
            some((4, CROPS * images, channels), low),
            some((4, 8, LANES), full),
            some((2, CROPS * images, channels), full),
            some((8, LANES), full),
            some((width, prototypes.shape[1]), low),
            some((prototypes.shape[1], width), low),
            some((queue.shape[0], width), full),
        ),
        in_specs=[vmem] * 4 + [anywhere] * 2 + [vmem] * 4,
        out_specs=(anywhere,) * 9 + (vmem,) * 8,
        scratch_shapes=[
            pltpu.VMEM((rows, channels), low),
            pltpu.VMEM((height, middle), low),
            pltpu.VMEM(mid.shape, low),
            pltpu.VMEM((height, middle), low),
            pltpu.VMEM((height, share), low),
            pltpu.VMEM((height, narrow), low),
            pltpu.VMEM((span, 2, height, middle), low),
            pltpu.VMEM((TAPS, span, 2, mid.shape[1], middle), low),
            pltpu.VMEM((span, 2, height, middle), low),
            pltpu.VMEM((span, 2, height // 4, narrow), low),
            pltpu.VMEM((rows, TAPS * middle), low),
            pltpu.VMEM((rows, middle), low),
            pltpu.VMEM((rows, middle), low),
            pltpu.VMEM((rows, middle), full),
            pltpu.VMEM((rows, middle), full),
            pltpu.VMEM((rows, channels), full),
            pltpu.VMEM((2, 8, channels), full),
            pltpu.VMEM((CROPS * images, channels), full),
            pltpu.VMEM((3, middle), full),
            pltpu.VMEM((3, 3, middle), full),
            pltpu.VMEM((2, middle), full),
            pltpu.VMEM((3, 2, middle), full),
            pltpu.VMEM((2, channels), full),
            pltpu.VMEM((3, 2, channels), full),
            pltpu.VMEM((CROPS * images, channels), low),
            pltpu.VMEM((8, width), full),
            pltpu.SemaphoreType.DMA((copies,)),
            pltpu.SemaphoreType.DMA((copies,)),
            pltpu.SemaphoreType.DMA((17 + 6,)),
            pltpu.SemaphoreType.DMA((2,)),
        ],
        compiler_params=pltpu.CompilerParams(
            collective_id=collective_id, has_side_effects=True, vmem_limit_bytes=62 * MIB
        ),
        name="forward_trunk",
    )(outer, mid, hid, out, big, small, norms, live, queue, prototypes)


def plus(left, right):
    return left.astype(jnp.float32) + right.astype(jnp.float32)


def piece_list(height, mid_height, proto_height, refs):
    first, mid, last, proto = refs
    half, quarter = height // 2, height // 4
    pieces = [last + (0, 1, part * half, half, 2) for part in range(2)]
    for start, taps in ((0, 1), (1, 1), (2, 1), (3, 1), (4, 1), (5, 1), (6, 1), (7, 2)):
        pieces.append(mid + (start, taps, 0, mid_height, 1))
    pieces += [first + (0, 1, part * quarter, quarter, 0) for part in range(4)]
    return pieces + [proto + (0, 1, 0, proto_height, 5)]


def backward_kernel(n_dp, images, *refs):
    p_pool, slope_ref, stat_ref, norm_ref, live_ref, lives_ref, extra_ref, g_hid, g_some, g_proto = refs[:10]
    h_big, h_small, h_curve, h_normal, h_one, h_two, h_act, h_last, h_mid = refs[10:19]
    o_first, o_mid, o_last, o_hid, o_out, o_proto, o_vec, o_sq = refs[19:27]
    (
        x_ref, one, two, act_two, last_w, mid_w, act_one, wide_low, work, thin_low, g_first, g_mid,
        g_last, total, pair_land, pair_sum, row_land, grad_pool, sums_a, land_a, sums_b, land_b,
        sums_c, land_c, hid_in, hid_sum, hid_land, g_out, out_in, out_sum, out_land, vec, vec_land,
        sq_mine, sq_land, send_sem, recv_sem, own_sem, x_sem,
    ) = refs[27:66]
    bufs = refs[66:]
    at = Place(n_dp)
    links = Links(send_sem, recv_sem)
    span = at.span
    at.greet(at.dp_peers() + at.sub_peers())
    low = jnp.bfloat16
    rows, channels = x_ref.shape
    middle = one.shape[1]
    height = g_last.shape[3]
    mask = live_ref[...][:, :1]
    tile = rows // 4

    loads = {}
    for index, (name, source, target) in enumerate(
        (
            ("one", h_one, one), ("curve", h_curve, wide_low), ("normal", h_normal, x_ref),
            ("last", h_last, last_w), ("two", h_two, two), ("act", h_act, act_two), ("mid", h_mid, mid_w),
        )
    ):
        loads[name] = pltpu.make_async_copy(source, target, own_sem.at[index])
        loads[name].start()

    pair = [
        links(p_pool.at[2 * line + (1 - at.core)], pair_land.at[line], at.core_peer)
        for line in (1 - at.row, at.row)
    ]
    far_copies = [links(g_hid.at[:, 1 - at.far], hid_in, at.far_peer)]
    some = g_some.shape[0]
    block = g_out.at[pl.ds(at.sub * some, some)]
    own_out = pltpu.make_async_copy(g_some, block, own_sem.at[7])
    own_out.start()
    out_copies = [links(g_some, block, peer) for peer in at.sub_peers()]
    pair[0].wait()
    pair_sum[...] = plus(p_pool[2 * (1 - at.row) + at.core], pair_land[1 - at.row]).astype(low)
    over = links(pair_sum, row_land, at.row_peer)
    pair[1].wait()

    wholes = [(g_hid, hid_in, hid_sum, hid_land), (g_out, out_in, out_sum, out_land)]

    def whole_far(which):
        source, landed, summed, land = wholes[which]
        far_copies[which].wait()
        for near in range(span):
            summed[near] = plus(source[near, at.far], landed[near]).astype(low)
        return [
            links(summed.at[at.near_index(hop)], land.at[hop - 1], at.near_peer(hop))
            for hop in range(1, span)
        ]

    def whole_near(which, copies):
        source, landed, summed, land = wholes[which]
        wait_all(copies)
        value = summed[at.near].astype(jnp.float32)
        for hop in range(1, span):
            value = value + land[hop - 1].astype(jnp.float32)
        return value.astype(low)

    sq_mine[0] = jnp.zeros_like(sq_mine[0])

    def squares_of(matrix, value):
        value = value.astype(jnp.float32)
        line = jnp.sum(value * value, 0, keepdims=True)
        for lane in range(0, line.shape[1], LANES):
            sq_mine[0, pl.ds(matrix, 1), :] += line[:, lane : lane + LANES]

    pieces = piece_list(
        height,
        g_mid.shape[3],
        g_proto.shape[3],
        ((g_first, o_first), (g_mid, o_mid), (g_last, o_last), (g_proto, o_proto)),
    )
    proto = len(pieces) - 1
    mine, beside = lanes_of(at.sub), lanes_of(at.row_sub)
    state = [0] * len(pieces)
    flight = [None] * len(pieces)

    def loop(count, body):
        def step(index, carry):
            body(index)
            return carry

        lax.fori_loop(0, count, step, 0)

    def go(index):
        source, target, start, taps, line, size, matrix = pieces[index]
        held, second, third, nears = bufs[4 * index : 4 * index + 4]
        stage = state[index]
        state[index] += 1
        row_first = index % 2 == 0
        lines, some = pl.ds(line, size), pl.ds(start, taps)
        if stage == 0:
            flight[index] = [
                links(
                    source.at[some, :, :, lines, lanes_of(2 * row + (1 - at.core))],
                    held.at[row],
                    at.core_peer,
                )
                for row in range(2)
            ]
            return
        wait_all(flight[index])
        if stage == 1:
            for row in range(2):
                cols = lanes_of(2 * row + at.core)

                def body(at_block):
                    tap, near, far = at_block // (2 * span), at_block // 2 % span, at_block % 2
                    held[row, tap, near, far] = plus(
                        source[start + tap, near, far, lines, cols], held[row, tap, near, far]
                    ).astype(low)

                loop(taps * span * 2, body)
            if row_first:
                flight[index] = [links(held.at[1 - at.row], second, at.row_peer)]
            else:
                flight[index] = [links(held.at[:, :, :, 1 - at.far], second, at.far_peer)]
        elif stage == 2:
            if row_first:

                def body(at_block):
                    tap, near, far = at_block // (2 * span), at_block // 2 % span, at_block % 2
                    second[tap, near, far] = plus(
                        held[at.row, tap, near, far], second[tap, near, far]
                    ).astype(low)

                loop(taps * span * 2, body)
                flight[index] = [links(second.at[:, :, 1 - at.far], third, at.far_peer)]
            else:

                def body(at_block):
                    row, tap, near = at_block // (taps * span), at_block // span % taps, at_block % span
                    second[row, tap, near] = plus(
                        held[row, tap, near, at.far], second[row, tap, near]
                    ).astype(low)

                loop(taps * span * 2, body)
                flight[index] = [links(second.at[1 - at.row], third, at.row_peer)]
        elif stage == 3:

            def body(at_block):
                tap, near = at_block // span, at_block % span
                part = second[tap, near, at.far] if row_first else second[at.row, tap, near]
                third[tap, near] = plus(part, third[tap, near]).astype(low)

            loop(taps * span, body)
            flight[index] = [
                links(third.at[:, at.near_index(hop)], nears.at[hop - 1], at.near_peer(hop))
                for hop in range(1, span)
            ]
        elif stage == 4 and index == proto:
            value = third[0, at.near].astype(jnp.float32)
            for hop in range(1, span):
                value = value + nears[hop - 1, 0].astype(jnp.float32)
            o_proto[at.near, at.far, :, mine] = value.astype(low)
            slab = o_proto.at[at.near, at.far, :, mine]
            flight[index] = [links(slab, slab, at.near_peer(hop)) for hop in range(1, span)]
        elif stage == 5 and index == proto:
            slab = o_proto.at[:, at.far, :, mine]
            flight[index] = [links(slab, slab, at.far_peer)]
        elif stage == 6:
            slab = o_proto.at[:, :, :, mine]
            flight[index] = [links(slab, slab, at.row_peer)]
        elif stage == 7:
            slabs = [o_proto.at[:, :, :, cols] for cols in (mine, beside)]
            flight[index] = [links(slab, slab, at.core_peer) for slab in slabs]
        elif stage == 4:
            for tap in range(taps):
                value = third[tap, at.near].astype(jnp.float32)
                for hop in range(1, span):
                    value = value + nears[hop - 1, tap].astype(jnp.float32)
                value = value.astype(low)
                squares_of(matrix, value)
                target[start + tap, lines, mine] = value
            slab = target.at[some, lines, mine]
            flight[index] = [links(slab, slab, at.row_peer)]
        elif stage == 5:
            slabs = [target.at[some, lines, cols] for cols in (mine, beside)]
            flight[index] = [links(slab, slab, at.core_peer) for slab in slabs]

    go(proto)

    def go_pair(number):
        go(2 * number)
        go(2 * number + 1)

    count_all = jnp.sum(lives_ref[...][:, :1, :1], 0) * float(rows // images)
    sums = GroupSums(at, links)

    def terms(start, wide):
        cols = pl.ds(start, wide)
        mean, inverse = stat_ref[pl.ds(0, 1), cols], stat_ref[pl.ds(1, 1), cols]
        scale = norm_ref[pl.ds(0, 1), cols] * inverse
        return mean * inverse, inverse, scale, norm_ref[pl.ds(1, 1), cols] - scale * mean

    def slope_of(pre):
        sigma = sigmoid_of(pre)
        return sigma + pre * sigma * (1.0 - sigma)

    def pack(target, wide):
        target[pl.ds(0, 1), :] = jnp.sum(total[0, :, :wide], 0, keepdims=True)
        target[pl.ds(1, 1), :] = jnp.sum(total[1, :, :wide], 0, keepdims=True)

    center_one, inverse_one, scale_one, shift_one = terms(0, middle)
    center_two, inverse_two, scale_two, shift_two = terms(middle, middle)
    scale_three = terms(2 * middle, channels)[2]
    loads["one"].wait()

    def step_act(index):
        span_rows = rows_at(index * tile, tile)
        pre = one[span_rows, :] * scale_one + shift_one
        act_one[span_rows, :] = (pre * sigmoid_of(pre)).astype(low)

    loop(4, step_act)
    go(proto)
    own_out.wait()
    wait_all(out_copies)
    far_copies.append(links(g_out.at[:, 1 - at.far], out_in, at.far_peer))
    value = plus(p_pool[at.sub], pair_land[at.row])
    over.wait()
    value = value + row_land[...].astype(jnp.float32)
    big = NBIG * images
    grad_pool[pl.ds(0, big), :] = value[:big] * (1.0 / (BIG * BIG))
    grad_pool[pl.ds(big, NSMALL * images), :] = value[big:] * (1.0 / (SMALL * SMALL))
    for which in range(2):
        sums_c[pl.ds(which, 1), :] = jnp.sum(grad_pool[...] * slope_ref[which], 0, keepdims=True)
    sums.start(sums_c, land_c)
    loads["curve"].wait()
    loads["normal"].wait()
    both_three = sums.finish()
    vec[...] = extra_ref[...]
    vec[pl.ds(1, 1), :] = both_three[1:2]
    vec[pl.ds(3, 1), :] = both_three[0:1]
    both_three = both_three / count_all
    go(proto)

    chunk = channels // 4
    for quarter in range(4):
        cols = pl.ds(quarter * chunk, chunk)
        here = slice(quarter * chunk, (quarter + 1) * chunk)
        base = 0
        for extent, crops in ((BIG, NBIG), (SMALL, NSMALL)):
            lines = crops * images
            into = pl.ds(0, lines) if extent == BIG else pl.ds(big, lines)

            def step_grad(index):
                span_rows = rows_at(base + index * extent * lines, extent * lines)
                curve = wide_low[span_rows, cols].astype(jnp.float32)
                grad = curve.reshape(extent, lines, chunk) * grad_pool[into, cols]
                normal = x_ref[span_rows, cols].astype(jnp.float32)
                back = both_three[0:1, here] + normal * both_three[1:2, here]
                back = back.reshape(extent * crops, images, chunk) * mask
                grad = grad.reshape(extent * crops, images, chunk) - back
                grad = grad.reshape(extent * lines, chunk) * scale_three[:, here]
                wide_low[span_rows, cols] = grad.astype(low)

            loop(extent, step_grad)
            base += extent * extent * lines
    x_copies = copy_rows(h_big, h_small, x_ref, x_sem)
    loads["last"].wait()

    go(proto)
    near_hid, near_out = whole_far(0), whole_far(1)

    def norm_sums(grad, normal):
        total[0, :, :middle] += jnp.sum(grad.reshape(tile // 8, 8, middle), 0)
        total[1, :, :middle] += jnp.sum((grad * normal).reshape(tile // 8, 8, middle), 0)

    loads["two"].wait()
    loads["act"].wait()
    total[...] = jnp.zeros_like(total)

    def step_two(index):
        span_rows = rows_at(index * tile, tile)
        grad = jnp.dot(
            wide_low[span_rows, :],
            last_w[...].reshape(channels, middle),
            preferred_element_type=jnp.float32,
        )
        grad = grad * slope_of(two[span_rows, :] * scale_two + shift_two)
        work[span_rows, :] = grad
        norm_sums(grad, two[span_rows, :] * inverse_two - center_two)

    loop(4, step_two)
    pack(sums_a, middle)
    sums.start(sums_a, land_a)

    def weight_rows(target, left, right):
        part = 256
        shards = max(1, part // height)
        for index in range(channels // part):
            value = cross_rows(left[:, pl.ds(index * part, part)], right[...]).astype(low)
            if shards == 1:
                target[0, index // 2, index % 2] = value
            else:
                some = pl.ds(index * (shards // 2), shards // 2)
                target[0, some] = value.reshape(shards // 2, 2, height, middle)

    weight_rows(g_last, wide_low, act_two)
    go_pair(0)

    def settle_grad(source, center, inverse, scale, both):
        def step(index):
            span_rows = rows_at(index * tile, tile)
            normal = source[span_rows, :] * inverse - center
            back = both[0:1] + normal * both[1:2]
            back = (back.reshape(tile // 8, 8, middle) * mask).reshape(tile, middle)
            thin_low[span_rows, :] = ((work[span_rows, :] - back) * scale).astype(low)

        loop(4, step)

    both_two = sums.finish()
    settle_grad(two, center_two, inverse_two, scale_two, both_two / count_all)
    vec[pl.ds(0, 1), pl.ds(middle, middle)] = both_two[1:2]
    vec[pl.ds(0, 1), pl.ds(3 * middle, middle)] = both_two[0:1]
    go_pair(0)

    loads["mid"].wait()
    moves, zeros = tap_blocks(images, True)
    total[...] = jnp.zeros_like(total)
    for part in range(3):
        for slot in range(3):
            cols = pl.ds(slot * middle, middle)
            for target, start, size in moves[3 * part + slot]:
                wide_low[pl.ds(target, size), cols] = thin_low[pl.ds(start, size), :]
            for target, size in zeros[3 * part + slot]:
                wide_low[pl.ds(target, size), cols] = jnp.zeros((size, middle), low)

        for slot in range(3):
            value = cross_rows(act_one[...], wide_low[:, pl.ds(slot * middle, middle)]).astype(low)
            g_mid[3 * part + slot] = value.reshape(g_mid.shape[1:])
        for number in ((1,), (2, 3), (4,))[part]:
            go_pair(number)

        def step_one(index):
            span_rows = rows_at(index * tile, tile)
            grad = against(
                wide_low[span_rows, pl.ds(0, middle)], mid_w[3 * part].reshape(middle, middle)
            )
            for slot in range(1, 3):
                grad = grad + against(
                    wide_low[span_rows, pl.ds(slot * middle, middle)],
                    mid_w[3 * part + slot].reshape(middle, middle),
                )
            if part:
                grad = grad + work[span_rows, :]
            if part == 2:
                grad = grad * slope_of(one[span_rows, :] * scale_one + shift_one)
                norm_sums(grad, one[span_rows, :] * inverse_one - center_one)
            work[span_rows, :] = grad

        loop(4, step_one)
        if part == 2:
            pack(sums_b, middle)
            sums.start(sums_b, land_b)
        for number in ((0, 1), (0, 1, 2, 3), (0, 1, 2, 3, 4))[part]:
            go_pair(number)
    value = whole_near(0, near_hid)
    wide = g_hid.shape[3]
    squares_of(3, value)
    slabs = [o_hid.at[:, lanes_of(which, wide)] for which in (at.sub, at.row_sub)]
    o_hid[:, lanes_of(at.sub, wide)] = value
    hid_row = links(slabs[0], slabs[0], at.row_peer)
    value = whole_near(1, near_out)
    squares_of(4, value)
    o_out[...] = value
    go(proto)

    both_one = sums.finish()
    settle_grad(one, center_one, inverse_one, scale_one, both_one / count_all)
    vec[pl.ds(0, 1), pl.ds(0, middle)] = both_one[1:2]
    vec[pl.ds(0, 1), pl.ds(2 * middle, middle)] = both_one[0:1]
    wide = vec.shape[1] // 4
    vec_cols = lanes_of(at.sub, wide)
    vec_copies = [
        links(vec.at[:, vec_cols], vec_land.at[hop], peer)
        for hop, peer in enumerate(at.dp_peers())
    ]
    for number in range(1, 5):
        go_pair(number)
    hid_row.wait()
    final = [links(slab, slab, at.core_peer) for slab in slabs]

    for copy in x_copies:
        copy.wait()
    weight_rows(g_first, x_ref, thin_low)
    go_pair(5)
    go_pair(6)

    numbers = range(len(pieces) // 2)
    tick = 0
    sent = False
    while min(state[:proto]) < 6:
        for number in numbers:
            if state[2 * number] < 6:
                go_pair(number)
        if tick < 3:
            go(proto)
        if tick == 1:
            wait_all(vec_copies)
            value = vec[:, vec_cols]
            for hop in range(n_dp - 1):
                value = value + vec_land[hop]
            o_vec[:, vec_cols] = value
            vec_final = [
                links(o_vec.at[:, vec_cols], o_vec.at[:, vec_cols], peer)
                for peer in at.sub_peers()
            ]
        if not sent and min(state[:proto]) >= 5:
            sent = True
            sq_copies = [
                links(sq_mine.at[0], sq_land.at[hop], peer)
                for hop, peer in enumerate(at.dp_peers())
            ]
        tick += 1
    wait_all(sq_copies)
    value = sq_mine[0]
    for hop in range(n_dp - 1):
        value = value + sq_land[hop]
    sq_mine[1] = value
    sq_copies = [
        links(sq_mine.at[1], sq_land.at[n_dp - 1 + hop], peer)
        for hop, peer in enumerate(at.sub_peers())
    ]
    wait_all(sq_copies)
    for hop in range(3):
        value = value + sq_land[n_dp - 1 + hop]
    o_sq[...] = value
    for copies in flight:
        wait_all(copies)
    wait_all(final)
    wait_all(vec_final)


def backward_trunk(
    n_dp, collective_id, images, pooled, slopes, stat, norms, live, lives, extra, hid, out, proto, big,
    small, curve, normal, one, two, act, last, mid,
):
    span = n_dp // 2
    low, full = jnp.bfloat16, jnp.float32
    rows, channels = curve.shape
    middle = one.shape[1]
    height, mid_height = last.shape[2], mid.shape[3]
    narrow = out.shape[1]
    crops = CROPS * images
    some = jax.ShapeDtypeStruct
    bufs = []
    for index, piece in enumerate(piece_list(height, mid_height, proto.shape[0] // n_dp, ((0, 0),) * 4)):
        taps, block = piece[3], (piece[5], LANES)
        bufs.append(pltpu.VMEM((2, taps, span, 2) + block, low))
        if index % 2 == 0:
            bufs.append(pltpu.VMEM((taps, span, 2) + block, low))
        else:
            bufs.append(pltpu.VMEM((2, taps, span) + block, low))
        bufs.append(pltpu.VMEM((taps, span) + block, low))
        bufs.append(pltpu.VMEM((span - 1, taps) + block, low))
    copies = 15 * (span + 6) + 3 * (span + 4) + 2 * n_dp + 40
    vmem, anywhere = pl.BlockSpec(memory_space=pltpu.VMEM), pl.BlockSpec(memory_space=pl.ANY)
    return pl.pallas_call(
        functools.partial(backward_kernel, n_dp, images),
        out_shape=(
            some((1, height, middle), low),
            some((TAPS, mid_height, middle), low),
            some((1, height, middle), low),
            some((height, 4 * hid.shape[1]), low),
            some((height, narrow), low),
            some((span, 2, proto.shape[0] // n_dp, proto.shape[1]), low),
            some(extra.shape, full),
            some((8, LANES), full),
        ),
        in_specs=[vmem] * 10 + [anywhere] * 9,
        out_specs=(vmem,) * 8,
        scratch_shapes=[
            pltpu.VMEM((rows, channels), low),
            pltpu.VMEM((rows, middle), full),
            pltpu.VMEM((rows, middle), full),
            pltpu.VMEM((rows, middle), low),
            pltpu.VMEM((span, 2, height, middle), low),
            pltpu.VMEM((TAPS, span, 2, mid_height, middle), low),
            pltpu.VMEM((rows, middle), low),
            pltpu.VMEM((rows, channels), low),
            pltpu.VMEM((rows, middle), full),
            pltpu.VMEM((rows, middle), low),
            pltpu.VMEM((1, span, 2, height, middle), low),
            pltpu.VMEM((TAPS, span, 2, mid_height, middle), low),
            pltpu.VMEM((1, span, 2, height, middle), low),
            pltpu.VMEM((2, 8, middle), full),
            pltpu.VMEM((2, crops, channels), low),
            pltpu.VMEM((crops, channels), low),
            pltpu.VMEM((crops, channels), low),
            pltpu.VMEM((crops, channels), full),
            pltpu.VMEM((2, middle), full),
            pltpu.VMEM((3, 2, middle), full),
            pltpu.VMEM((2, middle), full),
            pltpu.VMEM((3, 2, middle), full),
            pltpu.VMEM((2, channels), full),
            pltpu.VMEM((3, 2, channels), full),
            pltpu.VMEM((span, height, hid.shape[1]), low),
            pltpu.VMEM((span, height, hid.shape[1]), low),
            pltpu.VMEM((span - 1, height, hid.shape[1]), low),
            pltpu.VMEM((span, 2, height, narrow), low),
            pltpu.VMEM((span, height, narrow), low),
            pltpu.VMEM((span, height, narrow), low),
            pltpu.VMEM((span - 1, height, narrow), low),
            pltpu.VMEM(extra.shape, full),
            pltpu.VMEM((n_dp - 1, extra.shape[0], extra.shape[1] // 4), full),
            pltpu.VMEM((2, 8, LANES), full),
            pltpu.VMEM((n_dp + 2, 8, LANES), full),
            pltpu.SemaphoreType.DMA((copies,)),
            pltpu.SemaphoreType.DMA((copies,)),
            pltpu.SemaphoreType.DMA((8,)),
            pltpu.SemaphoreType.DMA((2,)),
        ]
        + bufs,
        compiler_params=pltpu.CompilerParams(
            collective_id=collective_id, has_side_effects=True, vmem_limit_bytes=62 * MIB
        ),
        name="backward_trunk",
    )(
        pooled,
        slopes,
        stat,
        norms,
        live,
        lives,
        extra,
        hid.reshape(span, 2, height, hid.shape[1]),
        out.reshape(span // 4, 2, height, narrow),
        proto.reshape(1, span, 2, proto.shape[0] // n_dp, proto.shape[1]),
        big,
        small,
        curve,
        normal,
        one,
        two,
        act,
        last,
        mid,
    )


def sinkhorn_kernel(
    axis,
    count,
    protos,
    queue_ref,
    centers_ref,
    turned_ref,
    pooled_ref,
    hid_ref,
    out_ref,
    norm_ref,
    live_ref,
    lives_ref,
    weigh_ref,
    first_ref,
    proto_grad_ref,
    d_hid_ref,
    d_out_ref,
    back_ref,
    extra_ref,
    partial_ref,
    act,
    normal,
    grads,
    lows,
    embed_ref,
    four,
    four_land,
    grad,
    parts_land,
    kept,
    scores,
    mine,
    landed,
    shift,
    total,
    send_sem,
    recv_sem,
):
    me = lax.axis_index(axis)
    views, rows, _ = queue_ref.shape
    width = turned_ref.shape[1]
    images = live_ref.shape[0]
    tile = row_tile(rows)
    part = 512
    parts = range(0, width, part)
    mask = live_ref[...][:, :1]
    crops = CROPS * images
    share = hid_ref.shape[1]
    low = jnp.bfloat16
    greet(axis, count)

    slots = lax.broadcasted_iota(jnp.int32, (images, 1), 0).astype(jnp.float32)
    masks = [jnp.where(slots < lives_ref[member, :images, :1], 1.0, 0.0) for member in range(count)]
    live_group = sum(lives_ref[member, :1, :1] for member in range(count))
    count_crops = live_group * float(CROPS)

    def spread(values, member):
        return (values.reshape(CROPS, images, values.shape[1]) * masks[member]).reshape(values.shape)

    sums = jnp.zeros((1, share), jnp.float32)
    squares = jnp.zeros((1, share), jnp.float32)
    for member in range(count):
        value = jnp.dot(pooled_ref[member], hid_ref[...], preferred_element_type=jnp.float32)
        normal[member] = value
        masked = spread(value, member)
        sums = sums + jnp.sum(masked, 0, keepdims=True)
        squares = squares + jnp.sum(masked * value, 0, keepdims=True)
    mean = sums / count_crops
    inverse_four = lax.rsqrt(squares / count_crops - mean * mean + norm_eps)
    own = pl.ds(pl.multiple_of(norm_ref.shape[1] - count * share + me * share, LANES), share)
    gain, bias = norm_ref[pl.ds(0, 1), own], norm_ref[pl.ds(1, 1), own]
    for member in range(count):
        value = (normal[member] - mean) * inverse_four
        normal[member] = value
        pre = value * gain + bias
        act[member] = (pre * sigmoid_of(pre)).astype(low)
        partial_ref[member] = jnp.dot(act[member], out_ref[...], preferred_element_type=jnp.float32)

    def start_group(turn, source, target):
        copies = []
        for hop in range(1, count):
            to = lax.rem(me + hop, count)
            copy = pltpu.make_async_remote_copy(
                src_ref=source(to),
                dst_ref=target(hop),
                send_sem=send_sem.at[turn, hop],
                recv_sem=recv_sem.at[turn, hop],
                device_id={axis: to},
                device_id_type=MESH,
            )
            copy.start()
            copies.append(copy)
        return copies

    def to_group(turn, source, target):
        for copy in start_group(turn, source, target):
            copy.wait()

    to_group(ITERS, lambda to: partial_ref.at[to], lambda hop: parts_land.at[hop])
    embedding = partial_ref[me]
    for hop in range(1, count):
        embedding = embedding + parts_land[hop]
    inverse = lax.rsqrt(jnp.sum(embedding * embedding, 1, keepdims=True) + unit_eps)
    unit = embedding * inverse
    unit_low = unit.astype(jnp.bfloat16)

    def sum_group(turn):
        copies = []
        for hop in range(1, count):
            copy = pltpu.make_async_remote_copy(
                src_ref=mine.at[turn],
                dst_ref=landed.at[turn, hop],
                send_sem=send_sem.at[turn, hop],
                recv_sem=recv_sem.at[turn, hop],
                device_id={axis: lax.rem(me + hop, count)},
                device_id_type=MESH,
            )
            copy.start()
            copies.append(copy)
        for copy in copies:
            copy.wait()
        whole = mine[turn]
        for hop in range(1, count):
            whole = whole + landed[turn, hop]
        return whole

    for start in parts:
        cols = pl.ds(start, part)
        scores[:, cols] = jnp.dot(
            unit_low, turned_ref[:, cols], preferred_element_type=jnp.float32
        )
        for view in range(views):
            lines = pl.ds(view * images, images)
            shares = jnp.exp2(scores[lines, cols] * SINK2) * mask
            mine[0, pl.ds(view, 1), cols] = first_ref[pl.ds(view, 1), cols] + jnp.sum(
                shares, 0, keepdims=True
            )
    real = lax.broadcasted_iota(jnp.int32, (1, width), 1) < protos
    first = sum_group(0)
    shift[...] = jnp.where(real, jnp.log2(first), 1e30)

    for turn in range(1, ITERS):
        for view in range(views):
            lines = pl.ds(view * images, images)
            row = pl.ds(view, 1)
            if turn == 1:
                own = jnp.exp2(scores[lines, :] * SINK2 - shift[row, :]) * mask
                weight = jnp.sum(own, 1, keepdims=True)
            else:
                own = jnp.exp2(scores[lines, :] * SINK2 - first_log[row, :]) * mask
                weight = jnp.sum(own * shift[row, :], 1, keepdims=True)
            total[...] = own / (weight + (1.0 - mask))

            def step(index, carry):
                span = pl.ds(index * tile, tile)
                if turn == 1:
                    lines = queue_ref[view, span, :]
                sums = jnp.zeros((tile, LANES), jnp.float32)
                for start in parts:
                    cols = pl.ds(start, part)
                    if turn == 1:
                        raw = jnp.dot(lines, turned_ref[:, cols], preferred_element_type=jnp.float32)
                        shares = jnp.exp2(raw * SINK2 - shift[row, cols])
                        kept[view, span, cols] = shares
                    else:
                        shares = kept[view, span, cols] * shift[row, cols]
                    for lane in range(0, part, LANES):
                        sums = sums + shares[:, lane : lane + LANES]
                scale = 1.0 / jnp.sum(sums, 1, keepdims=True)
                for start in parts:
                    cols = pl.ds(start, part)
                    scaled = kept[view, span, cols] * scale
                    total[:, cols] += jnp.sum(scaled.reshape(tile // 8, 8, part), 0)
                return carry

            lax.fori_loop(0, rows // tile, step, 0)
            mine[turn, row, :] = jnp.sum(total[...], 0, keepdims=True)
        if turn == 1:
            first_log = shift[...]
        whole = sum_group(turn)
        shift[...] = jnp.where(real, 1.0 / whole, 0.0)

    codes = []
    for view in range(views):
        lines = pl.ds(view * images, images)
        own = jnp.exp2(scores[lines, :] * SINK2 - first_log[view : view + 1, :]) * mask
        own = own * shift[pl.ds(view, 1), :]
        codes.append(own / (jnp.sum(own, 1, keepdims=True) + (1.0 - mask)))
    code_total = codes[0] + codes[1]
    loss = jnp.zeros((images, 1), jnp.float32)
    for crop in range(CROPS):
        lines = pl.ds(crop * images, images)
        raw = jnp.where(real, scores[lines, :] * SOFT2, -1e30)
        raw = raw - jnp.max(raw, 1, keepdims=True)
        powers = jnp.exp2(raw)
        norm = jnp.sum(powers, 1, keepdims=True)
        others = code_total - codes[crop] if crop < NBIG else code_total
        logs = jnp.where(real, (raw - jnp.log2(norm)) / LOG2E, 0.0)
        loss = loss - jnp.sum(others * logs, 1, keepdims=True)
        weight = (NBIG - 1.0 if crop < NBIG else float(NBIG)) * mask / norm
        grad[lines, :] = (weight * powers - others) / (PAIRS * softmax_temp)
    grad_unit = jnp.zeros(unit.shape, jnp.float32)
    for start in parts:
        cols = pl.ds(start, part)
        some = grad[:, cols].astype(jnp.bfloat16)
        grad_unit = grad_unit + jnp.dot(
            some, centers_ref[cols, :], preferred_element_type=jnp.float32
        )
        for first in range(start, start + part, 256):
            value = cross_rows(grad[:, pl.ds(first, 256)].astype(jnp.bfloat16), unit_low)
            lines = pl.ds(first % (width // 4), 256)
            proto_grad_ref[lines, pl.ds(first // (width // 4) * LANES, LANES)] = value.astype(low)
    grad_embed = inverse * (
        grad_unit - unit * jnp.sum(unit * grad_unit, 1, keepdims=True)
    )
    embed_ref[me] = grad_embed.astype(jnp.bfloat16)
    to_group(ITERS + 1, lambda to: embed_ref.at[me], lambda hop: embed_ref.at[me])

    gain_sum = jnp.zeros((1, share), jnp.float32)
    bias_sum = jnp.zeros((1, share), jnp.float32)
    for member in range(count):
        value = against(embed_ref[member], out_ref[...])
        pre = normal[member] * gain + bias
        sigma = sigmoid_of(pre)
        value = value * (sigma + pre * sigma * (1.0 - sigma))
        grads[member] = value
        bias_sum = bias_sum + jnp.sum(value, 0, keepdims=True)
        gain_sum = gain_sum + jnp.sum(value * normal[member], 0, keepdims=True)
    four[pl.ds(0, 1), :] = gain_sum
    four[pl.ds(1, 1), :] = bias_sum
    four[pl.ds(2, 1), :] = jnp.broadcast_to(
        jnp.sum(loss, 0, keepdims=True) / PAIRS, (1, share)
    )
    copies = start_group(ITERS + 2, lambda to: four, lambda hop: four_land.at[hop])
    scale = gain * inverse_four
    for member in range(count):
        value = spread((bias_sum + normal[member] * gain_sum) / count_crops, member)
        lows[member] = ((grads[member] - value) * scale).astype(low)
    embeds = embed_ref[...].reshape(count * crops, embed_ref.shape[2])
    d_out_ref[...] = cross_rows(act[...].reshape(count * crops, share), embeds).astype(low)
    low_rows = lows[...].reshape(count * crops, share)
    for start in range(0, pooled_ref.shape[2], 256):
        left = pooled_ref[:, :, pl.ds(start, 256)].reshape(count * crops, 256)
        d_hid_ref[pl.ds(start, 256), :] = cross_rows(left, low_rows).astype(low)
        back = against(low_rows, hid_ref[pl.ds(start, 256), :]).astype(low)
        back_ref[:, :, pl.ds(start, 256)] = back.reshape(count, crops, 256)
    extra_ref[...] = jnp.zeros_like(extra_ref)
    for copy in copies:
        copy.wait()
    loss_group = jnp.zeros((1, 1), jnp.float32)
    for hop in range(count):
        source = (me + count - hop) % count
        value = four_land[hop] if hop else four[...]
        extra_ref[pl.ds(2, 1), lanes_of(source, share)] = value[0:1]
        extra_ref[pl.ds(4, 1), lanes_of(source, share)] = value[1:2]
        loss_group = loss_group + value[2:3, :1]
    lane = lax.broadcasted_iota(jnp.int32, (1, extra_ref.shape[1]), 1)
    line = jnp.where(lane == 0, loss_group, 0.0) + jnp.where(lane == 1, live_group, 0.0)
    for which in range(5):
        value = jnp.sum(weigh_ref[pl.ds(which, 1), :], 1, keepdims=True)
        line = line + jnp.where(lane == 2 + which, value, 0.0)
    extra_ref[pl.ds(5, 1), :] = line


def sinkhorn(
    sizes, collective_id, protos, queue, centers, turned, pooled, hid, out, norms, live, lives, weigh,
    first,
):
    count = sizes["sub"]
    views, rows, depth = queue.shape
    width = turned.shape[1]
    crops, channels = pooled.shape[1:]
    share = hid.shape[1]
    low, full = jnp.bfloat16, jnp.float32
    some = jax.ShapeDtypeStruct
    turns = ITERS + 3
    return pl.pallas_call(
        functools.partial(sinkhorn_kernel, "sub", count, protos),
        out_shape=(
            some((width // 4, 4 * depth), low),
            some((channels, share), low),
            some((share, depth), low),
            some((count, crops, channels), low),
            some((8, count * share), full),
        ),
        in_specs=[pl.BlockSpec(memory_space=pltpu.VMEM)] * 11,
        out_specs=(pl.BlockSpec(memory_space=pltpu.VMEM),) * 5,
        scratch_shapes=[
            pltpu.VMEM((count, crops, depth), full),
            pltpu.VMEM((count, crops, share), low),
            pltpu.VMEM((count, crops, share), full),
            pltpu.VMEM((count, crops, share), full),
            pltpu.VMEM((count, crops, share), low),
            pltpu.VMEM((count, crops, depth), low),
            pltpu.VMEM((3, share), full),
            pltpu.VMEM((count, 3, share), full),
            pltpu.VMEM((crops, width), full),
            pltpu.VMEM((count, crops, depth), full),
            pltpu.VMEM((views, rows, width), full),
            pltpu.VMEM((crops, width), full),
            pltpu.VMEM((ITERS, views, width), full),
            pltpu.VMEM((ITERS, count, views, width), full),
            pltpu.VMEM((views, width), full),
            pltpu.VMEM((8, width), full),
            pltpu.SemaphoreType.DMA((turns, count)),
            pltpu.SemaphoreType.DMA((turns, count)),
        ],
        compiler_params=pltpu.CompilerParams(
            collective_id=collective_id, has_side_effects=True, vmem_limit_bytes=54 * MIB
        ),
        name="sinkhorn",
    )(queue, centers, turned, pooled, hid, out, norms, live, lives, weigh, first)


def advance(weight, gradient, moment, average, trust):
    step_now = trust * gradient
    moment_new = momentum_rate * moment + step_now
    weight_new = weight - learn_rate * (step_now + momentum_rate * moment_new)
    average_new = average_rate * average + (1.0 - average_rate) * weight_new
    return (weight_new, moment_new, average_new)


def update_kernel(protos, *refs):
    g_first, g_mid, g_last, g_hid, g_out, vec, sq, centers = refs[:8]
    sources, targets = refs[8:26], refs[26:48]
    o_loss, o_count = refs[48:50]
    held, lows = refs[50:68], refs[68:72]
    proto_grad, norm_grad, square, load_sem, save_sem = refs[72:]
    o_loss[...] = vec[5:6, 0:1]
    o_count[...] = vec[5:6, 1:2]
    weights, moments, averages = held[:6], held[6:12], held[12:]
    w_outer, w_mid, w_hid, w_out, w_proto, w_norm = weights
    middle = g_first.shape[2]
    loads, saves = {}, []
    for which in (2, 1, 0, 3, 5, 4):
        loads[which] = []
        for part in range(3):
            index = 6 * part + which
            copy = pltpu.make_async_copy(sources[index], held[index], load_sem.at[index])
            copy.start()
            loads[which].append(copy)

    def trust_of(weights, grads):
        return trust_rate * jnp.sqrt(weights) / (jnp.sqrt(grads) + 1e-12)

    def put(which, at, grad, trust):
        new, moment, average = advance(
            weights[which][at],
            grad.astype(jnp.float32),
            moments[which][at],
            averages[which][at],
            trust,
        )
        weights[which][at] = new
        moments[which][at] = moment
        averages[which][at] = average
        if which < 4:
            lows[which][at] = new.astype(jnp.bfloat16)

    def load(which):
        for copy in loads[which]:
            copy.wait()

    def save(which):
        parts = [(held[6 * part + which], 6 * part + which) for part in range(3)]
        if which < 4:
            parts.append((lows[which], 18 + which))
        for source, index in parts:
            copy = pltpu.make_async_copy(source, targets[index], save_sem.at[index])
            copy.start()
            saves.append(copy)

    def matrix_trust(line, lane, share=1.0):
        grads = jnp.sum(sq[pl.ds(line, 1), :], 1, keepdims=True) * share
        return trust_of(vec[5:6, lane : lane + 1], grads)

    trust_hid = matrix_trust(3, 5)
    height = w_hid.shape[0] // 8 if w_hid.shape[0] >= 64 else 8
    load(2)

    def step_hid(index, carry):
        at = pl.ds(pl.multiple_of(index * height, 8), height)
        put(2, at, g_hid[at], trust_hid)
        return carry

    lax.fori_loop(0, w_hid.shape[0] // height, step_hid, 0)
    save(2)
    trust_mid = matrix_trust(1, 4)
    load(1)

    def step_mid(index, carry):
        put(1, index, g_mid[index], trust_mid)
        return carry

    lax.fori_loop(0, TAPS, step_mid, 0)
    save(1)
    load(0)
    for which, (grad, line) in enumerate(((g_first, 0), (g_last, 2))):
        trust = matrix_trust(line, 2 + which)
        height = grad.shape[1] // 4
        for index in range(4):
            lines = pl.ds(index * height, height)
            put(0, (which, lines), grad[0, lines], trust)
    save(0)
    load(3)
    whole = slice(None)
    put(3, whole, g_out[...], matrix_trust(4, 6, 0.25))
    save(3)

    for row, lines in enumerate((((0, 0), 1, 2), ((0, 1), 3, 4))):
        (line, half), wide, last = lines
        start = 2 * middle * half
        norm_grad[pl.ds(row, 1), pl.ds(0, 2 * middle)] = vec[line : line + 1, start : start + 2 * middle]
        size = vec.shape[1]
        norm_grad[pl.ds(row, 1), pl.ds(2 * middle, size)] = vec[wide : wide + 1, :]
        norm_grad[pl.ds(row, 1), pl.ds(2 * middle + size, size)] = vec[last : last + 1, :]
    load(5)
    weight, grad = w_norm[...], norm_grad[...]
    trust = trust_of(
        jnp.sum(weight * weight, 1, keepdims=True), jnp.sum(grad * grad, 1, keepdims=True)
    )
    put(5, whole, grad, trust)
    save(5)

    square[...] = jnp.zeros_like(square)
    load(4)
    fold = centers.shape[0]
    chunks = []
    for quarter in range(4):
        for start in range(0, fold, 256):
            here = quarter * fold + start
            size = min(256, fold - start, protos - here)
            if size > 0:
                chunks.append((pl.ds(here, size), pl.ds(start, size), pl.ds(quarter * LANES, LANES)))
    for at, lines, cols in chunks:
        weight, value = w_proto[at], centers[lines, cols].astype(jnp.float32)
        inverse = lax.rsqrt(jnp.sum(weight * weight, 1, keepdims=True) + unit_eps)
        unit = weight * inverse
        grad = inverse * (value - unit * jnp.sum(unit * value, 1, keepdims=True))
        proto_grad[at] = grad
        weigh(square, 0, weight)
        weigh(square, 1, grad)
    sums = jnp.sum(square[...], 1, keepdims=True)
    trust_proto = trust_of(sums[0:1], sums[1:2])
    for at, lines, cols in chunks:
        put(4, at, proto_grad[at], trust_proto)
    save(4)
    for copy in saves:
        copy.wait()


def update(grads, vec, sq, centers, weights, moments, averages):
    some = jax.ShapeDtypeStruct
    protos = weights[4].shape[0]
    shapes = tuple(some(value.shape, value.dtype) for value in weights)
    lows = tuple(some(value.shape, jnp.bfloat16) for value in weights[:4])
    vmem, anywhere = pl.BlockSpec(memory_space=pltpu.VMEM), pl.BlockSpec(memory_space=pl.ANY)
    results = pl.pallas_call(
        functools.partial(update_kernel, protos),
        out_shape=shapes * 3 + lows + (some((1, 1), jnp.float32),) * 2,
        in_specs=[vmem] * 8 + [anywhere] * 18,
        out_specs=(anywhere,) * 22 + (vmem,) * 2,
        scratch_shapes=[pltpu.VMEM(value.shape, value.dtype) for value in shapes * 3 + lows]
        + [
            pltpu.VMEM(weights[4].shape, jnp.float32),
            pltpu.VMEM(weights[5].shape, jnp.float32),
            pltpu.VMEM((8, LANES), jnp.float32),
            pltpu.SemaphoreType.DMA((18,)),
            pltpu.SemaphoreType.DMA((22,)),
        ],
        compiler_params=pltpu.CompilerParams(vmem_limit_bytes=56 * MIB),
        name="update",
    )(*grads, vec, sq, centers, *weights, *moments, *averages)
    return results


def per_device(
    sizes,
    big_maps,
    small_maps,
    live_counts,
    queue,
    bottleneck_outer,
    bottleneck_inner,
    proj_hidden,
    proj_out,
    prototypes,
    norm_params,
    mom_outer,
    mom_inner,
    mom_hidden,
    mom_out,
    mom_protos,
    mom_norms,
    avg_outer,
    avg_inner,
    avg_hidden,
    avg_out,
    avg_protos,
    avg_norms,
):
    n_dp, n_sub = sizes["dp"], sizes["sub"]
    exchange = Exchanger(sizes)
    images = big_maps.shape[0]
    channels = big_maps.shape[-1]
    middle = bottleneck_inner.shape[-1]
    hidden_width = proj_hidden.shape[1]
    out_width = proj_out.shape[1]
    proto_count = prototypes.shape[0]
    unit = max(512, 64 * n_dp)
    proto_width = -(-proto_count // unit) * unit
    share = hidden_width // n_sub

    image_mask = (jnp.arange(images) < live_counts[0]).astype(jnp.float32)[:, None]
    live_tile = jnp.broadcast_to(image_mask, (images, LANES))
    big = jnp.transpose(big_maps, (2, 3, 1, 0, 4)).reshape(-1, channels)
    small = jnp.transpose(small_maps, (2, 3, 1, 0, 4)).reshape(-1, channels)

    (
        inner_low, last_w, hidden_low, out_low, hidden_one, hidden_two, act_two, curve, normal,
        trunk_stat, pooled_all, lives, slopes, weights_sq, centers_low, turned, first_sums,
    ) = forward_trunk(
        n_dp,
        exchange.next_id(),
        images,
        bottleneck_outer,
        bottleneck_inner,
        proj_hidden,
        proj_out,
        big,
        small,
        norm_params,
        live_tile,
        queue,
        prototypes,
        proto_width,
    )

    grad_centers, d_hidden, d_out, pooled_back, extra = sinkhorn(
        sizes,
        exchange.next_id(),
        proto_count,
        queue,
        centers_low,
        turned,
        pooled_all,
        hidden_low.reshape(channels, share),
        out_low.reshape(share, out_width),
        norm_params,
        live_tile,
        lives,
        weights_sq,
        first_sums,
    )

    (
        shard_first, shard_inner, shard_last, shard_hidden, shard_out, centers_sum, vector, grad_sq,
    ) = backward_trunk(
        n_dp,
        exchange.next_id(),
        images,
        pooled_back,
        slopes,
        trunk_stat,
        norm_params,
        live_tile,
        lives,
        extra,
        d_hidden,
        d_out,
        grad_centers,
        big,
        small,
        curve,
        normal,
        hidden_one,
        hidden_two,
        act_two,
        last_w,
        inner_low,
    )
    results = update(
        (shard_first, shard_inner, shard_last, shard_hidden, shard_out),
        vector,
        grad_sq,
        centers_sum.reshape(proto_width // 4, 4 * out_width),
        (bottleneck_outer, bottleneck_inner, proj_hidden, proj_out, prototypes, norm_params),
        (mom_outer, mom_inner, mom_hidden, mom_out, mom_protos, mom_norms),
        (avg_outer, avg_inner, avg_hidden, avg_out, avg_protos, avg_norms),
    )
    return (results[22].reshape(()), results[23].reshape(())) + tuple(results[:22])


def solution(mesh):
    data = P(("dp", "sub"), None, None, None, None)
    trees = (P(None, "dp", None), P(None, "dp", None), P("dp", None), P("dp", None), P(), P())
    in_specs = (data, data, P(("dp", "sub")), P(None, ("dp", "sub"), None)) + trees * 3
    out_specs = (P(), P()) + trees * 3 + trees[:4]
    sizes = {axis: mesh.shape[axis] for axis in ("dp", "sub")}
    return jax.shard_map(
        functools.partial(per_device, sizes),
        mesh=mesh,
        in_specs=in_specs,
        out_specs=out_specs,
        check_vma=False,
    )
```

```python
import functools
import math

import jax
import jax.numpy as jnp
from jax import lax
from jax.experimental import pallas as pl
from jax.experimental.pallas import tpu as pltpu
from jax.sharding import PartitionSpec as P

NBIG = 2
NSMALL = 6
CROPS = NBIG + NSMALL
BIG = 7
SMALL = 3
TAPS = 9
ITERS = 3
LANES = 128

sink_temp = 0.05
softmax_temp = 0.1
norm_eps = 1e-05
unit_eps = 1e-12
trust_rate = 0.5
learn_rate = 1.0
momentum_rate = 0.5
average_rate = 0.5

MESH = pl.DeviceIdType.MESH
MIB = 1 << 20
LOG2E = math.log2(math.e)
SINK2 = LOG2E / sink_temp
SOFT2 = LOG2E / softmax_temp
PAIRS = NBIG * (CROPS - 1)


def cross_rows(left, right):
    return lax.dot_general(
        left, right, (((0,), (0,)), ((), ())), preferred_element_type=jnp.float32
    )


def against(left, right):
    return lax.dot_general(
        left, right, (((1,), (1,)), ((), ())), preferred_element_type=jnp.float32
    )


def greet(axis, count):
    me = lax.axis_index(axis)
    barrier = pltpu.get_barrier_semaphore()
    for hop in range(1, count):
        pl.semaphore_signal(
            barrier, inc=1, device_id={axis: lax.rem(me + hop, count)}, device_id_type=MESH
        )
    pl.semaphore_wait(barrier, count - 1)


class Exchanger:
    def __init__(self, sizes):
        self.sizes = sizes
        self.used = 0

    def next_id(self):
        self.used += 1
        return self.used


class Links:
    def __init__(self, send_sem, recv_sem):
        self.send_sem = send_sem
        self.recv_sem = recv_sem
        self.used = 0

    def __call__(self, source, target, device):
        copy = pltpu.make_async_remote_copy(
            src_ref=source,
            dst_ref=target,
            send_sem=self.send_sem.at[self.used],
            recv_sem=self.recv_sem.at[self.used],
            device_id=device,
            device_id_type=MESH,
        )
        self.used += 1
        copy.start()
        return copy


def wait_all(copies):
    for copy in copies:
        copy.wait()


def lanes_of(index, width=LANES):
    return pl.ds(pl.multiple_of(index * width, LANES), width)


class Place:
    def __init__(self, n_dp):
        self.n_dp = n_dp
        self.span = n_dp // 2
        dp, self.sub = lax.axis_index("dp"), lax.axis_index("sub")
        self.dp = dp
        self.near, self.far = dp // 2, dp % 2
        row, core = self.sub // 2, self.sub % 2
        self.row, self.core = row, core
        self.row_sub = 2 * (1 - row) + core
        self.core_sub = 2 * row + (1 - core)
        self.far_peer = {"dp": self.near * 2 + (1 - self.far)}
        self.row_peer = {"sub": self.row_sub}
        self.core_peer = {"sub": self.core_sub}

    def near_index(self, hop):
        return (self.near + hop) % self.span

    def near_peer(self, hop):
        return {"dp": self.near_index(hop) * 2 + self.far}

    def dp_peers(self):
        return [{"dp": (self.dp + hop) % self.n_dp} for hop in range(1, self.n_dp)]

    def sub_peers(self):
        return [{"sub": (self.sub + hop) % 4} for hop in range(1, 4)]

    def greet(self, peers):
        barrier = pltpu.get_barrier_semaphore()
        for peer in peers:
            pl.semaphore_signal(barrier, inc=1, device_id=peer, device_id_type=MESH)
        pl.semaphore_wait(barrier, len(peers))


ALL = slice(None)


def sigmoid_of(values):
    return 0.5 * jnp.tanh(0.5 * values) + 0.5


def rows_at(start, size):
    return pl.ds(start if isinstance(start, int) else pl.multiple_of(start, 16), size)


def tap_blocks(images, flip):
    moves = [[] for _ in range(TAPS)]
    zeros = [[] for _ in range(TAPS)]
    base = 0
    for extent, lines in ((BIG, NBIG * images), (SMALL, NSMALL * images)):
        for tap in range(TAPS):
            down, right = tap // 3 - 1, tap % 3 - 1
            if flip:
                down, right = -down, -right
            for row in range(extent):
                start = base + row * extent * lines
                if not 0 <= row + down < extent:
                    zeros[tap].append((start, extent * lines))
                    continue
                left, stop = max(0, -right), min(extent, extent - right)
                moves[tap].append(
                    (
                        start + left * lines,
                        base + ((row + down) * extent + left + right) * lines,
                        (stop - left) * lines,
                    )
                )
                if left:
                    zeros[tap].append((start, left * lines))
                if stop < extent:
                    zeros[tap].append((start + stop * lines, (extent - stop) * lines))
        base += extent * extent * lines
    return moves, zeros


def fill_columns(columns, source, images, flip):
    wide = source.shape[1]
    moves, zeros = tap_blocks(images, flip)
    for tap in range(TAPS):
        cols = pl.ds(tap * wide, wide)
        for target, start, size in moves[tap]:
            columns[pl.ds(target, size), cols] = source[pl.ds(start, size), :]
        for target, size in zeros[tap]:
            columns[pl.ds(target, size), cols] = jnp.zeros((size, wide), columns.dtype)


def masked_sums(values, mask, total):
    rows, wide = values.shape
    blocks = values.reshape(rows // 8, 8, wide)
    masked = blocks * mask
    total[0] += jnp.sum(masked, 0)
    total[1] += jnp.sum(masked * blocks, 0)


def row_tile(rows):
    return next(size for size in (192, 160, 128, 96, 64, 48, 32, 24, 16, 8) if rows % size == 0)


def centers_of(proto_ref, centers_ref, turned_ref):
    protos, depth = proto_ref.shape
    part = 256
    for start in range(0, turned_ref.shape[1], part):
        here = max(0, min(part, protos - start))
        values = jnp.zeros((part, depth), jnp.float32)
        if here:
            values = proto_ref[pl.ds(start, here), :]
            values = values * lax.rsqrt(jnp.sum(values * values, 1, keepdims=True) + unit_eps)
        if 0 < here < part:
            values = jnp.concatenate([values, jnp.zeros((part - here, depth), jnp.float32)], 0)
        centers_ref[pl.ds(start, part), :] = values.astype(jnp.bfloat16)
        turned_ref[:, pl.ds(start, part)] = values.T.astype(jnp.bfloat16)


def queue_sums(queue_ref, turned_ref, o_ref, total, view):
    rows, width = queue_ref.shape[1], turned_ref.shape[1]
    tile, part = row_tile(rows), 256
    total[...] = jnp.zeros_like(total)

    def step(index, carry):
        lines = queue_ref[view, pl.ds(index * tile, tile), :]
        for start in range(0, width, part):
            cols = pl.ds(start, part)
            scores = jnp.dot(lines, turned_ref[:, cols], preferred_element_type=jnp.float32)
            shares = jnp.exp2(scores * SINK2)
            total[:, cols] += jnp.sum(shares.reshape(tile // 8, 8, part), 0)
        return carry

    lax.fori_loop(0, rows // tile, step, 0)
    o_ref[pl.ds(view, 1), :] = jnp.sum(total[...], 0, keepdims=True)


class GroupSums:
    def __init__(self, at, links):
        self.at, self.links = at, links

    def start(self, mine, land):
        self.mine, self.land = mine, land
        self.copies = [
            self.links(mine, land.at[hop], peer) for hop, peer in enumerate(self.at.sub_peers())
        ]

    def finish(self):
        wait_all(self.copies)
        value = self.mine[...]
        for hop in range(3):
            value = value + self.land[hop]
        return value


def copy_rows(big, small, target, sem):
    split = big.shape[0]
    copies = [
        pltpu.make_async_copy(big, target.at[pl.ds(0, split)], sem.at[0]),
        pltpu.make_async_copy(small, target.at[pl.ds(split, small.shape[0])], sem.at[1]),
    ]
    for copy in copies:
        copy.start()
    return copies


def weigh(target, line, values):
    sums = jnp.sum(values * values, 0, keepdims=True)
    for lane in range(0, sums.shape[1], LANES):
        target[pl.ds(line, 1), :] += sums[:, lane : lane + LANES]


def forward_kernel(n_dp, images, *refs):
    i_outer, i_mid, i_hid, i_out, h_big, h_small, norm_ref, live_ref, queue_ref, proto_ref = refs[:10]
    (
        o_mid, o_last, o_hid, o_out, o_one, o_two, o_act, o_curve, o_normal, o_stat, o_pooled, o_live,
        o_slope, o_weigh, o_centers, o_turned, o_queue,
    ) = refs[10:27]
    (
        x_ref, w_first, w_mid, w_last, w_hid, w_out, first_w, mid_w, last_w, out_w, columns, act_one,
        act_two, one, two, three, total, pool, sums_a, land_a, sums_b, land_b, sums_c, land_c, pooled,
        queue_total, send_sem, recv_sem, own_sem, x_sem,
    ) = refs[27:]
    at = Place(n_dp)
    links = Links(send_sem, recv_sem)
    x_copies = copy_rows(h_big, h_small, x_ref, x_sem)
    share = w_hid.shape[1]
    w_first[...] = i_outer[0].astype(w_first.dtype)
    at.greet(
        [at.near_peer(hop) for hop in range(1, at.span)] + [at.far_peer] + at.sub_peers()
    )
    low = jnp.bfloat16
    middle = first_w.shape[3]
    channels = x_ref.shape[1]
    rows = x_ref.shape[0]
    mask = live_ref[...][:, :1]
    half = middle // 2

    def flat(source, target, start, size, split):
        line = source.shape[0] // 4
        some = pl.ds(start * line, size * line)
        return (
            lambda cols: source.at[some, cols],
            lambda near, far, cols: target.at[near, far, some, cols],
            split,
        )

    def taps(start, size, split):
        some = pl.ds(start, size)
        return (
            lambda cols: w_mid.at[some, :, cols],
            lambda near, far, cols: mid_w.at[some, near, far, :, cols],
            split,
        )

    quarter = w_out.shape[0] // 4
    out_rows = pl.ds(at.sub * quarter, quarter)
    pieces = [flat(w_first, first_w, 0, 2, 4), flat(w_first, first_w, 2, 2, 4)]
    groups = (((0, 1, 2), (1, 2, 4)), ((3, 1, 4), (4, 1, 2), (5, 2, 4)), ((7, 1, 4), (8, 1, 2)))
    last_of = []
    for group in groups:
        pieces += [taps(*some) for some in group]
        last_of.append(len(pieces))
    pieces += [flat(w_last, last_w, 0, 2, 4), flat(w_last, last_w, 2, 1, 2), flat(w_last, last_w, 3, 1, 4)]
    trunk_pieces = len(pieces)
    pieces += [flat(w_hid, o_hid, part, 1, 1) for part in range(4)]
    pieces.append(
        (
            lambda cols: w_out.at[out_rows],
            lambda near, far, cols: out_w.at[near, far],
            1,
        )
    )
    count = len(pieces)
    mine = {4: lanes_of(at.sub), 2: lanes_of(at.core, half), 1: ALL}
    own, first, second, third, fourth = [], [], [], [], []

    def begin(index):
        if index < count:
            source, target, split = pieces[index]
            cols = mine[split]
            copy = pltpu.make_async_copy(
                source(cols), target(at.near, at.far, cols), own_sem.at[index]
            )
            copy.start()
            own.append(copy)
            first.append(
                [
                    links(source(cols), target(at.near, at.far, cols), at.near_peer(hop))
                    for hop in range(1, at.span)
                ]
            )

    begin(0)
    begin(1)

    def cast_tap(index, carry):
        w_mid[index] = i_mid[index].astype(w_mid.dtype)
        return carry

    lax.fori_loop(0, TAPS, cast_tap, 0)
    begin(2)
    w_last[...] = i_outer[1].astype(w_last.dtype)
    w_hid[...] = i_hid[:, lanes_of(at.sub, share)].astype(w_hid.dtype)
    w_out[...] = i_out[...].astype(w_out.dtype)
    lag = 2
    clock = [0]

    def pump(times=1):
        for _ in range(times):
            tick(clock[0])
            clock[0] += 1

    def need(index):
        while clock[0] <= index + 2 * lag:
            pump()
        wait_all(fourth[index])

    def tick(now):
        if now < count:
            source, target, split = pieces[now]
            own[now].wait()
            wait_all(first[now])
            begin(now + 3)
            slab = target(ALL, at.far, mine[split])
            second.append(links(slab, slab, at.far_peer))
        past = now - lag
        if 0 <= past < count:
            source, target, split = pieces[past]
            second[past].wait()
            slab = target(ALL, ALL, mine[split])
            third.append(links(slab, slab, at.row_peer) if split == 4 else None)
            fourth.append([links(slab, slab, at.core_peer)] if split == 2 else [])
        past = now - 2 * lag
        if 0 <= past < count and pieces[past][2] == 4:
            source, target, split = pieces[past]
            third[past].wait()
            slabs = [target(ALL, ALL, cols) for cols in (mine[4], lanes_of(at.row_sub))]
            fourth[past] = [links(slab, slab, at.core_peer) for slab in slabs]

    tile = rows // 4
    sums = GroupSums(at, links)

    def pack(target, wide):
        target[pl.ds(0, 1), :] = jnp.sum(total[0, :, :wide], 0, keepdims=True)
        target[pl.ds(1, 1), :] = jnp.sum(total[1, :, :wide], 0, keepdims=True)

    def settle(value, count_all, start, wide):
        mean = value[0:1] / count_all
        inverse = lax.rsqrt(value[1:2] / count_all - mean * mean + norm_eps)
        o_stat[pl.ds(0, 1), pl.ds(start, wide)] = mean
        o_stat[pl.ds(1, 1), pl.ds(start, wide)] = inverse
        scale = norm_ref[pl.ds(0, 1), pl.ds(start, wide)] * inverse
        return scale, norm_ref[pl.ds(1, 1), pl.ds(start, wide)] - scale * mean

    centers_of(proto_ref, o_centers, o_turned)
    pump()
    queue_sums(queue_ref, o_turned, o_queue, queue_total, 0)
    pump()
    queue_sums(queue_ref, o_turned, o_queue, queue_total, 1)
    pump()
    o_weigh[...] = jnp.zeros_like(o_weigh)
    weigh(o_weigh, 0, i_outer[0])
    weigh(o_weigh, 1, i_outer[1])
    weigh(o_weigh, 4, i_out[...])

    def weigh_tap(index, carry):
        weigh(o_weigh, 2, i_mid[index])
        return carry

    lax.fori_loop(0, TAPS, weigh_tap, 0)
    pump()

    def weigh_part(index, carry):
        weigh(o_weigh, 3, i_hid[:, lanes_of(index, 512)])
        return carry

    lax.fori_loop(0, i_hid.shape[1] // 512, weigh_part, 0)
    need(0)
    need(1)
    pump()
    for copy in x_copies:
        copy.wait()

    total[...] = jnp.zeros_like(total)

    def step_one(index, carry):
        span = rows_at(index * tile, tile)
        value = jnp.dot(
            x_ref[span, :],
            first_w[...].reshape(channels, middle),
            preferred_element_type=jnp.float32,
        )
        one[span, :] = value
        masked_sums(value, mask, total.at[:, :, pl.ds(0, middle)])
        return carry

    lax.fori_loop(0, 4, step_one, 0)
    pack(sums_a, middle)
    live = jnp.sum(mask, 0, keepdims=True)
    sums_a[pl.ds(2, 1), :] = jnp.broadcast_to(live, (1, middle))
    sums.start(sums_a, land_a)
    pump()
    value = sums.finish()
    per_image = rows // images
    lives = value[2:3, :1]
    count_all = lives * per_image
    o_live[at.sub] = jnp.broadcast_to(live, o_live.shape[1:])
    for hop in range(3):
        o_live[(at.sub + 3 - hop) % 4] = jnp.broadcast_to(land_a[hop, 2:3, :1], o_live.shape[1:])
    scale, shift = settle(value, count_all, 0, middle)

    def step_act(source, target):
        def step(index, carry):
            span = rows_at(index * tile, tile)
            pre = source[span, :] * scale + shift
            target[span, :] = (pre * sigmoid_of(pre)).astype(low)
            return carry

        lax.fori_loop(0, 4, step, 0)

    step_act(one, act_one)
    save = [pltpu.make_async_copy(one, o_one, own_sem.at[count])]
    save[-1].start()
    pump()
    fill_columns(columns, act_one, images, False)

    total[...] = jnp.zeros_like(total)
    for part in range(3):
        for index in range(last_of[part] - len(groups[part]), last_of[part]):
            need(index)

        def step_two(index, carry):
            span = rows_at(index * tile, tile)
            value = jnp.dot(
                columns[span, pl.ds(part * 3 * middle, 3 * middle)],
                mid_w[pl.ds(part * 3, 3)].reshape(3 * middle, middle),
                preferred_element_type=jnp.float32,
            )
            if part:
                value = value + two[span, :]
            two[span, :] = value
            if part == 2:
                masked_sums(value, mask, total.at[:, :, pl.ds(0, middle)])
            return carry

        lax.fori_loop(0, 4, step_two, 0)
    save.append(pltpu.make_async_copy(mid_w, o_mid, own_sem.at[count + 2]))
    save[-1].start()
    pack(sums_b, middle)
    sums.start(sums_b, land_b)
    scale, shift = settle(sums.finish(), count_all, middle, middle)
    step_act(two, act_two)
    save.append(pltpu.make_async_copy(two, o_two, own_sem.at[count + 3]))
    save[-1].start()
    save.append(pltpu.make_async_copy(act_two, o_act, own_sem.at[count + 4]))
    save[-1].start()

    for index in range(trunk_pieces - 3, trunk_pieces):
        need(index)
    save.append(pltpu.make_async_copy(last_w, o_last, own_sem.at[count + 5]))
    save[-1].start()
    total[...] = jnp.zeros_like(total)

    def step_three(index, carry):
        span = rows_at(index * tile, tile)
        for quarter in range(4):
            wide = channels // 4
            cols = pl.ds(quarter * wide, wide)
            weights = last_w[pl.ds(quarter * (at.span // 4), at.span // 4)].reshape(wide, middle)
            value = against(act_two[span, :], weights)
            three[span, cols] = value
            masked_sums(value, mask, total.at[:, :, cols])
        return carry

    lax.fori_loop(0, 4, step_three, 0)
    pack(sums_c, channels)
    sums.start(sums_c, land_c)
    pump()
    scale, shift = settle(sums.finish(), count_all, 2 * middle, channels)

    pool[...] = jnp.zeros_like(pool)
    o_slope[...] = jnp.zeros_like(o_slope)
    wide = pl.ds(2 * middle, channels)
    center = o_stat[pl.ds(0, 1), wide] * o_stat[pl.ds(1, 1), wide]
    base = 0
    for extent, crops in ((BIG, NBIG), (SMALL, NSMALL)):
        lines = crops * images
        into = pl.ds(0, lines) if extent == BIG else pl.ds(NBIG * images, lines)

        def step_out(index, carry):
            span = rows_at(base + index * extent * lines, extent * lines)
            for start in range(0, channels, 512):
                cols = pl.ds(start, 512)
                pre = three[span, cols] * scale[:, start : start + 512]
                pre = pre + shift[:, start : start + 512] + x_ref[span, cols].astype(jnp.float32)
                sigma = sigmoid_of(pre)
                value = pre * sigma
                slope = sigma + value * (1.0 - sigma)
                normal = three[span, cols] * o_stat[1:2, 2 * middle + start : 2 * middle + start + 512]
                normal = normal - center[:, start : start + 512]
                columns[span, cols] = slope.astype(low)
                columns[span, pl.ds(channels + start, 512)] = normal.astype(low)
                pool[into, cols] += jnp.sum(value.reshape(extent, lines, 512), 0)
                o_slope[0, into, cols] += jnp.sum(slope.reshape(extent, lines, 512), 0)
                slope = slope * normal
                o_slope[1, into, cols] += jnp.sum(slope.reshape(extent, lines, 512), 0)
            return carry

        lax.fori_loop(0, extent, step_out, 0)
        pump()
        pooled[into, :] = (pool[into, :] * (1.0 / (extent * extent))).astype(low)
        base += extent * extent * lines

    for index, target in enumerate((o_curve, o_normal)):
        some = columns.at[:, pl.ds(index * channels, channels)]
        save.append(pltpu.make_async_copy(some, target, x_sem.at[index]))
        save[-1].start()

    over = links(pooled, o_pooled.at[at.sub], at.row_peer)
    pair = links(pooled, o_pooled.at[at.sub], at.core_peer)
    o_pooled[at.sub] = pooled[...]
    pump()
    over.wait()
    last = links(o_pooled.at[at.row_sub], o_pooled.at[at.row_sub], at.core_peer)
    need(count - 1)
    some = at.span // 4
    out_own = out_w.at[pl.ds(at.sub * some, some)]
    into = o_out.at[:, :, out_rows]
    own.append(pltpu.make_async_copy(out_own, into, own_sem.at[count - 1]))
    own[-1].start()
    out_copies = [
        links(out_w.at[pl.ds(peer["sub"] * some, some)], into, peer) for peer in at.sub_peers()
    ]
    pair.wait()
    last.wait()
    own[-1].wait()
    wait_all(out_copies)
    for copy in save:
        copy.wait()


def forward_trunk(
    n_dp, collective_id, images, outer, mid, hid, out, big, small, norms, live, queue, prototypes, width
):
    span = n_dp // 2
    height, middle = outer.shape[1:]
    rows, channels = big.shape[0] + small.shape[0], big.shape[1]
    share, narrow = hid.shape[1] // 4, out.shape[1]
    some = jax.ShapeDtypeStruct
    low, full = jnp.bfloat16, jnp.float32
    copies = 17 * (span + 4) + 16
    vmem, anywhere = pl.BlockSpec(memory_space=pltpu.VMEM), pl.BlockSpec(memory_space=pl.ANY)
    return pl.pallas_call(
        functools.partial(forward_kernel, n_dp, images),
        out_shape=(
            some((TAPS, span, 2, mid.shape[1], middle), low),
            some((span, 2, height, middle), low),
            some((span, 2, height, share), low),
            some((span // 4, 2, height, narrow), low),
            some((rows, middle), full),
            some((rows, middle), full),
            some((rows, middle), low),
            some((rows, channels), low),
            some((rows, channels), low),
            some((2, 2 * middle + channels), full),
            some((4, CROPS * images, channels), low),
            some((4, 8, LANES), full),
            some((2, CROPS * images, channels), full),
            some((8, LANES), full),
            some((width, prototypes.shape[1]), low),
            some((prototypes.shape[1], width), low),
            some((queue.shape[0], width), full),
        ),
        in_specs=[vmem] * 4 + [anywhere] * 2 + [vmem] * 4,
        out_specs=(anywhere,) * 9 + (vmem,) * 8,
        scratch_shapes=[
            pltpu.VMEM((rows, channels), low),
            pltpu.VMEM((height, middle), low),
            pltpu.VMEM(mid.shape, low),
            pltpu.VMEM((height, middle), low),
            pltpu.VMEM((height, share), low),
            pltpu.VMEM((height, narrow), low),
            pltpu.VMEM((span, 2, height, middle), low),
            pltpu.VMEM((TAPS, span, 2, mid.shape[1], middle), low),
            pltpu.VMEM((span, 2, height, middle), low),
            pltpu.VMEM((span, 2, height // 4, narrow), low),
            pltpu.VMEM((rows, TAPS * middle), low),
            pltpu.VMEM((rows, middle), low),
            pltpu.VMEM((rows, middle), low),
            pltpu.VMEM((rows, middle), full),
            pltpu.VMEM((rows, middle), full),
            pltpu.VMEM((rows, channels), full),
            pltpu.VMEM((2, 8, channels), full),
            pltpu.VMEM((CROPS * images, channels), full),
            pltpu.VMEM((3, middle), full),
            pltpu.VMEM((3, 3, middle), full),
            pltpu.VMEM((2, middle), full),
            pltpu.VMEM((3, 2, middle), full),
            pltpu.VMEM((2, channels), full),
            pltpu.VMEM((3, 2, channels), full),
            pltpu.VMEM((CROPS * images, channels), low),
            pltpu.VMEM((8, width), full),
            pltpu.SemaphoreType.DMA((copies,)),
            pltpu.SemaphoreType.DMA((copies,)),
            pltpu.SemaphoreType.DMA((17 + 6,)),
            pltpu.SemaphoreType.DMA((2,)),
        ],
        compiler_params=pltpu.CompilerParams(
            collective_id=collective_id, has_side_effects=True, vmem_limit_bytes=62 * MIB
        ),
        name="forward_trunk",
    )(outer, mid, hid, out, big, small, norms, live, queue, prototypes)


def plus(left, right):
    return left.astype(jnp.float32) + right.astype(jnp.float32)


def piece_list(height, mid_height, proto_height, refs):
    first, mid, last, proto = refs
    half, quarter = height // 2, height // 4
    pieces = [last + (0, 1, part * half, half, 2) for part in range(2)]
    for start, taps in ((0, 1), (1, 1), (2, 1), (3, 1), (4, 1), (5, 1), (6, 1), (7, 2)):
        pieces.append(mid + (start, taps, 0, mid_height, 1))
    pieces += [first + (0, 1, part * quarter, quarter, 0) for part in range(4)]
    return pieces + [proto + (0, 1, 0, proto_height, 5)]


def backward_kernel(n_dp, images, *refs):
    p_pool, slope_ref, stat_ref, norm_ref, live_ref, lives_ref, extra_ref, g_hid, g_some, g_proto = refs[:10]
    h_big, h_small, h_curve, h_normal, h_one, h_two, h_act, h_last, h_mid = refs[10:19]
    o_first, o_mid, o_last, o_hid, o_out, o_proto, o_vec, o_sq = refs[19:27]
    (
        x_ref, one, two, act_two, last_w, mid_w, act_one, wide_low, work, thin_low, g_first, g_mid,
        g_last, total, pair_land, pair_sum, row_land, grad_pool, sums_a, land_a, sums_b, land_b,
        sums_c, land_c, hid_in, hid_sum, hid_land, g_out, out_in, out_sum, out_land, vec, vec_land,
        sq_mine, sq_land, send_sem, recv_sem, own_sem, x_sem,
    ) = refs[27:66]
    bufs = refs[66:]
    at = Place(n_dp)
    links = Links(send_sem, recv_sem)
    span = at.span
    at.greet(at.dp_peers() + at.sub_peers())
    low = jnp.bfloat16
    rows, channels = x_ref.shape
    middle = one.shape[1]
    height = g_last.shape[3]
    mask = live_ref[...][:, :1]
    tile = rows // 4

    loads = {}
    for index, (name, source, target) in enumerate(
        (
            ("one", h_one, one), ("curve", h_curve, wide_low), ("normal", h_normal, x_ref),
            ("last", h_last, last_w), ("two", h_two, two), ("act", h_act, act_two), ("mid", h_mid, mid_w),
        )
    ):
        loads[name] = pltpu.make_async_copy(source, target, own_sem.at[index])
        loads[name].start()

    pair = [
        links(p_pool.at[2 * line + (1 - at.core)], pair_land.at[line], at.core_peer)
        for line in (1 - at.row, at.row)
    ]
    far_copies = [links(g_hid.at[:, 1 - at.far], hid_in, at.far_peer)]
    some = g_some.shape[0]
    block = g_out.at[pl.ds(at.sub * some, some)]
    own_out = pltpu.make_async_copy(g_some, block, own_sem.at[7])
    own_out.start()
    out_copies = [links(g_some, block, peer) for peer in at.sub_peers()]
    pair[0].wait()
    pair_sum[...] = plus(p_pool[2 * (1 - at.row) + at.core], pair_land[1 - at.row]).astype(low)
    over = links(pair_sum, row_land, at.row_peer)
    pair[1].wait()

    wholes = [(g_hid, hid_in, hid_sum, hid_land), (g_out, out_in, out_sum, out_land)]

    def whole_far(which):
        source, landed, summed, land = wholes[which]
        far_copies[which].wait()
        for near in range(span):
            summed[near] = plus(source[near, at.far], landed[near]).astype(low)
        return [
            links(summed.at[at.near_index(hop)], land.at[hop - 1], at.near_peer(hop))
            for hop in range(1, span)
        ]

    def whole_near(which, copies):
        source, landed, summed, land = wholes[which]
        wait_all(copies)
        value = summed[at.near].astype(jnp.float32)
        for hop in range(1, span):
            value = value + land[hop - 1].astype(jnp.float32)
        return value.astype(low)

    sq_mine[0] = jnp.zeros_like(sq_mine[0])

    def squares_of(matrix, value):
        value = value.astype(jnp.float32)
        line = jnp.sum(value * value, 0, keepdims=True)
        for lane in range(0, line.shape[1], LANES):
            sq_mine[0, pl.ds(matrix, 1), :] += line[:, lane : lane + LANES]

    pieces = piece_list(
        height,
        g_mid.shape[3],
        g_proto.shape[3],
        ((g_first, o_first), (g_mid, o_mid), (g_last, o_last), (g_proto, o_proto)),
    )
    proto = len(pieces) - 1
    mine, beside = lanes_of(at.sub), lanes_of(at.row_sub)
    state = [0] * len(pieces)
    flight = [None] * len(pieces)

    def loop(count, body):
        def step(index, carry):
            body(index)
            return carry

        lax.fori_loop(0, count, step, 0)

    def go(index):
        source, target, start, taps, line, size, matrix = pieces[index]
        held, second, third, nears = bufs[4 * index : 4 * index + 4]
        stage = state[index]
        state[index] += 1
        row_first = index % 2 == 0
        lines, some = pl.ds(line, size), pl.ds(start, taps)
        if stage == 0:
            flight[index] = [
                links(
                    source.at[some, :, :, lines, lanes_of(2 * row + (1 - at.core))],
                    held.at[row],
                    at.core_peer,
                )
                for row in range(2)
            ]
            return
        wait_all(flight[index])
        if stage == 1:
            for row in range(2):
                cols = lanes_of(2 * row + at.core)

                def body(at_block):
                    tap, near, far = at_block // (2 * span), at_block // 2 % span, at_block % 2
                    held[row, tap, near, far] = plus(
                        source[start + tap, near, far, lines, cols], held[row, tap, near, far]
                    ).astype(low)

                loop(taps * span * 2, body)
            if row_first:
                flight[index] = [links(held.at[1 - at.row], second, at.row_peer)]
            else:
                flight[index] = [links(held.at[:, :, :, 1 - at.far], second, at.far_peer)]
        elif stage == 2:
            if row_first:

                def body(at_block):
                    tap, near, far = at_block // (2 * span), at_block // 2 % span, at_block % 2
                    second[tap, near, far] = plus(
                        held[at.row, tap, near, far], second[tap, near, far]
                    ).astype(low)

                loop(taps * span * 2, body)
                flight[index] = [links(second.at[:, :, 1 - at.far], third, at.far_peer)]
            else:

                def body(at_block):
                    row, tap, near = at_block // (taps * span), at_block // span % taps, at_block % span
                    second[row, tap, near] = plus(
                        held[row, tap, near, at.far], second[row, tap, near]
                    ).astype(low)

                loop(taps * span * 2, body)
                flight[index] = [links(second.at[1 - at.row], third, at.row_peer)]
        elif stage == 3:

            def body(at_block):
                tap, near = at_block // span, at_block % span
                part = second[tap, near, at.far] if row_first else second[at.row, tap, near]
                third[tap, near] = plus(part, third[tap, near]).astype(low)

            loop(taps * span, body)
            flight[index] = [
                links(third.at[:, at.near_index(hop)], nears.at[hop - 1], at.near_peer(hop))
                for hop in range(1, span)
            ]
        elif stage == 4 and index == proto:
            value = third[0, at.near].astype(jnp.float32)
            for hop in range(1, span):
                value = value + nears[hop - 1, 0].astype(jnp.float32)
            o_proto[at.near, at.far, :, mine] = value.astype(low)
            slab = o_proto.at[at.near, at.far, :, mine]
            flight[index] = [links(slab, slab, at.near_peer(hop)) for hop in range(1, span)]
        elif stage == 5 and index == proto:
            slab = o_proto.at[:, at.far, :, mine]
            flight[index] = [links(slab, slab, at.far_peer)]
        elif stage == 6:
            slab = o_proto.at[:, :, :, mine]
            flight[index] = [links(slab, slab, at.row_peer)]
        elif stage == 7:
            slabs = [o_proto.at[:, :, :, cols] for cols in (mine, beside)]
            flight[index] = [links(slab, slab, at.core_peer) for slab in slabs]
        elif stage == 4:
            for tap in range(taps):
                value = third[tap, at.near].astype(jnp.float32)
                for hop in range(1, span):
                    value = value + nears[hop - 1, tap].astype(jnp.float32)
                value = value.astype(low)
                squares_of(matrix, value)
                target[start + tap, lines, mine] = value
            slab = target.at[some, lines, mine]
            flight[index] = [links(slab, slab, at.row_peer)]
        elif stage == 5:
            slabs = [target.at[some, lines, cols] for cols in (mine, beside)]
            flight[index] = [links(slab, slab, at.core_peer) for slab in slabs]

    go(proto)

    def go_pair(number):
        go(2 * number)
        go(2 * number + 1)

    count_all = jnp.sum(lives_ref[...][:, :1, :1], 0) * float(rows // images)
    sums = GroupSums(at, links)

    def terms(start, wide):
        cols = pl.ds(start, wide)
        mean, inverse = stat_ref[pl.ds(0, 1), cols], stat_ref[pl.ds(1, 1), cols]
        scale = norm_ref[pl.ds(0, 1), cols] * inverse
        return mean * inverse, inverse, scale, norm_ref[pl.ds(1, 1), cols] - scale * mean

    def slope_of(pre):
        sigma = sigmoid_of(pre)
        return sigma + pre * sigma * (1.0 - sigma)

    def pack(target, wide):
        target[pl.ds(0, 1), :] = jnp.sum(total[0, :, :wide], 0, keepdims=True)
        target[pl.ds(1, 1), :] = jnp.sum(total[1, :, :wide], 0, keepdims=True)

    center_one, inverse_one, scale_one, shift_one = terms(0, middle)
    center_two, inverse_two, scale_two, shift_two = terms(middle, middle)
    scale_three = terms(2 * middle, channels)[2]
    loads["one"].wait()

    def step_act(index):
        span_rows = rows_at(index * tile, tile)
        pre = one[span_rows, :] * scale_one + shift_one
        act_one[span_rows, :] = (pre * sigmoid_of(pre)).astype(low)

    loop(4, step_act)
    go(proto)
    own_out.wait()
    wait_all(out_copies)
    far_copies.append(links(g_out.at[:, 1 - at.far], out_in, at.far_peer))
    value = plus(p_pool[at.sub], pair_land[at.row])
    over.wait()
    value = value + row_land[...].astype(jnp.float32)
    big = NBIG * images
    grad_pool[pl.ds(0, big), :] = value[:big] * (1.0 / (BIG * BIG))
    grad_pool[pl.ds(big, NSMALL * images), :] = value[big:] * (1.0 / (SMALL * SMALL))
    for which in range(2):
        sums_c[pl.ds(which, 1), :] = jnp.sum(grad_pool[...] * slope_ref[which], 0, keepdims=True)
    sums.start(sums_c, land_c)
    loads["curve"].wait()
    loads["normal"].wait()
    both_three = sums.finish()
    vec[...] = extra_ref[...]
    vec[pl.ds(1, 1), :] = both_three[1:2]
    vec[pl.ds(3, 1), :] = both_three[0:1]
    both_three = both_three / count_all
    go(proto)

    chunk = channels // 4
    for quarter in range(4):
        cols = pl.ds(quarter * chunk, chunk)
        here = slice(quarter * chunk, (quarter + 1) * chunk)
        base = 0
        for extent, crops in ((BIG, NBIG), (SMALL, NSMALL)):
            lines = crops * images
            into = pl.ds(0, lines) if extent == BIG else pl.ds(big, lines)

            def step_grad(index):
                span_rows = rows_at(base + index * extent * lines, extent * lines)
                curve = wide_low[span_rows, cols].astype(jnp.float32)
                grad = curve.reshape(extent, lines, chunk) * grad_pool[into, cols]
                normal = x_ref[span_rows, cols].astype(jnp.float32)
                back = both_three[0:1, here] + normal * both_three[1:2, here]
                back = back.reshape(extent * crops, images, chunk) * mask
                grad = grad.reshape(extent * crops, images, chunk) - back
                grad = grad.reshape(extent * lines, chunk) * scale_three[:, here]
                wide_low[span_rows, cols] = grad.astype(low)

            loop(extent, step_grad)
            base += extent * extent * lines
    x_copies = copy_rows(h_big, h_small, x_ref, x_sem)
    loads["last"].wait()

    go(proto)
    near_hid, near_out = whole_far(0), whole_far(1)

    def norm_sums(grad, normal):
        total[0, :, :middle] += jnp.sum(grad.reshape(tile // 8, 8, middle), 0)
        total[1, :, :middle] += jnp.sum((grad * normal).reshape(tile // 8, 8, middle), 0)

    loads["two"].wait()
    loads["act"].wait()
    total[...] = jnp.zeros_like(total)

    def step_two(index):
        span_rows = rows_at(index * tile, tile)
        grad = jnp.dot(
            wide_low[span_rows, :],
            last_w[...].reshape(channels, middle),
            preferred_element_type=jnp.float32,
        )
        grad = grad * slope_of(two[span_rows, :] * scale_two + shift_two)
        work[span_rows, :] = grad
        norm_sums(grad, two[span_rows, :] * inverse_two - center_two)

    loop(4, step_two)
    pack(sums_a, middle)
    sums.start(sums_a, land_a)

    def weight_rows(target, left, right):
        part = 256
        shards = max(1, part // height)
        for index in range(channels // part):
            value = cross_rows(left[:, pl.ds(index * part, part)], right[...]).astype(low)
            if shards == 1:
                target[0, index // 2, index % 2] = value
            else:
                some = pl.ds(index * (shards // 2), shards // 2)
                target[0, some] = value.reshape(shards // 2, 2, height, middle)

    weight_rows(g_last, wide_low, act_two)
    go_pair(0)

    def settle_grad(source, center, inverse, scale, both):
        def step(index):
            span_rows = rows_at(index * tile, tile)
            normal = source[span_rows, :] * inverse - center
            back = both[0:1] + normal * both[1:2]
            back = (back.reshape(tile // 8, 8, middle) * mask).reshape(tile, middle)
            thin_low[span_rows, :] = ((work[span_rows, :] - back) * scale).astype(low)

        loop(4, step)

    both_two = sums.finish()
    settle_grad(two, center_two, inverse_two, scale_two, both_two / count_all)
    vec[pl.ds(0, 1), pl.ds(middle, middle)] = both_two[1:2]
    vec[pl.ds(0, 1), pl.ds(3 * middle, middle)] = both_two[0:1]
    go_pair(0)

    loads["mid"].wait()
    moves, zeros = tap_blocks(images, True)
    total[...] = jnp.zeros_like(total)
    for part in range(3):
        for slot in range(3):
            cols = pl.ds(slot * middle, middle)
            for target, start, size in moves[3 * part + slot]:
                wide_low[pl.ds(target, size), cols] = thin_low[pl.ds(start, size), :]
            for target, size in zeros[3 * part + slot]:
                wide_low[pl.ds(target, size), cols] = jnp.zeros((size, middle), low)

        for slot in range(3):
            value = cross_rows(act_one[...], wide_low[:, pl.ds(slot * middle, middle)]).astype(low)
            g_mid[3 * part + slot] = value.reshape(g_mid.shape[1:])
        for number in ((1,), (2, 3), (4,))[part]:
            go_pair(number)

        def step_one(index):
            span_rows = rows_at(index * tile, tile)
            grad = against(
                wide_low[span_rows, pl.ds(0, middle)], mid_w[3 * part].reshape(middle, middle)
            )
            for slot in range(1, 3):
                grad = grad + against(
                    wide_low[span_rows, pl.ds(slot * middle, middle)],
                    mid_w[3 * part + slot].reshape(middle, middle),
                )
            if part:
                grad = grad + work[span_rows, :]
            if part == 2:
                grad = grad * slope_of(one[span_rows, :] * scale_one + shift_one)
                norm_sums(grad, one[span_rows, :] * inverse_one - center_one)
            work[span_rows, :] = grad

        loop(4, step_one)
        if part == 2:
            pack(sums_b, middle)
            sums.start(sums_b, land_b)
        for number in ((0, 1), (0, 1, 2, 3), (0, 1, 2, 3, 4))[part]:
            go_pair(number)
    value = whole_near(0, near_hid)
    wide = g_hid.shape[3]
    squares_of(3, value)
    slabs = [o_hid.at[:, lanes_of(which, wide)] for which in (at.sub, at.row_sub)]
    o_hid[:, lanes_of(at.sub, wide)] = value
    hid_row = links(slabs[0], slabs[0], at.row_peer)
    value = whole_near(1, near_out)
    squares_of(4, value)
    o_out[...] = value
    go(proto)

    both_one = sums.finish()
    settle_grad(one, center_one, inverse_one, scale_one, both_one / count_all)
    vec[pl.ds(0, 1), pl.ds(0, middle)] = both_one[1:2]
    vec[pl.ds(0, 1), pl.ds(2 * middle, middle)] = both_one[0:1]
    wide = vec.shape[1] // 4
    vec_cols = lanes_of(at.sub, wide)
    vec_copies = [
        links(vec.at[:, vec_cols], vec_land.at[hop], peer)
        for hop, peer in enumerate(at.dp_peers())
    ]
    for number in range(1, 5):
        go_pair(number)
    hid_row.wait()
    final = [links(slab, slab, at.core_peer) for slab in slabs]

    for copy in x_copies:
        copy.wait()
    weight_rows(g_first, x_ref, thin_low)
    go_pair(5)
    go_pair(6)

    numbers = range(len(pieces) // 2)
    tick = 0
    sent = False
    while min(state[:proto]) < 6:
        for number in numbers:
            if state[2 * number] < 6:
                go_pair(number)
        if tick < 3:
            go(proto)
        if tick == 1:
            wait_all(vec_copies)
            value = vec[:, vec_cols]
            for hop in range(n_dp - 1):
                value = value + vec_land[hop]
            o_vec[:, vec_cols] = value
            vec_final = [
                links(o_vec.at[:, vec_cols], o_vec.at[:, vec_cols], peer)
                for peer in at.sub_peers()
            ]
        if not sent and min(state[:proto]) >= 5:
            sent = True
            sq_copies = [
                links(sq_mine.at[0], sq_land.at[hop], peer)
                for hop, peer in enumerate(at.dp_peers())
            ]
        tick += 1
    wait_all(sq_copies)
    value = sq_mine[0]
    for hop in range(n_dp - 1):
        value = value + sq_land[hop]
    sq_mine[1] = value
    sq_copies = [
        links(sq_mine.at[1], sq_land.at[n_dp - 1 + hop], peer)
        for hop, peer in enumerate(at.sub_peers())
    ]
    wait_all(sq_copies)
    for hop in range(3):
        value = value + sq_land[n_dp - 1 + hop]
    o_sq[...] = value
    for copies in flight:
        wait_all(copies)
    wait_all(final)
    wait_all(vec_final)


def backward_trunk(
    n_dp, collective_id, images, pooled, slopes, stat, norms, live, lives, extra, hid, out, proto, big,
    small, curve, normal, one, two, act, last, mid,
):
    span = n_dp // 2
    low, full = jnp.bfloat16, jnp.float32
    rows, channels = curve.shape
    middle = one.shape[1]
    height, mid_height = last.shape[2], mid.shape[3]
    narrow = out.shape[1]
    crops = CROPS * images
    some = jax.ShapeDtypeStruct
    bufs = []
    for index, piece in enumerate(piece_list(height, mid_height, proto.shape[0] // n_dp, ((0, 0),) * 4)):
        taps, block = piece[3], (piece[5], LANES)
        bufs.append(pltpu.VMEM((2, taps, span, 2) + block, low))
        if index % 2 == 0:
            bufs.append(pltpu.VMEM((taps, span, 2) + block, low))
        else:
            bufs.append(pltpu.VMEM((2, taps, span) + block, low))
        bufs.append(pltpu.VMEM((taps, span) + block, low))
        bufs.append(pltpu.VMEM((span - 1, taps) + block, low))
    copies = 15 * (span + 6) + 3 * (span + 4) + 2 * n_dp + 40
    vmem, anywhere = pl.BlockSpec(memory_space=pltpu.VMEM), pl.BlockSpec(memory_space=pl.ANY)
    return pl.pallas_call(
        functools.partial(backward_kernel, n_dp, images),
        out_shape=(
            some((1, height, middle), low),
            some((TAPS, mid_height, middle), low),
            some((1, height, middle), low),
            some((height, 4 * hid.shape[1]), low),
            some((height, narrow), low),
            some((span, 2, proto.shape[0] // n_dp, proto.shape[1]), low),
            some(extra.shape, full),
            some((8, LANES), full),
        ),
        in_specs=[vmem] * 10 + [anywhere] * 9,
        out_specs=(vmem,) * 8,
        scratch_shapes=[
            pltpu.VMEM((rows, channels), low),
            pltpu.VMEM((rows, middle), full),
            pltpu.VMEM((rows, middle), full),
            pltpu.VMEM((rows, middle), low),
            pltpu.VMEM((span, 2, height, middle), low),
            pltpu.VMEM((TAPS, span, 2, mid_height, middle), low),
            pltpu.VMEM((rows, middle), low),
            pltpu.VMEM((rows, channels), low),
            pltpu.VMEM((rows, middle), full),
            pltpu.VMEM((rows, middle), low),
            pltpu.VMEM((1, span, 2, height, middle), low),
            pltpu.VMEM((TAPS, span, 2, mid_height, middle), low),
            pltpu.VMEM((1, span, 2, height, middle), low),
            pltpu.VMEM((2, 8, middle), full),
            pltpu.VMEM((2, crops, channels), low),
            pltpu.VMEM((crops, channels), low),
            pltpu.VMEM((crops, channels), low),
            pltpu.VMEM((crops, channels), full),
            pltpu.VMEM((2, middle), full),
            pltpu.VMEM((3, 2, middle), full),
            pltpu.VMEM((2, middle), full),
            pltpu.VMEM((3, 2, middle), full),
            pltpu.VMEM((2, channels), full),
            pltpu.VMEM((3, 2, channels), full),
            pltpu.VMEM((span, height, hid.shape[1]), low),
            pltpu.VMEM((span, height, hid.shape[1]), low),
            pltpu.VMEM((span - 1, height, hid.shape[1]), low),
            pltpu.VMEM((span, 2, height, narrow), low),
            pltpu.VMEM((span, height, narrow), low),
            pltpu.VMEM((span, height, narrow), low),
            pltpu.VMEM((span - 1, height, narrow), low),
            pltpu.VMEM(extra.shape, full),
            pltpu.VMEM((n_dp - 1, extra.shape[0], extra.shape[1] // 4), full),
            pltpu.VMEM((2, 8, LANES), full),
            pltpu.VMEM((n_dp + 2, 8, LANES), full),
            pltpu.SemaphoreType.DMA((copies,)),
            pltpu.SemaphoreType.DMA((copies,)),
            pltpu.SemaphoreType.DMA((8,)),
            pltpu.SemaphoreType.DMA((2,)),
        ]
        + bufs,
        compiler_params=pltpu.CompilerParams(
            collective_id=collective_id, has_side_effects=True, vmem_limit_bytes=62 * MIB
        ),
        name="backward_trunk",
    )(
        pooled,
        slopes,
        stat,
        norms,
        live,
        lives,
        extra,
        hid.reshape(span, 2, height, hid.shape[1]),
        out.reshape(span // 4, 2, height, narrow),
        proto.reshape(1, span, 2, proto.shape[0] // n_dp, proto.shape[1]),
        big,
        small,
        curve,
        normal,
        one,
        two,
        act,
        last,
        mid,
    )


def sinkhorn_kernel(
    axis,
    count,
    protos,
    queue_ref,
    centers_ref,
    turned_ref,
    pooled_ref,
    hid_ref,
    out_ref,
    norm_ref,
    live_ref,
    lives_ref,
    weigh_ref,
    first_ref,
    proto_grad_ref,
    d_hid_ref,
    d_out_ref,
    back_ref,
    extra_ref,
    partial_ref,
    act,
    normal,
    grads,
    lows,
    embed_ref,
    four,
    four_land,
    grad,
    parts_land,
    kept,
    scores,
    mine,
    landed,
    shift,
    total,
    send_sem,
    recv_sem,
):
    me = lax.axis_index(axis)
    views, rows, _ = queue_ref.shape
    width = turned_ref.shape[1]
    images = live_ref.shape[0]
    tile = row_tile(rows)
    part = 512
    parts = range(0, width, part)
    mask = live_ref[...][:, :1]
    crops = CROPS * images
    share = hid_ref.shape[1]
    low = jnp.bfloat16
    greet(axis, count)

    slots = lax.broadcasted_iota(jnp.int32, (images, 1), 0).astype(jnp.float32)
    masks = [jnp.where(slots < lives_ref[member, :images, :1], 1.0, 0.0) for member in range(count)]
    live_group = sum(lives_ref[member, :1, :1] for member in range(count))
    count_crops = live_group * float(CROPS)

    def spread(values, member):
        return (values.reshape(CROPS, images, values.shape[1]) * masks[member]).reshape(values.shape)

    sums = jnp.zeros((1, share), jnp.float32)
    squares = jnp.zeros((1, share), jnp.float32)
    for member in range(count):
        value = jnp.dot(pooled_ref[member], hid_ref[...], preferred_element_type=jnp.float32)
        normal[member] = value
        masked = spread(value, member)
        sums = sums + jnp.sum(masked, 0, keepdims=True)
        squares = squares + jnp.sum(masked * value, 0, keepdims=True)
    mean = sums / count_crops
    inverse_four = lax.rsqrt(squares / count_crops - mean * mean + norm_eps)
    own = pl.ds(pl.multiple_of(norm_ref.shape[1] - count * share + me * share, LANES), share)
    gain, bias = norm_ref[pl.ds(0, 1), own], norm_ref[pl.ds(1, 1), own]
    for member in range(count):
        value = (normal[member] - mean) * inverse_four
        normal[member] = value
        pre = value * gain + bias
        act[member] = (pre * sigmoid_of(pre)).astype(low)
        partial_ref[member] = jnp.dot(act[member], out_ref[...], preferred_element_type=jnp.float32)

    def start_group(turn, source, target):
        copies = []
        for hop in range(1, count):
            to = lax.rem(me + hop, count)
            copy = pltpu.make_async_remote_copy(
                src_ref=source(to),
                dst_ref=target(hop),
                send_sem=send_sem.at[turn, hop],
                recv_sem=recv_sem.at[turn, hop],
                device_id={axis: to},
                device_id_type=MESH,
            )
            copy.start()
            copies.append(copy)
        return copies

    def to_group(turn, source, target):
        for copy in start_group(turn, source, target):
            copy.wait()

    to_group(ITERS, lambda to: partial_ref.at[to], lambda hop: parts_land.at[hop])
    embedding = partial_ref[me]
    for hop in range(1, count):
        embedding = embedding + parts_land[hop]
    inverse = lax.rsqrt(jnp.sum(embedding * embedding, 1, keepdims=True) + unit_eps)
    unit = embedding * inverse
    unit_low = unit.astype(jnp.bfloat16)

    def sum_group(turn):
        copies = []
        for hop in range(1, count):
            copy = pltpu.make_async_remote_copy(
                src_ref=mine.at[turn],
                dst_ref=landed.at[turn, hop],
                send_sem=send_sem.at[turn, hop],
                recv_sem=recv_sem.at[turn, hop],
                device_id={axis: lax.rem(me + hop, count)},
                device_id_type=MESH,
            )
            copy.start()
            copies.append(copy)
        for copy in copies:
            copy.wait()
        whole = mine[turn]
        for hop in range(1, count):
            whole = whole + landed[turn, hop]
        return whole

    for start in parts:
        cols = pl.ds(start, part)
        scores[:, cols] = jnp.dot(
            unit_low, turned_ref[:, cols], preferred_element_type=jnp.float32
        )
        for view in range(views):
            lines = pl.ds(view * images, images)
            shares = jnp.exp2(scores[lines, cols] * SINK2) * mask
            mine[0, pl.ds(view, 1), cols] = first_ref[pl.ds(view, 1), cols] + jnp.sum(
                shares, 0, keepdims=True
            )
    real = lax.broadcasted_iota(jnp.int32, (1, width), 1) < protos
    first = sum_group(0)
    shift[...] = jnp.where(real, jnp.log2(first), 1e30)

    for turn in range(1, ITERS):
        for view in range(views):
            lines = pl.ds(view * images, images)
            row = pl.ds(view, 1)
            if turn == 1:
                own = jnp.exp2(scores[lines, :] * SINK2 - shift[row, :]) * mask
                weight = jnp.sum(own, 1, keepdims=True)
            else:
                own = jnp.exp2(scores[lines, :] * SINK2 - first_log[row, :]) * mask
                weight = jnp.sum(own * shift[row, :], 1, keepdims=True)
            total[...] = own / (weight + (1.0 - mask))

            def step(index, carry):
                span = pl.ds(index * tile, tile)
                if turn == 1:
                    lines = queue_ref[view, span, :]
                sums = jnp.zeros((tile, LANES), jnp.float32)
                for start in parts:
                    cols = pl.ds(start, part)
                    if turn == 1:
                        raw = jnp.dot(lines, turned_ref[:, cols], preferred_element_type=jnp.float32)
                        shares = jnp.exp2(raw * SINK2 - shift[row, cols])
                        kept[view, span, cols] = shares
                    else:
                        shares = kept[view, span, cols] * shift[row, cols]
                    for lane in range(0, part, LANES):
                        sums = sums + shares[:, lane : lane + LANES]
                scale = 1.0 / jnp.sum(sums, 1, keepdims=True)
                for start in parts:
                    cols = pl.ds(start, part)
                    scaled = kept[view, span, cols] * scale
                    total[:, cols] += jnp.sum(scaled.reshape(tile // 8, 8, part), 0)
                return carry

            lax.fori_loop(0, rows // tile, step, 0)
            mine[turn, row, :] = jnp.sum(total[...], 0, keepdims=True)
        if turn == 1:
            first_log = shift[...]
        whole = sum_group(turn)
        shift[...] = jnp.where(real, 1.0 / whole, 0.0)

    codes = []
    for view in range(views):
        lines = pl.ds(view * images, images)
        own = jnp.exp2(scores[lines, :] * SINK2 - first_log[view : view + 1, :]) * mask
        own = own * shift[pl.ds(view, 1), :]
        codes.append(own / (jnp.sum(own, 1, keepdims=True) + (1.0 - mask)))
    code_total = codes[0] + codes[1]
    loss = jnp.zeros((images, 1), jnp.float32)
    for crop in range(CROPS):
        lines = pl.ds(crop * images, images)
        raw = jnp.where(real, scores[lines, :] * SOFT2, -1e30)
        raw = raw - jnp.max(raw, 1, keepdims=True)
        powers = jnp.exp2(raw)
        norm = jnp.sum(powers, 1, keepdims=True)
        others = code_total - codes[crop] if crop < NBIG else code_total
        logs = jnp.where(real, (raw - jnp.log2(norm)) / LOG2E, 0.0)
        loss = loss - jnp.sum(others * logs, 1, keepdims=True)
        weight = (NBIG - 1.0 if crop < NBIG else float(NBIG)) * mask / norm
        grad[lines, :] = (weight * powers - others) / (PAIRS * softmax_temp)
    grad_unit = jnp.zeros(unit.shape, jnp.float32)
    for start in parts:
        cols = pl.ds(start, part)
        some = grad[:, cols].astype(jnp.bfloat16)
        grad_unit = grad_unit + jnp.dot(
            some, centers_ref[cols, :], preferred_element_type=jnp.float32
        )
        for first in range(start, start + part, 256):
            value = cross_rows(grad[:, pl.ds(first, 256)].astype(jnp.bfloat16), unit_low)
            lines = pl.ds(first % (width // 4), 256)
            proto_grad_ref[lines, pl.ds(first // (width // 4) * LANES, LANES)] = value.astype(low)
    grad_embed = inverse * (
        grad_unit - unit * jnp.sum(unit * grad_unit, 1, keepdims=True)
    )
    embed_ref[me] = grad_embed.astype(jnp.bfloat16)
    to_group(ITERS + 1, lambda to: embed_ref.at[me], lambda hop: embed_ref.at[me])

    gain_sum = jnp.zeros((1, share), jnp.float32)
    bias_sum = jnp.zeros((1, share), jnp.float32)
    for member in range(count):
        value = against(embed_ref[member], out_ref[...])
        pre = normal[member] * gain + bias
        sigma = sigmoid_of(pre)
        value = value * (sigma + pre * sigma * (1.0 - sigma))
        grads[member] = value
        bias_sum = bias_sum + jnp.sum(value, 0, keepdims=True)
        gain_sum = gain_sum + jnp.sum(value * normal[member], 0, keepdims=True)
    four[pl.ds(0, 1), :] = gain_sum
    four[pl.ds(1, 1), :] = bias_sum
    four[pl.ds(2, 1), :] = jnp.broadcast_to(
        jnp.sum(loss, 0, keepdims=True) / PAIRS, (1, share)
    )
    copies = start_group(ITERS + 2, lambda to: four, lambda hop: four_land.at[hop])
    scale = gain * inverse_four
    for member in range(count):
        value = spread((bias_sum + normal[member] * gain_sum) / count_crops, member)
        lows[member] = ((grads[member] - value) * scale).astype(low)
    embeds = embed_ref[...].reshape(count * crops, embed_ref.shape[2])
    d_out_ref[...] = cross_rows(act[...].reshape(count * crops, share), embeds).astype(low)
    low_rows = lows[...].reshape(count * crops, share)
    for start in range(0, pooled_ref.shape[2], 256):
        left = pooled_ref[:, :, pl.ds(start, 256)].reshape(count * crops, 256)
        d_hid_ref[pl.ds(start, 256), :] = cross_rows(left, low_rows).astype(low)
        back = against(low_rows, hid_ref[pl.ds(start, 256), :]).astype(low)
        back_ref[:, :, pl.ds(start, 256)] = back.reshape(count, crops, 256)
    extra_ref[...] = jnp.zeros_like(extra_ref)
    for copy in copies:
        copy.wait()
    loss_group = jnp.zeros((1, 1), jnp.float32)
    for hop in range(count):
        source = (me + count - hop) % count
        value = four_land[hop] if hop else four[...]
        extra_ref[pl.ds(2, 1), lanes_of(source, share)] = value[0:1]
        extra_ref[pl.ds(4, 1), lanes_of(source, share)] = value[1:2]
        loss_group = loss_group + value[2:3, :1]
    lane = lax.broadcasted_iota(jnp.int32, (1, extra_ref.shape[1]), 1)
    line = jnp.where(lane == 0, loss_group, 0.0) + jnp.where(lane == 1, live_group, 0.0)
    for which in range(5):
        value = jnp.sum(weigh_ref[pl.ds(which, 1), :], 1, keepdims=True)
        line = line + jnp.where(lane == 2 + which, value, 0.0)
    extra_ref[pl.ds(5, 1), :] = line


def sinkhorn(
    sizes, collective_id, protos, queue, centers, turned, pooled, hid, out, norms, live, lives, weigh,
    first,
):
    count = sizes["sub"]
    views, rows, depth = queue.shape
    width = turned.shape[1]
    crops, channels = pooled.shape[1:]
    share = hid.shape[1]
    low, full = jnp.bfloat16, jnp.float32
    some = jax.ShapeDtypeStruct
    turns = ITERS + 3
    return pl.pallas_call(
        functools.partial(sinkhorn_kernel, "sub", count, protos),
        out_shape=(
            some((width // 4, 4 * depth), low),
            some((channels, share), low),
            some((share, depth), low),
            some((count, crops, channels), low),
            some((8, count * share), full),
        ),
        in_specs=[pl.BlockSpec(memory_space=pltpu.VMEM)] * 11,
        out_specs=(pl.BlockSpec(memory_space=pltpu.VMEM),) * 5,
        scratch_shapes=[
            pltpu.VMEM((count, crops, depth), full),
            pltpu.VMEM((count, crops, share), low),
            pltpu.VMEM((count, crops, share), full),
            pltpu.VMEM((count, crops, share), full),
            pltpu.VMEM((count, crops, share), low),
            pltpu.VMEM((count, crops, depth), low),
            pltpu.VMEM((3, share), full),
            pltpu.VMEM((count, 3, share), full),
            pltpu.VMEM((crops, width), full),
            pltpu.VMEM((count, crops, depth), full),
            pltpu.VMEM((views, rows, width), full),
            pltpu.VMEM((crops, width), full),
            pltpu.VMEM((ITERS, views, width), full),
            pltpu.VMEM((ITERS, count, views, width), full),
            pltpu.VMEM((views, width), full),
            pltpu.VMEM((8, width), full),
            pltpu.SemaphoreType.DMA((turns, count)),
            pltpu.SemaphoreType.DMA((turns, count)),
        ],
        compiler_params=pltpu.CompilerParams(
            collective_id=collective_id, has_side_effects=True, vmem_limit_bytes=54 * MIB
        ),
        name="sinkhorn",
    )(queue, centers, turned, pooled, hid, out, norms, live, lives, weigh, first)


def advance(weight, gradient, moment, average, trust):
    step_now = trust * gradient
    moment_new = momentum_rate * moment + step_now
    weight_new = weight - learn_rate * (step_now + momentum_rate * moment_new)
    average_new = average_rate * average + (1.0 - average_rate) * weight_new
    return (weight_new, moment_new, average_new)


def update_kernel(protos, *refs):
    g_first, g_mid, g_last, g_hid, g_out, vec, sq, centers = refs[:8]
    sources, targets = refs[8:26], refs[26:48]
    o_loss, o_count = refs[48:50]
    held, lows = refs[50:68], refs[68:72]
    proto_grad, norm_grad, square, load_sem, save_sem = refs[72:]
    o_loss[...] = vec[5:6, 0:1]
    o_count[...] = vec[5:6, 1:2]
    weights, moments, averages = held[:6], held[6:12], held[12:]
    w_outer, w_mid, w_hid, w_out, w_proto, w_norm = weights
    middle = g_first.shape[2]
    loads, saves = {}, []
    for which in (4, 2, 1, 0, 3, 5):
        loads[which] = []
        for part in range(3):
            index = 6 * part + which
            copy = pltpu.make_async_copy(sources[index], held[index], load_sem.at[index])
            copy.start()
            loads[which].append(copy)

    def trust_of(weights, grads):
        return trust_rate * jnp.sqrt(weights) / (jnp.sqrt(grads) + 1e-12)

    def put(which, at, grad, trust):
        new, moment, average = advance(
            weights[which][at],
            grad.astype(jnp.float32),
            moments[which][at],
            averages[which][at],
            trust,
        )
        weights[which][at] = new
        moments[which][at] = moment
        averages[which][at] = average
        if which < 4:
            lows[which][at] = new.astype(jnp.bfloat16)

    def load(which):
        for copy in loads[which]:
            copy.wait()

    def save(which):
        parts = [(held[6 * part + which], 6 * part + which) for part in range(3)]
        if which < 4:
            parts.append((lows[which], 18 + which))
        for source, index in parts:
            copy = pltpu.make_async_copy(source, targets[index], save_sem.at[index])
            copy.start()
            saves.append(copy)

    def matrix_trust(line, lane, share=1.0):
        grads = jnp.sum(sq[pl.ds(line, 1), :], 1, keepdims=True) * share
        return trust_of(vec[5:6, lane : lane + 1], grads)

    square[...] = jnp.zeros_like(square)
    load(4)
    fold = centers.shape[0]
    chunks = []
    for quarter in range(4):
        for start in range(0, fold, 256):
            here = quarter * fold + start
            size = min(256, fold - start, protos - here)
            if size > 0:
                chunks.append((pl.ds(here, size), pl.ds(start, size), pl.ds(quarter * LANES, LANES)))
    for at, lines, cols in chunks:
        weight, value = w_proto[at], centers[lines, cols].astype(jnp.float32)
        inverse = lax.rsqrt(jnp.sum(weight * weight, 1, keepdims=True) + unit_eps)
        unit = weight * inverse
        grad = inverse * (value - unit * jnp.sum(unit * value, 1, keepdims=True))
        proto_grad[at] = grad
        weigh(square, 0, weight)
        weigh(square, 1, grad)
    sums = jnp.sum(square[...], 1, keepdims=True)
    trust_proto = trust_of(sums[0:1], sums[1:2])
    for at, lines, cols in chunks:
        put(4, at, proto_grad[at], trust_proto)
    save(4)

    trust_hid = matrix_trust(3, 5)
    height = w_hid.shape[0] // 8 if w_hid.shape[0] >= 64 else 8
    load(2)

    def step_hid(index, carry):
        at = pl.ds(pl.multiple_of(index * height, 8), height)
        put(2, at, g_hid[at], trust_hid)
        return carry

    lax.fori_loop(0, w_hid.shape[0] // height, step_hid, 0)
    save(2)
    trust_mid = matrix_trust(1, 4)
    load(1)

    def step_mid(index, carry):
        put(1, index, g_mid[index], trust_mid)
        return carry

    lax.fori_loop(0, TAPS, step_mid, 0)
    save(1)
    load(0)
    for which, (grad, line) in enumerate(((g_first, 0), (g_last, 2))):
        trust = matrix_trust(line, 2 + which)
        height = grad.shape[1] // 4
        for index in range(4):
            lines = pl.ds(index * height, height)
            put(0, (which, lines), grad[0, lines], trust)
    save(0)
    load(3)
    whole = slice(None)
    put(3, whole, g_out[...], matrix_trust(4, 6, 0.25))
    save(3)

    for row, lines in enumerate((((0, 0), 1, 2), ((0, 1), 3, 4))):
        (line, half), wide, last = lines
        start = 2 * middle * half
        norm_grad[pl.ds(row, 1), pl.ds(0, 2 * middle)] = vec[line : line + 1, start : start + 2 * middle]
        size = vec.shape[1]
        norm_grad[pl.ds(row, 1), pl.ds(2 * middle, size)] = vec[wide : wide + 1, :]
        norm_grad[pl.ds(row, 1), pl.ds(2 * middle + size, size)] = vec[last : last + 1, :]
    load(5)
    weight, grad = w_norm[...], norm_grad[...]
    trust = trust_of(
        jnp.sum(weight * weight, 1, keepdims=True), jnp.sum(grad * grad, 1, keepdims=True)
    )
    put(5, whole, grad, trust)
    save(5)

    for copy in saves:
        copy.wait()


def update(grads, vec, sq, centers, weights, moments, averages):
    some = jax.ShapeDtypeStruct
    protos = weights[4].shape[0]
    shapes = tuple(some(value.shape, value.dtype) for value in weights)
    lows = tuple(some(value.shape, jnp.bfloat16) for value in weights[:4])
    vmem, anywhere = pl.BlockSpec(memory_space=pltpu.VMEM), pl.BlockSpec(memory_space=pl.ANY)
    results = pl.pallas_call(
        functools.partial(update_kernel, protos),
        out_shape=shapes * 3 + lows + (some((1, 1), jnp.float32),) * 2,
        in_specs=[vmem] * 8 + [anywhere] * 18,
        out_specs=(anywhere,) * 22 + (vmem,) * 2,
        scratch_shapes=[pltpu.VMEM(value.shape, value.dtype) for value in shapes * 3 + lows]
        + [
            pltpu.VMEM(weights[4].shape, jnp.float32),
            pltpu.VMEM(weights[5].shape, jnp.float32),
            pltpu.VMEM((8, LANES), jnp.float32),
            pltpu.SemaphoreType.DMA((18,)),
            pltpu.SemaphoreType.DMA((22,)),
        ],
        compiler_params=pltpu.CompilerParams(vmem_limit_bytes=56 * MIB),
        name="update",
    )(*grads, vec, sq, centers, *weights, *moments, *averages)
    return results


def per_device(
    sizes,
    big_maps,
    small_maps,
    live_counts,
    queue,
    bottleneck_outer,
    bottleneck_inner,
    proj_hidden,
    proj_out,
    prototypes,
    norm_params,
    mom_outer,
    mom_inner,
    mom_hidden,
    mom_out,
    mom_protos,
    mom_norms,
    avg_outer,
    avg_inner,
    avg_hidden,
    avg_out,
    avg_protos,
    avg_norms,
):
    n_dp, n_sub = sizes["dp"], sizes["sub"]
    exchange = Exchanger(sizes)
    images = big_maps.shape[0]
    channels = big_maps.shape[-1]
    middle = bottleneck_inner.shape[-1]
    hidden_width = proj_hidden.shape[1]
    out_width = proj_out.shape[1]
    proto_count = prototypes.shape[0]
    unit = max(512, 64 * n_dp)
    proto_width = -(-proto_count // unit) * unit
    share = hidden_width // n_sub

    image_mask = (jnp.arange(images) < live_counts[0]).astype(jnp.float32)[:, None]
    live_tile = jnp.broadcast_to(image_mask, (images, LANES))
    big = jnp.transpose(big_maps, (2, 3, 1, 0, 4)).reshape(-1, channels)
    small = jnp.transpose(small_maps, (2, 3, 1, 0, 4)).reshape(-1, channels)

    (
        inner_low, last_w, hidden_low, out_low, hidden_one, hidden_two, act_two, curve, normal,
        trunk_stat, pooled_all, lives, slopes, weights_sq, centers_low, turned, first_sums,
    ) = forward_trunk(
        n_dp,
        exchange.next_id(),
        images,
        bottleneck_outer,
        bottleneck_inner,
        proj_hidden,
        proj_out,
        big,
        small,
        norm_params,
        live_tile,
        queue,
        prototypes,
        proto_width,
    )

    grad_centers, d_hidden, d_out, pooled_back, extra = sinkhorn(
        sizes,
        exchange.next_id(),
        proto_count,
        queue,
        centers_low,
        turned,
        pooled_all,
        hidden_low.reshape(channels, share),
        out_low.reshape(share, out_width),
        norm_params,
        live_tile,
        lives,
        weights_sq,
        first_sums,
    )

    (
        shard_first, shard_inner, shard_last, shard_hidden, shard_out, centers_sum, vector, grad_sq,
    ) = backward_trunk(
        n_dp,
        exchange.next_id(),
        images,
        pooled_back,
        slopes,
        trunk_stat,
        norm_params,
        live_tile,
        lives,
        extra,
        d_hidden,
        d_out,
        grad_centers,
        big,
        small,
        curve,
        normal,
        hidden_one,
        hidden_two,
        act_two,
        last_w,
        inner_low,
    )
    results = update(
        (shard_first, shard_inner, shard_last, shard_hidden, shard_out),
        vector,
        grad_sq,
        centers_sum.reshape(proto_width // 4, 4 * out_width),
        (bottleneck_outer, bottleneck_inner, proj_hidden, proj_out, prototypes, norm_params),
        (mom_outer, mom_inner, mom_hidden, mom_out, mom_protos, mom_norms),
        (avg_outer, avg_inner, avg_hidden, avg_out, avg_protos, avg_norms),
    )
    return (results[22].reshape(()), results[23].reshape(())) + tuple(results[:22])


def solution(mesh):
    data = P(("dp", "sub"), None, None, None, None)
    trees = (P(None, "dp", None), P(None, "dp", None), P("dp", None), P("dp", None), P(), P())
    in_specs = (data, data, P(("dp", "sub")), P(None, ("dp", "sub"), None)) + trees * 3
    out_specs = (P(), P()) + trees * 3 + trees[:4]
    sizes = {axis: mesh.shape[axis] for axis in ("dp", "sub")}
    return jax.shard_map(
        functools.partial(per_device, sizes),
        mesh=mesh,
        in_specs=in_specs,
        out_specs=out_specs,
        check_vma=False,
    )
```
